32 devices in a mesh: seq: 8 (over z, y), head: 4 (over x, core).
Axes of the slice: x: 2, y: 2, z: 4, core: 2. Of those that a mesh axis runs over, the one named last changes fastest.
Arguments:
- tokens: bfloat16 [16384, 768], P(('seq', 'head')), may hold values from -6 to 6
- input_gain: float32 [768], replicated, may hold values from 0.25 to 1.75
- proj_gate: bfloat16 [768, 1536], P(None, 'head'), may hold values from -0.21875 to 0.21875
- proj_value: bfloat16 [768, 1536], P(None, 'head'), may hold values from -0.21875 to 0.21875
- proj_state: bfloat16 [768, 128], replicated, may hold values from -0.21875 to 0.21875
- proj_step: bfloat16 [2, 768, 24], P(None, None, 'head'), may hold values from -0.21875 to 0.21875
- step_bias: float32 [2, 24], P(None, 'head'), may hold values from -8.5 to -3
- decay_log: float32 [24], P('head'), may hold values from 0 to 2.3
- conv_value: float32 [4, 1536], P(None, 'head'), may hold values from -3 to 3
- conv_state: float32 [4, 128], replicated, may hold values from -3 to 3
- skip_gain: float32 [24], P('head'), may hold values from 0.5 to 1.5
- mixer_gain: float32 [1536], P('head'), may hold values from 0.25 to 1.75
- proj_out: bfloat16 [1536, 768], P('head'), may hold values from -0.15625 to 0.15625
- doc_lengths: int32 [64], replicated, may hold values from 1 to 4096, 16384 in all
- pad_mask: int32 [16384], P('seq'), may hold values 0 or 1
- cotangent: bfloat16 [16384, 768], P(('seq', 'head')), may hold values from -6 to 6
Outputs:
- layer_out: bfloat16 [16384, 768], P(('seq', 'head'))
- grad_tokens: bfloat16 [16384, 768], P(('seq', 'head'))
- grad_input_gain: float32 [768], replicated
- grad_proj_gate: float32 [768, 1536], P(None, 'head')
- grad_proj_value: float32 [768, 1536], P(None, 'head')
- grad_proj_state: float32 [768, 128], replicated
- grad_proj_step: float32 [2, 768, 24], P(None, None, 'head')
- grad_step_bias: float32 [2, 24], P(None, 'head')
- grad_decay_log: float32 [24], P('head')
- grad_conv_value: float32 [4, 1536], P(None, 'head')
- grad_conv_state: float32 [4, 128], replicated
- grad_skip_gain: float32 [24], P('head')
- grad_mixer_gain: float32 [1536], P('head')
- grad_proj_out: float32 [1536, 768], P('head')
The draws below stay inside these ranges and needn't reach their ends.
Inputs may be any that keep to these rules, and one draw needn't show every extreme that they name: `doc_lengths`: they sum to 16384, and the longest is exactly 4096.
All inputs are finite; a program needn't handle non-finite values. No bound on the sum of `pad_mask` on one device may be relied on, other than what follows from the above.
Results may differ from the reference program's by a relative error of at most 0.0089.
Values may be sent and summed in bfloat16 or wider, within the bound.
No kernel may reach another device: no remote copies, remote signals or barrier semaphores. Data moves between devices by JAX's collectives and lax.ppermute only.
A program may use at most 256 MiB of HBM per device.

```python
import math
import jax
import jax.numpy as jnp
import numpy as np
from jax import lax

D = 768
HEADS = 24
HDIM = 64
STATE = 64
CONV = 4
SPAN = 128
INNER = 1536
TOKENS = 16384
DOCS = 64
MAXLEN = 4096


def place_ends(array, rng, smallest, high):
    longest = array.shape.index(max(array.shape))
    spots = []
    for shift in (0, 1):
        where = [jax.random.randint(jax.random.fold_in(rng, axis), (), 0, length) for axis, length in enumerate(array.shape)]
        where[longest] = (where[longest] + shift) % array.shape[longest]
        spots.append(tuple(where))
    return array.at[spots[0]].set(smallest).at[spots[1]].set(high)


def block_scale(stream_key, dims, shards, smallest, top_value):
    def one(position, blocks):
        draws = jax.random.uniform(jax.random.fold_in(jax.random.fold_in(stream_key, 6), position), (blocks,), jnp.float32, smallest / len(shards), top_value / len(shards))
        return jnp.repeat(jnp.exp(draws), dims[position] // blocks).reshape((-1,) + (1,) * (len(dims) - position - 1))

    level = one(*shards[0])
    for cut in shards[1:]:
        level = level * one(*cut)
    return level


def split_up(count, total, bound, skew):
    loads = [(1 << 20) // math.isqrt(rank ** skew) + 1 for rank in range(2, count + 1)]
    spare, counts = total - bound - (count - 1), [1] * (count - 1)
    while spare > 0:
        free = [i for i in range(count - 1) if counts[i] < bound]
        pool, remaining = sum([loads[i] for i in free]), spare
        for i in free:
            addition = min(bound - counts[i], max(1, remaining * loads[i] // pool), spare)
            counts[i] = counts[i] + addition
            spare = spare - addition
    return np.array([bound] + counts)


def uneven_parts(own_key, amount, total, reach, skew):
    if amount == 2:
        one = jax.random.randint(own_key, (), max(1, total - reach), min(reach, total - 1) + 1)
        return jnp.stack([one, total - one])
    tallies = jnp.asarray(split_up(amount, total, reach, skew), jnp.int32)
    twos = (amount - 1) // 2
    source_of, sink = tallies[1:1 + 2 * twos:2], tallies[2:2 + 2 * twos:2]
    slack = jnp.minimum(source_of - 1, reach - sink)
    shifted = jax.random.randint(jax.random.fold_in(own_key, 1), (twos,), 0, 1 << 20) % (slack + 1)
    tallies = tallies.at[1:1 + 2 * twos:2].set(source_of - shifted).at[2:2 + 2 * twos:2].set(sink + shifted)
    return tallies[jax.random.permutation(jax.random.fold_in(own_key, 2), amount)]


def normal_values(own_key, dims, scale, bound, cuts=(), kind=jnp.bfloat16):
    values = jax.random.normal(own_key, dims, jnp.float32) * scale
    if len(cuts) > 0:
        values = block_scale(own_key, dims, cuts, -0.22, 0.18) * values
    return jnp.clip(values, min=-bound, max=bound).astype(kind)


def setup_inputs(seed: int = 0) -> dict:
    key_of = jax.random.split(jax.random.key(seed), 17)
    return {
        "tokens": normal_values(key_of[0], (TOKENS, D), 1.0, 6.0, ((0, 32),)),
        "input_gain": jnp.clip(1.0 + 0.15 * jax.random.normal(key_of[1], (D,), jnp.float32), 0.25, 1.75),
        "proj_gate": normal_values(key_of[2], (D, INNER), D ** -0.5, 0.21875, ((1, 4),)),
        "proj_value": normal_values(key_of[3], (D, INNER), D ** -0.5, 0.21875, ((1, 4),)),
        "proj_state": normal_values(key_of[4], (D, 2 * STATE), D ** -0.5, 0.21875),
        "proj_step": normal_values(key_of[5], (2, D, HEADS), D ** -0.5, 0.21875, ((2, 4),)),
        "step_bias": jnp.clip(-8.5 + 5.5 * jax.random.uniform(key_of[6], (2, HEADS), jnp.float32) ** block_scale(key_of[6], (2, HEADS), ((1, 4),), -0.2, 0.2), -8.5, -3.0),
        "decay_log": jnp.clip(2.3 * jax.random.uniform(key_of[7], (HEADS,), jnp.float32) ** block_scale(key_of[7], (HEADS,), ((0, 4),), -0.2, 0.2), 0.0, 2.3),
        "conv_value": normal_values(key_of[8], (CONV, INNER), 0.5, 3.0, ((1, 4),), jnp.float32),
        "conv_state": normal_values(key_of[9], (CONV, 2 * STATE), 0.5, 3.0, (), jnp.float32),
        "skip_gain": jnp.clip(0.5 + 1.0 * jax.random.uniform(key_of[10], (HEADS,), jnp.float32) ** block_scale(key_of[10], (HEADS,), ((0, 4),), -0.2, 0.2), 0.5, 1.5),
        "mixer_gain": jnp.clip(1.0 + 0.15 * jax.random.normal(key_of[11], (INNER,), jnp.float32), 0.25, 1.75),
        "proj_out": normal_values(key_of[12], (INNER, D), INNER ** -0.5, 0.15625, ((0, 4),)),
        "doc_lengths": uneven_parts(key_of[13], DOCS, TOKENS, MAXLEN, 2).astype(jnp.int32),
        "pad_mask": place_ends((jax.random.randint(key_of[14], (TOKENS,), 0, 16) < 15).astype(jnp.int32), jax.random.fold_in(key_of[14], 1), 0, 1),
        "cotangent": normal_values(key_of[15], (TOKENS, D), 1.0, 6.0, ((0, 32),)),
    }


PRECISE = lax.Precision.HIGHEST
EPSILON = 1e-05

@jax.custom_vjp
def low(v):
    return lax.optimization_barrier(v.astype(jnp.bfloat16)).astype(jnp.float32)

@jax.custom_vjp
def low_back(v):
    return v

def low_keep(v):
    return (low(v), None)

def low_pass(kept, grad):
    return (grad,)

def back_keep(v):
    return (v, None)

def back_low(kept, grad):
    return (low(grad),)
low.defvjp(low_keep, low_pass)
low_back.defvjp(back_keep, back_low)

def link_states(earlier, later):
    first_gate, first_state = earlier
    second_gate, second_state = later
    return (first_gate * second_gate, second_gate[..., None, None] * first_state + second_state)

def conv_rows(extended, kernel, start_flags, margin):
    length = extended.shape[0] - margin
    result = kernel[0] * extended[margin:]
    within = jnp.ones((length, 1), extended.dtype)
    for offset in range(1, margin + 1):
        within = within * (1.0 - start_flags[margin - offset + 1:margin - offset + 1 + length])[:, None]
        result = result + kernel[offset] * extended[margin - offset:margin - offset + length] * within
    return result

def block_parts(values, keys_in, queries, step_sizes, log_decay, starts, block_width):
    length, head_count, head_size = values.shape
    blocks = length // block_width
    values = values.reshape(blocks, block_width, head_count, head_size)
    keys_in = keys_in.reshape(blocks, block_width, -1)
    queries = queries.reshape(blocks, block_width, -1)
    step_sizes = step_sizes.reshape(blocks, block_width, head_count)
    running = jnp.cumsum(log_decay.reshape(blocks, block_width, head_count), axis=1)
    opened = jnp.cumsum(starts.reshape(blocks, block_width), axis=1)
    places = jnp.arange(block_width)
    paired = (places[:, None] > places[None, :])[None] & (opened[:, :, None] == opened[:, None, :])
    by_head = jnp.swapaxes(running, 1, 2)
    log_gaps = by_head[:, :, :, None] - by_head[:, :, None, :]
    decays = jnp.exp(jnp.where(paired[:, None], log_gaps, -1e+30))
    scores = jnp.einsum('ctn,csn->cts', queries, keys_in, precision=PRECISE)
    weighted = values * step_sizes[..., None]
    inside = jnp.einsum('chts,cshp->cthp', decays * scores[:, None], weighted, precision=PRECISE)
    final_log = running[:, -1, :]
    final_open = opened[:, -1]
    to_end = jnp.exp(jnp.where((opened == final_open[:, None])[:, :, None], final_log[:, None, :] - running, -1e+30))
    block_states = jnp.einsum('csn,cshp->chnp', keys_in, weighted * to_end[..., None], precision=PRECISE)
    block_gates = jnp.exp(final_log) * (final_open == 0)[:, None].astype(final_log.dtype)
    joined_gates, joined_states = lax.associative_scan(link_states, (block_gates, block_states), axis=0)
    prior_states = jnp.concatenate([jnp.zeros_like(joined_states[:1]), joined_states[:-1]], axis=0)
    entries = jnp.exp(running) * (opened == 0)[:, :, None].astype(running.dtype)
    carried = jnp.einsum('ctn,chnp->cthp', queries, prior_states, precision=PRECISE) * entries[..., None]
    output = (inside + carried).reshape(length, head_count, head_size)
    return (output, joined_gates[-1], joined_states[-1])

def all_heads(values, keys_in, queries, step_sizes, log_decay, starts):

    def one_head(operands):
        head_values, head_steps, head_logs = operands
        result, head_gate, head_state = block_parts(head_values[:, None, :], keys_in, queries, head_steps[:, None], head_logs[:, None], starts, SPAN)
        return result[:, 0, :]
    stacked = lax.map(jax.checkpoint(one_head), (jnp.swapaxes(values, 0, 1), jnp.swapaxes(step_sizes, 0, 1), jnp.swapaxes(log_decay, 0, 1)))
    return jnp.swapaxes(stacked, 0, 1)

def layer(tokens, input_gain, proj_gate, proj_value, proj_state, proj_step, step_bias, decay_log, conv_value, conv_state, skip_gain, mixer_gain, proj_out, forward_starts, backward_starts, live):
    row_count = tokens.shape[0]
    scale_rows = lax.rsqrt(lax.optimization_barrier(jnp.mean(tokens * tokens, axis=1, keepdims=True)) + EPSILON)
    normed = low(tokens * scale_rows * input_gain)
    gate_in = low_back(jnp.dot(normed, proj_gate, precision=PRECISE))
    value_in = low_back(jnp.dot(normed, proj_value, precision=PRECISE))
    state_in = low_back(jnp.dot(normed, proj_state, precision=PRECISE))
    step_raw = low_back(jnp.einsum('ld,kdh->lkh', normed, proj_step, precision=PRECISE))
    mixed_in = jnp.concatenate([value_in, state_in], axis=1)
    margin = conv_value.shape[0] - 1
    extended = jnp.concatenate([jnp.zeros((margin, mixed_in.shape[1]), mixed_in.dtype), mixed_in], axis=0)
    padded_flags = jnp.concatenate([jnp.zeros((margin,), forward_starts.dtype), forward_starts])
    kernel = jnp.concatenate([conv_value, conv_state], axis=1)
    activated = jax.nn.silu(conv_rows(extended, kernel, padded_flags, margin)) * live[:, None]
    inner_width = proj_value.shape[1]
    values = activated[:, :inner_width].reshape(row_count, HEADS, HDIM)
    keys_in = activated[:, inner_width:inner_width + STATE]
    queries = activated[:, inner_width + STATE:]
    step_sizes = jax.nn.softplus(step_raw + step_bias[None])
    log_decay = step_sizes * (-jnp.exp(decay_log))[None, None, :]
    ahead = all_heads(values, keys_in, queries, step_sizes[:, 0], log_decay[:, 0], forward_starts)
    behind = all_heads(values[::-1], keys_in[::-1], queries[::-1], step_sizes[::-1, 1], log_decay[::-1, 1], backward_starts)[::-1]
    mixed = (ahead + behind + skip_gain[None, :, None] * values).reshape(row_count, inner_width)
    gated = mixed * jax.nn.silu(gate_in)
    factor = lax.rsqrt(lax.optimization_barrier(jnp.mean(gated * gated, axis=1, keepdims=True)) + EPSILON)
    output_in = low(gated * factor * mixer_gain)
    return tokens + jnp.dot(output_in, proj_out, precision=PRECISE)

def reference(tokens, input_gain, proj_gate, proj_value, proj_state, proj_step, step_bias, decay_log, conv_value, conv_state, skip_gain, mixer_gain, proj_out, doc_lengths, pad_mask, cotangent):
    offsets = (jnp.cumsum(doc_lengths) - doc_lengths).astype(jnp.int32)
    places = jnp.arange(TOKENS + 1, dtype=jnp.int32)
    start_flags = (jnp.any(places[:, None] == offsets[None, :], axis=1) | (places == TOKENS)).astype(jnp.float32)
    forward_starts = start_flags[:TOKENS]
    backward_starts = start_flags[1:][::-1]
    live = pad_mask.astype(jnp.float32)
    params = [array_in.astype(jnp.float32) for array_in in (tokens, input_gain, proj_gate, proj_value, proj_state, proj_step, step_bias, decay_log, conv_value, conv_state, skip_gain, mixer_gain, proj_out)]

    def wrapped(*inputs):
        return layer(*inputs, forward_starts, backward_starts, live)
    result, pullback = jax.vjp(wrapped, *params)
    grads = pullback(cotangent.astype(jnp.float32))
    return (result.astype(jnp.bfloat16), grads[0].astype(jnp.bfloat16), grads[1], grads[2], grads[3], grads[4], grads[5], grads[6], grads[7], grads[8], grads[9], grads[10], grads[11], grads[12])
```

```python
from functools import partial

import jax
import jax.numpy as jnp
from jax import lax
from jax.experimental import pallas as pl
from jax.experimental.pallas import tpu as pltpu
from jax.sharding import PartitionSpec as P

SPAN = 128
HDIM = 64
LANES = 128
LONGEST = 4096
EPSILON = 1e-05
TINY = 1e-30
F32 = jnp.float32
BF16 = jnp.bfloat16
BLOCK = 256


def mm(a, b):
    return jnp.dot(a, b, preferred_element_type=F32)


def mm_nt(a, b):
    return lax.dot_general(a, b, (((1,), (1,)), ((), ())), preferred_element_type=F32)


def mm_tn(a, b):
    return lax.dot_general(a, b, (((0,), (0,)), ((), ())), preferred_element_type=F32)


def exact(a, b):
    return jnp.dot(a, b, precision=lax.Precision.HIGHEST, preferred_element_type=F32)


def exact_tn(a, b):
    return lax.dot_general(
        a, b, (((0,), (0,)), ((), ())), precision=lax.Precision.HIGHEST, preferred_element_type=F32
    )


def halves(v):
    high = v.astype(BF16)
    return high, (v - high.astype(F32)).astype(BF16)


def spread(v, ex):
    high, low = halves(v)
    return mm(high, ex) + mm(low, ex)


def gather_heads(v, ex):
    high, low = halves(v)
    return mm_nt(high, ex) + mm_nt(low, ex)


def sigmoid(v):
    return 1.0 / (1.0 + jnp.exp(-v))


def softplus(v):
    return jnp.maximum(v, 0.0) + jnp.log1p(jnp.exp(-jnp.abs(v)))


def iota(shape, dim):
    return lax.broadcasted_iota(jnp.int32, shape, dim)


def groups(width):
    found = []
    for at in range(0, width, LANES):
        wide = min(LANES, width - at)
        found.append((at, wide, [(at + k) // HDIM for k in range(0, wide, HDIM)]))
    return found


def stacked(v, wide):
    if wide == HDIM:
        return v
    first = iota(v.shape, 1) < HDIM
    zero = jnp.zeros_like(v)
    return jnp.concatenate([jnp.where(first, v, zero), jnp.where(first, zero, v)], axis=0)


def activated(conv, live):
    return conv * sigmoid(conv) * live


def front_kernel(
    nh,
    x_ref,
    halo_ref,
    gain_ref,
    wg_ref,
    wsv_ref,
    wst_ref,
    wstr_ref,
    pcol_ref,
    prow_ref,
    taps_ref,
    cols_ref,
    gm_ref,
    exf_ref,
    exb_ref,
    tril_ref,
    triu_ref,
    normed_ref,
    gate_ref,
    conv_ref,
    uv_ref,
    uvh_ref,
    z_ref,
    cc_ref,
    rowa_ref,
    rowp_ref,
    tot_ref,
    sf_ref,
    rb_ref,
    gf_ref,
    gb_ref,
    gfpre_ref,
    gbsuf_ref,
    gfsuf_ref,
    gbpre_ref,
    fmsg_ref,
    rmsg_ref,
    ubuf,
    state,
    incb,
):
    i = pl.program_id(0)
    tb = x_ref.shape[0]
    per = tb // SPAN
    nc = rb_ref.shape[0]

    def norm(x):
        xf = x.astype(F32)
        s = lax.rsqrt(jnp.mean(xf * xf, axis=1, keepdims=True) + EPSILON)
        return (xf * s * gain_ref[0:1, :]).astype(BF16)

    @pl.when(i == 0)
    def _():
        before = mm(norm(halo_ref[...]), wsv_ref[...])
        ubuf[0:8, :] = before
        uvh_ref[...] = before
        state[...] = jnp.zeros_like(state)

    @pl.when(i > 0)
    def _():
        ubuf[0:8, :] = ubuf[tb : tb + 8, :]

    nb = norm(x_ref[...])
    normed_ref[...] = nb
    gate_ref[...] = mm(nb, wg_ref[...])
    uv = mm(nb, wsv_ref[...])
    ubuf[8 : 8 + tb, :] = uv
    uv_ref[...] = uv.astype(BF16)
    conv = taps_ref[0:1, :] * uv
    for k in (1, 2, 3):
        conv = conv + taps_ref[k : k + 1, :] * ubuf[8 - k : 8 - k + tb, :] * cols_ref[:, k - 1 : k]
    conv_ref[...] = conv
    act = activated(conv, cols_ref[:, 3:4])
    z_all = mm(nb, wst_ref[...]) + pcol_ref[0:1, :]
    z_ref[...] = z_all
    zr_all = mm_nt(wstr_ref[...], nb)
    forward = iota((SPAN, LANES), 1) < nh
    forward_row = iota((16, SPAN), 0) < nh
    for j in range(per):
        rows = slice(j * SPAN, (j + 1) * SPAN)
        dt = softplus(z_all[rows])
        a = -dt * pcol_ref[1:2, :]
        total = exact(tril_ref[...], a)
        tot = total[SPAN - 1 : SPAN, :]
        cc = jnp.where(forward, total, total - a)
        cc_ref[rows, :] = cc
        tot8 = jnp.broadcast_to(tot, (8, LANES))
        tot_ref[j * 8 : j * 8 + 8, :] = tot8
        dtr = softplus(zr_all[:, rows] + prow_ref[:, :SPAN])
        ar = -dtr * prow_ref[:, SPAN:]
        run = exact(ar, triu_ref[...])
        rowa = jnp.where(forward_row, run, run - ar)
        ldt = jnp.log(jnp.maximum(dtr, TINY))
        rowa_ref[:, rows] = rowa
        rowp_ref[:, rows] = jnp.where(forward_row, rowa - ldt, rowa + ldt)
        gate8 = jnp.exp(tot8) * gm_ref[j * 8 : j * 8 + 8, :]
        gf = spread(gate8, exf_ref[...])
        gb = spread(gate8, exb_ref[...])
        keep = cols_ref[rows, :]
        w = (
            jnp.exp(jnp.where(forward, tot - cc, cc))
            * jnp.where(forward, keep[:, 6:7], keep[:, 8:9])
            * dt
        )
        x = act[rows, LANES:]
        b = act[rows, :HDIM].astype(BF16)
        c = i * per + j
        sf_ref[j] = state[...]
        state[...] = state[...] * gf[0:1, :] + mm_tn(b, (x * spread(w, exf_ref[...])).astype(BF16))
        incb[c] = mm_tn(b, (x * spread(w, exb_ref[...])).astype(BF16))
        gf_ref[c] = gf
        gb_ref[c] = gb

    @pl.when(i == pl.num_programs(0) - 1)
    def _():
        fmsg_ref[0:HDIM, :] = state[...]

        def up(c, carry):
            pf, pb = carry
            gfpre_ref[c] = pf
            gbpre_ref[c] = pb
            return pf * gf_ref[c], pb * gb_ref[c]

        one = jnp.ones(gf_ref.shape[1:], F32)
        pf, pb = lax.fori_loop(0, nc, up, (one, one))
        fmsg_ref[HDIM:, :] = pf
        rmsg_ref[HDIM:, :] = pb
        state[...] = jnp.zeros_like(state)

        def down(k, carry):
            c = nc - 1 - k
            pf, pb = carry
            gfsuf_ref[c] = pf
            gbsuf_ref[c] = pb
            rb_ref[c] = state[...]
            gb = gb_ref[c]
            state[...] = state[...] * gb[0:1, :] + incb[c]
            return pf * gf_ref[c], pb * gb

        lax.fori_loop(0, nc, down, (one, one))
        rmsg_ref[0:HDIM, :] = state[...]


def inner_kernel(
    nh,
    conv_ref,
    cols_ref,
    segrow_ref,
    cc_ref,
    rowp_ref,
    skip_ref,
    cot_ref,
    wo_ref,
    y_ref,
    dout_ref,
):
    tb, width = y_ref.shape
    dout_ref[...] = mm_nt(cot_ref[...], wo_ref[...])
    act = activated(conv_ref[...], cols_ref[:, 3:4])
    t_at = iota((SPAN, SPAN), 0)
    s_at = iota((SPAN, SPAN), 1)
    lower = t_at > s_at
    for j in range(tb // SPAN):
        rows = slice(j * SPAN, (j + 1) * SPAN)
        x = act[rows, LANES:]
        bc = act[rows, :LANES]
        b = bc[:, :HDIM].astype(BF16)
        c = pltpu.roll(bc, HDIM, 1)[:, :HDIM].astype(BF16)
        same = cols_ref[rows, 4:5] == segrow_ref[0:1, rows]
        score = jnp.where(same & (t_at != s_at), mm_nt(c, b), 0.0)
        cc = cc_ref[rows, :]
        for at, wide, heads in groups(width):
            xp = x[:, at : at + wide]
            mats = []
            for h in heads:
                gap = jnp.where(
                    lower,
                    cc[:, h : h + 1] - rowp_ref[h : h + 1, rows],
                    rowp_ref[nh + h : nh + h + 1, rows] - cc[:, nh + h : nh + h + 1],
                )
                mats.append((score * jnp.exp(gap)).astype(BF16))
            mats = jnp.concatenate(mats, axis=1) if len(mats) > 1 else mats[0]
            y_ref[rows, at : at + wide] = (
                mm(mats, stacked(xp.astype(BF16), wide)) + skip_ref[0:1, at : at + wide] * xp
            )


def merge_kernel(
    nh,
    conv_ref,
    cols_ref,
    cc_ref,
    tot_ref,
    sf_ref,
    rb_ref,
    gfpre_ref,
    gbsuf_ref,
    sent_ref,
    rent_ref,
    yin_ref,
    gate_ref,
    dout_ref,
    mg_ref,
    exf_ref,
    exb_ref,
    y_ref,
    stat_ref,
    sfull_ref,
    rfull_ref,
):
    tb, width = y_ref.shape
    forward = iota((SPAN, LANES), 1) < nh
    which = iota((8, width), 0)
    sel0 = jnp.where(which == 0, 1.0, 0.0).astype(BF16)
    sel1 = jnp.where(which == 1, 1.0, 0.0).astype(BF16)
    for j in range(tb // SPAN):
        rows = slice(j * SPAN, (j + 1) * SPAN)
        keep = cols_ref[rows, :]
        bc = activated(conv_ref[rows, :LANES], keep[:, 3:4])
        c = pltpu.roll(bc, HDIM, 1)[:, :HDIM].astype(BF16)
        cc = cc_ref[rows, :]
        tot = tot_ref[j * 8 : j * 8 + 1, :]
        w = jnp.exp(jnp.where(forward, cc, tot - cc)) * jnp.where(
            forward, keep[:, 5:6], keep[:, 7:8]
        )
        sfull = (sf_ref[j] + gfpre_ref[j][0:1, :] * sent_ref[...]).astype(BF16)
        rfull = (rb_ref[j] + gbsuf_ref[j][0:1, :] * rent_ref[...]).astype(BF16)
        sfull_ref[j] = sfull
        rfull_ref[j] = rfull
        y = (
            yin_ref[rows, :]
            + mm(c, sfull) * spread(w, exf_ref[...])
            + mm(c, rfull) * spread(w, exb_ref[...])
        )
        y_ref[rows, :] = y
        gate = gate_ref[rows, :]
        g = y * gate * sigmoid(gate)
        high, low = halves(g * g)
        stat = mm_nt(sel0, high) + mm_nt(sel0, low)
        high, low = halves(dout_ref[rows, :] * mg_ref[0:1, :] * g)
        stat_ref[:, rows] = stat + mm_nt(sel1, high) + mm_nt(sel1, low)


def turn_kernel(
    nh,
    inner,
    y_ref,
    gate_ref,
    dout_ref,
    mg_ref,
    stat_ref,
    conv_ref,
    cols_ref,
    cc_ref,
    tot_ref,
    gf_ref,
    gb_ref,
    gtf_ref,
    gtb_ref,
    exf_ref,
    exb_ref,
    eye_ref,
    dy_ref,
    dgate_ref,
    outin_ref,
    gmix_ref,
    gskip_ref,
    dso_ref,
    dro_ref,
    amsg_ref,
    bmsg_ref,
    state,
    incf,
):
    i = pl.program_id(0)
    tb, width = y_ref.shape
    per = tb // SPAN
    nc = dso_ref.shape[0]
    forward = iota((SPAN, LANES), 1) < nh

    @pl.when(i == 0)
    def _():
        gmix_ref[...] = jnp.zeros_like(gmix_ref)
        gskip_ref[...] = jnp.zeros_like(gskip_ref)
        state[...] = jnp.zeros_like(state)

    for j in range(per):
        rows = slice(j * SPAN, (j + 1) * SPAN)
        stats = exact_tn(stat_ref[:, rows], eye_ref[0:8, :])
        q = lax.rsqrt(stats[:, 0:1] * (1.0 / inner) + EPSILON)
        k3 = q * q * q * stats[:, 1:2] * (1.0 / inner)
        y = y_ref[rows, :]
        gate = gate_ref[rows, :]
        sig = sigmoid(gate)
        sg = gate * sig
        g = y * sg
        gq = g * q
        dout = dout_ref[rows, :]
        outin_ref[rows, :] = (gq * mg_ref[0:1, :]).astype(BF16)
        gmix_ref[0:1, :] += jnp.sum(dout * gq, axis=0, keepdims=True)
        dg = dout * mg_ref[0:1, :] * q - g * k3
        dy = dg * sg
        dyb = dy.astype(BF16)
        dy_ref[rows, :] = dyb
        dgate_ref[rows, :] = (dg * y * sig * (1.0 + gate * (1.0 - sig))).astype(BF16)
        keep = cols_ref[rows, :]
        act = activated(conv_ref[rows, :], keep[:, 3:4])
        gskip_ref[0:1, :] += jnp.sum(dy * act[:, LANES:], axis=0, keepdims=True)
        c = pltpu.roll(act[:, :LANES], HDIM, 1)[:, :HDIM].astype(BF16)
        cc = cc_ref[rows, :]
        tot = tot_ref[j * 8 : j * 8 + 1, :]
        w = jnp.exp(jnp.where(forward, cc, tot - cc)) * jnp.where(
            forward, keep[:, 5:6], keep[:, 7:8]
        )
        dyf = dyb.astype(F32)
        at = i * per + j
        incf[at] = mm_tn(c, (dyf * spread(w, exf_ref[...])).astype(BF16))
        dro_ref[j] = state[...]
        state[...] = state[...] * gb_ref[at][0:1, :] + mm_tn(
            c, (dyf * spread(w, exb_ref[...])).astype(BF16)
        )

    @pl.when(i == pl.num_programs(0) - 1)
    def _():
        bmsg_ref[0:HDIM, :] = state[...]
        bmsg_ref[HDIM:, :] = gtb_ref[...]
        amsg_ref[HDIM:, :] = gtf_ref[...]
        state[...] = jnp.zeros_like(state)

        def down(k, _):
            c = nc - 1 - k
            dso_ref[c] = state[...]
            state[...] = state[...] * gf_ref[c][0:1, :] + incf[c]
            return 0

        lax.fori_loop(0, nc, down, 0)
        amsg_ref[0:HDIM, :] = state[...]


def back_kernel(
    nh,
    conv_ref,
    cols_ref,
    halocols_ref,
    segrow_ref,
    cc_ref,
    z_ref,
    rowa_ref,
    tot_ref,
    dy_ref,
    sfull_ref,
    rfull_ref,
    dso_ref,
    dro_ref,
    gfsuf_ref,
    gbpre_ref,
    dsent_ref,
    drent_ref,
    gf_ref,
    gb_ref,
    uv_ref,
    uvh_ref,
    taps_ref,
    skip_ref,
    pcol_ref,
    exf_ref,
    exb_ref,
    tril_ref,
    triu_ref,
    eye_ref,
    dvs_ref,
    dst_ref,
    duh_ref,
    gconv_ref,
    gsmall_ref,
    dbuf,
    hbuf,
):
    i = pl.program_id(0)
    last = pl.num_programs(0) - 1
    tb = conv_ref.shape[0]
    width = conv_ref.shape[1] - LANES
    exf = exf_ref[...]
    exb = exb_ref[...]

    @pl.when(i == 0)
    def _():
        dbuf[tb : tb + 8, :] = jnp.zeros((8, LANES + width), F32)
        gconv_ref[...] = jnp.zeros_like(gconv_ref)
        gsmall_ref[...] = jnp.zeros_like(gsmall_ref)

    s_at = iota((SPAN, SPAN), 0)
    t_at = iota((SPAN, SPAN), 1)
    lower = t_at > s_at
    lane = iota((SPAN, LANES), 1)
    forward = lane < nh
    row16 = iota((16, SPAN), 0)
    front_half = lane < HDIM
    for j in reversed(range(tb // SPAN)):
        rows = slice(j * SPAN, (j + 1) * SPAN)
        keep = cols_ref[rows, :]
        conv = conv_ref[rows, :]
        sig = sigmoid(conv)
        act = conv * sig * keep[:, 3:4]
        xb = act[:, LANES:].astype(BF16)
        x = xb.astype(F32)
        dyb = dy_ref[rows, :]
        dy = dyb.astype(F32)
        bc = act[:, :LANES]
        cb = pltpu.roll(bc, HDIM, 1)
        b = bc[:, :HDIM].astype(BF16)
        c = cb[:, :HDIM].astype(BF16)
        cpad = jnp.where(front_half, cb, 0.0).astype(BF16)
        bpad = jnp.where(front_half, 0.0, cb).astype(BF16)
        within = (keep[:, 4:5] == segrow_ref[0:1, rows]) & (t_at != s_at)
        score = jnp.where(within, mm_nt(b, c), 0.0)
        cc = cc_ref[rows, :]
        z = z_ref[rows, :]
        dt = softplus(z)
        ldt = jnp.log(jnp.maximum(dt, TINY))
        pc = jnp.where(forward, cc - ldt, cc + ldt)
        dscore = jnp.zeros((SPAN, SPAN), F32)
        kc = jnp.zeros((SPAN, LANES), F32)
        qr = jnp.zeros((16, SPAN), F32)
        dx_parts = []
        for at, wide, heads in groups(width):
            dyp = dyb[:, at : at + wide]
            dmats = mm_nt(stacked(xb[:, at : at + wide], wide), dyp)
            mats = []
            for n, h in enumerate(heads):
                dmat = dmats[n * SPAN : (n + 1) * SPAN, :]
                decay = jnp.exp(
                    jnp.where(
                        lower,
                        rowa_ref[h : h + 1, rows] - pc[:, h : h + 1],
                        pc[:, nh + h : nh + h + 1] - rowa_ref[nh + h : nh + h + 1, rows],
                    )
                )
                spot = dmat * decay
                dscore = dscore + spot
                mats.append((score * decay).astype(BF16))
                pull = spot * score
                pull_low = jnp.where(lower, pull, 0.0)
                pull_up = pull - pull_low
                qr = jnp.where(row16 == h, jnp.sum(pull_low, axis=0, keepdims=True), qr)
                qr = jnp.where(row16 == nh + h, jnp.sum(pull_up, axis=0, keepdims=True), qr)
                kc = jnp.where(lane == h, jnp.sum(pull_low, axis=1, keepdims=True), kc)
                kc = jnp.where(lane == nh + h, jnp.sum(pull_up, axis=1, keepdims=True), kc)
            mats = jnp.concatenate(mats, axis=1) if len(mats) > 1 else mats[0]
            dx_parts.append(mm(mats, stacked(dyp, wide)))
        dscore = jnp.where(within, dscore, 0.0).astype(BF16)
        dbc = mm(dscore, cpad) + mm_tn(dscore, bpad)
        dx = jnp.concatenate(dx_parts, axis=1) if len(dx_parts) > 1 else dx_parts[0]

        tot = tot_ref[j * 8 : j * 8 + 1, :]
        to = jnp.exp(jnp.where(forward, tot - cc, cc)) * dt
        to = to * jnp.where(forward, keep[:, 6:7], keep[:, 8:9])
        fro = jnp.exp(jnp.where(forward, cc, tot - cc)) * jnp.where(
            forward, keep[:, 5:6], keep[:, 7:8]
        )
        dsfull = dso_ref[j] + gfsuf_ref[j][0:1, :] * dsent_ref[...]
        drfull = dro_ref[j] + gbpre_ref[j][0:1, :] * drent_ref[...]
        carried = jnp.zeros((SPAN, LANES), F32)
        leaving = jnp.zeros((SPAN, LANES), F32)
        through = jnp.zeros((8, LANES), F32)
        for ex, held, dheld, gates in (
            (exf, sfull_ref[j], dsfull, gf_ref[j]),
            (exb, rfull_ref[j], drfull, gb_ref[j]),
        ):
            to_wide = spread(to, ex)
            fro_wide = spread(fro, ex)
            dheld_low = dheld.astype(BF16)
            nothing = jnp.zeros_like(held)
            dbc = dbc + mm_nt(
                (x * to_wide).astype(BF16), jnp.concatenate([dheld_low, nothing], axis=0)
            )
            dbc = dbc + mm_nt(
                (dy * fro_wide).astype(BF16), jnp.concatenate([nothing, held], axis=0)
            )
            flow = mm(b, dheld_low) * to_wide
            dx = dx + flow
            carried = carried + gather_heads(dy * (mm(c, held) * fro_wide), ex)
            leaving = leaving + gather_heads(x * flow, ex)
            product = jnp.sum(dheld * held.astype(F32), axis=0, keepdims=True) * gates
            through = through + gather_heads(product, ex)
        moved = exact_tn(qr, eye_ref[...]) + carried - kc
        before = exact(tril_ref[...], jnp.where(forward, leaving, moved))
        after = exact(triu_ref[...], jnp.where(forward, moved, leaving))
        dlog = before + after - leaving + through[0:1, :]
        sigz = sigmoid(z)
        rate = pcol_ref[1:2, :]
        dstep = (kc + leaving) * (sigz / jnp.maximum(dt, TINY)) - dlog * rate * sigz
        dst_ref[rows, :] = dstep.astype(BF16)
        gsmall_ref[0:1, :] += jnp.sum(dstep, axis=0, keepdims=True)
        gsmall_ref[1:2, :] += jnp.sum(-dlog * dt * rate, axis=0, keepdims=True)
        dact = jnp.concatenate([dbc, dx + skip_ref[0:1, :] * dy], axis=1)
        dbuf[rows, :] = dact * keep[:, 3:4] * sig * (1.0 + conv * (1.0 - sig))

    dconv = dbuf[0:tb, :]
    uv = uv_ref[...].astype(F32)
    du = taps_ref[0:1, :] * dconv
    gconv_ref[0:1, :] += jnp.sum(uv * dconv, axis=0, keepdims=True)
    for k in (1, 2, 3):
        shifted = dbuf[k : k + tb, :] * cols_ref[:, 8 + k : 9 + k]
        du = du + taps_ref[k : k + 1, :] * shifted
        gconv_ref[k : k + 1, :] += jnp.sum(uv * shifted, axis=0, keepdims=True)
    dvs_ref[...] = du.astype(BF16)
    edge = dbuf[0:8, :]
    dbuf[tb : tb + 8, :] = edge

    @pl.when(i == last)
    def _():
        hbuf[0:8, :] = jnp.zeros_like(edge)
        hbuf[8:16, :] = edge
        duh = jnp.zeros_like(edge)
        for k in (1, 2, 3):
            shifted = hbuf[k : k + 8, :] * halocols_ref[:, k - 1 : k]
            duh = duh + taps_ref[k : k + 1, :] * shifted
            gconv_ref[k : k + 1, :] += jnp.sum(uvh_ref[...] * shifted, axis=0, keepdims=True)
        duh_ref[...] = duh


def whole(shape):
    return pl.BlockSpec(shape, lambda i: (0,) * len(shape))


def row_block(rows, width):
    return pl.BlockSpec((rows, width), lambda i: (i, 0))


def lane_block(rows, width):
    return pl.BlockSpec((rows, width), lambda i: (0, i))


def chunk_block(per, rows, width):
    return pl.BlockSpec((per, rows, width), lambda i: (i, 0, 0))


def sds(shape, dtype):
    return jax.ShapeDtypeStruct(shape, dtype)


def call(kernel, name, grid, ins, outs, scratch, flops, operands):
    moved = sum(o.size * o.dtype.itemsize for o in operands)
    moved += sum(s.size * s.dtype.itemsize for _, s in outs)
    return pl.pallas_call(
        kernel,
        name=name,
        grid=(grid,),
        in_specs=ins,
        out_specs=[spec for spec, _ in outs],
        out_shape=[shape for _, shape in outs],
        scratch_shapes=scratch,
        compiler_params=pltpu.CompilerParams(
            dimension_semantics=("arbitrary",), vmem_limit_bytes=56 * 1024 * 1024
        ),
        cost_estimate=pl.CostEstimate(
            flops=int(flops), bytes_accessed=int(moved), transcendentals=0
        ),
    )(*operands)


def shifted_in(array, axis, by):
    length = lax.axis_size(axis)
    pairs = [(i, i + by) for i in range(length) if 0 <= i + by < length]
    return lax.ppermute(array, axis, pairs)


def entering(message, hops, sign):
    parts = [shifted_in(message, "seq", sign * d) for d in range(1, hops + 1)]
    state = parts[-1][:HDIM]
    for part in reversed(parts[:-1]):
        state = part[:HDIM] + part[HDIM : HDIM + 1] * state
    return state


def sum_over(array, axis):
    size = lax.axis_size(axis)
    result = array
    for k in range(1, size):
        result = result + lax.ppermute(array, axis, [(i, i ^ k) for i in range(size)])
    return result


def per_device(
    tokens,
    input_gain,
    proj_gate,
    proj_value,
    proj_state,
    proj_step,
    step_bias,
    decay_log,
    conv_value,
    conv_state,
    skip_gain,
    mixer_gain,
    proj_out,
    doc_lengths,
    pad_mask,
    cotangent,
):
    head_devices = lax.axis_size("head")
    length = pad_mask.shape[0]
    model = tokens.shape[1]
    width = proj_gate.shape[1]
    nh = proj_step.shape[2]
    inner = width * head_devices
    nc = length // SPAN
    tb = BLOCK
    per = tb // SPAN
    grid = length // tb
    wide = LANES + width
    hops = -(-(LONGEST - 1) // length)
    seq_index = lax.axis_index("seq")
    first_place = seq_index * length
    all_tokens = length * lax.axis_size("seq")

    gathered = lax.all_gather(tokens, "head", axis=0, tiled=True)
    cot_all = lax.all_gather(cotangent, "head", axis=0, tiled=True)
    halo = shifted_in(gathered[length - 8 :], "seq", 1)

    offsets = jnp.cumsum(doc_lengths) - doc_lengths
    offsets = jnp.concatenate([offsets, jnp.full((1,), all_tokens, offsets.dtype)])
    places = first_place - 8 + jnp.arange(length + 16, dtype=jnp.int32)
    segs = jnp.sum((offsets[None, :] <= places[:, None]).astype(jnp.int32), axis=1).astype(F32)
    seg = segs[8 : 8 + length]
    by_chunk = seg.reshape(nc, SPAN)
    chunk_first = by_chunk[:, 0]
    chunk_last = by_chunk[:, -1]
    prev_last = jnp.concatenate([segs[7:8], chunk_last[:-1]])
    next_first = jnp.concatenate([chunk_first[1:], segs[8 + length : 9 + length]])
    live = pad_mask.astype(F32)

    def tap_mask(at, k):
        return (seg == segs[8 + at : 8 + at + length]).astype(F32)

    def edge_mask(edge):
        return (by_chunk == edge[:, None]).astype(F32).reshape(length)

    zeros = jnp.zeros((length,), F32)
    cols = jnp.stack(
        [tap_mask(-k, k) for k in (1, 2, 3)]
        + [live, seg]
        + [edge_mask(prev_last), edge_mask(chunk_last), edge_mask(next_first), edge_mask(chunk_first)]
        + [tap_mask(k, k) for k in (1, 2, 3)]
        + [zeros] * 4,
        axis=1,
    )
    halo_cols = jnp.stack(
        [(segs[:8] == segs[k : 8 + k]).astype(F32) for k in (1, 2, 3)] + [jnp.zeros((8,), F32)] * 13,
        axis=1,
    )
    seg_row = jnp.broadcast_to(seg[None, :], (8, length))
    lanes = jnp.arange(LANES)
    gate_mask = jnp.where(
        lanes[None, :] < nh,
        (chunk_last == prev_last).astype(F32)[:, None],
        (chunk_first == next_first).astype(F32)[:, None],
    )
    gate_mask = jnp.broadcast_to(gate_mask[:, None, :], (nc, 8, LANES)).reshape(nc * 8, LANES)
    head_of = jnp.arange(width)[None, :] // HDIM
    exf = (lanes[:, None] == head_of).astype(BF16)
    exb = (lanes[:, None] == head_of + nh).astype(BF16)
    at = jnp.arange(SPAN)
    tril = (at[:, None] >= at[None, :]).astype(F32)
    triu = (at[:, None] <= at[None, :]).astype(F32)
    eye = (jnp.arange(16)[:, None] == lanes[None, :]).astype(F32)

    rate = jnp.exp(decay_log)
    bias_line = jnp.concatenate([step_bias[0], step_bias[1]])
    rate_line = jnp.concatenate([rate, rate])
    pcol = jnp.zeros((8, LANES), F32)
    pcol = pcol.at[0, : 2 * nh].set(bias_line).at[1, : 2 * nh].set(rate_line)
    pad16 = jnp.zeros((16 - 2 * nh,), F32)
    prow = jnp.concatenate(
        [
            jnp.broadcast_to(jnp.concatenate([bias_line, pad16])[:, None], (16, SPAN)),
            jnp.broadcast_to(jnp.concatenate([rate_line, pad16])[:, None], (16, SPAN)),
        ],
        axis=1,
    )
    steps = jnp.concatenate([proj_step[0], proj_step[1]], axis=1)
    wst = jnp.pad(steps, ((0, 0), (0, LANES - 2 * nh)))
    wstr = jnp.pad(steps.T, ((0, 16 - 2 * nh), (0, 0)))
    wsv = jnp.concatenate([proj_state, proj_value], axis=1)
    taps = jnp.pad(jnp.concatenate([conv_state, conv_value], axis=1), ((0, 4), (0, 0)))
    gain = jnp.broadcast_to(input_gain[None, :], (8, model))
    mg = jnp.broadcast_to(mixer_gain[None, :], (8, width))
    skip = jnp.broadcast_to(jnp.repeat(skip_gain, HDIM)[None, :], (8, width))

    rows = partial(row_block, tb)
    states = sds((nc, HDIM, width), F32)
    gates = sds((nc, 8, width), F32)
    message = sds((HDIM + 8, width), F32)
    state_block = chunk_block(per, HDIM, width)
    gate_block = chunk_block(per, 8, width)
    tot_block = row_block(per * 8, LANES)

    (
        normed,
        gate_in,
        conv,
        uv,
        uvh,
        z,
        cc,
        rowa,
        rowp,
        tot,
        sf,
        rb,
        gf,
        gb,
        gfpre,
        gbsuf,
        gfsuf,
        gbpre,
        fmsg,
        rmsg,
    ) = call(
        partial(front_kernel, nh),
        "front",
        grid,
        [
            rows(model),
            whole((8, model)),
            whole((8, model)),
            whole((model, width)),
            whole((model, wide)),
            whole((model, LANES)),
            whole((16, model)),
            whole((8, LANES)),
            whole((16, 2 * SPAN)),
            whole((8, wide)),
            rows(16),
            tot_block,
            whole((LANES, width)),
            whole((LANES, width)),
            whole((SPAN, SPAN)),
            whole((SPAN, SPAN)),
        ],
        [
            (rows(model), sds((length, model), BF16)),
            (rows(width), sds((length, width), F32)),
            (rows(wide), sds((length, wide), F32)),
            (rows(wide), sds((length, wide), BF16)),
            (whole((8, wide)), sds((8, wide), F32)),
            (rows(LANES), sds((length, LANES), F32)),
            (rows(LANES), sds((length, LANES), F32)),
            (lane_block(16, tb), sds((16, length), F32)),
            (lane_block(16, tb), sds((16, length), F32)),
            (tot_block, sds((nc * 8, LANES), F32)),
            (state_block, states),
            (whole(states.shape), states),
            (whole(gates.shape), gates),
            (whole(gates.shape), gates),
            (whole(gates.shape), gates),
            (whole(gates.shape), gates),
            (whole(gates.shape), gates),
            (whole(gates.shape), gates),
            (whole(message.shape), message),
            (whole(message.shape), message),
        ],
        [
            pltpu.VMEM((tb + 8, wide), F32),
            pltpu.VMEM((HDIM, width), F32),
            pltpu.VMEM((nc, HDIM, width), F32),
        ],
        2 * length * model * (2 * width + 3 * LANES),
        [
            gathered,
            halo,
            gain,
            proj_gate,
            wsv,
            wst,
            wstr,
            pcol,
            prow,
            taps,
            cols,
            gate_mask,
            exf,
            exb,
            tril,
            triu,
        ],
    )

    sent = entering(fmsg, hops, 1)
    rent = entering(rmsg, hops, -1)

    yin, dout = call(
        partial(inner_kernel, nh),
        "inner",
        grid,
        [
            rows(wide),
            rows(16),
            lane_block(8, tb),
            rows(LANES),
            lane_block(16, tb),
            whole((8, width)),
            rows(model),
            whole((width, model)),
        ],
        [
            (rows(width), sds((length, width), F32)),
            (rows(width), sds((length, width), F32)),
        ],
        [],
        2 * length * width * (model + 2 * SPAN),
        [conv, cols, seg_row, cc, rowp, skip, cot_all, proj_out],
    )

    y, stat, sfull, rfull = call(
        partial(merge_kernel, nh),
        "merge",
        grid,
        [
            row_block(tb, LANES),
            rows(16),
            rows(LANES),
            tot_block,
            state_block,
            state_block,
            gate_block,
            gate_block,
            whole((HDIM, width)),
            whole((HDIM, width)),
            rows(width),
            rows(width),
            rows(width),
            whole((8, width)),
            whole((LANES, width)),
            whole((LANES, width)),
        ],
        [
            (rows(width), sds((length, width), F32)),
            (lane_block(8, tb), sds((8, length), F32)),
            (state_block, sds((nc, HDIM, width), BF16)),
            (state_block, sds((nc, HDIM, width), BF16)),
        ],
        [],
        2 * length * width * 2 * (HDIM + LANES),
        [conv, cols, cc, tot, sf, rb, gfpre, gbsuf, sent, rent, yin, gate_in, dout, mg, exf, exb],
    )

    stat = sum_over(stat, "head")

    dy, dgate, outin, gmix, gskip, dso, dro, amsg, bmsg = call(
        partial(turn_kernel, nh, inner),
        "turn",
        grid,
        [
            rows(width),
            rows(width),
            rows(width),
            whole((8, width)),
            lane_block(8, tb),
            rows(wide),
            rows(16),
            rows(LANES),
            tot_block,
            whole(gates.shape),
            whole(gates.shape),
            whole((8, width)),
            whole((8, width)),
            whole((LANES, width)),
            whole((LANES, width)),
            whole((16, LANES)),
        ],
        [
            (rows(width), sds((length, width), BF16)),
            (rows(width), sds((length, width), BF16)),
            (rows(width), sds((length, width), BF16)),
            (whole((8, width)), sds((8, width), F32)),
            (whole((8, width)), sds((8, width), F32)),
            (whole(states.shape), states),
            (state_block, states),
            (whole(message.shape), message),
            (whole(message.shape), message),
        ],
        [pltpu.VMEM((HDIM, width), F32), pltpu.VMEM((nc, HDIM, width), F32)],
        2 * length * width * 2 * (HDIM + LANES),
        [
            y,
            gate_in,
            dout,
            mg,
            stat,
            conv,
            cols,
            cc,
            tot,
            gf,
            gb,
            fmsg[HDIM:],
            rmsg[HDIM:],
            exf,
            exb,
            eye,
        ],
    )

    dsent = entering(amsg, hops, -1)
    drent = entering(bmsg, hops, 1)

    back = lambda i: grid - 1 - i

    def rev(spec):
        return pl.BlockSpec(spec.block_shape, lambda i: spec.index_map(back(i)))

    dvs, dst, duh, gconv, gsmall = call(
        partial(back_kernel, nh),
        "back",
        grid,
        [
            rev(rows(wide)),
            rev(rows(16)),
            whole((8, 16)),
            rev(lane_block(8, tb)),
            rev(rows(LANES)),
            rev(rows(LANES)),
            rev(lane_block(16, tb)),
            rev(tot_block),
            rev(rows(width)),
            rev(state_block),
            rev(state_block),
            rev(state_block),
            rev(state_block),
            rev(gate_block),
            rev(gate_block),
            whole((HDIM, width)),
            whole((HDIM, width)),
            rev(gate_block),
            rev(gate_block),
            rev(rows(wide)),
            whole((8, wide)),
            whole((8, wide)),
            whole((8, width)),
            whole((8, LANES)),
            whole((LANES, width)),
            whole((LANES, width)),
            whole((SPAN, SPAN)),
            whole((SPAN, SPAN)),
            whole((16, LANES)),
        ],
        [
            (rev(rows(wide)), sds((length, wide), BF16)),
            (rev(rows(LANES)), sds((length, LANES), BF16)),
            (whole((8, wide)), sds((8, wide), F32)),
            (whole((8, wide)), sds((8, wide), F32)),
            (whole((8, LANES)), sds((8, LANES), F32)),
        ],
        [pltpu.VMEM((tb + 8, wide), F32), pltpu.VMEM((16, wide), F32)],
        2 * length * width * (4 * SPAN + 6 * HDIM + 8 * LANES),
        [
            conv,
            cols,
            halo_cols,
            seg_row,
            cc,
            z,
            rowa,
            tot,
            dy,
            sfull,
            rfull,
            dso,
            dro,
            gfsuf,
            gbpre,
            dsent,
            drent,
            gf,
            gb,
            uv,
            uvh,
            taps,
            skip,
            pcol,
            exf,
            exb,
            tril,
            triu,
            eye,
        ],
    )

    returned = shifted_in(duh, "seq", -1)
    dvs = dvs.at[length - 8 :].add(returned.astype(BF16))

    mixer = lax.psum_scatter(
        jnp.dot(outin, proj_out, preferred_element_type=F32).astype(BF16),
        "head",
        scatter_dimension=0,
        tiled=True,
    )
    layer_out = (tokens.astype(F32) + mixer.astype(F32)).astype(BF16)

    def weight_grad(a, b):
        return lax.dot_general(a, b, (((0,), (0,)), ((), ())), preferred_element_type=F32)

    grad_proj_out = weight_grad(outin, cot_all)
    grad_proj_gate = weight_grad(normed, dgate)
    grad_vs = weight_grad(normed, dvs)
    grad_st = weight_grad(normed, dst)

    def back_dot(a, w):
        return lax.dot_general(a, w, (((1,), (1,)), ((), ())), preferred_element_type=F32)

    partial_in = back_dot(dgate, proj_gate) + back_dot(dvs, wsv) + back_dot(dst, wst)
    grad_gain = jnp.sum(partial_in * normed.astype(F32), axis=0) / input_gain
    own_in = lax.psum_scatter(
        partial_in.astype(BF16), "head", scatter_dimension=0, tiled=True
    ).astype(F32)
    token_values = tokens.astype(F32)
    scale_rows = lax.rsqrt(jnp.mean(token_values * token_values, axis=1, keepdims=True) + EPSILON)
    scaled = own_in * input_gain
    grad_tokens = (
        cotangent.astype(F32)
        + scale_rows * scaled
        - token_values * scale_rows**3 * jnp.mean(scaled * token_values, axis=1, keepdims=True)
    ).astype(BF16)

    grad_bias = gsmall[0, : 2 * nh].reshape(2, nh)
    grad_decay = gsmall[1, :nh] + gsmall[1, nh : 2 * nh]
    seq_sums = lax.psum(
        (
            grad_proj_gate,
            grad_vs[:, LANES:],
            grad_st[:, : 2 * nh],
            grad_proj_out,
            gconv[:4, LANES:],
            grad_bias,
            grad_decay,
            gskip[0],
            gmix[0],
        ),
        "seq",
    )
    shared = lax.psum((grad_vs[:, :LANES], gconv[:4, :LANES], grad_gain), ("seq", "head"))
    grad_step = jnp.stack([seq_sums[2][:, :nh], seq_sums[2][:, nh:]], axis=0)
    return (
        layer_out,
        grad_tokens,
        shared[2],
        seq_sums[0],
        seq_sums[1],
        shared[0],
        grad_step,
        seq_sums[5],
        seq_sums[6],
        seq_sums[4],
        shared[1],
        jnp.sum(seq_sums[7].reshape(nh, HDIM), axis=1),
        seq_sums[8],
        seq_sums[3],
    )


def solution(mesh):
    return jax.shard_map(
        per_device,
        mesh=mesh,
        in_specs=(
            P(("seq", "head"), None),
            P(),
            P(None, "head"),
            P(None, "head"),
            P(),
            P(None, None, "head"),
            P(None, "head"),
            P("head"),
            P(None, "head"),
            P(),
            P("head"),
            P("head"),
            P("head", None),
            P(),
            P("seq"),
            P(("seq", "head"), None),
        ),
        out_specs=(
            P(("seq", "head"), None),
            P(("seq", "head"), None),
            P(),
            P(None, "head"),
            P(None, "head"),
            P(),
            P(None, None, "head"),
            P(None, "head"),
            P("head"),
            P(None, "head"),
            P(),
            P("head"),
            P("head"),
            P("head", None),
        ),
        check_vma=False,
    )
```

```python
from functools import partial

import jax
import jax.numpy as jnp
from jax import lax
from jax.experimental import pallas as pl
from jax.experimental.pallas import tpu as pltpu
from jax.sharding import PartitionSpec as P

SPAN = 128
HDIM = 64
LANES = 128
LONGEST = 4096
EPSILON = 1e-05
TINY = 1e-30
F32 = jnp.float32
BF16 = jnp.bfloat16
BLOCK = 256


def mm(a, b):
    return jnp.dot(a, b, preferred_element_type=F32)


def mm_nt(a, b):
    return lax.dot_general(a, b, (((1,), (1,)), ((), ())), preferred_element_type=F32)


def mm_tn(a, b):
    return lax.dot_general(a, b, (((0,), (0,)), ((), ())), preferred_element_type=F32)


def exact(a, b):
    return jnp.dot(a, b, precision=lax.Precision.HIGHEST, preferred_element_type=F32)


def exact_tn(a, b):
    return lax.dot_general(
        a, b, (((0,), (0,)), ((), ())), precision=lax.Precision.HIGHEST, preferred_element_type=F32
    )


def halves(v):
    high = v.astype(BF16)
    return high, (v - high.astype(F32)).astype(BF16)


def spread(v, ex):
    high, low = halves(v)
    return mm(high, ex) + mm(low, ex)


def gather_heads(v, ex):
    high, low = halves(v)
    return mm_nt(high, ex) + mm_nt(low, ex)


def sigmoid(v):
    return 1.0 / (1.0 + jnp.exp(-v))


def softplus(v):
    return jnp.maximum(v, 0.0) + jnp.log1p(jnp.exp(-jnp.abs(v)))


def iota(shape, dim):
    return lax.broadcasted_iota(jnp.int32, shape, dim)


def groups(width):
    found = []
    for at in range(0, width, LANES):
        wide = min(LANES, width - at)
        found.append((at, wide, [(at + k) // HDIM for k in range(0, wide, HDIM)]))
    return found


def stacked(v, wide):
    if wide == HDIM:
        return v
    first = iota(v.shape, 1) < HDIM
    zero = jnp.zeros_like(v)
    return jnp.concatenate([jnp.where(first, v, zero), jnp.where(first, zero, v)], axis=0)


def activated(conv, live):
    return conv * sigmoid(conv) * live


def front_kernel(
    nh,
    x_ref,
    halo_ref,
    gain_ref,
    wg_ref,
    wsv_ref,
    wst_ref,
    wstr_ref,
    pcol_ref,
    prow_ref,
    taps_ref,
    cols_ref,
    gm_ref,
    exf_ref,
    exb_ref,
    tril_ref,
    triu_ref,
    normed_ref,
    normh_ref,
    gate_ref,
    conv_ref,
    uv_ref,
    uvh_ref,
    z_ref,
    cc_ref,
    rowa_ref,
    rowp_ref,
    tot_ref,
    sf_ref,
    rb_ref,
    gf_ref,
    gb_ref,
    gfpre_ref,
    gbsuf_ref,
    gfsuf_ref,
    gbpre_ref,
    fmsg_ref,
    rmsg_ref,
    ubuf,
    state,
    incb,
):
    i = pl.program_id(0)
    tb = x_ref.shape[0]
    per = tb // SPAN
    nc = rb_ref.shape[0]

    def norm(x):
        xf = x.astype(F32)
        s = lax.rsqrt(jnp.mean(xf * xf, axis=1, keepdims=True) + EPSILON)
        return (xf * s * gain_ref[0:1, :]).astype(BF16)

    @pl.when(i == 0)
    def _():
        edge = norm(halo_ref[...])
        normh_ref[...] = edge
        before = mm(edge, wsv_ref[...])
        ubuf[0:8, :] = before
        uvh_ref[...] = before
        state[...] = jnp.zeros_like(state)

    @pl.when(i > 0)
    def _():
        ubuf[0:8, :] = ubuf[tb : tb + 8, :]

    nb = norm(x_ref[...])
    normed_ref[...] = nb
    gate_ref[...] = mm(nb, wg_ref[...])
    uv = mm(nb, wsv_ref[...])
    ubuf[8 : 8 + tb, :] = uv
    uv_ref[...] = uv.astype(BF16)
    conv = taps_ref[0:1, :] * uv
    for k in (1, 2, 3):
        conv = conv + taps_ref[k : k + 1, :] * ubuf[8 - k : 8 - k + tb, :] * cols_ref[:, k - 1 : k]
    conv_ref[...] = conv
    act = activated(conv, cols_ref[:, 3:4])
    z_all = mm(nb, wst_ref[...]) + pcol_ref[0:1, :]
    z_ref[...] = z_all
    zr_all = mm_nt(wstr_ref[...], nb)
    forward = iota((SPAN, LANES), 1) < nh
    forward_row = iota((16, SPAN), 0) < nh
    for j in range(per):
        rows = slice(j * SPAN, (j + 1) * SPAN)
        dt = softplus(z_all[rows])
        a = -dt * pcol_ref[1:2, :]
        total = exact(tril_ref[...], a)
        tot = total[SPAN - 1 : SPAN, :]
        cc = jnp.where(forward, total, total - a)
        cc_ref[rows, :] = cc
        tot8 = jnp.broadcast_to(tot, (8, LANES))
        tot_ref[j * 8 : j * 8 + 8, :] = tot8
        dtr = softplus(zr_all[:, rows] + prow_ref[:, :SPAN])
        ar = -dtr * prow_ref[:, SPAN:]
        run = exact(ar, triu_ref[...])
        rowa = jnp.where(forward_row, run, run - ar)
        ldt = jnp.log(jnp.maximum(dtr, TINY))
        rowa_ref[:, rows] = rowa
        rowp_ref[:, rows] = jnp.where(forward_row, rowa - ldt, rowa + ldt)
        gate8 = jnp.exp(tot8) * gm_ref[j * 8 : j * 8 + 8, :]
        gf = spread(gate8, exf_ref[...])
        gb = spread(gate8, exb_ref[...])
        keep = cols_ref[rows, :]
        w = (
            jnp.exp(jnp.where(forward, tot - cc, cc))
            * jnp.where(forward, keep[:, 6:7], keep[:, 8:9])
            * dt
        )
        x = act[rows, LANES:]
        b = act[rows, :HDIM].astype(BF16)
        c = i * per + j
        sf_ref[j] = state[...]
        state[...] = state[...] * gf[0:1, :] + mm_tn(b, (x * spread(w, exf_ref[...])).astype(BF16))
        incb[c] = mm_tn(b, (x * spread(w, exb_ref[...])).astype(BF16))
        gf_ref[c] = gf
        gb_ref[c] = gb

    @pl.when(i == pl.num_programs(0) - 1)
    def _():
        fmsg_ref[0:HDIM, :] = state[...]

        def up(c, carry):
            pf, pb = carry
            gfpre_ref[c] = pf
            gbpre_ref[c] = pb
            return pf * gf_ref[c], pb * gb_ref[c]

        one = jnp.ones(gf_ref.shape[1:], F32)
        pf, pb = lax.fori_loop(0, nc, up, (one, one))
        fmsg_ref[HDIM:, :] = pf
        rmsg_ref[HDIM:, :] = pb
        state[...] = jnp.zeros_like(state)

        def down(k, carry):
            c = nc - 1 - k
            pf, pb = carry
            gfsuf_ref[c] = pf
            gbsuf_ref[c] = pb
            rb_ref[c] = state[...]
            gb = gb_ref[c]
            state[...] = state[...] * gb[0:1, :] + incb[c]
            return pf * gf_ref[c], pb * gb

        lax.fori_loop(0, nc, down, (one, one))
        rmsg_ref[0:HDIM, :] = state[...]


def inner_kernel(
    nh,
    conv_ref,
    cols_ref,
    segrow_ref,
    cc_ref,
    rowp_ref,
    skip_ref,
    cot_ref,
    wo_ref,
    y_ref,
    dout_ref,
):
    tb, width = y_ref.shape
    dout_ref[...] = mm_nt(cot_ref[...], wo_ref[...])
    act = activated(conv_ref[...], cols_ref[:, 3:4])
    t_at = iota((SPAN, SPAN), 0)
    s_at = iota((SPAN, SPAN), 1)
    lower = t_at > s_at
    for j in range(tb // SPAN):
        rows = slice(j * SPAN, (j + 1) * SPAN)
        x = act[rows, LANES:]
        bc = act[rows, :LANES]
        b = bc[:, :HDIM].astype(BF16)
        c = pltpu.roll(bc, HDIM, 1)[:, :HDIM].astype(BF16)
        same = cols_ref[rows, 4:5] == segrow_ref[0:1, rows]
        score = jnp.where(same & (t_at != s_at), mm_nt(c, b), 0.0)
        cc = cc_ref[rows, :]
        for at, wide, heads in groups(width):
            xp = x[:, at : at + wide]
            mats = []
            for h in heads:
                gap = jnp.where(
                    lower,
                    cc[:, h : h + 1] - rowp_ref[h : h + 1, rows],
                    rowp_ref[nh + h : nh + h + 1, rows] - cc[:, nh + h : nh + h + 1],
                )
                mats.append((score * jnp.exp(gap)).astype(BF16))
            mats = jnp.concatenate(mats, axis=1) if len(mats) > 1 else mats[0]
            y_ref[rows, at : at + wide] = (
                mm(mats, stacked(xp.astype(BF16), wide)) + skip_ref[0:1, at : at + wide] * xp
            )


def merge_kernel(
    nh,
    conv_ref,
    cols_ref,
    cc_ref,
    tot_ref,
    sf_ref,
    rb_ref,
    gfpre_ref,
    gbsuf_ref,
    sent_ref,
    rent_ref,
    yin_ref,
    gate_ref,
    dout_ref,
    mg_ref,
    exf_ref,
    exb_ref,
    y_ref,
    stat_ref,
    sfull_ref,
    rfull_ref,
):
    tb, width = y_ref.shape
    forward = iota((SPAN, LANES), 1) < nh
    which = iota((8, width), 0)
    sel0 = jnp.where(which == 0, 1.0, 0.0).astype(BF16)
    sel1 = jnp.where(which == 1, 1.0, 0.0).astype(BF16)
    for j in range(tb // SPAN):
        rows = slice(j * SPAN, (j + 1) * SPAN)
        keep = cols_ref[rows, :]
        bc = activated(conv_ref[rows, :LANES], keep[:, 3:4])
        c = pltpu.roll(bc, HDIM, 1)[:, :HDIM].astype(BF16)
        cc = cc_ref[rows, :]
        tot = tot_ref[j * 8 : j * 8 + 1, :]
        w = jnp.exp(jnp.where(forward, cc, tot - cc)) * jnp.where(
            forward, keep[:, 5:6], keep[:, 7:8]
        )
        sfull = (sf_ref[j] + gfpre_ref[j][0:1, :] * sent_ref[...]).astype(BF16)
        rfull = (rb_ref[j] + gbsuf_ref[j][0:1, :] * rent_ref[...]).astype(BF16)
        sfull_ref[j] = sfull
        rfull_ref[j] = rfull
        y = (
            yin_ref[rows, :]
            + mm(c, sfull) * spread(w, exf_ref[...])
            + mm(c, rfull) * spread(w, exb_ref[...])
        )
        y_ref[rows, :] = y
        gate = gate_ref[rows, :]
        g = y * gate * sigmoid(gate)
        high, low = halves(g * g)
        stat = mm_nt(sel0, high) + mm_nt(sel0, low)
        high, low = halves(dout_ref[rows, :] * mg_ref[0:1, :] * g)
        stat_ref[:, rows] = stat + mm_nt(sel1, high) + mm_nt(sel1, low)


def turn_kernel(
    nh,
    inner,
    y_ref,
    gate_ref,
    dout_ref,
    mg_ref,
    stat_ref,
    conv_ref,
    cols_ref,
    cc_ref,
    tot_ref,
    gf_ref,
    gb_ref,
    gtf_ref,
    gtb_ref,
    exf_ref,
    exb_ref,
    eye_ref,
    dy_ref,
    dgate_ref,
    outin_ref,
    gmix_ref,
    gskip_ref,
    dso_ref,
    dro_ref,
    amsg_ref,
    bmsg_ref,
    state,
    incf,
):
    i = pl.program_id(0)
    tb, width = y_ref.shape
    per = tb // SPAN
    nc = dso_ref.shape[0]
    forward = iota((SPAN, LANES), 1) < nh

    @pl.when(i == 0)
    def _():
        gmix_ref[...] = jnp.zeros_like(gmix_ref)
        gskip_ref[...] = jnp.zeros_like(gskip_ref)
        state[...] = jnp.zeros_like(state)

    for j in range(per):
        rows = slice(j * SPAN, (j + 1) * SPAN)
        stats = exact_tn(stat_ref[:, rows], eye_ref[0:8, :])
        q = lax.rsqrt(stats[:, 0:1] * (1.0 / inner) + EPSILON)
        k3 = q * q * q * stats[:, 1:2] * (1.0 / inner)
        y = y_ref[rows, :]
        gate = gate_ref[rows, :]
        sig = sigmoid(gate)
        sg = gate * sig
        g = y * sg
        gq = g * q
        dout = dout_ref[rows, :]
        outin_ref[rows, :] = (gq * mg_ref[0:1, :]).astype(BF16)
        gmix_ref[0:1, :] += jnp.sum(dout * gq, axis=0, keepdims=True)
        dg = dout * mg_ref[0:1, :] * q - g * k3
        dy = dg * sg
        dyb = dy.astype(BF16)
        dy_ref[rows, :] = dyb
        dgate_ref[rows, :] = (dg * y * sig * (1.0 + gate * (1.0 - sig))).astype(BF16)
        keep = cols_ref[rows, :]
        act = activated(conv_ref[rows, :], keep[:, 3:4])
        gskip_ref[0:1, :] += jnp.sum(dy * act[:, LANES:], axis=0, keepdims=True)
        c = pltpu.roll(act[:, :LANES], HDIM, 1)[:, :HDIM].astype(BF16)
        cc = cc_ref[rows, :]
        tot = tot_ref[j * 8 : j * 8 + 1, :]
        w = jnp.exp(jnp.where(forward, cc, tot - cc)) * jnp.where(
            forward, keep[:, 5:6], keep[:, 7:8]
        )
        dyf = dyb.astype(F32)
        at = i * per + j
        incf[at] = mm_tn(c, (dyf * spread(w, exf_ref[...])).astype(BF16))
        dro_ref[j] = state[...]
        state[...] = state[...] * gb_ref[at][0:1, :] + mm_tn(
            c, (dyf * spread(w, exb_ref[...])).astype(BF16)
        )

    @pl.when(i == pl.num_programs(0) - 1)
    def _():
        bmsg_ref[0:HDIM, :] = state[...]
        bmsg_ref[HDIM:, :] = gtb_ref[...]
        amsg_ref[HDIM:, :] = gtf_ref[...]
        state[...] = jnp.zeros_like(state)

        def down(k, _):
            c = nc - 1 - k
            dso_ref[c] = state[...]
            state[...] = state[...] * gf_ref[c][0:1, :] + incf[c]
            return 0

        lax.fori_loop(0, nc, down, 0)
        amsg_ref[0:HDIM, :] = state[...]


def back_kernel(
    nh,
    peers,
    at_ref,
    conv_ref,
    cols_ref,
    halocols_ref,
    segrow_ref,
    cc_ref,
    z_ref,
    rowa_ref,
    tot_ref,
    dy_ref,
    sfull_ref,
    rfull_ref,
    dso_ref,
    dro_ref,
    gfsuf_ref,
    gbpre_ref,
    dsent_ref,
    drent_ref,
    gf_ref,
    gb_ref,
    uv_ref,
    uvh_ref,
    taps_ref,
    skip_ref,
    pcol_ref,
    exf_ref,
    exb_ref,
    tril_ref,
    triu_ref,
    eye_ref,
    normed_ref,
    normh_ref,
    dgate_ref,
    wg_ref,
    wcat_ref,
    gmix_ref,
    gskip_ref,
    part_ref,
    parth_ref,
    *rest,
):
    chunks = rest[:peers]
    dbuf, hbuf, dcat, acc, lines = rest[peers:]
    i = pl.program_id(0)
    last = pl.num_programs(0) - 1
    model = normed_ref.shape[1]
    tb = conv_ref.shape[0]
    width = conv_ref.shape[1] - LANES
    exf = exf_ref[...]
    exb = exb_ref[...]

    @pl.when(i == 0)
    def _():
        dbuf[tb : tb + 8, :] = jnp.zeros((8, LANES + width), F32)
        acc[...] = jnp.zeros_like(acc)
        lines[...] = jnp.zeros_like(lines)

    s_at = iota((SPAN, SPAN), 0)
    t_at = iota((SPAN, SPAN), 1)
    lower = t_at > s_at
    lane = iota((SPAN, LANES), 1)
    forward = lane < nh
    row16 = iota((16, SPAN), 0)
    front_half = lane < HDIM
    for j in reversed(range(tb // SPAN)):
        rows = slice(j * SPAN, (j + 1) * SPAN)
        keep = cols_ref[rows, :]
        conv = conv_ref[rows, :]
        sig = sigmoid(conv)
        act = conv * sig * keep[:, 3:4]
        xb = act[:, LANES:].astype(BF16)
        x = xb.astype(F32)
        dyb = dy_ref[rows, :]
        dy = dyb.astype(F32)
        bc = act[:, :LANES]
        cb = pltpu.roll(bc, HDIM, 1)
        b = bc[:, :HDIM].astype(BF16)
        c = cb[:, :HDIM].astype(BF16)
        cpad = jnp.where(front_half, cb, 0.0).astype(BF16)
        bpad = jnp.where(front_half, 0.0, cb).astype(BF16)
        within = (keep[:, 4:5] == segrow_ref[0:1, rows]) & (t_at != s_at)
        score = jnp.where(within, mm_nt(b, c), 0.0)
        cc = cc_ref[rows, :]
        z = z_ref[rows, :]
        dt = softplus(z)
        ldt = jnp.log(jnp.maximum(dt, TINY))
        pc = jnp.where(forward, cc - ldt, cc + ldt)
        dscore = jnp.zeros((SPAN, SPAN), F32)
        kc = jnp.zeros((SPAN, LANES), F32)
        qr = jnp.zeros((16, SPAN), F32)
        dx_parts = []
        for at, wide, heads in groups(width):
            dyp = dyb[:, at : at + wide]
            dmats = mm_nt(stacked(xb[:, at : at + wide], wide), dyp)
            mats = []
            for n, h in enumerate(heads):
                dmat = dmats[n * SPAN : (n + 1) * SPAN, :]
                decay = jnp.exp(
                    jnp.where(
                        lower,
                        rowa_ref[h : h + 1, rows] - pc[:, h : h + 1],
                        pc[:, nh + h : nh + h + 1] - rowa_ref[nh + h : nh + h + 1, rows],
                    )
                )
                spot = dmat * decay
                dscore = dscore + spot
                mats.append((score * decay).astype(BF16))
                pull = spot * score
                pull_low = jnp.where(lower, pull, 0.0)
                pull_up = pull - pull_low
                qr = jnp.where(row16 == h, jnp.sum(pull_low, axis=0, keepdims=True), qr)
                qr = jnp.where(row16 == nh + h, jnp.sum(pull_up, axis=0, keepdims=True), qr)
                kc = jnp.where(lane == h, jnp.sum(pull_low, axis=1, keepdims=True), kc)
                kc = jnp.where(lane == nh + h, jnp.sum(pull_up, axis=1, keepdims=True), kc)
            mats = jnp.concatenate(mats, axis=1) if len(mats) > 1 else mats[0]
            dx_parts.append(mm(mats, stacked(dyp, wide)))
        dscore = jnp.where(within, dscore, 0.0).astype(BF16)
        dbc = mm(dscore, cpad) + mm_tn(dscore, bpad)
        dx = jnp.concatenate(dx_parts, axis=1) if len(dx_parts) > 1 else dx_parts[0]

        tot = tot_ref[j * 8 : j * 8 + 1, :]
        to = jnp.exp(jnp.where(forward, tot - cc, cc)) * dt
        to = to * jnp.where(forward, keep[:, 6:7], keep[:, 8:9])
        fro = jnp.exp(jnp.where(forward, cc, tot - cc)) * jnp.where(
            forward, keep[:, 5:6], keep[:, 7:8]
        )
        dsfull = dso_ref[j] + gfsuf_ref[j][0:1, :] * dsent_ref[...]
        drfull = dro_ref[j] + gbpre_ref[j][0:1, :] * drent_ref[...]
        carried = jnp.zeros((SPAN, LANES), F32)
        leaving = jnp.zeros((SPAN, LANES), F32)
        through = jnp.zeros((8, LANES), F32)
        for ex, held, dheld, gates in (
            (exf, sfull_ref[j], dsfull, gf_ref[j]),
            (exb, rfull_ref[j], drfull, gb_ref[j]),
        ):
            to_wide = spread(to, ex)
            fro_wide = spread(fro, ex)
            dheld_low = dheld.astype(BF16)
            nothing = jnp.zeros_like(held)
            dbc = dbc + mm_nt(
                (x * to_wide).astype(BF16), jnp.concatenate([dheld_low, nothing], axis=0)
            )
            dbc = dbc + mm_nt(
                (dy * fro_wide).astype(BF16), jnp.concatenate([nothing, held], axis=0)
            )
            flow = mm(b, dheld_low) * to_wide
            dx = dx + flow
            carried = carried + gather_heads(dy * (mm(c, held) * fro_wide), ex)
            leaving = leaving + gather_heads(x * flow, ex)
            product = jnp.sum(dheld * held.astype(F32), axis=0, keepdims=True) * gates
            through = through + gather_heads(product, ex)
        moved = exact_tn(qr, eye_ref[...]) + carried - kc
        before = exact(tril_ref[...], jnp.where(forward, leaving, moved))
        after = exact(triu_ref[...], jnp.where(forward, moved, leaving))
        dlog = before + after - leaving + through[0:1, :]
        sigz = sigmoid(z)
        rate = pcol_ref[1:2, :]
        dstep = (kc + leaving) * (sigz / jnp.maximum(dt, TINY)) - dlog * rate * sigz
        dcat[rows, :LANES] = dstep.astype(BF16)
        lines[7:8, :LANES] += jnp.sum(dstep, axis=0, keepdims=True)
        lines[8:9, :LANES] += jnp.sum(-dlog * dt * rate, axis=0, keepdims=True)
        dact = jnp.concatenate([dbc, dx + skip_ref[0:1, :] * dy], axis=1)
        dbuf[rows, :] = dact * keep[:, 3:4] * sig * (1.0 + conv * (1.0 - sig))

    dconv = dbuf[0:tb, :]
    uv = uv_ref[...].astype(F32)
    du = taps_ref[0:1, :] * dconv
    taps_at = slice(0, LANES + width)
    lines[1:2, taps_at] += jnp.sum(uv * dconv, axis=0, keepdims=True)
    for k in (1, 2, 3):
        shifted = dbuf[k : k + tb, :] * cols_ref[:, 8 + k : 9 + k]
        du = du + taps_ref[k : k + 1, :] * shifted
        lines[1 + k : 2 + k, taps_at] += jnp.sum(uv * shifted, axis=0, keepdims=True)
    dcat[:, LANES:] = du.astype(BF16)
    edge = dbuf[0:8, :]
    dbuf[tb : tb + 8, :] = edge
    normed = normed_ref[...]
    d_all = dcat[...]
    part = mm_nt(dgate_ref[...], wg_ref[...]) + mm_nt(d_all, wcat_ref[...])
    part_ref[0] = part.astype(BF16)
    lines[0:1, :] += jnp.sum(part * normed.astype(F32), axis=0, keepdims=True)
    acc[...] += mm_tn(normed, d_all)

    @pl.when(i == last)
    def _():
        hbuf[0:8, :] = jnp.zeros_like(edge)
        hbuf[8:16, :] = edge
        duh = jnp.zeros_like(edge)
        for k in (1, 2, 3):
            shifted = hbuf[k : k + 8, :] * halocols_ref[:, k - 1 : k]
            duh = duh + taps_ref[k : k + 1, :] * shifted
            lines[1 + k : 2 + k, taps_at] += jnp.sum(uvh_ref[...] * shifted, axis=0, keepdims=True)
        duh = duh.astype(BF16)
        normh = normh_ref[...]
        parth = mm_nt(duh, wcat_ref[:, LANES:])
        parth_ref[...] = parth
        lines[0:1, :] += jnp.sum(parth * normh.astype(F32), axis=0, keepdims=True)
        lines[5:6, :width] = gskip_ref[0:1, :]
        lines[6:7, :width] = gmix_ref[0:1, :]
        acc[:, LANES:] += mm_tn(normh, duh)
        placed = jnp.where(iota((16, LANES), 1) == iota((16, LANES), 0) + 16, 1.0, 0.0)
        acc[:, :LANES] += exact_tn(lines[...], placed)
        size = model // peers
        for k in range(peers):
            start = pl.multiple_of((at_ref[0] ^ k) * size, 8)
            chunks[k][...] = acc[pl.ds(start, size), :].astype(BF16)


def finish_kernel(nh, peers, at_ref, *refs):
    chunks = refs[:peers]
    eye_ref = refs[peers]
    gain_ref, value_ref, state_ref, step_ref, bias_ref, decay_ref = refs[peers + 1 : peers + 7]
    convv_ref, convs_ref, skip_ref, mixer_ref, extra = refs[peers + 7 :]
    size = chunks[0].shape[0]
    width = value_ref.shape[1]
    for k in range(peers):
        rows = pl.ds(pl.multiple_of((at_ref[0] ^ k) * size, 8), size)
        extra[rows, :] = chunks[k][:, :LANES].astype(F32)
        state_ref[rows, :] = chunks[k][:, LANES : 2 * LANES].astype(F32)
        value_ref[rows, :] = chunks[k][:, 2 * LANES :].astype(F32)
    found = extra[...]
    step_ref[0] = found[:, :nh]
    step_ref[1] = found[:, nh : 2 * nh]
    lines = mm_nt(eye_ref[...], found.astype(BF16))
    gain_ref[...] = lines[0:1, :]
    convs_ref[...] = lines[1:5, :LANES]
    convv_ref[...] = lines[1:5, LANES : LANES + width]
    skip_ref[...] = lines[5:6, :width]
    mixer_ref[...] = lines[6:7, :width]
    bias_ref[...] = lines[7:8, : 2 * nh]
    decay_ref[...] = lines[8:9, :nh] + lines[8:9, nh : 2 * nh]


def whole(shape):
    return pl.BlockSpec(shape, lambda i, *_: (0,) * len(shape))


def row_block(rows, width):
    return pl.BlockSpec((rows, width), lambda i, *_: (i, 0))


def lane_block(rows, width):
    return pl.BlockSpec((rows, width), lambda i, *_: (0, i))


def chunk_block(per, rows, width):
    return pl.BlockSpec((per, rows, width), lambda i, *_: (i, 0, 0))


def sds(shape, dtype):
    return jax.ShapeDtypeStruct(shape, dtype)


def call(kernel, name, grid, ins, outs, scratch, flops, operands, scalars=()):
    moved = sum(o.size * o.dtype.itemsize for o in operands)
    moved += sum(s.size * s.dtype.itemsize for _, s in outs)
    return pl.pallas_call(
        kernel,
        name=name,
        grid_spec=pltpu.PrefetchScalarGridSpec(
            num_scalar_prefetch=len(scalars),
            grid=(grid,),
            in_specs=ins,
            out_specs=[spec for spec, _ in outs],
            scratch_shapes=scratch,
        ),
        out_shape=[shape for _, shape in outs],
        compiler_params=pltpu.CompilerParams(
            dimension_semantics=("arbitrary",), vmem_limit_bytes=56 * 1024 * 1024
        ),
        cost_estimate=pl.CostEstimate(
            flops=int(flops), bytes_accessed=int(moved), transcendentals=0
        ),
    )(*scalars, *operands)


def shifted_in(array, axis, by):
    length = lax.axis_size(axis)
    pairs = [(i, i + by) for i in range(length) if 0 <= i + by < length]
    return lax.ppermute(array, axis, pairs)


def entering(message, hops, sign):
    parts = [shifted_in(message, "seq", sign * d) for d in range(1, hops + 1)]
    state = parts[-1][:HDIM]
    for part in reversed(parts[:-1]):
        state = part[:HDIM] + part[HDIM : HDIM + 1] * state
    return state


def sum_over(array, axis):
    size = lax.axis_size(axis)
    result = array
    for k in range(1, size):
        result = result + lax.ppermute(array, axis, [(i, i ^ k) for i in range(size)])
    return result


def per_device(
    tokens,
    input_gain,
    proj_gate,
    proj_value,
    proj_state,
    proj_step,
    step_bias,
    decay_log,
    conv_value,
    conv_state,
    skip_gain,
    mixer_gain,
    proj_out,
    doc_lengths,
    pad_mask,
    cotangent,
):
    head_devices = lax.axis_size("head")
    length = pad_mask.shape[0]
    model = tokens.shape[1]
    width = proj_gate.shape[1]
    nh = proj_step.shape[2]
    inner = width * head_devices
    nc = length // SPAN
    tb = BLOCK
    per = tb // SPAN
    grid = length // tb
    wide = LANES + width
    hops = -(-(LONGEST - 1) // length)
    seq_index = lax.axis_index("seq")
    first_place = seq_index * length
    all_tokens = length * lax.axis_size("seq")

    gathered = lax.all_gather(tokens, "head", axis=0, tiled=True)
    cot_all = lax.all_gather(cotangent, "head", axis=0, tiled=True)
    halo = shifted_in(gathered[length - 8 :], "seq", 1)

    offsets = jnp.cumsum(doc_lengths) - doc_lengths
    offsets = jnp.concatenate([offsets, jnp.full((1,), all_tokens, offsets.dtype)])
    places = first_place - 8 + jnp.arange(length + 16, dtype=jnp.int32)
    segs = jnp.sum((offsets[None, :] <= places[:, None]).astype(jnp.int32), axis=1).astype(F32)
    seg = segs[8 : 8 + length]
    by_chunk = seg.reshape(nc, SPAN)
    chunk_first = by_chunk[:, 0]
    chunk_last = by_chunk[:, -1]
    prev_last = jnp.concatenate([segs[7:8], chunk_last[:-1]])
    next_first = jnp.concatenate([chunk_first[1:], segs[8 + length : 9 + length]])
    live = pad_mask.astype(F32)

    def tap_mask(at, k):
        return (seg == segs[8 + at : 8 + at + length]).astype(F32)

    def edge_mask(edge):
        return (by_chunk == edge[:, None]).astype(F32).reshape(length)

    zeros = jnp.zeros((length,), F32)
    cols = jnp.stack(
        [tap_mask(-k, k) for k in (1, 2, 3)]
        + [live, seg]
        + [edge_mask(prev_last), edge_mask(chunk_last), edge_mask(next_first), edge_mask(chunk_first)]
        + [tap_mask(k, k) for k in (1, 2, 3)]
        + [zeros] * 4,
        axis=1,
    )
    halo_cols = jnp.stack(
        [(segs[:8] == segs[k : 8 + k]).astype(F32) for k in (1, 2, 3)] + [jnp.zeros((8,), F32)] * 13,
        axis=1,
    )
    seg_row = jnp.broadcast_to(seg[None, :], (8, length))
    lanes = jnp.arange(LANES)
    gate_mask = jnp.where(
        lanes[None, :] < nh,
        (chunk_last == prev_last).astype(F32)[:, None],
        (chunk_first == next_first).astype(F32)[:, None],
    )
    gate_mask = jnp.broadcast_to(gate_mask[:, None, :], (nc, 8, LANES)).reshape(nc * 8, LANES)
    head_of = jnp.arange(width)[None, :] // HDIM
    exf = (lanes[:, None] == head_of).astype(BF16)
    exb = (lanes[:, None] == head_of + nh).astype(BF16)
    at = jnp.arange(SPAN)
    tril = (at[:, None] >= at[None, :]).astype(F32)
    triu = (at[:, None] <= at[None, :]).astype(F32)
    eye = (jnp.arange(16)[:, None] == lanes[None, :]).astype(F32)

    rate = jnp.exp(decay_log)
    bias_line = jnp.concatenate([step_bias[0], step_bias[1]])
    rate_line = jnp.concatenate([rate, rate])
    pcol = jnp.zeros((8, LANES), F32)
    pcol = pcol.at[0, : 2 * nh].set(bias_line).at[1, : 2 * nh].set(rate_line)
    pad16 = jnp.zeros((16 - 2 * nh,), F32)
    prow = jnp.concatenate(
        [
            jnp.broadcast_to(jnp.concatenate([bias_line, pad16])[:, None], (16, SPAN)),
            jnp.broadcast_to(jnp.concatenate([rate_line, pad16])[:, None], (16, SPAN)),
        ],
        axis=1,
    )
    steps = jnp.concatenate([proj_step[0], proj_step[1]], axis=1)
    wst = jnp.pad(steps, ((0, 0), (0, LANES - 2 * nh)))
    wstr = jnp.pad(steps.T, ((0, 16 - 2 * nh), (0, 0)))
    wsv = jnp.concatenate([proj_state, proj_value], axis=1)
    taps = jnp.pad(jnp.concatenate([conv_state, conv_value], axis=1), ((0, 4), (0, 0)))
    gain = jnp.broadcast_to(input_gain[None, :], (8, model))
    mg = jnp.broadcast_to(mixer_gain[None, :], (8, width))
    skip = jnp.broadcast_to(jnp.repeat(skip_gain, HDIM)[None, :], (8, width))

    rows = partial(row_block, tb)
    states = sds((nc, HDIM, width), F32)
    gates = sds((nc, 8, width), F32)
    message = sds((HDIM + 8, width), F32)
    state_block = chunk_block(per, HDIM, width)
    gate_block = chunk_block(per, 8, width)
    tot_block = row_block(per * 8, LANES)

    (
        normed,
        normh,
        gate_in,
        conv,
        uv,
        uvh,
        z,
        cc,
        rowa,
        rowp,
        tot,
        sf,
        rb,
        gf,
        gb,
        gfpre,
        gbsuf,
        gfsuf,
        gbpre,
        fmsg,
        rmsg,
    ) = call(
        partial(front_kernel, nh),
        "front",
        grid,
        [
            rows(model),
            whole((8, model)),
            whole((8, model)),
            whole((model, width)),
            whole((model, wide)),
            whole((model, LANES)),
            whole((16, model)),
            whole((8, LANES)),
            whole((16, 2 * SPAN)),
            whole((8, wide)),
            rows(16),
            tot_block,
            whole((LANES, width)),
            whole((LANES, width)),
            whole((SPAN, SPAN)),
            whole((SPAN, SPAN)),
        ],
        [
            (rows(model), sds((length, model), BF16)),
            (whole((8, model)), sds((8, model), BF16)),
            (rows(width), sds((length, width), F32)),
            (rows(wide), sds((length, wide), F32)),
            (rows(wide), sds((length, wide), BF16)),
            (whole((8, wide)), sds((8, wide), F32)),
            (rows(LANES), sds((length, LANES), F32)),
            (rows(LANES), sds((length, LANES), F32)),
            (lane_block(16, tb), sds((16, length), F32)),
            (lane_block(16, tb), sds((16, length), F32)),
            (tot_block, sds((nc * 8, LANES), F32)),
            (state_block, states),
            (whole(states.shape), states),
            (whole(gates.shape), gates),
            (whole(gates.shape), gates),
            (whole(gates.shape), gates),
            (whole(gates.shape), gates),
            (whole(gates.shape), gates),
            (whole(gates.shape), gates),
            (whole(message.shape), message),
            (whole(message.shape), message),
        ],
        [
            pltpu.VMEM((tb + 8, wide), F32),
            pltpu.VMEM((HDIM, width), F32),
            pltpu.VMEM((nc, HDIM, width), F32),
        ],
        2 * length * model * (2 * width + 3 * LANES),
        [
            gathered,
            halo,
            gain,
            proj_gate,
            wsv,
            wst,
            wstr,
            pcol,
            prow,
            taps,
            cols,
            gate_mask,
            exf,
            exb,
            tril,
            triu,
        ],
    )

    sent = entering(fmsg, hops, 1)
    rent = entering(rmsg, hops, -1)

    yin, dout = call(
        partial(inner_kernel, nh),
        "inner",
        grid,
        [
            rows(wide),
            rows(16),
            lane_block(8, tb),
            rows(LANES),
            lane_block(16, tb),
            whole((8, width)),
            rows(model),
            whole((width, model)),
        ],
        [
            (rows(width), sds((length, width), F32)),
            (rows(width), sds((length, width), F32)),
        ],
        [],
        2 * length * width * (model + 2 * SPAN),
        [conv, cols, seg_row, cc, rowp, skip, cot_all, proj_out],
    )

    y, stat, sfull, rfull = call(
        partial(merge_kernel, nh),
        "merge",
        grid,
        [
            row_block(tb, LANES),
            rows(16),
            rows(LANES),
            tot_block,
            state_block,
            state_block,
            gate_block,
            gate_block,
            whole((HDIM, width)),
            whole((HDIM, width)),
            rows(width),
            rows(width),
            rows(width),
            whole((8, width)),
            whole((LANES, width)),
            whole((LANES, width)),
        ],
        [
            (rows(width), sds((length, width), F32)),
            (lane_block(8, tb), sds((8, length), F32)),
            (state_block, sds((nc, HDIM, width), BF16)),
            (state_block, sds((nc, HDIM, width), BF16)),
        ],
        [],
        2 * length * width * 2 * (HDIM + LANES),
        [conv, cols, cc, tot, sf, rb, gfpre, gbsuf, sent, rent, yin, gate_in, dout, mg, exf, exb],
    )

    stat = sum_over(stat, "head")

    dy, dgate, outin, gmix, gskip, dso, dro, amsg, bmsg = call(
        partial(turn_kernel, nh, inner),
        "turn",
        grid,
        [
            rows(width),
            rows(width),
            rows(width),
            whole((8, width)),
            lane_block(8, tb),
            rows(wide),
            rows(16),
            rows(LANES),
            tot_block,
            whole(gates.shape),
            whole(gates.shape),
            whole((8, width)),
            whole((8, width)),
            whole((LANES, width)),
            whole((LANES, width)),
            whole((16, LANES)),
        ],
        [
            (rows(width), sds((length, width), BF16)),
            (rows(width), sds((length, width), BF16)),
            (rows(width), sds((length, width), BF16)),
            (whole((8, width)), sds((8, width), F32)),
            (whole((8, width)), sds((8, width), F32)),
            (whole(states.shape), states),
            (state_block, states),
            (whole(message.shape), message),
            (whole(message.shape), message),
        ],
        [pltpu.VMEM((HDIM, width), F32), pltpu.VMEM((nc, HDIM, width), F32)],
        2 * length * width * 2 * (HDIM + LANES),
        [
            y,
            gate_in,
            dout,
            mg,
            stat,
            conv,
            cols,
            cc,
            tot,
            gf,
            gb,
            fmsg[HDIM:],
            rmsg[HDIM:],
            exf,
            exb,
            eye,
        ],
    )

    dsent = entering(amsg, hops, -1)
    drent = entering(bmsg, hops, 1)

    back = lambda i: grid - 1 - i

    def rev(spec):
        return pl.BlockSpec(spec.block_shape, lambda i, *_: spec.index_map(back(i)))

    peers = lax.axis_size("seq")
    own = length // head_devices
    bits = head_devices.bit_length() - 1
    here = lax.axis_index("head")
    scalars = [jnp.stack([seq_index, here]).astype(jnp.int32)]
    wcat = jnp.concatenate([wst, wsv], axis=1)
    size = model // peers

    def part_at(i, at):
        row = back(i) * tb
        slot = (row // own) ^ at[1]
        place = sum(((slot >> b) & 1) << (bits - 1 - b) for b in range(bits))
        return place, (row % own) // tb, 0

    part, parth, *chunks = call(
        partial(back_kernel, nh, peers),
        "back",
        grid,
        [
            rev(rows(wide)),
            rev(rows(16)),
            whole((8, 16)),
            rev(lane_block(8, tb)),
            rev(rows(LANES)),
            rev(rows(LANES)),
            rev(lane_block(16, tb)),
            rev(tot_block),
            rev(rows(width)),
            rev(state_block),
            rev(state_block),
            rev(state_block),
            rev(state_block),
            rev(gate_block),
            rev(gate_block),
            whole((HDIM, width)),
            whole((HDIM, width)),
            rev(gate_block),
            rev(gate_block),
            rev(rows(wide)),
            whole((8, wide)),
            whole((8, wide)),
            whole((8, width)),
            whole((8, LANES)),
            whole((LANES, width)),
            whole((LANES, width)),
            whole((SPAN, SPAN)),
            whole((SPAN, SPAN)),
            whole((16, LANES)),
            rev(rows(model)),
            whole((8, model)),
            rev(rows(width)),
            whole((model, width)),
            whole((model, LANES + wide)),
            whole((8, width)),
            whole((8, width)),
        ],
        [
            (pl.BlockSpec((1, tb, model), part_at), sds((head_devices, own, model), BF16)),
            (whole((8, model)), sds((8, model), F32)),
        ]
        + [(whole((size, LANES + wide)), sds((size, LANES + wide), BF16))] * peers,
        [
            pltpu.VMEM((tb + 8, wide), F32),
            pltpu.VMEM((16, wide), F32),
            pltpu.VMEM((tb, LANES + wide), BF16),
            pltpu.VMEM((model, LANES + wide), F32),
            pltpu.VMEM((16, model), F32),
        ],
        2 * length * (width * (4 * SPAN + 6 * HDIM + 8 * LANES) + model * (3 * width + 4 * LANES)),
        [
            conv,
            cols,
            halo_cols,
            seg_row,
            cc,
            z,
            rowa,
            tot,
            dy,
            sfull,
            rfull,
            dso,
            dro,
            gfsuf,
            gbpre,
            dsent,
            drent,
            gf,
            gb,
            uv,
            uvh,
            taps,
            skip,
            pcol,
            exf,
            exb,
            tril,
            triu,
            eye,
            normed,
            normh,
            dgate,
            proj_gate,
            wcat,
            gmix,
            gskip,
        ],
        scalars,
    )

    def swap(array, axis, k):
        n = lax.axis_size(axis)
        return lax.ppermute(array, axis, [(i, i ^ k) for i in range(n)])

    summed = chunks[0].astype(F32)
    for k in range(1, peers):
        summed = summed + swap(chunks[k], "seq", k).astype(F32)
    shared = summed[:, : 2 * LANES]
    row_at = seq_index * size + jnp.arange(size)[:, None]
    lane_at = jnp.arange(2 * LANES)[None, :]
    common = (lane_at >= LANES) | (lane_at == 16)
    common = common | ((lane_at > 16) & (lane_at < 21) & (row_at < LANES))
    shared = jnp.where(common, sum_over(shared, "head"), shared)
    reduced = jnp.concatenate([shared, summed[:, 2 * LANES :]], axis=1).astype(BF16)
    spread_out = [reduced] + [swap(reduced, "seq", k) for k in range(1, peers)]

    returned = shifted_in(parth, "seq", -1)
    last_slot = (head_devices - 1) ^ here
    last_slot = sum(((last_slot >> b) & 1) << (bits - 1 - b) for b in range(bits))
    tail = lax.dynamic_slice(part, (last_slot, own - 8, 0), (1, 8, model))
    tail = (tail.astype(F32) + returned[None]).astype(BF16)
    own_in = lax.dynamic_update_slice(part, tail, (last_slot, own - 8, 0))
    for b in range(bits):
        half = own_in.shape[0] // 2
        got = swap(own_in[half:], "head", 1 << b)
        own_in = own_in[:half].astype(F32) + got.astype(F32)
        if b < bits - 1:
            own_in = own_in.astype(BF16)
    own_in = own_in[0]

    mixer = lax.psum_scatter(
        jnp.dot(outin, proj_out, preferred_element_type=F32).astype(BF16),
        "head",
        scatter_dimension=0,
        tiled=True,
    )
    layer_out = (tokens.astype(F32) + mixer.astype(F32)).astype(BF16)

    def weight_grad(a, b):
        return lax.dot_general(a, b, (((0,), (0,)), ((), ())), preferred_element_type=F32)

    grad_proj_out = weight_grad(outin, cot_all).astype(BF16)
    grad_proj_gate = weight_grad(normed, dgate).astype(BF16)
    grad_proj_out, grad_proj_gate = lax.psum((grad_proj_out, grad_proj_gate), "seq")

    token_values = tokens.astype(F32)
    scale_rows = lax.rsqrt(jnp.mean(token_values * token_values, axis=1, keepdims=True) + EPSILON)
    scaled = own_in * input_gain
    grad_tokens = (
        cotangent.astype(F32)
        + scale_rows * scaled
        - token_values * scale_rows**3 * jnp.mean(scaled * token_values, axis=1, keepdims=True)
    ).astype(BF16)

    finals = [
        sds((1, model), F32),
        sds((model, width), F32),
        sds((model, LANES), F32),
        sds((2, model, nh), F32),
        sds((1, 2 * nh), F32),
        sds((1, nh), F32),
        sds((4, width), F32),
        sds((4, LANES), F32),
        sds((1, width), F32),
        sds((1, width), F32),
    ]
    picked = (jnp.arange(16)[:, None] + 16 == lanes[None, :]).astype(BF16)
    ggain, gvalue, gstate, gstep, gbias, gdecay, gconvv, gconvs, gskips, gmixer = call(
        partial(finish_kernel, nh, peers),
        "finish",
        1,
        [whole((size, LANES + wide))] * peers + [whole((16, LANES))],
        [(whole(f.shape), f) for f in finals],
        [pltpu.VMEM((model, LANES), F32)],
        0,
        spread_out + [picked],
        scalars,
    )
    return (
        layer_out,
        grad_tokens,
        ggain[0] / input_gain,
        grad_proj_gate.astype(F32),
        gvalue,
        gstate,
        gstep,
        gbias.reshape(2, nh),
        gdecay[0],
        gconvv,
        gconvs,
        jnp.sum(gskips.reshape(nh, HDIM), axis=1),
        gmixer[0],
        grad_proj_out.astype(F32),
    )


def solution(mesh):
    return jax.shard_map(
        per_device,
        mesh=mesh,
        in_specs=(
            P(("seq", "head"), None),
            P(),
            P(None, "head"),
            P(None, "head"),
            P(),
            P(None, None, "head"),
            P(None, "head"),
            P("head"),
            P(None, "head"),
            P(),
            P("head"),
            P("head"),
            P("head", None),
            P(),
            P("seq"),
            P(("seq", "head"), None),
        ),
        out_specs=(
            P(("seq", "head"), None),
            P(("seq", "head"), None),
            P(),
            P(None, "head"),
            P(None, "head"),
            P(),
            P(None, None, "head"),
            P(None, "head"),
            P("head"),
            P(None, "head"),
            P(),
            P("head"),
            P("head"),
            P("head", None),
        ),
        check_vma=False,
    )
```

```python
from functools import partial

import jax
import jax.numpy as jnp
import numpy as np
from jax import lax
from jax.experimental import pallas as pl
from jax.experimental.pallas import tpu as pltpu
from jax.sharding import PartitionSpec as P

SPAN = 128
HDIM = 64
LANES = 128
LONGEST = 4096
EPSILON = 1e-05
TINY = 1e-30
F32 = jnp.float32
BF16 = jnp.bfloat16
BLOCK = 256


def mm(a, b):
    return jnp.dot(a, b, preferred_element_type=F32)


def mm_nt(a, b):
    return lax.dot_general(a, b, (((1,), (1,)), ((), ())), preferred_element_type=F32)


def mm_tn(a, b):
    return lax.dot_general(a, b, (((0,), (0,)), ((), ())), preferred_element_type=F32)


def pieces(v):
    high = v.astype(BF16)
    rest = v - high.astype(F32)
    mid = rest.astype(BF16)
    return high, mid, (rest - mid.astype(F32)).astype(BF16)


def exact_tn(a, b):
    return lax.dot_general(
        a, b, (((0,), (0,)), ((), ())), precision=lax.Precision.HIGHEST, preferred_element_type=F32
    )


def split(v, axis):
    high = v.astype(BF16)
    return jnp.concatenate([high, (v - high.astype(F32)).astype(BF16)], axis=axis)


def sigmoid(v):
    return 1.0 / (1.0 + jnp.exp(-v))


def softplus(v):
    return jnp.maximum(v, 0.0) + jnp.log1p(jnp.exp(-jnp.abs(v)))


def iota(shape, dim):
    return lax.broadcasted_iota(jnp.int32, shape, dim)


def groups(width):
    return [(n, n * LANES, (2 * n, 2 * n + 1)) for n in range(width // LANES)]


def sides(v, width):
    tiles = [v[:, at : at + LANES] for at in range(0, 2 * width, LANES)]
    return jnp.concatenate(tiles[::2], axis=1), jnp.concatenate(tiles[1::2], axis=1)


def stacked(v):
    first = iota(v.shape, 1) < HDIM
    zero = jnp.zeros_like(v)
    return jnp.concatenate([jnp.where(first, v, zero), jnp.where(first, zero, v)], axis=0)


def source_weights(pack, tot, dt, lane, nh):
    forward = lane < nh
    gap = jnp.where(forward, tot - pack, pack)
    kept = jnp.where(forward, pack[:, 38:39], pack[:, 40:41])
    return jnp.where(lane < 16, jnp.exp(jnp.where(lane < 16, gap, 0.0)) * kept * dt, 0.0)


def target_weights(pack, tot, lane, nh):
    forward = lane < nh
    gap = jnp.where(forward, pack, tot - pack)
    kept = jnp.where(forward, pack[:, 37:38], pack[:, 39:40])
    return jnp.where(lane < 16, jnp.exp(jnp.where(lane < 16, gap, 0.0)) * kept, 0.0)


def send_sides(at_ref, hops, up, down, refs):
    for d in range(1, hops + 1):
        low = (at_ref[0] // d) % 2 == 0
        refs[2 * d - 2][...] = jnp.where(low, up, down)
        refs[2 * d - 1][...] = jnp.where(low, down, up)


def land_sides(at_ref, hops, refs, from_earlier, from_later):
    for d in range(hops, 0, -1):
        low = (at_ref[0] // d) % 2 == 0
        first, second = refs[2 * d - 2][...], refs[2 * d - 1][...]
        for state, part in (
            (from_earlier, jnp.where(low, second, first)),
            (from_later, jnp.where(low, first, second)),
        ):
            if d == hops:
                state[...] = part[:HDIM]
            else:
                state[...] = part[:HDIM] + part[HDIM : HDIM + 1] * state[...]


def documents(off_ref, places):
    count = jnp.zeros(places.shape, F32)
    for at in range(0, off_ref.shape[1], LANES):
        begun = off_ref[0:1, at : at + LANES] <= places
        count = count + jnp.sum(jnp.where(begun, 1.0, 0.0), axis=1, keepdims=True)
    return count


def front_kernel(
    nh,
    hops,
    shares,
    own,
    at_ref,
    *refs,
):
    front_body(nh, hops, own, at_ref, refs[:shares], *refs[shares:])


def front_body(
    nh,
    hops,
    own,
    at_ref,
    x_refs,
    halo_ref,
    gain_ref,
    wg_ref,
    wsv_ref,
    wst_ref,
    wstr_ref,
    pcol_ref,
    prow_ref,
    taps_ref,
    off_ref,
    live_ref,
    ex_ref,
    tril_ref,
    triu_ref,
    normed_ref,
    normh_ref,
    gate_ref,
    act_ref,
    slope_ref,
    uv_ref,
    uvh_ref,
    pack_ref,
    rowa_ref,
    rowp_ref,
    segrow_ref,
    halocols_ref,
    tot_ref,
    sf_ref,
    rb_ref,
    gates_ref,
    gpre_ref,
    gsuf_ref,
    gtot_ref,
    *rest,
):
    messages = rest[: 2 * hops]
    ubuf, state, incb, marks, ends, docs = rest[2 * hops :]
    i = pl.program_id(0)
    tb = normed_ref.shape[0]
    per = tb // SPAN
    nc = rb_ref.shape[0]
    width = gate_ref.shape[1]
    piece = i * tb // own ^ at_ref[1]

    def norm(x):
        xf = x.astype(F32)
        s = lax.rsqrt(jnp.mean(xf * xf, axis=1, keepdims=True) + EPSILON)
        return (xf * s * gain_ref[0:1, :]).astype(BF16)

    @pl.when(i == 0)
    def _():
        edge = norm(halo_ref[...])
        normh_ref[...] = edge
        before = mm(edge, wsv_ref[...])
        ubuf[0:8, :] = before
        uvh_ref[...] = before
        state[...] = jnp.zeros_like(state)
        place = at_ref[2] - 8 + iota((8, 1), 0)
        here = documents(off_ref, place)
        lane8 = iota((8, LANES), 1)
        halo = jnp.zeros((8, LANES), F32)
        for k in (1, 2, 3):
            same = jnp.where(documents(off_ref, place + k) == here, 1.0, 0.0)
            halo = jnp.where(lane8 == k - 1, same, halo)
        halocols_ref[...] = halo

    @pl.when(i > 0)
    def _():
        ubuf[0:8, :] = ubuf[tb : tb + 8, :]

    for at in range(0, tb, 64):
        x = x_refs[0][at : at + 64, :]
        for k in range(1, len(x_refs)):
            x = jnp.where(piece == k, x_refs[k][at : at + 64, :], x)
        normed_ref[at : at + 64, :] = norm(x)
    nb = normed_ref[...]
    for at in range(0, width, LANES):
        tile = slice(at, at + LANES)
        gate_ref[:, tile] = mm(nb, wg_ref[:, tile]).astype(BF16)
    zr_all = mm_nt(wstr_ref[...], nb)
    lane = iota((SPAN, LANES), 1)
    forward = lane < nh
    forward_row = iota((16, SPAN), 0) < nh
    gate_lane = iota((8, LANES), 1) < nh
    for j in range(per):
        rows = slice(j * SPAN, (j + 1) * SPAN)
        base = at_ref[2] + (i * per + j) * SPAN
        around = documents(off_ref, base - 8 + iota((SPAN + 16, 1), 0))
        docs[...] = jnp.broadcast_to(around, docs.shape)
        seg = docs[8 : 8 + SPAN, :]
        prev_last, first = docs[7:8, :], docs[8:9, :]
        last, next_first = docs[7 + SPAN : 8 + SPAN, :], docs[8 + SPAN : 9 + SPAN, :]
        live = jnp.transpose(jnp.broadcast_to(live_ref[0:1, rows], (SPAN, SPAN)).astype(F32))
        mark = jnp.where(lane == 35, live, jnp.where(lane == 36, seg, 0.0))
        for k in (1, 2, 3):
            same = jnp.where(docs[8 - k : 8 - k + SPAN, :] == seg, 1.0, 0.0)
            mark = jnp.where(lane == 31 + k, same, mark)
            same = jnp.where(docs[8 + k : 8 + k + SPAN, :] == seg, 1.0, 0.0)
            mark = jnp.where(lane == 40 + k, same, mark)
        for k, bound in enumerate((prev_last, last, next_first, first)):
            mark = jnp.where(lane == 37 + k, jnp.where(seg == bound, 1.0, 0.0), mark)
        marks[rows, :] = mark
        opened = jnp.where(gate_lane, last - prev_last, next_first - first)
        ends[j * 8 : j * 8 + 8, :] = jnp.where(opened == 0.0, 1.0, 0.0)
        segrow_ref[:, rows] = jnp.transpose(seg)[:8]
    for at in range(0, LANES + width, LANES):
        tile = slice(at, at + LANES)
        uv = mm(nb, wsv_ref[:, tile])
        ubuf[8 : 8 + tb, tile] = uv
        uv_ref[:, tile] = uv.astype(BF16)
        for j in range(per):
            rows = slice(j * SPAN, (j + 1) * SPAN)
            keep = marks[rows, :]
            conv = taps_ref[0:1, tile] * ubuf[8 + j * SPAN : 8 + (j + 1) * SPAN, tile]
            for k in (1, 2, 3):
                moved = ubuf[8 - k + j * SPAN : 8 - k + (j + 1) * SPAN, tile]
                conv = conv + taps_ref[k : k + 1, tile] * moved * keep[:, 31 + k : 32 + k]
            sig = sigmoid(conv)
            live = keep[:, 35:36]
            act_ref[rows, tile] = (conv * sig * live).astype(BF16)
            slope_ref[rows, tile] = (live * sig * (1.0 + conv * (1.0 - sig))).astype(BF16)
    z_all = mm(nb, wst_ref[...])
    for j in range(per):
        rows = slice(j * SPAN, (j + 1) * SPAN)
        z = z_all[rows] + pcol_ref[0:1, :]
        dt = softplus(z)
        a = -dt * pcol_ref[1:2, :]
        total = mm(tril_ref[...], jnp.concatenate(pieces(a), axis=0))
        tot = total[SPAN - 1 : SPAN, :]
        cc = jnp.where(forward, total, total - a)
        pack = jnp.where(lane < 16, cc, jnp.where(lane < 32, z, marks[rows, :]))
        pack_ref[rows, :] = pack
        tot8 = jnp.broadcast_to(tot, (8, LANES))
        tot_ref[j * 8 : j * 8 + 8, :] = tot8
        dtr = softplus(zr_all[:, rows] + prow_ref[:, :SPAN])
        ar = -dtr * prow_ref[:, SPAN:]
        run = mm(jnp.concatenate(pieces(ar), axis=1), triu_ref[...])
        rowa = jnp.where(forward_row, run, run - ar)
        ldt = jnp.log(jnp.maximum(dtr, TINY))
        rowa_ref[:, rows] = rowa
        rowp_ref[:, rows] = jnp.where(forward_row, rowa - ldt, rowa + ldt)
        gates = split(jnp.exp(tot8) * ends[j * 8 : j * 8 + 8, :], 1)
        w = split(source_weights(pack, tot, dt, lane, nh), 1)
        bt = jnp.transpose(act_ref[rows, :LANES].astype(F32))[:HDIM].astype(BF16)
        c = i * per + j
        for n, at, _ in groups(width):
            tile = slice(at, at + LANES)
            both = slice(2 * at, 2 * at + 2 * LANES)
            x = act_ref[rows, LANES + at : 2 * LANES + at].astype(F32)
            wide = mm(w, ex_ref[:, both])
            fed = jnp.concatenate(
                [(x * wide[:, :LANES]).astype(BF16), (x * wide[:, LANES:]).astype(BF16)], axis=1
            )
            inc = mm(bt, fed)
            gate = mm(gates, ex_ref[:, both])
            gates_ref[c, :, both] = gate
            sf_ref[j, :, tile] = state[:, tile]
            state[:, tile] = state[:, tile] * gate[0:1, :LANES] + inc[:, :LANES]
            incb[c, :, tile] = inc[:, LANES:]

    @pl.when(i == pl.num_programs(0) - 1)
    def _():
        last_state = state[...]
        one = jnp.ones(gates_ref.shape[1:], F32)

        def up(c, p):
            gpre_ref[c] = p
            return p * gates_ref[c]

        p = lax.fori_loop(0, nc, up, one)
        tot_f, tot_b = sides(p, width)
        gtot_ref[:, :width] = tot_f
        gtot_ref[:, width:] = tot_b
        state[...] = jnp.zeros_like(state)

        def down(k, p):
            c = nc - 1 - k
            gsuf_ref[c] = p
            rb_ref[c] = state[...]
            gate = gates_ref[c]
            for n, at, _ in groups(width):
                tile = slice(at, at + LANES)
                second = slice(2 * at + LANES, 2 * at + 2 * LANES)
                state[:, tile] = state[:, tile] * gate[0:1, second] + incb[c, :, tile]
            return p * gate

        lax.fori_loop(0, nc, down, one)
        send_sides(
            at_ref,
            hops,
            jnp.concatenate([last_state, tot_f], axis=0),
            jnp.concatenate([state[...], tot_b], axis=0),
            messages,
        )


def inner_kernel(
    nh,
    act_ref,
    pack_ref,
    segrow_ref,
    rowp_ref,
    skip_ref,
    cot_ref,
    wo_ref,
    y_ref,
    dout_ref,
):
    tb, width = y_ref.shape
    for at in range(0, width, LANES):
        tile = slice(at, at + LANES)
        dout_ref[:, tile] = mm_nt(cot_ref[...], wo_ref[tile, :]).astype(BF16)
    t_at = iota((SPAN, SPAN), 0)
    s_at = iota((SPAN, SPAN), 1)
    lower = t_at > s_at
    for j in range(tb // SPAN):
        rows = slice(j * SPAN, (j + 1) * SPAN)
        bc = act_ref[rows, :LANES].astype(F32)
        b = bc[:, :HDIM].astype(BF16)
        c = pltpu.roll(bc, HDIM, 1)[:, :HDIM].astype(BF16)
        pack = pack_ref[rows, :]
        within = (pack[:, 36:37] == segrow_ref[0:1, rows]) & (t_at != s_at)
        score = jnp.where(within, mm_nt(c, b), 0.0)
        for n, at, heads in groups(width):
            tile = slice(at, at + LANES)
            mats = []
            for h in heads:
                gap = jnp.where(
                    lower,
                    pack[:, h : h + 1] - rowp_ref[h : h + 1, rows],
                    rowp_ref[nh + h : nh + h + 1, rows] - pack[:, nh + h : nh + h + 1],
                )
                mats.append((score * jnp.exp(gap)).astype(BF16))
            xp = act_ref[rows, LANES + at : 2 * LANES + at]
            y = mm(jnp.concatenate(mats, axis=1), stacked(xp))
            y_ref[rows, tile] = (y + skip_ref[0:1, tile] * xp.astype(F32)).astype(BF16)


def merge_kernel(
    nh,
    hops,
    at_ref,
    bc_ref,
    pack_ref,
    tot_ref,
    sf_ref,
    rb_ref,
    gpre_ref,
    gsuf_ref,
    yin_ref,
    gate_ref,
    dout_ref,
    mg_ref,
    ex_ref,
    *rest,
):
    arrived = rest[: 2 * hops]
    y_ref, stat_ref, full_ref, sent_ref, rent_ref = rest[2 * hops :]
    tb, width = y_ref.shape

    @pl.when(pl.program_id(0) == 0)
    def _():
        land_sides(at_ref, hops, arrived, sent_ref, rent_ref)

    lane = iota((SPAN, LANES), 1)
    row8 = iota((8, SPAN), 0)
    for j in range(tb // SPAN):
        rows = slice(j * SPAN, (j + 1) * SPAN)
        pack = pack_ref[rows, :]
        bc = bc_ref[rows, :].astype(F32)
        c = pltpu.roll(bc, HDIM, 1)[:, :HDIM].astype(BF16)
        w = split(target_weights(pack, tot_ref[j * 8 : j * 8 + 1, :], lane, nh), 1)
        energy = jnp.zeros((SPAN, LANES), F32)
        cross = jnp.zeros((SPAN, LANES), F32)
        for n, at, _ in groups(width):
            tile = slice(at, at + LANES)
            both = slice(2 * at, 2 * at + 2 * LANES)
            second = slice(2 * at + LANES, 2 * at + 2 * LANES)
            first = slice(2 * at, 2 * at + LANES)
            sfull = sf_ref[j, :, tile] + gpre_ref[j, 0:1, first] * sent_ref[:, tile]
            rfull = rb_ref[j, :, tile] + gsuf_ref[j, 0:1, second] * rent_ref[:, tile]
            held = jnp.concatenate([sfull.astype(BF16), rfull.astype(BF16)], axis=1)
            full_ref[j, :, both] = held
            seen = mm(c, held) * mm(w, ex_ref[:, both])
            y = (yin_ref[rows, tile].astype(F32) + seen[:, :LANES] + seen[:, LANES:]).astype(BF16)
            y_ref[rows, tile] = y
            gate = gate_ref[rows, tile].astype(F32)
            g = y.astype(F32) * gate * sigmoid(gate)
            energy = energy + g * g
            cross = cross + dout_ref[rows, tile].astype(F32) * mg_ref[0:1, tile] * g
        energy = jnp.sum(jnp.transpose(energy), axis=0, keepdims=True)
        cross = jnp.sum(jnp.transpose(cross), axis=0, keepdims=True)
        stat_ref[:, rows] = jnp.where(row8 == 0, energy, jnp.where(row8 == 1, cross, 0.0))


def turn_kernel(
    nh,
    inner,
    shares,
    hops,
    at_ref,
    y_ref,
    gate_ref,
    dout_ref,
    mg_ref,
    act_ref,
    pack_ref,
    tot_ref,
    gates_ref,
    gtot_ref,
    ex_ref,
    eye_ref,
    normed_ref,
    cot_ref,
    wo_ref,
    *rest,
):
    stats_in = rest[:shares]
    (
        mixer_ref,
        dy_ref,
        dgate_ref,
        gmix_ref,
        gskip_ref,
        gout_ref,
        ggate_ref,
        dso_ref,
        dro_ref,
        *messages,
        state,
        incf,
        outin,
        gout,
        ggate,
    ) = rest[shares:]
    i = pl.program_id(0)
    tb, width = y_ref.shape
    model = normed_ref.shape[1]
    per = tb // SPAN
    nc = dso_ref.shape[0]
    lane = iota((SPAN, LANES), 1)

    @pl.when(i == 0)
    def _():
        gmix_ref[...] = jnp.zeros_like(gmix_ref)
        gskip_ref[...] = jnp.zeros_like(gskip_ref)
        state[...] = jnp.zeros_like(state)
        gout[...] = jnp.zeros_like(gout)
        ggate[...] = jnp.zeros_like(ggate)

    for j in range(per):
        rows = slice(j * SPAN, (j + 1) * SPAN)
        stat = stats_in[0][:, rows]
        for more in stats_in[1:]:
            stat = stat + more[:, rows]
        stat = exact_tn(stat, eye_ref[0:8, :])
        q = lax.rsqrt(stat[:, 0:1] * (1.0 / inner) + EPSILON)
        k3 = q * q * q * stat[:, 1:2] * (1.0 / inner)
        pack = pack_ref[rows, :]
        w = split(target_weights(pack, tot_ref[j * 8 : j * 8 + 1, :], lane, nh), 1)
        ct = jnp.transpose(act_ref[rows, :LANES].astype(F32))[HDIM:].astype(BF16)
        c = i * per + j
        for n, at, _ in groups(width):
            tile = slice(at, at + LANES)
            both = slice(2 * at, 2 * at + 2 * LANES)
            second = slice(2 * at + LANES, 2 * at + 2 * LANES)
            y = y_ref[rows, tile].astype(F32)
            gate = gate_ref[rows, tile].astype(F32)
            sig = sigmoid(gate)
            sg = gate * sig
            g = y * sg
            gq = g * q
            dout = dout_ref[rows, tile].astype(F32)
            mg = mg_ref[0:1, tile]
            outin[rows, tile] = (gq * mg).astype(BF16)
            gmix_ref[0:1, tile] += jnp.sum(dout * gq, axis=0, keepdims=True)
            dg = dout * mg * q - g * k3
            dyb = (dg * sg).astype(BF16)
            dy_ref[rows, tile] = dyb
            dgate_ref[rows, tile] = (dg * y * (sig + sg * (1.0 - sig))).astype(BF16)
            dy = dyb.astype(F32)
            x = act_ref[rows, LANES + at : 2 * LANES + at].astype(F32)
            gskip_ref[0:1, tile] += jnp.sum(dy * x, axis=0, keepdims=True)
            wide = mm(w, ex_ref[:, both])
            fed = jnp.concatenate(
                [(dy * wide[:, :LANES]).astype(BF16), (dy * wide[:, LANES:]).astype(BF16)], axis=1
            )
            inc = mm(ct, fed)
            incf[c, :, tile] = inc[:, :LANES]
            dro_ref[j, :, tile] = state[:, tile]
            state[:, tile] = state[:, tile] * gates_ref[c, 0:1, second] + inc[:, LANES:]

    for at in range(0, model, 2 * LANES):
        tile = slice(at, at + 2 * LANES)
        mixer_ref[:, tile] = mm(outin[...], wo_ref[:, tile]).astype(BF16)
    for at in range(0, width, LANES):
        tile = slice(at, at + LANES)
        gout[tile, :] += mm_tn(outin[:, tile], cot_ref[...])
    for at in range(0, model, LANES):
        tile = slice(at, at + LANES)
        ggate[tile, :] += mm_tn(normed_ref[:, tile], dgate_ref[...])

    @pl.when(i == pl.num_programs(0) - 1)
    def _():
        gout_ref[...] = gout[...].astype(BF16)
        ggate_ref[...] = ggate[...].astype(BF16)
        last_state = state[...]
        state[...] = jnp.zeros_like(state)

        def down(k, _):
            c = nc - 1 - k
            dso_ref[c] = state[...]
            for n, at, _ in groups(width):
                tile = slice(at, at + LANES)
                first = slice(2 * at, 2 * at + LANES)
                state[:, tile] = state[:, tile] * gates_ref[c, 0:1, first] + incf[c, :, tile]
            return 0

        lax.fori_loop(0, nc, down, 0)
        send_sides(
            at_ref,
            hops,
            jnp.concatenate([last_state, gtot_ref[:, width:]], axis=0),
            jnp.concatenate([state[...], gtot_ref[:, :width]], axis=0),
            messages,
        )


def mid_kernel(
    nh,
    act_ref,
    pack_ref,
    segrow_ref,
    rowa_ref,
    dy_ref,
    eye_ref,
    dx_ref,
    dbc_ref,
    pulls_ref,
):
    tb, width = dx_ref.shape
    s_at = iota((SPAN, SPAN), 0)
    t_at = iota((SPAN, SPAN), 1)
    lower = t_at > s_at
    lane = iota((SPAN, LANES), 1)
    row16 = iota((16, SPAN), 0)
    front_half = lane < HDIM
    for j in range(tb // SPAN):
        rows = slice(j * SPAN, (j + 1) * SPAN)
        pack = pack_ref[rows, :]
        bc = act_ref[rows, :LANES].astype(F32)
        cb = pltpu.roll(bc, HDIM, 1)
        within = (pack[:, 36:37] == segrow_ref[0:1, rows]) & (t_at != s_at)
        score = mm_nt(bc[:, :HDIM].astype(BF16), cb[:, :HDIM].astype(BF16))
        score = jnp.where(within, score, 0.0)
        ldt = jnp.log(jnp.maximum(softplus(pltpu.roll(pack, LANES - 16, 1)), TINY))
        pc = jnp.where(lane < nh, pack - ldt, pack + ldt)
        dscore = jnp.zeros((SPAN, SPAN), F32)
        kc = jnp.zeros((SPAN, LANES), F32)
        qr = jnp.zeros((16, SPAN), F32)
        for n, at, heads in groups(width):
            tile = slice(at, at + LANES)
            dyp = dy_ref[rows, tile]
            dmats = mm_nt(stacked(act_ref[rows, LANES + at : 2 * LANES + at]), dyp)
            mats = []
            for m, h in enumerate(heads):
                decay = jnp.exp(
                    jnp.where(
                        lower,
                        rowa_ref[h : h + 1, rows] - pc[:, h : h + 1],
                        pc[:, nh + h : nh + h + 1] - rowa_ref[nh + h : nh + h + 1, rows],
                    )
                )
                spot = dmats[m * SPAN : (m + 1) * SPAN, :] * decay
                dscore = dscore + spot
                mats.append((score * decay).astype(BF16))
                pull = spot * score
                pull_low = jnp.where(lower, pull, 0.0)
                pull_up = pull - pull_low
                qr = jnp.where(row16 == h, jnp.sum(pull_low, axis=0, keepdims=True), qr)
                qr = jnp.where(row16 == nh + h, jnp.sum(pull_up, axis=0, keepdims=True), qr)
                kc = jnp.where(lane == h, jnp.sum(pull_low, axis=1, keepdims=True), kc)
                kc = jnp.where(lane == nh + h, jnp.sum(pull_up, axis=1, keepdims=True), kc)
            dx_ref[rows, tile] = mm(jnp.concatenate(mats, axis=1), stacked(dyp)).astype(BF16)
        dscore = jnp.where(within, dscore, 0.0).astype(BF16)
        cpad = jnp.where(front_half, cb, 0.0).astype(BF16)
        bpad = jnp.where(front_half, 0.0, cb).astype(BF16)
        dbc_ref[rows, :] = mm(dscore, cpad) + mm_tn(dscore, bpad)
        pulls_ref[rows, :] = kc + exact_tn(qr, eye_ref[...])


def back_kernel(
    nh,
    peers,
    hops,
    own,
    at_ref,
    act_ref,
    slope_ref,
    pack_ref,
    tot_ref,
    dy_ref,
    full_ref,
    dso_ref,
    dro_ref,
    gsuf_ref,
    gpre_ref,
    gates_ref,
    dxin_ref,
    dbc_ref,
    pulls_ref,
    uv_ref,
    uvh_ref,
    halocols_ref,
    taps_ref,
    skip_ref,
    pcol_ref,
    ex_ref,
    ext_ref,
    tril_ref,
    triu_ref,
    normed_ref,
    normh_ref,
    dgate_ref,
    wg_ref,
    wcat_ref,
    gmix_ref,
    gskip_ref,
    *rest,
):
    arrived = rest[: 2 * hops]
    mine_ref, theirs_ref, *chunks = rest[2 * hops : 2 * hops + 2 + peers]
    dbuf, hbuf, dcat, acc, lines, dsent_ref, drent_ref, parts = rest[2 * hops + 2 + peers :]
    i = pl.program_id(0)
    last = pl.num_programs(0) - 1
    tb = act_ref.shape[0]
    width = act_ref.shape[1] - LANES
    model = normed_ref.shape[1]

    @pl.when(i == 0)
    def _():
        dbuf[tb : tb + 8, :] = jnp.zeros((8, LANES + width), F32)
        acc[...] = jnp.zeros_like(acc)
        lines[...] = jnp.zeros_like(lines)
        land_sides(at_ref, hops, arrived, drent_ref, dsent_ref)

    lane = iota((SPAN, LANES), 1)
    forward = lane < nh
    head_lane = lane < 16
    none = jnp.zeros((HDIM, 2 * LANES), BF16)
    for j in reversed(range(tb // SPAN)):
        rows = slice(j * SPAN, (j + 1) * SPAN)
        pack = pack_ref[rows, :]
        tot = tot_ref[j * 8 : j * 8 + 1, :]
        z = pltpu.roll(pack, LANES - 16, 1)
        dt = softplus(z)
        w = jnp.concatenate(
            [
                split(source_weights(pack, tot, dt, lane, nh), 1),
                split(target_weights(pack, tot, lane, nh), 1),
            ],
            axis=0,
        )
        bc = act_ref[rows, :LANES].astype(F32)
        b = bc[:, :HDIM].astype(BF16)
        c = pltpu.roll(bc, HDIM, 1)[:, :HDIM].astype(BF16)
        dbc = dbc_ref[rows, :]
        carried = jnp.zeros((SPAN, LANES), F32)
        leaving = jnp.zeros((SPAN, LANES), F32)
        through = jnp.zeros((8, LANES), F32)
        for n, at, _ in groups(width):
            tile = slice(at, at + LANES)
            wtile = slice(LANES + at, 2 * LANES + at)
            both = slice(2 * at, 2 * at + 2 * LANES)
            first = slice(2 * at, 2 * at + LANES)
            second = slice(2 * at + LANES, 2 * at + 2 * LANES)
            wide = mm(w, ex_ref[:, both])
            x = act_ref[rows, wtile].astype(F32)
            dy = dy_ref[rows, tile].astype(F32)
            x2 = jnp.concatenate([x, x], axis=1)
            dy2 = jnp.concatenate([dy, dy], axis=1)
            held = full_ref[j, :, both]
            dheld = jnp.concatenate(
                [
                    dso_ref[j, :, tile] + gsuf_ref[j, 0:1, first] * dsent_ref[:, tile],
                    dro_ref[j, :, tile] + gpre_ref[j, 0:1, second] * drent_ref[:, tile],
                ],
                axis=1,
            )
            dheld_low = dheld.astype(BF16)
            to_wide = wide[:SPAN]
            fro_wide = wide[SPAN:]
            flow = mm(b, dheld_low) * to_wide
            seen = mm(c, held) * fro_wide
            dbc = dbc + mm_nt((x2 * to_wide).astype(BF16), jnp.concatenate([dheld_low, none], axis=0))
            dbc = dbc + mm_nt((dy2 * fro_wide).astype(BF16), jnp.concatenate([none, held], axis=0))
            ext = ext_ref[both, :]
            carried = carried + mm((dy2 * seen).astype(BF16), ext)
            leaving = leaving + mm((x2 * flow).astype(BF16), ext)
            product = jnp.sum(dheld * held.astype(F32), axis=0, keepdims=True) * gates_ref[j, :, both]
            through = through + mm(product.astype(BF16), ext)
            dx = dxin_ref[rows, tile].astype(F32) + flow[:, :LANES] + flow[:, LANES:]
            dx = dx + skip_ref[0:1, tile] * dy
            dbuf[rows, wtile] = dx * slope_ref[rows, wtile].astype(F32)
        dbuf[rows, :LANES] = dbc * slope_ref[rows, :LANES].astype(F32)
        pulls = pulls_ref[rows, :]
        kc = jnp.where(head_lane, pulls, 0.0)
        moved = jnp.where(head_lane, pltpu.roll(pulls, LANES - 16, 1), 0.0) + carried - kc
        before = mm(tril_ref[:, : 2 * SPAN], split(jnp.where(forward, leaving, moved), 0))
        after = mm(triu_ref[:, : 2 * SPAN], split(jnp.where(forward, moved, leaving), 0))
        dlog = before + after - leaving + through[0:1, :]
        sigz = sigmoid(z)
        rate = pcol_ref[1:2, :]
        dstep = (kc + leaving) * (sigz / jnp.maximum(dt, TINY)) - dlog * rate * sigz
        dstep = jnp.where(head_lane, dstep, 0.0)
        dcat[rows, :LANES] = dstep.astype(BF16)
        lines[7:8, :LANES] += jnp.sum(dstep, axis=0, keepdims=True)
        ends = jnp.where(head_lane, -dlog * dt * rate, 0.0)
        lines[8:9, :LANES] += jnp.sum(ends, axis=0, keepdims=True)
        for at in range(0, LANES + width, LANES):
            tile = slice(at, at + LANES)
            dconv = dbuf[rows, tile]
            uv = uv_ref[rows, tile].astype(F32)
            du = taps_ref[0:1, tile] * dconv
            lines[1:2, tile] += jnp.sum(uv * dconv, axis=0, keepdims=True)
            for k in (1, 2, 3):
                shifted = dbuf[j * SPAN + k : (j + 1) * SPAN + k, tile] * pack[:, 40 + k : 41 + k]
                du = du + taps_ref[k : k + 1, tile] * shifted
                lines[1 + k : 2 + k, tile] += jnp.sum(uv * shifted, axis=0, keepdims=True)
            dcat[rows, LANES + at : 2 * LANES + at] = du.astype(BF16)

    edge = dbuf[0:8, :]
    dbuf[tb : tb + 8, :] = edge
    for at in range(0, model, LANES):
        tile = slice(at, at + LANES)
        part = mm_nt(dgate_ref[...], wg_ref[tile, :]) + mm_nt(dcat[...], wcat_ref[tile, :])
        parts[:, tile] = part.astype(BF16)
        normed = normed_ref[:, tile]
        lines[0:1, tile] += jnp.sum(part * normed.astype(F32), axis=0, keepdims=True)
        acc[tile, :] += mm_tn(normed, dcat[...])
    side = ((last - i) * tb // own ^ at_ref[1]) % 2

    @pl.when(side == 0)
    def _():
        mine_ref[0] = parts[...]

    @pl.when(side == 1)
    def _():
        theirs_ref[0] = parts[...]

    @pl.when(i == last)
    def _():
        taps_at = slice(0, LANES + width)
        hbuf[0:8, :] = jnp.zeros_like(edge)
        hbuf[8:16, :] = edge
        duh = jnp.zeros_like(edge)
        for k in (1, 2, 3):
            shifted = hbuf[k : k + 8, :] * halocols_ref[:, k - 1 : k]
            duh = duh + taps_ref[k : k + 1, :] * shifted
            lines[1 + k : 2 + k, taps_at] += jnp.sum(uvh_ref[...] * shifted, axis=0, keepdims=True)
        duh = duh.astype(BF16)
        normh = normh_ref[...]
        parth = mm_nt(duh, wcat_ref[:, LANES:])
        lines[0:1, :] += jnp.sum(parth * normh.astype(F32), axis=0, keepdims=True)
        skips = jnp.zeros((8, LANES), F32)
        for n, at, _ in groups(width):
            ext = ext_ref[2 * at : 2 * at + LANES, :]
            high = gskip_ref[:, at : at + LANES].astype(BF16)
            low = (gskip_ref[:, at : at + LANES] - high.astype(F32)).astype(BF16)
            skips = skips + mm(high, ext) + mm(low, ext)
        lines[5:6, :LANES] = skips[0:1, :]
        lines[6:7, :width] = gmix_ref[0:1, :]
        acc[:, LANES:] += mm_tn(normh, duh)
        placed = jnp.where(iota((16, LANES), 1) == iota((16, LANES), 0) + 16, 1.0, 0.0)
        acc[:, :LANES] += exact_tn(lines[...], placed)
        row8 = iota((8, LANES), 0)
        taken = iota((8, LANES), 1) == 19 + 3 * at_ref[0] + row8
        taken = taken & (row8 > 4) & (at_ref[0] > 0)
        acc[:, :LANES] += exact_tn(parth, jnp.where(taken, 1.0, 0.0))
        size = model // peers
        for k in range(peers):
            start = pl.multiple_of((at_ref[0] ^ k) * size, 8)
            chunks[k][...] = acc[pl.ds(start, size), :].astype(BF16)


def token_grads(cot, x, s, dn, gain):
    scaled = dn * gain
    inside = jnp.mean(scaled * x, axis=1, keepdims=True)
    return (cot + s * scaled - x * (s * s * s) * inside).astype(BF16)


def finish_kernel(nh, peers, shares, at_ref, *refs):
    chunks = refs[:peers]
    eye_ref, ingain_ref, x_ref, cot_ref, dn_ref = refs[peers : peers + 5]
    gain_ref, value_ref, state_ref, step_ref, bias_ref, decay_ref = refs[peers + 5 : peers + 11]
    convv_ref, convs_ref, skip_ref, mixer_ref, late_ref, extra = refs[peers + 11 :]
    size = chunks[0].shape[0]
    real_width = value_ref.shape[1]
    heads = step_ref.shape[0]
    for k in range(peers):
        rows = pl.ds(pl.multiple_of((at_ref[0] ^ k) * size, 8), size)
        extra[rows, :] = chunks[k][:, :LANES].astype(F32)
        state_ref[rows, :] = chunks[k][:, LANES : 2 * LANES].astype(F32)
        value_ref[rows, :] = chunks[k][:, 2 * LANES : 2 * LANES + real_width].astype(F32)
    found = extra[...].astype(BF16)
    lines = mm_nt(eye_ref[...], found)
    row16 = iota((16, LANES), 0)
    taken = iota((16, LANES), 1) == 27 + 3 * at_ref[0] + row16 - 13
    taken = taken & (row16 > 12) & (at_ref[1] == shares - 1)
    late = mm_nt(jnp.where(taken, 1.0, 0.0).astype(BF16), found)
    x = x_ref[...].astype(F32)
    s = lax.rsqrt(jnp.mean(x * x, axis=1, keepdims=True) + EPSILON)
    cot = cot_ref[...].astype(F32)
    late_ref[...] = token_grads(cot, x, s, dn_ref[...] + late, ingain_ref[...])
    for h in range(heads):
        step_ref[h, 0:1, :] = lines[h : h + 1, :]
        step_ref[h, 1:2, :] = lines[nh + h : nh + h + 1, :]
    gain_ref[...] = lines[16:17, :] / ingain_ref[...]
    convs_ref[...] = lines[17:21, :LANES]
    convv_ref[...] = lines[17:21, LANES : LANES + real_width]
    skip_ref[...] = lines[21:22, :heads]
    mixer_ref[...] = lines[22:23, :real_width]
    bias_ref[0:1, :] = lines[23:24, :heads]
    bias_ref[1:2, :] = lines[23:24, nh : nh + heads]
    decay_ref[...] = lines[24:25, :heads] + lines[24:25, nh : nh + heads]


def whole(shape):
    return pl.BlockSpec(shape, lambda i, *_: (0,) * len(shape))


def row_block(rows, width):
    return pl.BlockSpec((rows, width), lambda i, *_: (i, 0))


def lane_block(rows, width):
    return pl.BlockSpec((rows, width), lambda i, *_: (0, i))


def chunk_block(per, rows, width):
    return pl.BlockSpec((per, rows, width), lambda i, *_: (i, 0, 0))


def sds(shape, dtype):
    return jax.ShapeDtypeStruct(shape, dtype)


def call(kernel, name, grid, ins, outs, scratch, flops, operands, scalars=()):
    return pl.pallas_call(
        kernel,
        name=name,
        grid_spec=pltpu.PrefetchScalarGridSpec(
            num_scalar_prefetch=len(scalars),
            grid=(grid,),
            in_specs=ins,
            out_specs=[spec for spec, _ in outs],
            scratch_shapes=scratch,
        ),
        out_shape=[shape for _, shape in outs],
        compiler_params=pltpu.CompilerParams(
            dimension_semantics=("arbitrary",), vmem_limit_bytes=56 * 1024 * 1024
        ),
        cost_estimate=pl.CostEstimate(
            flops=int(flops), bytes_accessed=1, transcendentals=0
        ),
    )(*scalars, *operands)


def shifted_in(array, axis, by):
    length = lax.axis_size(axis)
    pairs = [(i, i + by) for i in range(length) if 0 <= i + by < length]
    return lax.ppermute(array, axis, pairs)


def exchange_sides(messages, hops):
    size = lax.axis_size("seq")
    arrived = []
    for d in range(1, hops + 1):
        for side in (0, 1):
            pairs = [(i, i + d) for i in range(size - d) if (i // d) % 2 == side]
            both = pairs + [(b, a) for a, b in pairs]
            arrived.append(lax.ppermute(messages[len(arrived)], "seq", both))
    return arrived


def swap(array, axis, k):
    n = lax.axis_size(axis)
    return lax.ppermute(array, axis, [(i, i ^ k) for i in range(n)])


def sum_over(array, axis):
    size = lax.axis_size(axis)
    result = array
    for k in range(1, size):
        result = result + lax.ppermute(array, axis, [(i, i ^ k) for i in range(size)])
    return result


def per_device(
    tokens,
    input_gain,
    proj_gate,
    proj_value,
    proj_state,
    proj_step,
    step_bias,
    decay_log,
    conv_value,
    conv_state,
    skip_gain,
    mixer_gain,
    proj_out,
    doc_lengths,
    pad_mask,
    cotangent,
):
    head_devices = lax.axis_size("head")
    length = pad_mask.shape[0]
    model = tokens.shape[1]
    real_width = proj_gate.shape[1]
    real_heads = proj_step.shape[2]
    inner = real_width * head_devices
    width = -(-real_width // LANES) * LANES
    nh = width // HDIM

    def padded(array, axis, size):
        if array.shape[axis] == size:
            return array
        widths = [(0, 0)] * array.ndim
        widths[axis] = (0, size - array.shape[axis])
        return jnp.pad(array, widths)

    proj_gate = padded(proj_gate, 1, width)
    proj_value = padded(proj_value, 1, width)
    proj_step = padded(proj_step, 2, nh)
    step_bias = padded(step_bias, 1, nh)
    conv_value = padded(conv_value, 1, width)
    skip_gain = padded(skip_gain, 0, nh)
    mixer_gain = padded(mixer_gain, 0, width)
    proj_out = padded(proj_out, 0, width)
    nc = length // SPAN
    tb = BLOCK
    per = tb // SPAN
    grid = length // tb
    wide = LANES + width
    hops = -(-(LONGEST - 1) // length)
    seq_index = lax.axis_index("seq")
    first_place = seq_index * length
    all_tokens = length * lax.axis_size("seq")

    edge_rows = shifted_in(tokens[tokens.shape[0] - 8 :], "seq", 1)
    here = lax.axis_index("head")
    halo = jnp.where(here == head_devices - 1, edge_rows, 0)
    for k in range(1, head_devices):
        halo = halo + jnp.where(here ^ k == head_devices - 1, swap(edge_rows, "head", k), 0)

    offsets = jnp.cumsum(doc_lengths) - doc_lengths
    room = -(-(offsets.shape[0] + 1) // LANES) * LANES - offsets.shape[0]
    fill = jnp.where(jnp.arange(room) == 0, all_tokens, 2 * all_tokens).astype(offsets.dtype)
    offsets = jnp.concatenate([offsets, fill])[None, :]
    live_row = pad_mask[None, :]
    lanes = np.arange(LANES)
    column = np.arange(2 * width)
    head_of = column // (2 * LANES) * 2 + column % LANES // HDIM
    head_of = head_of + np.where(column % (2 * LANES) >= LANES, nh, 0)
    ext = jnp.asarray(head_of[:, None] == lanes[None, :], BF16)
    ex = jnp.asarray(np.tile(head_of[None, :] == lanes[:, None], (2, 1)), BF16)
    at = np.arange(SPAN)
    tril = jnp.asarray(np.tile(at[:, None] >= at[None, :], (1, 3)), BF16)
    triu = at[:, None] <= at[None, :]
    triu_wide = jnp.asarray(np.tile(triu, (1, 2)), BF16)
    triu_tall = jnp.asarray(np.tile(triu, (3, 1)), BF16)
    eye = jnp.asarray(np.arange(16)[:, None] == lanes[None, :], F32)
    eye16 = jnp.asarray(np.arange(16)[:, None] + 16 == lanes[None, :], F32)
    picked = jnp.asarray(np.arange(32)[:, None] == lanes[None, :], BF16)
    peers = lax.axis_size("seq")
    own = length // head_devices
    bits = head_devices.bit_length() - 1
    scalars = [jnp.stack([seq_index, here, first_place]).astype(jnp.int32)]
    size = model // peers

    rate = padded(jnp.exp(decay_log), 0, nh)
    bias_line = jnp.concatenate([step_bias[0], step_bias[1]])
    rate_line = jnp.concatenate([rate, rate])
    pcol = jnp.zeros((8, LANES), F32)
    pcol = pcol.at[0, : 2 * nh].set(bias_line).at[1, : 2 * nh].set(rate_line)
    pcol = pcol.at[0, 16 : 16 + 2 * nh].set(bias_line)
    pad16 = jnp.zeros((16 - 2 * nh,), F32)
    prow = jnp.concatenate(
        [
            jnp.broadcast_to(jnp.concatenate([bias_line, pad16])[:, None], (16, SPAN)),
            jnp.broadcast_to(jnp.concatenate([rate_line, pad16])[:, None], (16, SPAN)),
        ],
        axis=1,
    )
    steps = jnp.concatenate([proj_step[0], proj_step[1]], axis=1)
    wst = jnp.pad(steps, ((0, 0), (0, 16 - 2 * nh)))
    wst = jnp.pad(jnp.tile(wst, (1, 2)), ((0, 0), (0, LANES - 32)))
    wback = jnp.pad(steps, ((0, 0), (0, LANES - 2 * nh)))
    wstr = jnp.pad(steps.T, ((0, 16 - 2 * nh), (0, 0)))
    wsv = jnp.concatenate([proj_state, proj_value], axis=1)
    taps = jnp.pad(jnp.concatenate([conv_state, conv_value], axis=1), ((0, 4), (0, 0)))
    gain = jnp.broadcast_to(input_gain[None, :], (8, model))
    mg = jnp.broadcast_to(mixer_gain[None, :], (8, width))
    skip = jnp.broadcast_to(jnp.repeat(skip_gain, HDIM)[None, :], (8, width))

    wcat = jnp.concatenate([wback, wsv], axis=1)
    pieces_of = {0: tokens}
    for bit in [1 << b for b in range(bits - 1, 0, -1)]:
        pieces_of.update({k | bit: swap(v, "head", bit) for k, v in pieces_of.items()})
    prelims = (halo, offsets, live_row, pcol, prow, wst, wstr, wsv, taps, gain, mg, skip, wcat)
    pieces_of, late, prelims, scalars = lax.optimization_barrier(
        (pieces_of, cotangent, prelims, scalars)
    )
    halo, offsets, live_row, pcol, prow, wst, wstr, wsv, taps, gain, mg, skip, wcat = prelims
    pieces_of.update({k | 1: swap(v, "head", 1) for k, v in pieces_of.items()})
    token_pieces = [pieces_of[k] for k in range(head_devices)]
    cot_all = lax.all_gather(late, "head", axis=0, tiled=True)

    rows = partial(row_block, tb)
    states = sds((nc, HDIM, width), F32)
    gates_of = sds((nc, 8, 2 * width), F32)
    message = sds((HDIM + 8, width), F32)
    state_block = chunk_block(per, HDIM, width)
    gate_block = chunk_block(per, 8, 2 * width)
    tot_block = row_block(per * 8, LANES)
    messages = [(whole(message.shape), message)] * (2 * hops)

    def taller(factor):
        big = tb * factor
        return (
            grid // factor,
            partial(row_block, big),
            partial(lane_block, width=big),
            partial(chunk_block, per * factor),
            row_block(per * factor * 8, LANES),
        )

    def slot_of(j, at):
        place = j ^ at[1]
        return sum(((place >> b) & 1) << (bits - 1 - b) for b in range(bits))

    each = own // tb

    def piece_block(k):
        def index(i, at):
            return jnp.clip(i - (at[1] ^ k) * each, 0, each - 1), 0

        return pl.BlockSpec((tb, model), index)

    def side_block(side):
        def index(i, at):
            row = grid - 1 - i
            j, sub = row // each, row % each
            ours = (j ^ at[1]) % 2 == side
            first = j == head_devices - 1
            j = jnp.where(ours, j, jnp.where(first, j - 1, j + 1))
            sub = jnp.where(ours, sub, jnp.where(first, each - 1, 0))
            return slot_of(j, at) % (head_devices // 2), sub, 0

        return pl.BlockSpec((1, tb, model), index)

    (
        normed,
        normh,
        gate_in,
        acted,
        slope,
        uv,
        uvh,
        pack,
        rowa,
        rowp,
        seg_row,
        halo_cols,
        tot,
        sf,
        rb,
        gates,
        gpre,
        gsuf,
        gtot,
        *ahead,
    ) = call(
        partial(front_kernel, nh, hops, head_devices, own),
        "front",
        grid,
        [piece_block(k) for k in range(head_devices)]
        + [
            whole((8, model)),
            whole((8, model)),
            whole((model, width)),
            whole((model, wide)),
            whole((model, LANES)),
            whole((16, model)),
            whole((8, LANES)),
            whole((16, 2 * SPAN)),
            whole((8, wide)),
            whole(offsets.shape),
            lane_block(1, tb),
            whole(ex.shape),
            whole(tril.shape),
            whole(triu_tall.shape),
        ],
        [
            (rows(model), sds((length, model), BF16)),
            (whole((8, model)), sds((8, model), BF16)),
            (rows(width), sds((length, width), BF16)),
            (rows(wide), sds((length, wide), BF16)),
            (rows(wide), sds((length, wide), BF16)),
            (rows(wide), sds((length, wide), BF16)),
            (whole((8, wide)), sds((8, wide), F32)),
            (rows(LANES), sds((length, LANES), F32)),
            (lane_block(16, tb), sds((16, length), F32)),
            (lane_block(16, tb), sds((16, length), F32)),
            (lane_block(8, tb), sds((8, length), F32)),
            (whole((8, LANES)), sds((8, LANES), F32)),
            (tot_block, sds((nc * 8, LANES), F32)),
            (state_block, states),
            (whole(states.shape), states),
            (whole(gates_of.shape), gates_of),
            (whole(gates_of.shape), gates_of),
            (whole(gates_of.shape), gates_of),
            (whole((8, 2 * width)), sds((8, 2 * width), F32)),
        ]
        + messages,
        [
            pltpu.VMEM((tb + 8, wide), F32),
            pltpu.VMEM((HDIM, width), F32),
            pltpu.VMEM((nc, HDIM, width), F32),
            pltpu.VMEM((tb, LANES), F32),
            pltpu.VMEM((per * 8, LANES), F32),
            pltpu.VMEM((SPAN + 16, LANES), F32),
        ],
        25e9,
        token_pieces
        + [
            halo,
            gain,
            proj_gate,
            wsv,
            wst,
            wstr,
            pcol,
            prow,
            taps,
            offsets,
            live_row,
            ex,
            tril,
            triu_tall,
        ],
        scalars,
    )

    ahead = exchange_sides(ahead, hops)

    big_grid, big_rows, big_lanes, big_chunks, big_tot = taller(2)
    yin, dout = call(
        partial(inner_kernel, nh),
        "inner",
        big_grid,
        [
            big_rows(wide),
            big_rows(LANES),
            big_lanes(8),
            big_lanes(16),
            whole((8, width)),
            big_rows(model),
            whole((width, model)),
        ],
        [
            (big_rows(width), sds((length, width), BF16)),
            (big_rows(width), sds((length, width), BF16)),
        ],
        [],
        6e9,
        [acted, pack, seg_row, rowp, skip, cot_all, proj_out],
    )

    y, stat, full = call(
        partial(merge_kernel, nh, hops),
        "merge",
        big_grid,
        [
            big_rows(LANES),
            big_rows(LANES),
            big_tot,
            big_chunks(HDIM, width),
            big_chunks(HDIM, width),
            big_chunks(8, 2 * width),
            big_chunks(8, 2 * width),
            big_rows(width),
            big_rows(width),
            big_rows(width),
            whole((8, width)),
            whole(ex.shape),
        ]
        + [whole(message.shape)] * (2 * hops),
        [
            (big_rows(width), sds((length, width), BF16)),
            (big_lanes(8), sds((8, length), F32)),
            (big_chunks(HDIM, 2 * width), sds((nc, HDIM, 2 * width), BF16)),
        ],
        [pltpu.VMEM((HDIM, width), F32)] * 2,
        6e9,
        [acted, pack, tot, sf, rb, gpre, gsuf, yin, gate_in, dout, mg, ex] + ahead,
        scalars,
    )

    shares = [stat]
    for k in range(1, head_devices):
        shares.append(lax.ppermute(stat, "head", [(i, i ^ k) for i in range(head_devices)]))

    mixer, dy, dgate, gmix, gskip, gout, ggate, dso, dro, *behind = call(
        partial(turn_kernel, nh, inner, head_devices, hops),
        "turn",
        grid,
        [
            rows(width),
            rows(width),
            rows(width),
            whole((8, width)),
            rows(wide),
            rows(LANES),
            tot_block,
            whole(gates_of.shape),
            whole((8, 2 * width)),
            whole(ex.shape),
            whole((16, LANES)),
            rows(model),
            rows(model),
            whole((width, model)),
        ]
        + [lane_block(8, tb)] * head_devices,
        [
            (rows(model), sds((length, model), BF16)),
            (rows(width), sds((length, width), BF16)),
            (rows(width), sds((length, width), BF16)),
            (whole((8, width)), sds((8, width), F32)),
            (whole((8, width)), sds((8, width), F32)),
            (whole((width, model)), sds((width, model), BF16)),
            (whole((model, width)), sds((model, width), BF16)),
            (whole(states.shape), states),
            (state_block, states),
        ]
        + messages,
        [
            pltpu.VMEM((HDIM, width), F32),
            pltpu.VMEM((nc, HDIM, width), F32),
            pltpu.VMEM((tb, width), BF16),
            pltpu.VMEM((width, model), F32),
            pltpu.VMEM((model, width), F32),
        ],
        24e9,
        [
            y,
            gate_in,
            dout,
            mg,
            acted,
            pack,
            tot,
            gates,
            gtot,
            ex,
            eye,
            normed,
            cot_all,
            proj_out,
        ]
        + shares,
        scalars,
    )

    grad_proj_out, grad_proj_gate = lax.psum((gout, ggate), "seq")
    mixer = lax.psum_scatter(mixer, "head", scatter_dimension=0, tiled=True)
    behind = exchange_sides(behind, hops)

    dxin, dbc, pulls = call(
        partial(mid_kernel, nh),
        "mid",
        grid,
        [
            rows(wide),
            rows(LANES),
            lane_block(8, tb),
            lane_block(16, tb),
            rows(width),
            whole((16, LANES)),
        ],
        [
            (rows(width), sds((length, width), BF16)),
            (rows(LANES), sds((length, LANES), F32)),
            (rows(LANES), sds((length, LANES), F32)),
        ],
        [],
        18e9,
        [acted, pack, seg_row, rowa, dy, eye16],
    )

    back = lambda i: grid - 1 - i

    def rev(spec):
        return pl.BlockSpec(spec.block_shape, lambda i, *_: spec.index_map(back(i)))

    mine, theirs, *chunks = call(
        partial(back_kernel, nh, peers, hops, own),
        "back",
        grid,
        [
            rev(rows(wide)),
            rev(rows(wide)),
            rev(rows(LANES)),
            rev(tot_block),
            rev(rows(width)),
            rev(chunk_block(per, HDIM, 2 * width)),
            rev(state_block),
            rev(state_block),
            rev(gate_block),
            rev(gate_block),
            rev(gate_block),
            rev(rows(width)),
            rev(rows(LANES)),
            rev(rows(LANES)),
            rev(rows(wide)),
            whole((8, wide)),
            whole((8, LANES)),
            whole((8, wide)),
            whole((8, width)),
            whole((8, LANES)),
            whole(ex.shape),
            whole(ext.shape),
            whole(tril.shape),
            whole(triu_wide.shape),
            rev(rows(model)),
            whole((8, model)),
            rev(rows(width)),
            whole((model, width)),
            whole((model, LANES + wide)),
            whole((8, width)),
            whole((8, width)),
        ]
        + [whole(message.shape)] * (2 * hops),
        [
            (side_block(0), sds((head_devices // 2, own, model), BF16)),
            (side_block(1), sds((head_devices // 2, own, model), BF16)),
        ]
        + [(whole((size, LANES + wide)), sds((size, LANES + wide), BF16))] * peers,
        [
            pltpu.VMEM((tb + 8, wide), F32),
            pltpu.VMEM((16, wide), F32),
            pltpu.VMEM((tb, LANES + wide), BF16),
            pltpu.VMEM((model, LANES + wide), F32),
            pltpu.VMEM((16, model), F32),
            pltpu.VMEM((HDIM, width), F32),
            pltpu.VMEM((HDIM, width), F32),
            pltpu.VMEM((tb, model), BF16),
        ],
        33e9,
        [
            acted,
            slope,
            pack,
            tot,
            dy,
            full,
            dso,
            dro,
            gsuf,
            gpre,
            gates,
            dxin,
            dbc,
            pulls,
            uv,
            uvh,
            halo_cols,
            taps,
            skip,
            pcol,
            ex,
            ext,
            tril,
            triu_wide,
            normed,
            normh,
            dgate,
            proj_gate,
            wcat,
            gmix,
            gskip,
        ]
        + behind,
        scalars,
    )

    got = swap(theirs, "head", 1)
    summed = chunks[0].astype(F32)
    for k in range(1, peers):
        summed = summed + swap(chunks[k], "seq", k).astype(F32)
    shared = summed[:, : 2 * LANES]
    row_at = seq_index * size + jnp.arange(size)[:, None]
    lane_at = jnp.arange(2 * LANES)[None, :]
    common = (lane_at == 16) | (lane_at > 26)
    common = common | ((lane_at > 16) & (lane_at < 21) & (row_at < LANES))
    shared = jnp.where(common, sum_over(shared, "head"), shared)

    own_in = mine.astype(F32) + got.astype(F32)
    for b in range(1, bits):
        half = own_in.shape[0] // 2
        own_in = own_in[:half] + swap(own_in[half:].astype(BF16), "head", 1 << b).astype(F32)
    own_in = own_in[0]

    reduced = jnp.concatenate([shared, summed[:, 2 * LANES :]], axis=1).astype(BF16)
    spread_out = [reduced] + [swap(reduced, "seq", k) for k in range(1, peers)]
    layer_out = (tokens.astype(F32) + mixer.astype(F32)).astype(BF16)

    token_values = tokens.astype(F32)
    scale_rows = lax.rsqrt(jnp.mean(token_values * token_values, axis=1, keepdims=True) + EPSILON)
    grad_tokens = token_grads(cotangent.astype(F32), token_values, scale_rows, own_in, input_gain)

    finals = [
        sds((1, model), F32),
        sds((model, real_width), F32),
        sds((model, LANES), F32),
        sds((real_heads, 2, model), F32),
        sds((2, real_heads), F32),
        sds((1, real_heads), F32),
        sds((4, real_width), F32),
        sds((4, LANES), F32),
        sds((1, real_heads), F32),
        sds((1, real_width), F32),
        sds((16, model), BF16),
    ]
    ggain, gvalue, gstate, gstep, gbias, gdecay, gconvv, gconvs, gskips, gmixer, late = call(
        partial(finish_kernel, nh, peers, head_devices),
        "finish",
        1,
        [whole((size, LANES + wide))] * peers
        + [whole((32, LANES)), whole((1, model))]
        + [whole((16, model))] * 3,
        [(whole(f.shape), f) for f in finals],
        [pltpu.VMEM((model, LANES), F32)],
        3e9,
        spread_out
        + [picked, input_gain[None, :]]
        + [tokens[own - 16 :], cotangent[own - 16 :], own_in[own - 16 :]],
        scalars,
    )
    grad_tokens = lax.dynamic_update_slice(grad_tokens, late, (own - 16, 0))
    return (
        layer_out,
        grad_tokens,
        ggain[0],
        grad_proj_gate[:, :real_width].astype(F32),
        gvalue,
        gstate,
        jnp.transpose(gstep, (1, 2, 0)),
        gbias,
        gdecay[0],
        gconvv,
        gconvs,
        gskips[0],
        gmixer[0],
        grad_proj_out[:real_width].astype(F32),
    )


def solution(mesh):
    return jax.shard_map(
        per_device,
        mesh=mesh,
        in_specs=(
            P(("seq", "head"), None),
            P(),
            P(None, "head"),
            P(None, "head"),
            P(),
            P(None, None, "head"),
            P(None, "head"),
            P("head"),
            P(None, "head"),
            P(),
            P("head"),
            P("head"),
            P("head", None),
            P(),
            P("seq"),
            P(("seq", "head"), None),
        ),
        out_specs=(
            P(("seq", "head"), None),
            P(("seq", "head"), None),
            P(),
            P(None, "head"),
            P(None, "head"),
            P(),
            P(None, None, "head"),
            P(None, "head"),
            P("head"),
            P(None, "head"),
            P(),
            P("head"),
            P("head"),
            P("head", None),
        ),
        check_vma=False,
    )
```

```python
from functools import partial

import jax
import jax.numpy as jnp
import numpy as np
from jax import lax
from jax.experimental import pallas as pl
from jax.experimental.pallas import tpu as pltpu
from jax.sharding import PartitionSpec as P

SPAN = 128
HDIM = 64
LANES = 128
LONGEST = 4096
EPSILON = 1e-05
TINY = 1e-30
F32 = jnp.float32
BF16 = jnp.bfloat16
BLOCK = 512
ASIDE = 256


def mm(a, b):
    return jnp.dot(a, b, preferred_element_type=F32)


def mm_nt(a, b):
    return lax.dot_general(a, b, (((1,), (1,)), ((), ())), preferred_element_type=F32)


def mm_tn(a, b):
    return lax.dot_general(a, b, (((0,), (0,)), ((), ())), preferred_element_type=F32)


def pieces(v):
    high = v.astype(BF16)
    rest = v - high.astype(F32)
    mid = rest.astype(BF16)
    return high, mid, (rest - mid.astype(F32)).astype(BF16)


def exact_tn(a, b):
    return lax.dot_general(
        a, b, (((0,), (0,)), ((), ())), precision=lax.Precision.HIGHEST, preferred_element_type=F32
    )


def split(v, axis):
    high = v.astype(BF16)
    return jnp.concatenate([high, (v - high.astype(F32)).astype(BF16)], axis=axis)


def two_part(v, ex):
    high = v.astype(BF16)
    return mm(high, ex) + mm((v - high.astype(F32)).astype(BF16), ex)


def sigmoid(v):
    return 1.0 / (1.0 + jnp.exp(-v))


def softplus(v):
    return jnp.maximum(v, 0.0) + jnp.log1p(jnp.exp(-jnp.abs(v)))


def iota(shape, dim):
    return lax.broadcasted_iota(jnp.int32, shape, dim)


def wide_tiles(width):
    return [slice(at, min(at + 2 * LANES, width)) for at in range(0, width, 2 * LANES)]


def groups(width):
    return [(n, n * LANES, (2 * n, 2 * n + 1)) for n in range(width // LANES)]


def sides(v, width):
    tiles = [v[:, at : at + LANES] for at in range(0, 2 * width, LANES)]
    return jnp.concatenate(tiles[::2], axis=1), jnp.concatenate(tiles[1::2], axis=1)


def stacked(v):
    first = iota(v.shape, 1) < HDIM
    zero = jnp.zeros_like(v)
    return jnp.concatenate([jnp.where(first, v, zero), jnp.where(first, zero, v)], axis=0)


def source_weights(pack, tot, dt, lane, nh):
    forward = lane < nh
    gap = jnp.where(forward, tot - pack, pack)
    kept = jnp.where(forward, pack[:, 38:39], pack[:, 40:41])
    return jnp.where(lane < 16, jnp.exp(jnp.where(lane < 16, gap, 0.0)) * kept * dt, 0.0)


def target_weights(pack, tot, lane, nh):
    forward = lane < nh
    gap = jnp.where(forward, pack, tot - pack)
    kept = jnp.where(forward, pack[:, 37:38], pack[:, 39:40])
    return jnp.where(lane < 16, jnp.exp(jnp.where(lane < 16, gap, 0.0)) * kept, 0.0)


def send_sides(at_ref, hops, up, down, refs):
    for d in range(1, hops + 1):
        low = (at_ref[0] // d) % 2 == 0
        refs[2 * d - 2][...] = jnp.where(low, up, down)
        refs[2 * d - 1][...] = jnp.where(low, down, up)


def land_sides(at_ref, hops, refs, from_earlier, from_later):
    for d in range(hops, 0, -1):
        low = (at_ref[0] // d) % 2 == 0
        first, second = refs[2 * d - 2][...], refs[2 * d - 1][...]
        for state, part in (
            (from_earlier, jnp.where(low, second, first)),
            (from_later, jnp.where(low, first, second)),
        ):
            if d == hops:
                state[...] = part[:HDIM]
            else:
                state[...] = part[:HDIM] + part[HDIM : HDIM + 1] * state[...]


def documents(off_ref, places):
    count = jnp.zeros(places.shape, F32)
    for at in range(0, off_ref.shape[1], LANES):
        begun = off_ref[0:1, at : at + LANES] <= places
        count = count + jnp.sum(jnp.where(begun, 1.0, 0.0), axis=1, keepdims=True)
    return count


def front_kernel(
    nh,
    hops,
    shares,
    own,
    at_ref,
    *refs,
):
    front_body(nh, hops, own, at_ref, refs[:shares], *refs[shares:])


def front_body(
    nh,
    hops,
    own,
    at_ref,
    x_refs,
    halo_ref,
    gain_ref,
    wg_ref,
    wsv_ref,
    wst_ref,
    wstr_ref,
    pcol_ref,
    prow_ref,
    taps_ref,
    off_ref,
    live_ref,
    ex_ref,
    tril_ref,
    triu_ref,
    normed_ref,
    normh_ref,
    gate_ref,
    act_ref,
    slope_ref,
    uv_ref,
    uvh_ref,
    pack_ref,
    rowa_ref,
    rowp_ref,
    segrow_ref,
    halocols_ref,
    tot_ref,
    sf_ref,
    rb_ref,
    gates_ref,
    gpre_ref,
    gsuf_ref,
    gtot_ref,
    *rest,
):
    messages = rest[: 2 * hops]
    ubuf, state, incb, marks, ends, docs = rest[2 * hops :]
    i = pl.program_id(0)
    tb = normed_ref.shape[0]
    per = tb // SPAN
    nc = rb_ref.shape[0]
    width = gate_ref.shape[1]
    piece = i * tb // own ^ at_ref[1]

    def norm(x):
        xf = x.astype(F32)
        s = lax.rsqrt(jnp.mean(xf * xf, axis=1, keepdims=True) + EPSILON)
        return (xf * s * gain_ref[0:1, :]).astype(BF16)

    @pl.when(i == 0)
    def _():
        edge = norm(halo_ref[...])
        normh_ref[...] = edge
        before = mm(edge, wsv_ref[...])
        ubuf[0:8, :] = before
        uvh_ref[...] = before
        state[...] = jnp.zeros_like(state)
        place = at_ref[2] - 8 + iota((8, 1), 0)
        here = documents(off_ref, place)
        lane8 = iota((8, LANES), 1)
        halo = jnp.zeros((8, LANES), F32)
        for k in (1, 2, 3):
            same = jnp.where(documents(off_ref, place + k) == here, 1.0, 0.0)
            halo = jnp.where(lane8 == k - 1, same, halo)
        halocols_ref[...] = halo

    @pl.when(i > 0)
    def _():
        ubuf[0:8, :] = ubuf[tb : tb + 8, :]

    for at in range(0, tb, 64):
        x = x_refs[0][at : at + 64, :]
        for k in range(1, len(x_refs)):
            x = jnp.where(piece == k, x_refs[k][at : at + 64, :], x)
        normed_ref[at : at + 64, :] = norm(x)
    nb = normed_ref[...]
    for tile in wide_tiles(width):
        gate_ref[:, tile] = mm(nb, wg_ref[:, tile]).astype(BF16)
    for tile in wide_tiles(LANES + width):
        uv = mm(nb, wsv_ref[:, tile])
        ubuf[8 : 8 + tb, tile] = uv
        uv_ref[:, tile] = uv.astype(BF16)
    zr_all = mm_nt(wstr_ref[...], nb)
    lane = iota((SPAN, LANES), 1)
    forward = lane < nh
    forward_row = iota((16, SPAN), 0) < nh
    gate_lane = iota((8, LANES), 1) < nh
    for j in range(per):
        rows = slice(j * SPAN, (j + 1) * SPAN)
        base = at_ref[2] + (i * per + j) * SPAN
        around = documents(off_ref, base - 8 + iota((SPAN + 16, 1), 0))
        docs[...] = jnp.broadcast_to(around, docs.shape)
        seg = docs[8 : 8 + SPAN, :]
        prev_last, first = docs[7:8, :], docs[8:9, :]
        last, next_first = docs[7 + SPAN : 8 + SPAN, :], docs[8 + SPAN : 9 + SPAN, :]
        live = jnp.transpose(jnp.broadcast_to(live_ref[0:1, rows], (SPAN, SPAN)).astype(F32))
        mark = jnp.where(lane == 35, live, jnp.where(lane == 36, seg, 0.0))
        for k in (1, 2, 3):
            same = jnp.where(docs[8 - k : 8 - k + SPAN, :] == seg, 1.0, 0.0)
            mark = jnp.where(lane == 31 + k, same, mark)
            same = jnp.where(docs[8 + k : 8 + k + SPAN, :] == seg, 1.0, 0.0)
            mark = jnp.where(lane == 40 + k, same, mark)
        for k, bound in enumerate((prev_last, last, next_first, first)):
            mark = jnp.where(lane == 37 + k, jnp.where(seg == bound, 1.0, 0.0), mark)
        marks[rows, :] = mark
        opened = jnp.where(gate_lane, last - prev_last, next_first - first)
        ends[j * 8 : j * 8 + 8, :] = jnp.where(opened == 0.0, 1.0, 0.0)
        segrow_ref[:, rows] = jnp.transpose(seg)[:8]
    for at in range(0, LANES + width, LANES):
        tile = slice(at, at + LANES)
        for j in range(per):
            rows = slice(j * SPAN, (j + 1) * SPAN)
            keep = marks[rows, :]
            conv = taps_ref[0:1, tile] * ubuf[8 + j * SPAN : 8 + (j + 1) * SPAN, tile]
            for k in (1, 2, 3):
                moved = ubuf[8 - k + j * SPAN : 8 - k + (j + 1) * SPAN, tile]
                conv = conv + taps_ref[k : k + 1, tile] * moved * keep[:, 31 + k : 32 + k]
            sig = sigmoid(conv)
            live = keep[:, 35:36]
            act_ref[rows, tile] = (conv * sig * live).astype(BF16)
            slope_ref[rows, tile] = (live * sig * (1.0 + conv * (1.0 - sig))).astype(BF16)
    z_all = mm(nb, wst_ref[...])
    for j in range(per):
        rows = slice(j * SPAN, (j + 1) * SPAN)
        z = z_all[rows] + pcol_ref[0:1, :]
        dt = softplus(z)
        a = -dt * pcol_ref[1:2, :]
        total = mm(tril_ref[...], jnp.concatenate(pieces(a), axis=0))
        tot = total[SPAN - 1 : SPAN, :]
        cc = jnp.where(forward, total, total - a)
        pack = jnp.where(lane < 16, cc, jnp.where(lane < 32, z, marks[rows, :]))
        pack_ref[rows, :] = pack
        tot8 = jnp.broadcast_to(tot, (8, LANES))
        tot_ref[j * 8 : j * 8 + 8, :] = tot8
        dtr = softplus(zr_all[:, rows] + prow_ref[:, :SPAN])
        ar = -dtr * prow_ref[:, SPAN:]
        run = mm(jnp.concatenate(pieces(ar), axis=1), triu_ref[...])
        rowa = jnp.where(forward_row, run, run - ar)
        ldt = jnp.log(jnp.maximum(dtr, TINY))
        rowa_ref[:, rows] = rowa
        rowp_ref[:, rows] = jnp.where(forward_row, rowa - ldt, rowa + ldt)
        gates = split(jnp.exp(tot8) * ends[j * 8 : j * 8 + 8, :], 1)
        w = split(source_weights(pack, tot, dt, lane, nh), 1)
        bt = jnp.transpose(act_ref[rows, :LANES].astype(F32))[:HDIM].astype(BF16)
        c = i * per + j
        for n, at, _ in groups(width):
            tile = slice(at, at + LANES)
            both = slice(2 * at, 2 * at + 2 * LANES)
            x = act_ref[rows, LANES + at : 2 * LANES + at].astype(F32)
            wide = mm(w, ex_ref[:, both])
            fed = jnp.concatenate(
                [(x * wide[:, :LANES]).astype(BF16), (x * wide[:, LANES:]).astype(BF16)], axis=1
            )
            inc = mm(bt, fed)
            gate = mm(gates, ex_ref[:, both])
            gates_ref[c, :, both] = gate
            sf_ref[j, :, tile] = state[:, tile]
            state[:, tile] = state[:, tile] * gate[0:1, :LANES] + inc[:, :LANES]
            incb[c, :, tile] = inc[:, LANES:]

    @pl.when(i == pl.num_programs(0) - 1)
    def _():
        last_state = state[...]
        one = jnp.ones(gates_ref.shape[1:], F32)

        def up(c, p):
            gpre_ref[c] = p
            return p * gates_ref[c]

        p = lax.fori_loop(0, nc, up, one)
        tot_f, tot_b = sides(p, width)
        gtot_ref[:, :width] = tot_f
        gtot_ref[:, width:] = tot_b
        state[...] = jnp.zeros_like(state)

        def down(k, p):
            c = nc - 1 - k
            gsuf_ref[c] = p
            rb_ref[c] = state[...]
            gate = gates_ref[c]
            for n, at, _ in groups(width):
                tile = slice(at, at + LANES)
                second = slice(2 * at + LANES, 2 * at + 2 * LANES)
                state[:, tile] = state[:, tile] * gate[0:1, second] + incb[c, :, tile]
            return p * gate

        lax.fori_loop(0, nc, down, one)
        send_sides(
            at_ref,
            hops,
            jnp.concatenate([last_state, tot_f], axis=0),
            jnp.concatenate([state[...], tot_b], axis=0),
            messages,
        )


def inner_kernel(
    nh,
    act_ref,
    pack_ref,
    segrow_ref,
    rowp_ref,
    skip_ref,
    cot_ref,
    wo_ref,
    y_ref,
    dout_ref,
):
    tb, width = y_ref.shape
    for tile in wide_tiles(width):
        dout_ref[:, tile] = mm_nt(cot_ref[...], wo_ref[tile, :]).astype(BF16)
    t_at = iota((SPAN, SPAN), 0)
    s_at = iota((SPAN, SPAN), 1)
    lower = t_at > s_at
    for j in range(tb // SPAN):
        rows = slice(j * SPAN, (j + 1) * SPAN)
        bc = act_ref[rows, :LANES].astype(F32)
        b = bc[:, :HDIM].astype(BF16)
        c = pltpu.roll(bc, HDIM, 1)[:, :HDIM].astype(BF16)
        pack = pack_ref[rows, :]
        within = (pack[:, 36:37] == segrow_ref[0:1, rows]) & (t_at != s_at)
        score = jnp.where(within, mm_nt(c, b), 0.0)
        for n, at, heads in groups(width):
            tile = slice(at, at + LANES)
            mats = []
            for h in heads:
                gap = jnp.where(
                    lower,
                    pack[:, h : h + 1] - rowp_ref[h : h + 1, rows],
                    rowp_ref[nh + h : nh + h + 1, rows] - pack[:, nh + h : nh + h + 1],
                )
                mats.append((score * jnp.exp(gap)).astype(BF16))
            xp = act_ref[rows, LANES + at : 2 * LANES + at]
            y = mm(jnp.concatenate(mats, axis=1), stacked(xp))
            y_ref[rows, tile] = y + skip_ref[0:1, tile] * xp.astype(F32)


def merge_kernel(
    nh,
    hops,
    at_ref,
    bc_ref,
    pack_ref,
    tot_ref,
    sf_ref,
    rb_ref,
    gpre_ref,
    gsuf_ref,
    yin_ref,
    gate_ref,
    dout_ref,
    mg_ref,
    ex_ref,
    *rest,
):
    arrived = rest[: 2 * hops]
    y_ref, stat_ref, full_ref, sent_ref, rent_ref = rest[2 * hops :]
    tb, width = y_ref.shape

    @pl.when(pl.program_id(0) == 0)
    def _():
        land_sides(at_ref, hops, arrived, sent_ref, rent_ref)

    lane = iota((SPAN, LANES), 1)
    row8 = iota((8, SPAN), 0)
    for j in range(tb // SPAN):
        rows = slice(j * SPAN, (j + 1) * SPAN)
        pack = pack_ref[rows, :]
        bc = bc_ref[rows, :].astype(F32)
        c = pltpu.roll(bc, HDIM, 1)[:, :HDIM].astype(BF16)
        w = split(target_weights(pack, tot_ref[j * 8 : j * 8 + 1, :], lane, nh), 1)
        energy = jnp.zeros((SPAN, LANES), F32)
        cross = jnp.zeros((SPAN, LANES), F32)
        for n, at, _ in groups(width):
            tile = slice(at, at + LANES)
            both = slice(2 * at, 2 * at + 2 * LANES)
            second = slice(2 * at + LANES, 2 * at + 2 * LANES)
            first = slice(2 * at, 2 * at + LANES)
            sfull = sf_ref[j, :, tile] + gpre_ref[j, 0:1, first] * sent_ref[:, tile]
            rfull = rb_ref[j, :, tile] + gsuf_ref[j, 0:1, second] * rent_ref[:, tile]
            held = jnp.concatenate([sfull.astype(BF16), rfull.astype(BF16)], axis=1)
            full_ref[j, :, both] = held
            seen = mm(c, held) * mm(w, ex_ref[:, both])
            y = (yin_ref[rows, tile] + seen[:, :LANES] + seen[:, LANES:]).astype(BF16)
            y_ref[rows, tile] = y
            gate = gate_ref[rows, tile].astype(F32)
            g = y.astype(F32) * gate * sigmoid(gate)
            energy = energy + g * g
            cross = cross + dout_ref[rows, tile].astype(F32) * mg_ref[0:1, tile] * g
        energy = jnp.sum(jnp.transpose(energy), axis=0, keepdims=True)
        cross = jnp.sum(jnp.transpose(cross), axis=0, keepdims=True)
        stat_ref[:, rows] = jnp.where(row8 == 0, energy, jnp.where(row8 == 1, cross, 0.0))


def turn_kernel(
    inner,
    shares,
    y_ref,
    gate_ref,
    dout_ref,
    mg_ref,
    act_ref,
    eye_ref,
    normed_ref,
    cot_ref,
    wo_ref,
    *rest,
):
    stats_in = rest[:shares]
    (
        aside_ref,
        outin_ref,
        dy_ref,
        dgate_ref,
        gmix_ref,
        gskip_ref,
        gout_ref,
        ggate_ref,
        gout,
        ggate,
    ) = rest[shares:]
    i = pl.program_id(0)
    tb, width = y_ref.shape
    model = normed_ref.shape[1]

    @pl.when(i == 0)
    def _():
        gmix_ref[...] = jnp.zeros_like(gmix_ref)
        gskip_ref[...] = jnp.zeros_like(gskip_ref)
        gout[...] = jnp.zeros_like(gout)
        ggate[...] = jnp.zeros_like(ggate)

    for j in range(tb // SPAN):
        rows = slice(j * SPAN, (j + 1) * SPAN)
        stat = stats_in[0][:, rows]
        for more in stats_in[1:]:
            stat = stat + more[:, rows]
        stat = exact_tn(stat, eye_ref[0:8, :])
        q = lax.rsqrt(stat[:, 0:1] * (1.0 / inner) + EPSILON)
        k3 = q * q * q * stat[:, 1:2] * (1.0 / inner)
        for n, at, _ in groups(width):
            tile = slice(at, at + LANES)
            y = y_ref[rows, tile].astype(F32)
            gate = gate_ref[rows, tile].astype(F32)
            sig = sigmoid(gate)
            sg = gate * sig
            g = y * sg
            gq = g * q
            dout = dout_ref[rows, tile].astype(F32)
            mg = mg_ref[0:1, tile]
            outin_ref[rows, tile] = (gq * mg).astype(BF16)
            gmix_ref[0:1, tile] += jnp.sum(dout * gq, axis=0, keepdims=True)
            dg = dout * mg * q - g * k3
            dyb = (dg * sg).astype(BF16)
            dy_ref[rows, tile] = dyb
            dgate_ref[rows, tile] = (dg * y * (sig + sg * (1.0 - sig))).astype(BF16)
            x = act_ref[rows, LANES + at : 2 * LANES + at].astype(F32)
            gskip_ref[0:1, tile] += jnp.sum(dyb.astype(F32) * x, axis=0, keepdims=True)

    for tile in wide_tiles(model):
        aside_ref[:, tile] = mm(outin_ref[:ASIDE, :], wo_ref[:, tile]).astype(BF16)
    for at in range(0, width, LANES):
        tile = slice(at, at + LANES)
        gout[tile, :] += mm_tn(outin_ref[:, tile], cot_ref[...])
    for at in range(0, model, LANES):
        tile = slice(at, at + LANES)
        ggate[tile, :] += mm_tn(normed_ref[:, tile], dgate_ref[...])

    @pl.when(i == pl.num_programs(0) - 1)
    def _():
        gout_ref[...] = gout[...].astype(BF16)
        ggate_ref[...] = ggate[...].astype(BF16)


def adjoint_kernel(
    nh,
    shares,
    hops,
    own,
    at_ref,
    act_ref,
    pack_ref,
    tot_ref,
    gates_ref,
    gtot_ref,
    ex_ref,
    dy_ref,
    outin_ref,
    wo_ref,
    *rest,
):
    pieces_out = rest[:shares]
    dso_ref, dro_ref, *messages, state, incf = rest[shares:]
    i = pl.program_id(0)
    tb, width = dy_ref.shape
    model = wo_ref.shape[1]
    per = tb // SPAN
    nc = dso_ref.shape[0]
    lane = iota((SPAN, LANES), 1)

    @pl.when(i == 0)
    def _():
        state[...] = jnp.zeros_like(state)

    for j in range(per):
        rows = slice(j * SPAN, (j + 1) * SPAN)
        pack = pack_ref[rows, :]
        w = split(target_weights(pack, tot_ref[j * 8 : j * 8 + 1, :], lane, nh), 1)
        ct = jnp.transpose(act_ref[rows, :].astype(F32))[HDIM:].astype(BF16)
        c = i * per + j
        for n, at, _ in groups(width):
            tile = slice(at, at + LANES)
            both = slice(2 * at, 2 * at + 2 * LANES)
            second = slice(2 * at + LANES, 2 * at + 2 * LANES)
            dy = dy_ref[rows, tile].astype(F32)
            wide = mm(w, ex_ref[:, both])
            fed = jnp.concatenate(
                [(dy * wide[:, :LANES]).astype(BF16), (dy * wide[:, LANES:]).astype(BF16)], axis=1
            )
            inc = mm(ct, fed)
            incf[c, :, tile] = inc[:, :LANES]
            dro_ref[j, :, tile] = state[:, tile]
            state[:, tile] = state[:, tile] * gates_ref[c, 0:1, second] + inc[:, LANES:]

    for k in range(shares):

        @pl.when((i * tb // own ^ at_ref[1]) == k)
        def _():
            for tile in wide_tiles(model):
                pieces_out[k][:, tile] = mm(outin_ref[ASIDE:, :], wo_ref[:, tile]).astype(BF16)

    @pl.when(i == pl.num_programs(0) - 1)
    def _():
        last_state = state[...]
        state[...] = jnp.zeros_like(state)

        def down(k, _):
            c = nc - 1 - k
            dso_ref[c] = state[...]
            for n, at, _ in groups(width):
                tile = slice(at, at + LANES)
                first = slice(2 * at, 2 * at + LANES)
                state[:, tile] = state[:, tile] * gates_ref[c, 0:1, first] + incf[c, :, tile]
            return 0

        lax.fori_loop(0, nc, down, 0)
        send_sides(
            at_ref,
            hops,
            jnp.concatenate([last_state, gtot_ref[:, width:]], axis=0),
            jnp.concatenate([state[...], gtot_ref[:, :width]], axis=0),
            messages,
        )


def mid_kernel(
    nh,
    act_ref,
    pack_ref,
    segrow_ref,
    rowa_ref,
    dy_ref,
    eye_ref,
    dx_ref,
    dbc_ref,
    pulls_ref,
):
    tb, width = dx_ref.shape
    s_at = iota((SPAN, SPAN), 0)
    t_at = iota((SPAN, SPAN), 1)
    lower = t_at > s_at
    lane = iota((SPAN, LANES), 1)
    row16 = iota((16, SPAN), 0)
    front_half = lane < HDIM
    for j in range(tb // SPAN):
        rows = slice(j * SPAN, (j + 1) * SPAN)
        pack = pack_ref[rows, :]
        bc = act_ref[rows, :LANES].astype(F32)
        cb = pltpu.roll(bc, HDIM, 1)
        within = (pack[:, 36:37] == segrow_ref[0:1, rows]) & (t_at != s_at)
        score = mm_nt(bc[:, :HDIM].astype(BF16), cb[:, :HDIM].astype(BF16))
        score = jnp.where(within, score, 0.0)
        ldt = jnp.log(jnp.maximum(softplus(pltpu.roll(pack, LANES - 16, 1)), TINY))
        pc = jnp.where(lane < nh, pack - ldt, pack + ldt)
        dscore = jnp.zeros((SPAN, SPAN), F32)
        kc = jnp.zeros((SPAN, LANES), F32)
        qr = jnp.zeros((16, SPAN), F32)
        for n, at, heads in groups(width):
            tile = slice(at, at + LANES)
            dyp = dy_ref[rows, tile]
            dmats = mm_nt(stacked(act_ref[rows, LANES + at : 2 * LANES + at]), dyp)
            mats = []
            for m, h in enumerate(heads):
                decay = jnp.exp(
                    jnp.where(
                        lower,
                        rowa_ref[h : h + 1, rows] - pc[:, h : h + 1],
                        pc[:, nh + h : nh + h + 1] - rowa_ref[nh + h : nh + h + 1, rows],
                    )
                )
                spot = dmats[m * SPAN : (m + 1) * SPAN, :] * decay
                dscore = dscore + spot
                mats.append((score * decay).astype(BF16))
                pull = spot * score
                pull_low = jnp.where(lower, pull, 0.0)
                pull_up = pull - pull_low
                qr = jnp.where(row16 == h, jnp.sum(pull_low, axis=0, keepdims=True), qr)
                qr = jnp.where(row16 == nh + h, jnp.sum(pull_up, axis=0, keepdims=True), qr)
                kc = jnp.where(lane == h, jnp.sum(pull_low, axis=1, keepdims=True), kc)
                kc = jnp.where(lane == nh + h, jnp.sum(pull_up, axis=1, keepdims=True), kc)
            dx_ref[rows, tile] = mm(jnp.concatenate(mats, axis=1), stacked(dyp)).astype(BF16)
        dscore = jnp.where(within, dscore, 0.0).astype(BF16)
        cpad = jnp.where(front_half, cb, 0.0).astype(BF16)
        bpad = jnp.where(front_half, 0.0, cb).astype(BF16)
        dbc_ref[rows, :] = mm(dscore, cpad) + mm_tn(dscore, bpad)
        pulls_ref[rows, :] = kc + exact_tn(qr, eye_ref[...])


def back_kernel(
    nh,
    peers,
    hops,
    own,
    at_ref,
    act_ref,
    slope_ref,
    pack_ref,
    tot_ref,
    dy_ref,
    full_ref,
    dso_ref,
    dro_ref,
    gsuf_ref,
    gpre_ref,
    gates_ref,
    dxin_ref,
    dbc_ref,
    pulls_ref,
    uv_ref,
    uvh_ref,
    halocols_ref,
    taps_ref,
    skip_ref,
    pcol_ref,
    ex_ref,
    ext_ref,
    tril_ref,
    triu_ref,
    normed_ref,
    normh_ref,
    dgate_ref,
    wg_ref,
    wcat_ref,
    gmix_ref,
    gskip_ref,
    *rest,
):
    arrived = rest[: 2 * hops]
    mine_ref, theirs_ref, *chunks = rest[2 * hops : 2 * hops + 2 + peers]
    dbuf, hbuf, dcat, acc, lines, dsent_ref, drent_ref, parts = rest[2 * hops + 2 + peers :]
    i = pl.program_id(0)
    last = pl.num_programs(0) - 1
    tb = act_ref.shape[0]
    width = act_ref.shape[1] - LANES
    model = normed_ref.shape[1]

    @pl.when(i == 0)
    def _():
        dbuf[tb : tb + 8, :] = jnp.zeros((8, LANES + width), F32)
        acc[...] = jnp.zeros_like(acc)
        lines[...] = jnp.zeros_like(lines)
        land_sides(at_ref, hops, arrived, drent_ref, dsent_ref)

    lane = iota((SPAN, LANES), 1)
    forward = lane < nh
    head_lane = lane < 16
    none = jnp.zeros((HDIM, 2 * LANES), BF16)
    for j in reversed(range(tb // SPAN)):
        rows = slice(j * SPAN, (j + 1) * SPAN)
        pack = pack_ref[rows, :]
        tot = tot_ref[j * 8 : j * 8 + 1, :]
        z = pltpu.roll(pack, LANES - 16, 1)
        dt = softplus(z)
        w = jnp.concatenate(
            [
                split(source_weights(pack, tot, dt, lane, nh), 1),
                split(target_weights(pack, tot, lane, nh), 1),
            ],
            axis=0,
        )
        bc = act_ref[rows, :LANES].astype(F32)
        b = bc[:, :HDIM].astype(BF16)
        c = pltpu.roll(bc, HDIM, 1)[:, :HDIM].astype(BF16)
        dbc = dbc_ref[rows, :]
        carried = jnp.zeros((SPAN, LANES), F32)
        leaving = jnp.zeros((SPAN, LANES), F32)
        through = jnp.zeros((8, LANES), F32)
        for n, at, _ in groups(width):
            tile = slice(at, at + LANES)
            wtile = slice(LANES + at, 2 * LANES + at)
            both = slice(2 * at, 2 * at + 2 * LANES)
            first = slice(2 * at, 2 * at + LANES)
            second = slice(2 * at + LANES, 2 * at + 2 * LANES)
            wide = mm(w, ex_ref[:, both])
            x = act_ref[rows, wtile].astype(F32)
            dy = dy_ref[rows, tile].astype(F32)
            x2 = jnp.concatenate([x, x], axis=1)
            dy2 = jnp.concatenate([dy, dy], axis=1)
            held = full_ref[j, :, both]
            dheld = jnp.concatenate(
                [
                    dso_ref[j, :, tile] + gsuf_ref[j, 0:1, first] * dsent_ref[:, tile],
                    dro_ref[j, :, tile] + gpre_ref[j, 0:1, second] * drent_ref[:, tile],
                ],
                axis=1,
            )
            dheld_low = dheld.astype(BF16)
            to_wide = wide[:SPAN]
            fro_wide = wide[SPAN:]
            flow = mm(b, dheld_low) * to_wide
            seen = mm(c, held) * fro_wide
            dbc = dbc + mm_nt((x2 * to_wide).astype(BF16), jnp.concatenate([dheld_low, none], axis=0))
            dbc = dbc + mm_nt((dy2 * fro_wide).astype(BF16), jnp.concatenate([none, held], axis=0))
            ext = ext_ref[both, :]
            carried = carried + two_part(dy2 * seen, ext)
            leaving = leaving + two_part(x2 * flow, ext)
            product = jnp.sum(dheld * held.astype(F32), axis=0, keepdims=True) * gates_ref[j, :, both]
            through = through + mm(product.astype(BF16), ext)
            dx = dxin_ref[rows, tile].astype(F32) + flow[:, :LANES] + flow[:, LANES:]
            dx = dx + skip_ref[0:1, tile] * dy
            dbuf[rows, wtile] = dx * slope_ref[rows, wtile].astype(F32)
        dbuf[rows, :LANES] = dbc * slope_ref[rows, :LANES].astype(F32)
        pulls = pulls_ref[rows, :]
        kc = jnp.where(head_lane, pulls, 0.0)
        moved = jnp.where(head_lane, pltpu.roll(pulls, LANES - 16, 1), 0.0) + carried - kc
        before = mm(tril_ref[:, : 2 * SPAN], split(jnp.where(forward, leaving, moved), 0))
        after = mm(triu_ref[:, : 2 * SPAN], split(jnp.where(forward, moved, leaving), 0))
        dlog = before + after - leaving + through[0:1, :]
        sigz = sigmoid(z)
        rate = pcol_ref[1:2, :]
        dstep = (kc + leaving) * (sigz / jnp.maximum(dt, TINY)) - dlog * rate * sigz
        dstep = jnp.where(head_lane, dstep, 0.0)
        dcat[rows, :LANES] = dstep.astype(BF16)
        lines[7:8, :LANES] += jnp.sum(dstep, axis=0, keepdims=True)
        ends = jnp.where(head_lane, -dlog * dt * rate, 0.0)
        lines[8:9, :LANES] += jnp.sum(ends, axis=0, keepdims=True)
        for at in range(0, LANES + width, LANES):
            tile = slice(at, at + LANES)
            dconv = dbuf[rows, tile]
            uv = uv_ref[rows, tile].astype(F32)
            du = taps_ref[0:1, tile] * dconv
            lines[1:2, tile] += jnp.sum(uv * dconv, axis=0, keepdims=True)
            for k in (1, 2, 3):
                shifted = dbuf[j * SPAN + k : (j + 1) * SPAN + k, tile] * pack[:, 40 + k : 41 + k]
                du = du + taps_ref[k : k + 1, tile] * shifted
                lines[1 + k : 2 + k, tile] += jnp.sum(uv * shifted, axis=0, keepdims=True)
            dcat[rows, LANES + at : 2 * LANES + at] = du.astype(BF16)

    edge = dbuf[0:8, :]
    dbuf[tb : tb + 8, :] = edge
    for tile in wide_tiles(model):
        part = mm_nt(dgate_ref[...], wg_ref[tile, :]) + mm_nt(dcat[...], wcat_ref[tile, :])
        parts[:, tile] = part.astype(BF16)
        normed = normed_ref[:, tile]
        lines[0:1, tile] += jnp.sum(part * normed.astype(F32), axis=0, keepdims=True)
        acc[tile, :] += mm_tn(normed, dcat[...])
    side = ((last - i) * tb // own ^ at_ref[1]) % 2

    @pl.when(side == 0)
    def _():
        mine_ref[0] = parts[...]

    @pl.when(side == 1)
    def _():
        theirs_ref[0] = parts[...]

    @pl.when(i == last)
    def _():
        taps_at = slice(0, LANES + width)
        hbuf[0:8, :] = jnp.zeros_like(edge)
        hbuf[8:16, :] = edge
        duh = jnp.zeros_like(edge)
        for k in (1, 2, 3):
            shifted = hbuf[k : k + 8, :] * halocols_ref[:, k - 1 : k]
            duh = duh + taps_ref[k : k + 1, :] * shifted
            lines[1 + k : 2 + k, taps_at] += jnp.sum(uvh_ref[...] * shifted, axis=0, keepdims=True)
        duh = duh.astype(BF16)
        normh = normh_ref[...]
        parth = mm_nt(duh, wcat_ref[:, LANES:])
        lines[0:1, :] += jnp.sum(parth * normh.astype(F32), axis=0, keepdims=True)
        skips = jnp.zeros((8, LANES), F32)
        for n, at, _ in groups(width):
            ext = ext_ref[2 * at : 2 * at + LANES, :]
            high = gskip_ref[:, at : at + LANES].astype(BF16)
            low = (gskip_ref[:, at : at + LANES] - high.astype(F32)).astype(BF16)
            skips = skips + mm(high, ext) + mm(low, ext)
        lines[5:6, :LANES] = skips[0:1, :]
        lines[6:7, :width] = gmix_ref[0:1, :]
        acc[:, LANES:] += mm_tn(normh, duh)
        placed = jnp.where(iota((16, LANES), 1) == iota((16, LANES), 0) + 16, 1.0, 0.0)
        acc[:, :LANES] += exact_tn(lines[...], placed)
        row8 = iota((8, LANES), 0)
        taken = iota((8, LANES), 1) == 19 + 3 * at_ref[0] + row8
        taken = taken & (row8 > 4) & (at_ref[0] > 0)
        acc[:, :LANES] += exact_tn(parth, jnp.where(taken, 1.0, 0.0))
        size = model // peers
        for k in range(peers):
            start = pl.multiple_of((at_ref[0] ^ k) * size, 8)
            chunks[k][...] = acc[pl.ds(start, size), :].astype(BF16)


def finish_kernel(nh, peers, shares, at_ref, *refs):
    chunks = refs[:peers]
    eye_ref, ingain_ref, x_ref, cot_ref, kept_ref, got_ref = refs[peers : peers + 6]
    gain_ref, value_ref, state_ref, step_ref, bias_ref, decay_ref = refs[peers + 6 : peers + 12]
    convv_ref, convs_ref, skip_ref, mixer_ref, tokens_ref, extra = refs[peers + 12 :]
    size = chunks[0].shape[0]
    real_width = value_ref.shape[1]
    heads = step_ref.shape[0]
    for k in range(peers):
        rows = pl.ds(pl.multiple_of((at_ref[0] ^ k) * size, 8), size)
        extra[rows, :] = chunks[k][:, :LANES].astype(F32)
        state_ref[rows, :] = chunks[k][:, LANES : 2 * LANES].astype(F32)
        value_ref[rows, :] = chunks[k][:, 2 * LANES : 2 * LANES + real_width].astype(F32)
    found = extra[...].astype(BF16)
    lines = mm_nt(eye_ref[...], found)
    row16 = iota((16, LANES), 0)
    taken = iota((16, LANES), 1) == 27 + 3 * at_ref[0] + row16 - 13
    taken = taken & (row16 > 12) & (at_ref[1] == shares - 1)
    late = mm_nt(jnp.where(taken, 1.0, 0.0).astype(BF16), found)

    def token_rows(rows, more):
        x = x_ref[rows, :].astype(F32)
        s = lax.rsqrt(jnp.mean(x * x, axis=1, keepdims=True) + EPSILON)
        dn = kept_ref[0, rows, :] + got_ref[0, rows, :].astype(F32) + more
        scaled = dn * ingain_ref[...]
        inside = jnp.mean(scaled * x, axis=1, keepdims=True)
        cot = cot_ref[rows, :].astype(F32)
        tokens_ref[rows, :] = (cot + s * scaled - x * (s * s * s) * inside).astype(BF16)

    own = x_ref.shape[0]
    for at in range(0, own, 32):
        token_rows(slice(at, at + 32), 0.0)
    token_rows(slice(own - 16, own), late)
    for h in range(heads):
        step_ref[h, 0:1, :] = lines[h : h + 1, :]
        step_ref[h, 1:2, :] = lines[nh + h : nh + h + 1, :]
    gain_ref[...] = (lines[16:17, :] / ingain_ref[...])[0]
    convs_ref[...] = lines[17:21, :LANES]
    convv_ref[...] = lines[17:21, LANES : LANES + real_width]
    skip_ref[...] = lines[21:22, :heads]
    mixer_ref[...] = lines[22, :real_width]
    bias_ref[0:1, :] = lines[23:24, :heads]
    bias_ref[1:2, :] = lines[23:24, nh : nh + heads]
    decay_ref[...] = lines[24:25, :heads] + lines[24:25, nh : nh + heads]


def whole(shape):
    return pl.BlockSpec(shape, lambda i, *_: (0,) * len(shape))


def row_block(rows, width):
    return pl.BlockSpec((rows, width), lambda i, *_: (i, 0))


def lane_block(rows, width):
    return pl.BlockSpec((rows, width), lambda i, *_: (0, i))


def chunk_block(per, rows, width):
    return pl.BlockSpec((per, rows, width), lambda i, *_: (i, 0, 0))


def sds(shape, dtype):
    return jax.ShapeDtypeStruct(shape, dtype)


def call(kernel, name, grid, ins, outs, scratch, flops, operands, scalars=()):
    return pl.pallas_call(
        kernel,
        name=name,
        grid_spec=pltpu.PrefetchScalarGridSpec(
            num_scalar_prefetch=len(scalars),
            grid=(grid,),
            in_specs=ins,
            out_specs=[spec for spec, _ in outs],
            scratch_shapes=scratch,
        ),
        out_shape=[shape for _, shape in outs],
        compiler_params=pltpu.CompilerParams(
            dimension_semantics=("arbitrary",), vmem_limit_bytes=56 * 1024 * 1024
        ),
        cost_estimate=pl.CostEstimate(
            flops=int(flops), bytes_accessed=1, transcendentals=0
        ),
    )(*scalars, *operands)


def shifted_in(array, axis, by):
    length = lax.axis_size(axis)
    pairs = [(i, i + by) for i in range(length) if 0 <= i + by < length]
    return lax.ppermute(array, axis, pairs)


def exchange_sides(messages, hops):
    size = lax.axis_size("seq")
    arrived = []
    for d in range(1, hops + 1):
        for side in (0, 1):
            pairs = [(i, i + d) for i in range(size - d) if (i // d) % 2 == side]
            both = pairs + [(b, a) for a, b in pairs]
            arrived.append(lax.ppermute(messages[len(arrived)], "seq", both))
    return arrived


def swap(array, axis, k):
    n = lax.axis_size(axis)
    return lax.ppermute(array, axis, [(i, i ^ k) for i in range(n)])


def sum_over(array, axis):
    size = lax.axis_size(axis)
    result = array
    for k in range(1, size):
        result = result + lax.ppermute(array, axis, [(i, i ^ k) for i in range(size)])
    return result


def per_device(
    tokens,
    input_gain,
    proj_gate,
    proj_value,
    proj_state,
    proj_step,
    step_bias,
    decay_log,
    conv_value,
    conv_state,
    skip_gain,
    mixer_gain,
    proj_out,
    doc_lengths,
    pad_mask,
    cotangent,
):
    head_devices = lax.axis_size("head")
    length = pad_mask.shape[0]
    model = tokens.shape[1]
    real_width = proj_gate.shape[1]
    real_heads = proj_step.shape[2]
    inner = real_width * head_devices
    width = -(-real_width // LANES) * LANES
    nh = width // HDIM

    def padded(array, axis, size):
        if array.shape[axis] == size:
            return array
        widths = [(0, 0)] * array.ndim
        widths[axis] = (0, size - array.shape[axis])
        return jnp.pad(array, widths)

    proj_gate = padded(proj_gate, 1, width)
    proj_value = padded(proj_value, 1, width)
    proj_step = padded(proj_step, 2, nh)
    step_bias = padded(step_bias, 1, nh)
    conv_value = padded(conv_value, 1, width)
    skip_gain = padded(skip_gain, 0, nh)
    mixer_gain = padded(mixer_gain, 0, width)
    proj_out = padded(proj_out, 0, width)
    nc = length // SPAN
    tb = BLOCK
    per = tb // SPAN
    grid = length // tb
    wide = LANES + width
    hops = -(-(LONGEST - 1) // length)
    seq_index = lax.axis_index("seq")
    first_place = seq_index * length
    all_tokens = length * lax.axis_size("seq")

    edge_rows = shifted_in(tokens[tokens.shape[0] - 8 :], "seq", 1)
    here = lax.axis_index("head")
    halo = jnp.where(here == head_devices - 1, edge_rows, 0)
    for k in range(1, head_devices):
        halo = halo + jnp.where(here ^ k == head_devices - 1, swap(edge_rows, "head", k), 0)

    offsets = jnp.cumsum(doc_lengths) - doc_lengths
    room = -(-(offsets.shape[0] + 1) // LANES) * LANES - offsets.shape[0]
    fill = jnp.where(jnp.arange(room) == 0, all_tokens, 2 * all_tokens).astype(offsets.dtype)
    offsets = jnp.concatenate([offsets, fill])[None, :]
    live_row = pad_mask[None, :]
    lanes = np.arange(LANES)
    column = np.arange(2 * width)
    head_of = column // (2 * LANES) * 2 + column % LANES // HDIM
    head_of = head_of + np.where(column % (2 * LANES) >= LANES, nh, 0)
    ext = jnp.asarray(head_of[:, None] == lanes[None, :], BF16)
    ex = jnp.asarray(np.tile(head_of[None, :] == lanes[:, None], (2, 1)), BF16)
    at = np.arange(SPAN)
    tril = jnp.asarray(np.tile(at[:, None] >= at[None, :], (1, 3)), BF16)
    triu = at[:, None] <= at[None, :]
    triu_wide = jnp.asarray(np.tile(triu, (1, 2)), BF16)
    triu_tall = jnp.asarray(np.tile(triu, (3, 1)), BF16)
    eye = jnp.asarray(np.arange(16)[:, None] == lanes[None, :], F32)
    eye16 = jnp.asarray(np.arange(16)[:, None] + 16 == lanes[None, :], F32)
    picked = jnp.asarray(np.arange(32)[:, None] == lanes[None, :], BF16)
    peers = lax.axis_size("seq")
    own = length // head_devices
    bits = head_devices.bit_length() - 1
    scalars = [jnp.stack([seq_index, here, first_place]).astype(jnp.int32)]
    size = model // peers

    rate = padded(jnp.exp(decay_log), 0, nh)
    bias_line = jnp.concatenate([step_bias[0], step_bias[1]])
    rate_line = jnp.concatenate([rate, rate])
    pcol = jnp.zeros((8, LANES), F32)
    pcol = pcol.at[0, : 2 * nh].set(bias_line).at[1, : 2 * nh].set(rate_line)
    pcol = pcol.at[0, 16 : 16 + 2 * nh].set(bias_line)
    pad16 = jnp.zeros((16 - 2 * nh,), F32)
    prow = jnp.concatenate(
        [
            jnp.broadcast_to(jnp.concatenate([bias_line, pad16])[:, None], (16, SPAN)),
            jnp.broadcast_to(jnp.concatenate([rate_line, pad16])[:, None], (16, SPAN)),
        ],
        axis=1,
    )
    steps = jnp.concatenate([proj_step[0], proj_step[1]], axis=1)
    wst = jnp.pad(steps, ((0, 0), (0, 16 - 2 * nh)))
    wst = jnp.pad(jnp.tile(wst, (1, 2)), ((0, 0), (0, LANES - 32)))
    wback = jnp.pad(steps, ((0, 0), (0, LANES - 2 * nh)))
    wstr = jnp.pad(steps.T, ((0, 16 - 2 * nh), (0, 0)))
    wsv = jnp.concatenate([proj_state, proj_value], axis=1)
    taps = jnp.pad(jnp.concatenate([conv_state, conv_value], axis=1), ((0, 4), (0, 0)))
    gain = jnp.broadcast_to(input_gain[None, :], (8, model))
    mg = jnp.broadcast_to(mixer_gain[None, :], (8, width))
    skip = jnp.broadcast_to(jnp.repeat(skip_gain, HDIM)[None, :], (8, width))

    wcat = jnp.concatenate([wback, wsv], axis=1)
    pieces_of = {0: tokens}
    for bit in [1 << b for b in range(bits - 1, 0, -1)]:
        pieces_of.update({k | bit: swap(v, "head", bit) for k, v in pieces_of.items()})
    prelims = (halo, offsets, live_row, pcol, prow, wst, wstr, wsv, taps, gain, mg, skip, wcat)
    pieces_of, late, prelims, scalars = lax.optimization_barrier(
        (pieces_of, cotangent, prelims, scalars)
    )
    halo, offsets, live_row, pcol, prow, wst, wstr, wsv, taps, gain, mg, skip, wcat = prelims
    pieces_of.update({k | 1: swap(v, "head", 1) for k, v in pieces_of.items()})
    token_pieces = [pieces_of[k] for k in range(head_devices)]
    cot_all = lax.all_gather(late, "head", axis=0, tiled=True)

    rows = partial(row_block, tb)
    states = sds((nc, HDIM, width), F32)
    gates_of = sds((nc, 8, 2 * width), F32)
    message = sds((HDIM + 8, width), F32)
    state_block = chunk_block(per, HDIM, width)
    gate_block = chunk_block(per, 8, 2 * width)
    tot_block = row_block(per * 8, LANES)
    messages = [(whole(message.shape), message)] * (2 * hops)

    def sized(block):
        return (
            length // block,
            partial(row_block, block),
            partial(lane_block, width=block),
            partial(chunk_block, block // SPAN),
            row_block(block // SPAN * 8, LANES),
        )

    def slot_of(j, at):
        place = j ^ at[1]
        return sum(((place >> b) & 1) << (bits - 1 - b) for b in range(bits))

    each = own // tb

    def piece_block(k):
        def index(i, at):
            return jnp.clip(i - (at[1] ^ k) * each, 0, each - 1), 0

        return pl.BlockSpec((tb, model), index)

    def side_block(side):
        def index(i, at):
            row = grid - 1 - i
            j, sub = row // each, row % each
            ours = (j ^ at[1]) % 2 == side
            first = j == head_devices - 1
            j = jnp.where(ours, j, jnp.where(first, j - 1, j + 1))
            sub = jnp.where(ours, sub, jnp.where(first, each - 1, 0))
            return slot_of(j, at) % (head_devices // 2), sub, 0

        return pl.BlockSpec((1, tb, model), index)

    (
        normed,
        normh,
        gate_in,
        acted,
        slope,
        uv,
        uvh,
        pack,
        rowa,
        rowp,
        seg_row,
        halo_cols,
        tot,
        sf,
        rb,
        gates,
        gpre,
        gsuf,
        gtot,
        *ahead,
    ) = call(
        partial(front_kernel, nh, hops, head_devices, own),
        "front",
        grid,
        [piece_block(k) for k in range(head_devices)]
        + [
            whole((8, model)),
            whole((8, model)),
            whole((model, width)),
            whole((model, wide)),
            whole((model, LANES)),
            whole((16, model)),
            whole((8, LANES)),
            whole((16, 2 * SPAN)),
            whole((8, wide)),
            whole(offsets.shape),
            lane_block(1, tb),
            whole(ex.shape),
            whole(tril.shape),
            whole(triu_tall.shape),
        ],
        [
            (rows(model), sds((length, model), BF16)),
            (whole((8, model)), sds((8, model), BF16)),
            (rows(width), sds((length, width), BF16)),
            (rows(wide), sds((length, wide), BF16)),
            (rows(wide), sds((length, wide), BF16)),
            (rows(wide), sds((length, wide), BF16)),
            (whole((8, wide)), sds((8, wide), F32)),
            (rows(LANES), sds((length, LANES), F32)),
            (lane_block(16, tb), sds((16, length), F32)),
            (lane_block(16, tb), sds((16, length), F32)),
            (lane_block(8, tb), sds((8, length), F32)),
            (whole((8, LANES)), sds((8, LANES), F32)),
            (tot_block, sds((nc * 8, LANES), F32)),
            (state_block, states),
            (whole(states.shape), states),
            (whole(gates_of.shape), gates_of),
            (whole(gates_of.shape), gates_of),
            (whole(gates_of.shape), gates_of),
            (whole((8, 2 * width)), sds((8, 2 * width), F32)),
        ]
        + messages,
        [
            pltpu.VMEM((tb + 8, wide), F32),
            pltpu.VMEM((HDIM, width), F32),
            pltpu.VMEM((nc, HDIM, width), F32),
            pltpu.VMEM((tb, LANES), F32),
            pltpu.VMEM((per * 8, LANES), F32),
            pltpu.VMEM((SPAN + 16, LANES), F32),
        ],
        25e9,
        token_pieces
        + [
            halo,
            gain,
            proj_gate,
            wsv,
            wst,
            wstr,
            pcol,
            prow,
            taps,
            offsets,
            live_row,
            ex,
            tril,
            triu_tall,
        ],
        scalars,
    )

    ahead = exchange_sides(ahead, hops)

    big_grid, big_rows, big_lanes, big_chunks, big_tot = sized(512)
    yin, dout = call(
        partial(inner_kernel, nh),
        "inner",
        big_grid,
        [
            big_rows(wide),
            big_rows(LANES),
            big_lanes(8),
            big_lanes(16),
            whole((8, width)),
            big_rows(model),
            whole((width, model)),
        ],
        [
            (big_rows(width), sds((length, width), F32)),
            (big_rows(width), sds((length, width), BF16)),
        ],
        [],
        6e9,
        [acted, pack, seg_row, rowp, skip, cot_all, proj_out],
    )

    y, stat, full = call(
        partial(merge_kernel, nh, hops),
        "merge",
        big_grid,
        [
            big_rows(LANES),
            big_rows(LANES),
            big_tot,
            big_chunks(HDIM, width),
            big_chunks(HDIM, width),
            big_chunks(8, 2 * width),
            big_chunks(8, 2 * width),
            big_rows(width),
            big_rows(width),
            big_rows(width),
            whole((8, width)),
            whole(ex.shape),
        ]
        + [whole(message.shape)] * (2 * hops),
        [
            (big_rows(width), sds((length, width), BF16)),
            (big_lanes(8), sds((8, length), F32)),
            (big_chunks(HDIM, 2 * width), sds((nc, HDIM, 2 * width), BF16)),
        ],
        [pltpu.VMEM((HDIM, width), F32)] * 2,
        6e9,
        [acted, pack, tot, sf, rb, gpre, gsuf, yin, gate_in, dout, mg, ex] + ahead,
        scalars,
    )

    shares = [stat]
    for k in range(1, head_devices):
        shares.append(lax.ppermute(stat, "head", [(i, i ^ k) for i in range(head_devices)]))

    aside, outin, dy, dgate, gmix, gskip, gout, ggate = call(
        partial(turn_kernel, inner, head_devices),
        "turn",
        grid,
        [
            rows(width),
            rows(width),
            rows(width),
            whole((8, width)),
            rows(wide),
            whole((16, LANES)),
            rows(model),
            rows(model),
            whole((width, model)),
        ]
        + [lane_block(8, tb)] * head_devices,
        [
            (row_block(ASIDE, model), sds((head_devices * ASIDE, model), BF16)),
            (rows(width), sds((length, width), BF16)),
            (rows(width), sds((length, width), BF16)),
            (rows(width), sds((length, width), BF16)),
            (whole((8, width)), sds((8, width), F32)),
            (whole((8, width)), sds((8, width), F32)),
            (whole((width, model)), sds((width, model), BF16)),
            (whole((model, width)), sds((model, width), BF16)),
        ],
        [pltpu.VMEM((width, model), F32), pltpu.VMEM((model, width), F32)],
        4e9,
        [y, gate_in, dout, mg, acted, eye, normed, cot_all, proj_out] + shares,
    )
    outs = call(
        partial(adjoint_kernel, nh, head_devices, hops, own),
        "adjoint",
        grid,
        [
            rows(LANES),
            rows(LANES),
            tot_block,
            whole(gates_of.shape),
            whole((8, 2 * width)),
            whole(ex.shape),
            rows(width),
            rows(width),
            whole((width, model)),
        ],
        [(whole((own - ASIDE, model)), sds((own - ASIDE, model), BF16))] * head_devices
        + [
            (whole(states.shape), states),
            (state_block, states),
        ]
        + messages,
        [pltpu.VMEM((HDIM, width), F32), pltpu.VMEM((nc, HDIM, width), F32)],
        1e8,
        [acted, pack, tot, gates, gtot, ex, dy, outin, proj_out],
        scalars,
    )
    mixers = outs[:head_devices]
    dso, dro, *behind = outs[head_devices:]

    grad_proj_out, grad_proj_gate = lax.psum((gout, ggate), "seq")
    aside = lax.psum_scatter(aside, "head", scatter_dimension=0, tiled=True)
    behind = exchange_sides(behind, hops)
    mixer_shares = [mixers[0]] + [swap(mixers[k], "head", k) for k in range(1, head_devices)]

    mid_grid, mid_rows, mid_lanes, *_ = sized(256)
    dxin, dbc, pulls = call(
        partial(mid_kernel, nh),
        "mid",
        mid_grid,
        [
            mid_rows(wide),
            mid_rows(LANES),
            mid_lanes(8),
            mid_lanes(16),
            mid_rows(width),
            whole((16, LANES)),
        ],
        [
            (mid_rows(width), sds((length, width), BF16)),
            (mid_rows(LANES), sds((length, LANES), F32)),
            (mid_rows(LANES), sds((length, LANES), F32)),
        ],
        [],
        1e8,
        [acted, pack, seg_row, rowa, dy, eye16],
    )

    back = lambda i: grid - 1 - i

    def rev(spec):
        return pl.BlockSpec(spec.block_shape, lambda i, *_: spec.index_map(back(i)))

    mine, theirs, *chunks = call(
        partial(back_kernel, nh, peers, hops, own),
        "back",
        grid,
        [
            rev(rows(wide)),
            rev(rows(wide)),
            rev(rows(LANES)),
            rev(tot_block),
            rev(rows(width)),
            rev(chunk_block(per, HDIM, 2 * width)),
            rev(state_block),
            rev(state_block),
            rev(gate_block),
            rev(gate_block),
            rev(gate_block),
            rev(rows(width)),
            rev(rows(LANES)),
            rev(rows(LANES)),
            rev(rows(wide)),
            whole((8, wide)),
            whole((8, LANES)),
            whole((8, wide)),
            whole((8, width)),
            whole((8, LANES)),
            whole(ex.shape),
            whole(ext.shape),
            whole(tril.shape),
            whole(triu_wide.shape),
            rev(rows(model)),
            whole((8, model)),
            rev(rows(width)),
            whole((model, width)),
            whole((model, LANES + wide)),
            whole((8, width)),
            whole((8, width)),
        ]
        + [whole(message.shape)] * (2 * hops),
        [
            (side_block(0), sds((head_devices // 2, own, model), BF16)),
            (side_block(1), sds((head_devices // 2, own, model), BF16)),
        ]
        + [(whole((size, LANES + wide)), sds((size, LANES + wide), BF16))] * peers,
        [
            pltpu.VMEM((tb + 8, wide), F32),
            pltpu.VMEM((16, wide), F32),
            pltpu.VMEM((tb, LANES + wide), BF16),
            pltpu.VMEM((model, LANES + wide), F32),
            pltpu.VMEM((16, model), F32),
            pltpu.VMEM((HDIM, width), F32),
            pltpu.VMEM((HDIM, width), F32),
            pltpu.VMEM((tb, model), BF16),
        ],
        1e8,
        [
            acted,
            slope,
            pack,
            tot,
            dy,
            full,
            dso,
            dro,
            gsuf,
            gpre,
            gates,
            dxin,
            dbc,
            pulls,
            uv,
            uvh,
            halo_cols,
            taps,
            skip,
            pcol,
            ex,
            ext,
            tril,
            triu_wide,
            normed,
            normh,
            dgate,
            proj_gate,
            wcat,
            gmix,
            gskip,
        ]
        + behind,
        scalars,
    )

    chunks, theirs, mixer_shares = lax.optimization_barrier((chunks, theirs, mixer_shares))
    got = swap(theirs, "head", 1)
    summed = chunks[0].astype(F32)
    for k in range(1, peers):
        summed = summed + swap(chunks[k], "seq", k).astype(F32)
    shared = summed[:, : 2 * LANES]
    row_at = seq_index * size + jnp.arange(size)[:, None]
    lane_at = jnp.arange(2 * LANES)[None, :]
    common = (lane_at == 16) | (lane_at > 26)
    common = common | ((lane_at > 16) & (lane_at < 21) & (row_at < LANES))
    shared = jnp.where(common, sum_over(shared, "head"), shared)

    half = head_devices // 4
    own_in = mine[:half].astype(F32) + got[:half].astype(F32)
    going = (mine[half:].astype(F32) + got[half:].astype(F32)).astype(BF16)
    for b in range(1, bits):
        if b == 1:
            going, shared = lax.optimization_barrier((going, shared))
        got = swap(going, "head", 1 << b)
        if b < bits - 1:
            half = half // 2
            going = (own_in[half:] + got[half:].astype(F32)).astype(BF16)
            own_in = own_in[:half] + got[:half].astype(F32)

    reduced = jnp.concatenate([shared, summed[:, 2 * LANES :]], axis=1).astype(BF16)
    reduced, grad_proj_out, grad_proj_gate, mixer_shares = lax.optimization_barrier(
        (reduced, grad_proj_out, grad_proj_gate, mixer_shares)
    )
    spread_out = [reduced] + [swap(reduced, "seq", k) for k in range(1, peers)]
    grad_proj_out = grad_proj_out[:real_width].astype(F32)
    grad_proj_gate = grad_proj_gate[:, :real_width].astype(F32)
    mixer = sum(share.astype(F32) for share in mixer_shares)
    mixer = jnp.concatenate([aside.astype(F32), mixer], axis=0)
    layer_out = (tokens.astype(F32) + mixer).astype(BF16)
    spread_out, layer_out, grad_proj_out, grad_proj_gate = lax.optimization_barrier(
        (spread_out, layer_out, grad_proj_out, grad_proj_gate)
    )

    finals = [
        sds((model,), F32),
        sds((model, real_width), F32),
        sds((model, LANES), F32),
        sds((real_heads, 2, model), F32),
        sds((2, real_heads), F32),
        sds((1, real_heads), F32),
        sds((4, real_width), F32),
        sds((4, LANES), F32),
        sds((1, real_heads), F32),
        sds((real_width,), F32),
        sds((own, model), BF16),
    ]
    ggain, gvalue, gstate, gstep, gbias, gdecay, gconvv, gconvs, gskips, gmixer, grad_tokens = call(
        partial(finish_kernel, nh, peers, head_devices),
        "finish",
        1,
        [whole((size, LANES + wide))] * peers
        + [whole((32, LANES)), whole((1, model))]
        + [whole((own, model))] * 2
        + [whole((1, own, model))] * 2,
        [(whole(f.shape), f) for f in finals],
        [pltpu.VMEM((model, LANES), F32)],
        3e9,
        spread_out
        + [picked, input_gain[None, :]]
        + [tokens, cotangent, own_in, got],
        scalars,
    )
    return (
        layer_out,
        grad_tokens,
        ggain,
        grad_proj_gate,
        gvalue,
        gstate,
        jnp.transpose(gstep, (1, 2, 0)),
        gbias,
        gdecay[0],
        gconvv,
        gconvs,
        gskips[0],
        gmixer,
        grad_proj_out,
    )


def solution(mesh):
    return jax.shard_map(
        per_device,
        mesh=mesh,
        in_specs=(
            P(("seq", "head"), None),
            P(),
            P(None, "head"),
            P(None, "head"),
            P(),
            P(None, None, "head"),
            P(None, "head"),
            P("head"),
            P(None, "head"),
            P(),
            P("head"),
            P("head"),
            P("head", None),
            P(),
            P("seq"),
            P(("seq", "head"), None),
        ),
        out_specs=(
            P(("seq", "head"), None),
            P(("seq", "head"), None),
            P(),
            P(None, "head"),
            P(None, "head"),
            P(),
            P(None, None, "head"),
            P(None, "head"),
            P("head"),
            P(None, "head"),
            P(),
            P("head"),
            P("head"),
            P("head", None),
        ),
        check_vma=False,
    )
```

```python
from functools import partial

import jax
import jax.numpy as jnp
import numpy as np
from jax import lax
from jax.experimental import pallas as pl
from jax.experimental.pallas import tpu as pltpu
from jax.sharding import PartitionSpec as P

SPAN = 128
HDIM = 64
LANES = 128
LONGEST = 4096
EPSILON = 1e-05
TINY = 1e-30
F32 = jnp.float32
BF16 = jnp.bfloat16
BLOCK = 512
ASIDE = 256


def mm(a, b):
    return jnp.dot(a, b, preferred_element_type=F32)


def mm_nt(a, b):
    return lax.dot_general(a, b, (((1,), (1,)), ((), ())), preferred_element_type=F32)


def mm_tn(a, b):
    return lax.dot_general(a, b, (((0,), (0,)), ((), ())), preferred_element_type=F32)


def pieces(v):
    high = v.astype(BF16)
    rest = v - high.astype(F32)
    mid = rest.astype(BF16)
    return high, mid, (rest - mid.astype(F32)).astype(BF16)


def exact_tn(a, b):
    return lax.dot_general(
        a, b, (((0,), (0,)), ((), ())), precision=lax.Precision.HIGHEST, preferred_element_type=F32
    )


def split(v, axis):
    high = v.astype(BF16)
    return jnp.concatenate([high, (v - high.astype(F32)).astype(BF16)], axis=axis)


def sigmoid(v):
    return 1.0 / (1.0 + jnp.exp(-v))


def softplus(v):
    return jnp.maximum(v, 0.0) + jnp.log1p(jnp.exp(-jnp.abs(v)))


def iota(shape, dim):
    return lax.broadcasted_iota(jnp.int32, shape, dim)


def wide_tiles(width):
    return [slice(at, min(at + 2 * LANES, width)) for at in range(0, width, 2 * LANES)]


def groups(width):
    return [(n, n * LANES, (2 * n, 2 * n + 1)) for n in range(width // LANES)]


def sides(v, width):
    tiles = [v[:, at : at + LANES] for at in range(0, 2 * width, LANES)]
    return jnp.concatenate(tiles[::2], axis=1), jnp.concatenate(tiles[1::2], axis=1)


def stacked(v):
    first = iota(v.shape, 1) < HDIM
    zero = jnp.zeros_like(v)
    return jnp.concatenate([jnp.where(first, v, zero), jnp.where(first, zero, v)], axis=0)


def source_weights(pack, tot, dt, lane, nh):
    forward = lane < nh
    gap = jnp.where(forward, tot - pack, pack)
    kept = jnp.where(forward, pack[:, 38:39], pack[:, 40:41])
    return jnp.where(lane < 16, jnp.exp(jnp.where(lane < 16, gap, 0.0)) * kept * dt, 0.0)


def target_weights(pack, tot, lane, nh):
    forward = lane < nh
    gap = jnp.where(forward, pack, tot - pack)
    kept = jnp.where(forward, pack[:, 37:38], pack[:, 39:40])
    return jnp.where(lane < 16, jnp.exp(jnp.where(lane < 16, gap, 0.0)) * kept, 0.0)


def send_sides(at_ref, hops, up, down, refs):
    for d in range(1, hops + 1):
        low = (at_ref[0] // d) % 2 == 0
        refs[2 * d - 2][...] = jnp.where(low, up, down)
        refs[2 * d - 1][...] = jnp.where(low, down, up)


def land_sides(at_ref, hops, refs, from_earlier, from_later):
    for d in range(hops, 0, -1):
        low = (at_ref[0] // d) % 2 == 0
        first, second = refs[2 * d - 2][...], refs[2 * d - 1][...]
        for state, part in (
            (from_earlier, jnp.where(low, second, first)),
            (from_later, jnp.where(low, first, second)),
        ):
            if d == hops:
                state[...] = part[:HDIM]
            else:
                state[...] = part[:HDIM] + part[HDIM : HDIM + 1] * state[...]


def documents(off_ref, places):
    count = jnp.zeros(places.shape, F32)
    for at in range(0, off_ref.shape[1], LANES):
        begun = off_ref[0:1, at : at + LANES] <= places
        count = count + jnp.sum(jnp.where(begun, 1.0, 0.0), axis=1, keepdims=True)
    return count


def front_kernel(
    nh,
    hops,
    shares,
    own,
    at_ref,
    *refs,
):
    front_body(nh, hops, own, at_ref, refs[:shares], *refs[shares:])


def front_body(
    nh,
    hops,
    own,
    at_ref,
    x_refs,
    halo_ref,
    gain_ref,
    wg_ref,
    ws_ref,
    wv_ref,
    wst_ref,
    wstr_ref,
    pcol_ref,
    prow_ref,
    taps_ref,
    off_ref,
    live_ref,
    ex_ref,
    tril_ref,
    triu_ref,
    normed_ref,
    normh_ref,
    gate_ref,
    act_ref,
    slope_ref,
    uv_ref,
    uvh_ref,
    pack_ref,
    rowa_ref,
    rowp_ref,
    segrow_ref,
    halocols_ref,
    tot_ref,
    sf_ref,
    rb_ref,
    gates_ref,
    gpre_ref,
    gsuf_ref,
    gtot_ref,
    *rest,
):
    messages = rest[: 2 * hops]
    ubuf, state, incb, marks, ends, docs, wbuf, wides, bts = rest[2 * hops :]
    i = pl.program_id(0)
    tb = normed_ref.shape[0]
    per = tb // SPAN
    nc = rb_ref.shape[0]
    width = gate_ref.shape[1]
    piece = i * tb // own ^ at_ref[1]

    def norm(x):
        xf = x.astype(F32)
        s = lax.rsqrt(jnp.mean(xf * xf, axis=1, keepdims=True) + EPSILON)
        return (xf * s * gain_ref[0:1, :]).astype(BF16)

    @pl.when(i == 0)
    def _():
        edge = norm(halo_ref[...])
        normh_ref[...] = edge
        ubuf[0:8, :LANES] = mm(edge, ws_ref[...])
        ubuf[0:8, LANES:] = mm(edge, wv_ref[...])
        uvh_ref[...] = ubuf[0:8, :]
        state[...] = jnp.zeros_like(state)
        place = at_ref[2] - 8 + iota((8, 1), 0)
        here = documents(off_ref, place)
        lane8 = iota((8, LANES), 1)
        halo = jnp.zeros((8, LANES), F32)
        for k in (1, 2, 3):
            same = jnp.where(documents(off_ref, place + k) == here, 1.0, 0.0)
            halo = jnp.where(lane8 == k - 1, same, halo)
        halocols_ref[...] = halo

    @pl.when(i > 0)
    def _():
        ubuf[0:8, :] = ubuf[tb : tb + 8, :]

    for at in range(0, tb, 64):
        x = x_refs[0][at : at + 64, :]
        for k in range(1, len(x_refs)):
            x = jnp.where(piece == k, x_refs[k][at : at + 64, :], x)
        normed_ref[at : at + 64, :] = norm(x)
    nb = normed_ref[...]
    for tile in wide_tiles(width):
        gate_ref[:, tile] = mm(nb, wg_ref[:, tile]).astype(BF16)
    uv = mm(nb, ws_ref[...])
    ubuf[8 : 8 + tb, :LANES] = uv
    uv_ref[:, :LANES] = uv.astype(BF16)
    for tile in wide_tiles(width):
        uv = mm(nb, wv_ref[:, tile])
        at = slice(LANES + tile.start, LANES + tile.stop)
        ubuf[8 : 8 + tb, at] = uv
        uv_ref[:, at] = uv.astype(BF16)
    zr_all = mm_nt(wstr_ref[...], nb)
    lane = iota((SPAN, LANES), 1)
    forward = lane < nh
    forward_row = iota((16, SPAN), 0) < nh
    gate_lane = iota((8, LANES), 1) < nh
    for j in range(per):
        rows = slice(j * SPAN, (j + 1) * SPAN)
        base = at_ref[2] + (i * per + j) * SPAN
        around = documents(off_ref, base - 8 + iota((SPAN + 16, 1), 0))
        docs[...] = jnp.broadcast_to(around, docs.shape)
        seg = docs[8 : 8 + SPAN, :]
        prev_last, first = docs[7:8, :], docs[8:9, :]
        last, next_first = docs[7 + SPAN : 8 + SPAN, :], docs[8 + SPAN : 9 + SPAN, :]
        live = jnp.transpose(jnp.broadcast_to(live_ref[0:1, rows], (SPAN, SPAN)).astype(F32))
        mark = jnp.where(lane == 35, live, jnp.where(lane == 36, seg, 0.0))
        for k in (1, 2, 3):
            same = jnp.where(docs[8 - k : 8 - k + SPAN, :] == seg, 1.0, 0.0)
            mark = jnp.where(lane == 31 + k, same, mark)
            same = jnp.where(docs[8 + k : 8 + k + SPAN, :] == seg, 1.0, 0.0)
            mark = jnp.where(lane == 40 + k, same, mark)
        for k, bound in enumerate((prev_last, last, next_first, first)):
            mark = jnp.where(lane == 37 + k, jnp.where(seg == bound, 1.0, 0.0), mark)
        marks[rows, :] = mark
        opened = jnp.where(gate_lane, last - prev_last, next_first - first)
        ends[j * 8 : j * 8 + 8, :] = jnp.where(opened == 0.0, 1.0, 0.0)
        segrow_ref[:, rows] = jnp.transpose(seg)[:8]
    for at in range(0, LANES + width, LANES):
        tile = slice(at, at + LANES)
        for j in range(per):
            rows = slice(j * SPAN, (j + 1) * SPAN)
            keep = marks[rows, :]
            conv = taps_ref[0:1, tile] * ubuf[8 + j * SPAN : 8 + (j + 1) * SPAN, tile]
            for k in (1, 2, 3):
                moved = ubuf[8 - k + j * SPAN : 8 - k + (j + 1) * SPAN, tile]
                conv = conv + taps_ref[k : k + 1, tile] * moved * keep[:, 31 + k : 32 + k]
            sig = sigmoid(conv)
            live = keep[:, 35:36]
            act_ref[rows, tile] = (conv * sig * live).astype(BF16)
            slope_ref[rows, tile] = (live * sig * (1.0 + conv * (1.0 - sig))).astype(BF16)
    z_all = mm(nb, wst_ref[...])
    for j in range(per):
        rows = slice(j * SPAN, (j + 1) * SPAN)
        z = z_all[rows] + pcol_ref[0:1, :]
        dt = softplus(z)
        a = -dt * pcol_ref[1:2, :]
        total = mm(tril_ref[...], jnp.concatenate(pieces(a), axis=0))
        tot = total[SPAN - 1 : SPAN, :]
        cc = jnp.where(forward, total, total - a)
        pack = jnp.where(lane < 16, cc, jnp.where(lane < 32, z, marks[rows, :]))
        pack_ref[rows, :] = pack
        tot8 = jnp.broadcast_to(tot, (8, LANES))
        tot_ref[j * 8 : j * 8 + 8, :] = tot8
        dtr = softplus(zr_all[:, rows] + prow_ref[:, 0:1])
        ar = -dtr * prow_ref[:, 1:2]
        run = mm(jnp.concatenate(pieces(ar), axis=1), triu_ref[...])
        rowa = jnp.where(forward_row, run, run - ar)
        ldt = jnp.log(jnp.maximum(dtr, TINY))
        rowa_ref[:, rows] = rowa
        rowp_ref[:, rows] = jnp.where(forward_row, rowa - ldt, rowa + ldt)
        gate8 = jnp.exp(tot8) * ends[j * 8 : j * 8 + 8, :]
        bts[j * HDIM : (j + 1) * HDIM, :] = jnp.transpose(act_ref[rows, :LANES].astype(F32))[
            :HDIM
        ].astype(BF16)
        wbuf[rows, :] = split(source_weights(pack, tot, dt, lane, nh), 1)
        wbuf[tb + 16 * j : tb + 16 * j + 16, :] = split(jnp.concatenate([gate8, gate8], axis=0), 1)
    for n, at, _ in groups(width):
        tile = slice(at, at + LANES)
        both = slice(2 * at, 2 * at + 2 * LANES)
        wides[...] = mm(wbuf[...], ex_ref[:, both])
        for j in range(per):
            rows = slice(j * SPAN, (j + 1) * SPAN)
            c = i * per + j
            x = act_ref[rows, LANES + at : 2 * LANES + at].astype(F32)
            fed = jnp.concatenate(
                [
                    (x * wides[rows, :LANES]).astype(BF16),
                    (x * wides[rows, LANES:]).astype(BF16),
                ],
                axis=1,
            )
            bt = bts[j * HDIM : (j + 1) * HDIM, :]
            inc = mm(bt, fed)
            gate = wides[tb + 16 * j : tb + 16 * j + 8, :]
            gates_ref[c, :, both] = gate
            sf_ref[j, :, tile] = state[:, tile]
            state[:, tile] = state[:, tile] * gate[0:1, :LANES] + inc[:, :LANES]
            incb[c, :, tile] = inc[:, LANES:]
    @pl.when(i == pl.num_programs(0) - 1)
    def _():
        last_state = state[...]
        one = jnp.ones(gates_ref.shape[1:], F32)

        def up(c, p):
            gpre_ref[c] = p
            return p * gates_ref[c]

        p = lax.fori_loop(0, nc, up, one)
        tot_f, tot_b = sides(p, width)
        gtot_ref[:, :width] = tot_f
        gtot_ref[:, width:] = tot_b
        state[...] = jnp.zeros_like(state)

        def down(k, p):
            c = nc - 1 - k
            gsuf_ref[c] = p
            rb_ref[c] = state[...]
            gate = gates_ref[c]
            for n, at, _ in groups(width):
                tile = slice(at, at + LANES)
                second = slice(2 * at + LANES, 2 * at + 2 * LANES)
                state[:, tile] = state[:, tile] * gate[0:1, second] + incb[c, :, tile]
            return p * gate

        lax.fori_loop(0, nc, down, one)
        send_sides(
            at_ref,
            hops,
            jnp.concatenate([last_state, tot_f], axis=0),
            jnp.concatenate([state[...], tot_b], axis=0),
            messages,
        )


def inner_kernel(
    nh,
    act_ref,
    pack_ref,
    segrow_ref,
    rowp_ref,
    skip_ref,
    cot_ref,
    wo_ref,
    y_ref,
    dout_ref,
):
    tb, width = y_ref.shape
    for tile in wide_tiles(width):
        dout_ref[:, tile] = mm_nt(cot_ref[...], wo_ref[tile, :]).astype(BF16)
    t_at = iota((SPAN, SPAN), 0)
    s_at = iota((SPAN, SPAN), 1)
    lower = t_at > s_at
    for j in range(tb // SPAN):
        rows = slice(j * SPAN, (j + 1) * SPAN)
        bc = act_ref[rows, :LANES].astype(F32)
        b = bc[:, :HDIM].astype(BF16)
        c = pltpu.roll(bc, HDIM, 1)[:, :HDIM].astype(BF16)
        pack = pack_ref[rows, :]
        within = (pack[:, 36:37] == segrow_ref[0:1, rows]) & (t_at != s_at)
        score = jnp.where(within, mm_nt(c, b), 0.0)
        for n, at, heads in groups(width):
            tile = slice(at, at + LANES)
            mats = []
            for h in heads:
                gap = jnp.where(
                    lower,
                    pack[:, h : h + 1] - rowp_ref[h : h + 1, rows],
                    rowp_ref[nh + h : nh + h + 1, rows] - pack[:, nh + h : nh + h + 1],
                )
                mats.append((score * jnp.exp(gap)).astype(BF16))
            xp = act_ref[rows, LANES + at : 2 * LANES + at]
            y = mm(jnp.concatenate(mats, axis=1), stacked(xp))
            y_ref[rows, tile] = y + skip_ref[0:1, tile] * xp.astype(F32)


def merge_kernel(
    nh,
    hops,
    at_ref,
    bc_ref,
    pack_ref,
    tot_ref,
    sf_ref,
    rb_ref,
    gpre_ref,
    gsuf_ref,
    yin_ref,
    gate_ref,
    dout_ref,
    mg_ref,
    ex_ref,
    *rest,
):
    arrived = rest[: 2 * hops]
    y_ref, stat_ref, full_ref, sent_ref, rent_ref = rest[2 * hops :]
    tb, width = y_ref.shape

    @pl.when(pl.program_id(0) == 0)
    def _():
        land_sides(at_ref, hops, arrived, sent_ref, rent_ref)

    lane = iota((SPAN, LANES), 1)
    row8 = iota((8, SPAN), 0)
    for j in range(tb // SPAN):
        rows = slice(j * SPAN, (j + 1) * SPAN)
        pack = pack_ref[rows, :]
        bc = bc_ref[rows, :].astype(F32)
        c = pltpu.roll(bc, HDIM, 1)[:, :HDIM].astype(BF16)
        w = split(target_weights(pack, tot_ref[j * 8 : j * 8 + 1, :], lane, nh), 1)
        energy = jnp.zeros((SPAN, LANES), F32)
        cross = jnp.zeros((SPAN, LANES), F32)
        for n, at, _ in groups(width):
            tile = slice(at, at + LANES)
            both = slice(2 * at, 2 * at + 2 * LANES)
            second = slice(2 * at + LANES, 2 * at + 2 * LANES)
            first = slice(2 * at, 2 * at + LANES)
            sfull = sf_ref[j, :, tile] + gpre_ref[j, 0:1, first] * sent_ref[:, tile]
            rfull = rb_ref[j, :, tile] + gsuf_ref[j, 0:1, second] * rent_ref[:, tile]
            held = jnp.concatenate([sfull.astype(BF16), rfull.astype(BF16)], axis=1)
            full_ref[j, :, both] = held
            seen = mm(c, held) * mm(w, ex_ref[:, both])
            y = (yin_ref[rows, tile] + seen[:, :LANES] + seen[:, LANES:]).astype(BF16)
            y_ref[rows, tile] = y
            gate = gate_ref[rows, tile].astype(F32)
            g = y.astype(F32) * gate * sigmoid(gate)
            energy = energy + g * g
            cross = cross + dout_ref[rows, tile].astype(F32) * mg_ref[0:1, tile] * g
        energy = jnp.sum(jnp.transpose(energy), axis=0, keepdims=True)
        cross = jnp.sum(jnp.transpose(cross), axis=0, keepdims=True)
        stat_ref[:, rows] = jnp.where(row8 == 0, energy, jnp.where(row8 == 1, cross, 0.0))


def turn_kernel(
    inner,
    shares,
    y_ref,
    gate_ref,
    dout_ref,
    mg_ref,
    act_ref,
    eye_ref,
    normed_ref,
    cot_ref,
    wo_ref,
    *rest,
):
    stats_in = rest[:shares]
    (
        aside_ref,
        outin_ref,
        dy_ref,
        dgate_ref,
        gmix_ref,
        gskip_ref,
        gout_ref,
        ggate_ref,
        gout,
        ggate,
    ) = rest[shares:]
    i = pl.program_id(0)
    tb, width = y_ref.shape
    model = normed_ref.shape[1]

    @pl.when(i == 0)
    def _():
        gmix_ref[...] = jnp.zeros_like(gmix_ref)
        gskip_ref[...] = jnp.zeros_like(gskip_ref)
        gout[...] = jnp.zeros_like(gout)
        ggate[...] = jnp.zeros_like(ggate)

    for j in range(tb // SPAN):
        rows = slice(j * SPAN, (j + 1) * SPAN)
        stat = stats_in[0][:, rows]
        for more in stats_in[1:]:
            stat = stat + more[:, rows]
        stat = exact_tn(stat, eye_ref[0:8, :])
        q = lax.rsqrt(stat[:, 0:1] * (1.0 / inner) + EPSILON)
        k3 = q * q * q * stat[:, 1:2] * (1.0 / inner)
        for n, at, _ in groups(width):
            tile = slice(at, at + LANES)
            y = y_ref[rows, tile].astype(F32)
            gate = gate_ref[rows, tile].astype(F32)
            sig = sigmoid(gate)
            sg = gate * sig
            g = y * sg
            gq = g * q
            dout = dout_ref[rows, tile].astype(F32)
            mg = mg_ref[0:1, tile]
            outin_ref[rows, tile] = (gq * mg).astype(BF16)
            gmix_ref[0:1, tile] += jnp.sum(dout * gq, axis=0, keepdims=True)
            dg = dout * mg * q - g * k3
            dyb = (dg * sg).astype(BF16)
            dy_ref[rows, tile] = dyb
            dgate_ref[rows, tile] = (dg * y * (sig + sg * (1.0 - sig))).astype(BF16)
            x = act_ref[rows, LANES + at : 2 * LANES + at].astype(F32)
            gskip_ref[0:1, tile] += jnp.sum(dyb.astype(F32) * x, axis=0, keepdims=True)

    for tile in wide_tiles(model):
        aside_ref[:, tile] = mm(outin_ref[:ASIDE, :], wo_ref[:, tile]).astype(BF16)
    for at in range(0, width, LANES):
        tile = slice(at, at + LANES)
        gout[tile, :] += mm_tn(outin_ref[:, tile], cot_ref[...])
    for at in range(0, model, LANES):
        tile = slice(at, at + LANES)
        ggate[tile, :] += mm_tn(normed_ref[:, tile], dgate_ref[...])

    @pl.when(i == pl.num_programs(0) - 1)
    def _():
        gout_ref[...] = gout[...].astype(BF16)
        ggate_ref[...] = ggate[...].astype(BF16)


def adjoint_kernel(
    nh,
    shares,
    hops,
    own,
    at_ref,
    act_ref,
    pack_ref,
    tot_ref,
    gates_ref,
    gtot_ref,
    ex_ref,
    dy_ref,
    outin_ref,
    wo_ref,
    *rest,
):
    pieces_out = rest[:shares]
    dso_ref, dro_ref, *messages, state, incf, wbuf, wides, cts = rest[shares:]
    i = pl.program_id(0)
    tb, width = dy_ref.shape
    model = wo_ref.shape[1]
    per = tb // SPAN
    nc = dso_ref.shape[0]
    lane = iota((SPAN, LANES), 1)

    @pl.when(i == 0)
    def _():
        state[...] = jnp.zeros_like(state)

    for j in range(per):
        rows = slice(j * SPAN, (j + 1) * SPAN)
        pack = pack_ref[rows, :]
        tot = tot_ref[j * 8 : j * 8 + 1, :]
        wbuf[rows, :] = split(target_weights(pack, tot, lane, nh), 1)
        cts[j * HDIM : (j + 1) * HDIM, :] = jnp.transpose(act_ref[rows, :].astype(F32))[
            HDIM:
        ].astype(BF16)
    for n, at, _ in groups(width):
        tile = slice(at, at + LANES)
        both = slice(2 * at, 2 * at + 2 * LANES)
        second = slice(2 * at + LANES, 2 * at + 2 * LANES)
        wides[...] = mm(wbuf[...], ex_ref[:, both])
        for j in range(per):
            rows = slice(j * SPAN, (j + 1) * SPAN)
            c = i * per + j
            dy = dy_ref[rows, tile].astype(F32)
            fed = jnp.concatenate(
                [
                    (dy * wides[rows, :LANES]).astype(BF16),
                    (dy * wides[rows, LANES:]).astype(BF16),
                ],
                axis=1,
            )
            inc = mm(cts[j * HDIM : (j + 1) * HDIM, :], fed)
            incf[c, :, tile] = inc[:, :LANES]
            dro_ref[j, :, tile] = state[:, tile]
            state[:, tile] = state[:, tile] * gates_ref[c, 0:1, second] + inc[:, LANES:]

    for k in range(shares):

        @pl.when((i * tb // own ^ at_ref[1]) == k)
        def _():
            for tile in wide_tiles(model):
                pieces_out[k][:, tile] = mm(outin_ref[ASIDE:, :], wo_ref[:, tile]).astype(BF16)

    @pl.when(i == pl.num_programs(0) - 1)
    def _():
        last_state = state[...]
        state[...] = jnp.zeros_like(state)

        def down(k, _):
            c = nc - 1 - k
            dso_ref[c] = state[...]
            for n, at, _ in groups(width):
                tile = slice(at, at + LANES)
                first = slice(2 * at, 2 * at + LANES)
                state[:, tile] = state[:, tile] * gates_ref[c, 0:1, first] + incf[c, :, tile]
            return 0

        lax.fori_loop(0, nc, down, 0)
        send_sides(
            at_ref,
            hops,
            jnp.concatenate([last_state, gtot_ref[:, width:]], axis=0),
            jnp.concatenate([state[...], gtot_ref[:, :width]], axis=0),
            messages,
        )


def mid_kernel(
    nh,
    act_ref,
    pack_ref,
    segrow_ref,
    rowa_ref,
    dy_ref,
    eye_ref,
    dx_ref,
    dbc_ref,
    pulls_ref,
    qbuf,
    places,
):
    tb, width = dx_ref.shape

    @pl.when(pl.program_id(0) == 0)
    def _():
        qbuf[...] = jnp.zeros_like(qbuf)
        spot_row = iota((4 * SPAN, LANES), 0) < 2 * SPAN
        spot_lane = iota((4 * SPAN, LANES), 1)
        for h in range(nh):
            up = jnp.where(spot_lane == nh + h, jnp.where(spot_row, -1.0, 1.0), 0.0)
            places[h] = jnp.where(spot_row & (spot_lane == h), 1.0, up).astype(BF16)

    s_at = iota((SPAN, SPAN), 0)
    t_at = iota((SPAN, SPAN), 1)
    lower = t_at > s_at
    lane = iota((SPAN, LANES), 1)
    front_half = lane < HDIM
    for j in range(tb // SPAN):
        rows = slice(j * SPAN, (j + 1) * SPAN)
        pack = pack_ref[rows, :]
        bc = act_ref[rows, :LANES].astype(F32)
        cb = pltpu.roll(bc, HDIM, 1)
        within = (pack[:, 36:37] == segrow_ref[0:1, rows]) & (t_at != s_at)
        score = mm_nt(bc[:, :HDIM].astype(BF16), cb[:, :HDIM].astype(BF16))
        score = jnp.where(within, score, 0.0)
        ldt = jnp.log(jnp.maximum(softplus(pltpu.roll(pack, LANES - 16, 1)), TINY))
        pc = jnp.where(lane < nh, pack - ldt, pack + ldt)
        dscore = jnp.zeros((SPAN, SPAN), F32)
        kc = jnp.zeros((SPAN, LANES), F32)
        for n, at, heads in groups(width):
            tile = slice(at, at + LANES)
            dyp = dy_ref[rows, tile]
            dmats = mm_nt(stacked(act_ref[rows, LANES + at : 2 * LANES + at]), dyp)
            mats = []
            for m, h in enumerate(heads):
                decay = jnp.exp(
                    jnp.where(
                        lower,
                        rowa_ref[h : h + 1, rows] - pc[:, h : h + 1],
                        pc[:, nh + h : nh + h + 1] - rowa_ref[nh + h : nh + h + 1, rows],
                    )
                )
                spot = dmats[m * SPAN : (m + 1) * SPAN, :] * decay
                dscore = dscore + spot
                mats.append((score * decay).astype(BF16))
                pull = spot * score
                pull_low = jnp.where(lower, pull, 0.0)
                down = jnp.sum(pull_low, axis=0, keepdims=True)
                qbuf[h : h + 1, :] = down
                qbuf[nh + h : nh + h + 1, :] = jnp.sum(pull, axis=0, keepdims=True) - down
                both = jnp.concatenate([split(pull_low, 1), split(pull, 1)], axis=1)
                kc = kc + mm(both, places[h])
            dx_ref[rows, tile] = mm(jnp.concatenate(mats, axis=1), stacked(dyp)).astype(BF16)
        dscore = jnp.where(within, dscore, 0.0).astype(BF16)
        cpad = jnp.where(front_half, cb, 0.0).astype(BF16)
        bpad = jnp.where(front_half, 0.0, cb).astype(BF16)
        dbc_ref[rows, :] = mm(dscore, cpad) + mm_tn(dscore, bpad)
        pulls_ref[rows, :] = kc + exact_tn(qbuf[...], eye_ref[...])


def back_kernel(
    nh,
    peers,
    hops,
    own,
    at_ref,
    act_ref,
    slope_ref,
    pack_ref,
    tot_ref,
    dy_ref,
    full_ref,
    dso_ref,
    dro_ref,
    gsuf_ref,
    gpre_ref,
    gates_ref,
    dxin_ref,
    dbc_ref,
    pulls_ref,
    uv_ref,
    uvh_ref,
    halocols_ref,
    taps_ref,
    skip_ref,
    pcol_ref,
    ex_ref,
    ext_ref,
    tril_ref,
    triu_ref,
    normed_ref,
    normh_ref,
    dgate_ref,
    wg_ref,
    wcat_ref,
    gmix_ref,
    gskip_ref,
    *rest,
):
    arrived = rest[: 2 * hops]
    mine_ref, theirs_ref, *chunks = rest[2 * hops : 2 * hops + 2 + peers]
    scratch = rest[2 * hops + 2 + peers :]
    dbuf, hbuf, dcat, acc, lines, dsent_ref, drent_ref, parts, wbuf, wides, pbuf, sums = scratch
    i = pl.program_id(0)
    last = pl.num_programs(0) - 1
    tb = act_ref.shape[0]
    width = act_ref.shape[1] - LANES
    model = normed_ref.shape[1]

    @pl.when(i == 0)
    def _():
        dbuf[tb : tb + 8, :] = jnp.zeros((8, LANES + width), F32)
        acc[...] = jnp.zeros_like(acc)
        lines[...] = jnp.zeros_like(lines)
        land_sides(at_ref, hops, arrived, drent_ref, dsent_ref)

    lane = iota((SPAN, LANES), 1)
    forward = lane < nh
    head_lane = lane < 16
    none = jnp.zeros((HDIM, 2 * LANES), BF16)
    per = tb // SPAN
    pair = 2 * LANES

    def part_of(kind, j):
        return slice((kind * per + j) * SPAN, (kind * per + j + 1) * SPAN)

    for j in range(per):
        rows = slice(j * SPAN, (j + 1) * SPAN)
        pack = pack_ref[rows, :]
        tot = tot_ref[j * 8 : j * 8 + 1, :]
        dt = softplus(pltpu.roll(pack, LANES - 16, 1))
        wbuf[part_of(0, j), :] = split(source_weights(pack, tot, dt, lane, nh), 1)
        wbuf[part_of(1, j), :] = split(target_weights(pack, tot, lane, nh), 1)
        dbuf[rows, :LANES] = dbc_ref[rows, :]
    for n, at, _ in groups(width):
        tile = slice(at, at + LANES)
        wtile = slice(LANES + at, 2 * LANES + at)
        both = slice(2 * at, 2 * at + 2 * LANES)
        first = slice(2 * at, 2 * at + LANES)
        second = slice(2 * at + LANES, 2 * at + 2 * LANES)
        wides[...] = mm(wbuf[...], ex_ref[:, both])
        for j in range(per):
            rows = slice(j * SPAN, (j + 1) * SPAN)
            bc = act_ref[rows, :LANES].astype(F32)
            b = bc[:, :HDIM].astype(BF16)
            c = pltpu.roll(bc, HDIM, 1)[:, :HDIM].astype(BF16)
            x = act_ref[rows, wtile].astype(F32)
            dy = dy_ref[rows, tile].astype(F32)
            x2 = jnp.concatenate([x, x], axis=1)
            dy2 = jnp.concatenate([dy, dy], axis=1)
            held = full_ref[j, :, both]
            dheld = jnp.concatenate(
                [
                    dso_ref[j, :, tile] + gsuf_ref[j, 0:1, first] * dsent_ref[:, tile],
                    dro_ref[j, :, tile] + gpre_ref[j, 0:1, second] * drent_ref[:, tile],
                ],
                axis=1,
            )
            dheld_low = dheld.astype(BF16)
            to_wide = wides[part_of(0, j), :]
            fro_wide = wides[part_of(1, j), :]
            flow = mm(b, dheld_low) * to_wide
            seen = mm(c, held) * fro_wide
            dbc = mm_nt((x2 * to_wide).astype(BF16), jnp.concatenate([dheld_low, none], axis=0))
            dbc = dbc + mm_nt((dy2 * fro_wide).astype(BF16), jnp.concatenate([none, held], axis=0))
            dbuf[rows, :LANES] += dbc
            pbuf[part_of(0, j), :] = split(dy2 * seen, 1)
            pbuf[part_of(1, j), :] = split(x2 * flow, 1)
            product = jnp.sum(dheld * held.astype(F32), axis=0, keepdims=True) * gates_ref[j, :, both]
            pbuf[2 * tb + 16 * j : 2 * tb + 16 * j + 16, :] = split(
                jnp.concatenate([product, product], axis=0), 1
            )
            dx = dxin_ref[rows, tile].astype(F32) + flow[:, :LANES] + flow[:, LANES:]
            dx = dx + skip_ref[0:1, tile] * dy
            dbuf[rows, wtile] = dx * slope_ref[rows, wtile].astype(F32)
        ext = ext_ref[both, :]
        found = mm(pbuf[:, :pair], ext) + mm(pbuf[:, pair:], ext)
        if n == 0:
            sums[...] = found
        else:
            sums[...] += found
    for j in range(per):
        rows = slice(j * SPAN, (j + 1) * SPAN)
        pack = pack_ref[rows, :]
        z = pltpu.roll(pack, LANES - 16, 1)
        dt = softplus(z)
        carried = sums[part_of(0, j), :]
        leaving = sums[part_of(1, j), :]
        through = sums[2 * tb + 16 * j : 2 * tb + 16 * j + 8, :]
        dbuf[rows, :LANES] = dbuf[rows, :LANES] * slope_ref[rows, :LANES].astype(F32)
        pulls = pulls_ref[rows, :]
        kc = jnp.where(head_lane, pulls, 0.0)
        moved = jnp.where(head_lane, pltpu.roll(pulls, LANES - 16, 1), 0.0) + carried - kc
        before = mm(tril_ref[:, : 2 * SPAN], split(jnp.where(forward, leaving, moved), 0))
        after = mm(triu_ref[:, : 2 * SPAN], split(jnp.where(forward, moved, leaving), 0))
        dlog = before + after - leaving + through[0:1, :]
        sigz = sigmoid(z)
        rate = pcol_ref[1:2, :]
        dstep = (kc + leaving) * (sigz / jnp.maximum(dt, TINY)) - dlog * rate * sigz
        dstep = jnp.where(head_lane, dstep, 0.0)
        dcat[rows, :LANES] = dstep.astype(BF16)
        lines[7:8, :LANES] += jnp.sum(dstep, axis=0, keepdims=True)
        ends = jnp.where(head_lane, -dlog * dt * rate, 0.0)
        lines[8:9, :LANES] += jnp.sum(ends, axis=0, keepdims=True)
    for j in range(per):
        rows = slice(j * SPAN, (j + 1) * SPAN)
        pack = pack_ref[rows, :]
        for at in range(0, LANES + width, LANES):
            tile = slice(at, at + LANES)
            dconv = dbuf[rows, tile]
            uv = uv_ref[rows, tile].astype(F32)
            du = taps_ref[0:1, tile] * dconv
            lines[1:2, tile] += jnp.sum(uv * dconv, axis=0, keepdims=True)
            for k in (1, 2, 3):
                shifted = dbuf[j * SPAN + k : (j + 1) * SPAN + k, tile] * pack[:, 40 + k : 41 + k]
                du = du + taps_ref[k : k + 1, tile] * shifted
                lines[1 + k : 2 + k, tile] += jnp.sum(uv * shifted, axis=0, keepdims=True)
            dcat[rows, LANES + at : 2 * LANES + at] = du.astype(BF16)

    edge = dbuf[0:8, :]
    dbuf[tb : tb + 8, :] = edge
    for tile in wide_tiles(model):
        part = mm_nt(dgate_ref[...], wg_ref[tile, :])
        part = part + mm_nt(dcat[...], wcat_ref[tile, :])
        parts[:, tile] = part.astype(BF16)
        normed = normed_ref[:, tile]
        lines[0:1, tile] += jnp.sum(part * normed.astype(F32), axis=0, keepdims=True)
        acc[tile, :] += mm_tn(normed, dcat[...])
    side = ((last - i) * tb // own ^ at_ref[1]) % 2

    @pl.when(side == 0)
    def _():
        mine_ref[0] = parts[...]

    @pl.when(side == 1)
    def _():
        theirs_ref[0] = parts[...]

    @pl.when(i == last)
    def _():
        taps_at = slice(0, LANES + width)
        hbuf[0:8, :] = jnp.zeros_like(edge)
        hbuf[8:16, :] = edge
        duh = jnp.zeros_like(edge)
        for k in (1, 2, 3):
            shifted = hbuf[k : k + 8, :] * halocols_ref[:, k - 1 : k]
            duh = duh + taps_ref[k : k + 1, :] * shifted
            lines[1 + k : 2 + k, taps_at] += jnp.sum(uvh_ref[...] * shifted, axis=0, keepdims=True)
        duh = duh.astype(BF16)
        normh = normh_ref[...]
        parth = mm_nt(duh, wcat_ref[:, LANES:])
        lines[0:1, :] += jnp.sum(parth * normh.astype(F32), axis=0, keepdims=True)
        skips = jnp.zeros((8, LANES), F32)
        for n, at, _ in groups(width):
            ext = ext_ref[2 * at : 2 * at + LANES, :]
            high = gskip_ref[:, at : at + LANES].astype(BF16)
            low = (gskip_ref[:, at : at + LANES] - high.astype(F32)).astype(BF16)
            skips = skips + mm(high, ext) + mm(low, ext)
        lines[5:6, :LANES] = skips[0:1, :]
        lines[6:7, :width] = gmix_ref[0:1, :]
        acc[:, LANES:] += mm_tn(normh, duh)
        placed = jnp.where(iota((16, LANES), 1) == iota((16, LANES), 0) + 16, 1.0, 0.0)
        acc[:, :LANES] += exact_tn(lines[...], placed)
        row8 = iota((8, LANES), 0)
        taken = iota((8, LANES), 1) == 19 + 3 * at_ref[0] + row8
        taken = taken & (row8 > 4) & (at_ref[0] > 0)
        acc[:, :LANES] += exact_tn(parth, jnp.where(taken, 1.0, 0.0))
        size = model // peers
        for k in range(peers):
            start = pl.multiple_of((at_ref[0] ^ k) * size, 8)
            chunks[k][...] = acc[pl.ds(start, size), :].astype(BF16)


def finish_kernel(nh, peers, shares, at_ref, *refs):
    chunks = refs[:peers]
    eye_ref, ingain_ref, x_ref, cot_ref, kept_ref, got_ref = refs[peers : peers + 6]
    gain_ref, value_ref, state_ref, step_ref, bias_ref, decay_ref = refs[peers + 6 : peers + 12]
    convv_ref, convs_ref, skip_ref, mixer_ref, tokens_ref, extra = refs[peers + 12 :]
    size = chunks[0].shape[0]
    real_width = value_ref.shape[1]
    heads = step_ref.shape[0]
    for k in range(peers):
        rows = pl.ds(pl.multiple_of((at_ref[0] ^ k) * size, 8), size)
        extra[rows, :] = chunks[k][:, :LANES].astype(F32)
        state_ref[rows, :] = chunks[k][:, LANES : 2 * LANES].astype(F32)
        value_ref[rows, :] = chunks[k][:, 2 * LANES : 2 * LANES + real_width].astype(F32)
    found = extra[...].astype(BF16)
    lines = mm_nt(eye_ref[...], found)
    row16 = iota((16, LANES), 0)
    taken = iota((16, LANES), 1) == 27 + 3 * at_ref[0] + row16 - 13
    taken = taken & (row16 > 12) & (at_ref[1] == shares - 1)
    late = mm_nt(jnp.where(taken, 1.0, 0.0).astype(BF16), found)

    def token_rows(rows, more):
        x = x_ref[rows, :].astype(F32)
        s = lax.rsqrt(jnp.mean(x * x, axis=1, keepdims=True) + EPSILON)
        dn = kept_ref[0, rows, :] + got_ref[0, rows, :].astype(F32) + more
        scaled = dn * ingain_ref[...]
        inside = jnp.mean(scaled * x, axis=1, keepdims=True)
        cot = cot_ref[rows, :].astype(F32)
        tokens_ref[rows, :] = (cot + s * scaled - x * (s * s * s) * inside).astype(BF16)

    own = x_ref.shape[0]
    for at in range(0, own, 32):
        token_rows(slice(at, at + 32), 0.0)
    token_rows(slice(own - 16, own), late)
    for h in range(heads):
        step_ref[h, 0:1, :] = lines[h : h + 1, :]
        step_ref[h, 1:2, :] = lines[nh + h : nh + h + 1, :]
    gain_ref[...] = (lines[16:17, :] / ingain_ref[...])[0]
    convs_ref[...] = lines[17:21, :LANES]
    convv_ref[...] = lines[17:21, LANES : LANES + real_width]
    skip_ref[...] = lines[21:22, :heads]
    mixer_ref[...] = lines[22, :real_width]
    bias_ref[0:1, :] = lines[23:24, :heads]
    bias_ref[1:2, :] = lines[23:24, nh : nh + heads]
    decay_ref[...] = lines[24:25, :heads] + lines[24:25, nh : nh + heads]


def whole(shape):
    return pl.BlockSpec(shape, lambda i, *_: (0,) * len(shape))


def row_block(rows, width):
    return pl.BlockSpec((rows, width), lambda i, *_: (i, 0))


def lane_block(rows, width):
    return pl.BlockSpec((rows, width), lambda i, *_: (0, i))


def chunk_block(per, rows, width):
    return pl.BlockSpec((per, rows, width), lambda i, *_: (i, 0, 0))


def sds(shape, dtype):
    return jax.ShapeDtypeStruct(shape, dtype)


def call(kernel, name, grid, ins, outs, scratch, flops, operands, scalars=()):
    return pl.pallas_call(
        kernel,
        name=name,
        grid_spec=pltpu.PrefetchScalarGridSpec(
            num_scalar_prefetch=len(scalars),
            grid=(grid,),
            in_specs=ins,
            out_specs=[spec for spec, _ in outs],
            scratch_shapes=scratch,
        ),
        out_shape=[shape for _, shape in outs],
        compiler_params=pltpu.CompilerParams(
            dimension_semantics=("arbitrary",), vmem_limit_bytes=56 * 1024 * 1024
        ),
        cost_estimate=pl.CostEstimate(
            flops=int(flops), bytes_accessed=1, transcendentals=0
        ),
    )(*scalars, *operands)


def shifted_in(array, axis, by):
    length = lax.axis_size(axis)
    pairs = [(i, i + by) for i in range(length) if 0 <= i + by < length]
    return lax.ppermute(array, axis, pairs)


def exchange_sides(messages, hops):
    size = lax.axis_size("seq")
    arrived = []
    for d in range(1, hops + 1):
        for side in (0, 1):
            pairs = [(i, i + d) for i in range(size - d) if (i // d) % 2 == side]
            both = pairs + [(b, a) for a, b in pairs]
            arrived.append(lax.ppermute(messages[len(arrived)], "seq", both))
    return arrived


def swap(array, axis, k):
    n = lax.axis_size(axis)
    return lax.ppermute(array, axis, [(i, i ^ k) for i in range(n)])


def sum_over(array, axis):
    size = lax.axis_size(axis)
    result = array
    for k in range(1, size):
        result = result + lax.ppermute(array, axis, [(i, i ^ k) for i in range(size)])
    return result


def per_device(
    tokens,
    input_gain,
    proj_gate,
    proj_value,
    proj_state,
    proj_step,
    step_bias,
    decay_log,
    conv_value,
    conv_state,
    skip_gain,
    mixer_gain,
    proj_out,
    doc_lengths,
    pad_mask,
    cotangent,
):
    head_devices = lax.axis_size("head")
    length = pad_mask.shape[0]
    model = tokens.shape[1]
    real_width = proj_gate.shape[1]
    real_heads = proj_step.shape[2]
    inner = real_width * head_devices
    width = -(-real_width // LANES) * LANES
    nh = width // HDIM

    def padded(array, axis, size):
        if array.shape[axis] == size:
            return array
        widths = [(0, 0)] * array.ndim
        widths[axis] = (0, size - array.shape[axis])
        return jnp.pad(array, widths)

    proj_gate = padded(proj_gate, 1, width)
    proj_value = padded(proj_value, 1, width)
    proj_step = padded(proj_step, 2, nh)
    step_bias = padded(step_bias, 1, nh)
    conv_value = padded(conv_value, 1, width)
    skip_gain = padded(skip_gain, 0, nh)
    mixer_gain = padded(mixer_gain, 0, width)
    proj_out = padded(proj_out, 0, width)
    nc = length // SPAN
    tb = BLOCK
    per = tb // SPAN
    grid = length // tb
    wide = LANES + width
    hops = -(-(LONGEST - 1) // length)
    seq_index = lax.axis_index("seq")
    first_place = seq_index * length
    all_tokens = length * lax.axis_size("seq")

    edge_rows = shifted_in(tokens[tokens.shape[0] - 8 :], "seq", 1)
    here = lax.axis_index("head")
    halo = jnp.where(here == head_devices - 1, edge_rows, 0)
    for k in range(1, head_devices):
        halo = halo + jnp.where(here ^ k == head_devices - 1, swap(edge_rows, "head", k), 0)

    offsets = jnp.cumsum(doc_lengths) - doc_lengths
    room = -(-(offsets.shape[0] + 1) // LANES) * LANES - offsets.shape[0]
    fill = jnp.where(jnp.arange(room) == 0, all_tokens, 2 * all_tokens).astype(offsets.dtype)
    offsets = jnp.concatenate([offsets, fill])[None, :]
    live_row = pad_mask[None, :]
    lanes = np.arange(LANES)
    column = np.arange(2 * width)
    head_of = column // (2 * LANES) * 2 + column % LANES // HDIM
    head_of = head_of + np.where(column % (2 * LANES) >= LANES, nh, 0)
    ext = jnp.asarray(head_of[:, None] == lanes[None, :], BF16)
    ex = jnp.asarray(np.tile(head_of[None, :] == lanes[:, None], (2, 1)), BF16)
    at = np.arange(SPAN)
    tril = jnp.asarray(np.tile(at[:, None] >= at[None, :], (1, 3)), BF16)
    triu = at[:, None] <= at[None, :]
    triu_wide = jnp.asarray(np.tile(triu, (1, 2)), BF16)
    triu_tall = jnp.asarray(np.tile(triu, (3, 1)), BF16)
    eye = jnp.asarray(np.arange(16)[:, None] == lanes[None, :], F32)
    eye16 = jnp.asarray(np.arange(16)[:, None] + 16 == lanes[None, :], F32)
    picked = jnp.asarray(np.arange(32)[:, None] == lanes[None, :], BF16)
    peers = lax.axis_size("seq")
    own = length // head_devices
    bits = head_devices.bit_length() - 1
    scalars = [jnp.stack([seq_index, here, first_place]).astype(jnp.int32)]
    size = model // peers

    rate = padded(jnp.exp(decay_log), 0, nh)
    gap = 16 - 2 * nh
    bias16 = jnp.pad(step_bias.reshape(-1), (0, gap))
    rate16 = jnp.pad(jnp.concatenate([rate, rate]), (0, gap))
    prow = jnp.stack([bias16, rate16], axis=1)
    wide_bias = jnp.pad(jnp.concatenate([bias16, bias16]), (0, LANES - 32))
    pcol = jnp.stack([wide_bias, jnp.pad(rate16, (0, LANES - 16))], axis=0)
    steps = jnp.concatenate([proj_step[0], proj_step[1]], axis=1)
    steps = jnp.pad(steps, ((0, 0), (0, gap)))
    wst = jnp.pad(jnp.concatenate([steps, steps], axis=1), ((0, 0), (0, LANES - 32)))
    wstr = steps.T
    taps = jnp.concatenate([conv_state, conv_value], axis=1)
    gain = input_gain[None, :]
    mg = mixer_gain[None, :]
    skip = jnp.repeat(skip_gain, HDIM)[None, :]
    pieces_of = {0: tokens}
    for bit in [1 << b for b in range(bits - 1, 0, -1)]:
        pieces_of.update({k | bit: swap(v, "head", bit) for k, v in pieces_of.items()})
    wcat = jnp.concatenate([wst, proj_state, proj_value], axis=1)
    prelims = (halo, offsets, live_row, pcol, prow, wst, wstr, taps, wcat)
    pieces_of, late, prelims, scalars = lax.optimization_barrier(
        (pieces_of, cotangent, prelims, scalars)
    )
    halo, offsets, live_row, pcol, prow, wst, wstr, taps, wcat = prelims
    pieces_of.update({k | 1: swap(v, "head", 1) for k, v in pieces_of.items()})
    token_pieces = [pieces_of[k] for k in range(head_devices)]
    cot_all = lax.all_gather(late, "head", axis=0, tiled=True)

    rows = partial(row_block, tb)
    states = sds((nc, HDIM, width), F32)
    gates_of = sds((nc, 8, 2 * width), F32)
    message = sds((HDIM + 8, width), F32)
    state_block = chunk_block(per, HDIM, width)
    gate_block = chunk_block(per, 8, 2 * width)
    tot_block = row_block(per * 8, LANES)
    messages = [(whole(message.shape), message)] * (2 * hops)

    def sized(block):
        return (
            length // block,
            partial(row_block, block),
            partial(lane_block, width=block),
            partial(chunk_block, block // SPAN),
            row_block(block // SPAN * 8, LANES),
        )

    def slot_of(j, at):
        place = j ^ at[1]
        return sum(((place >> b) & 1) << (bits - 1 - b) for b in range(bits))

    each = own // tb

    def piece_block(k):
        def index(i, at):
            return jnp.clip(i - (at[1] ^ k) * each, 0, each - 1), 0

        return pl.BlockSpec((tb, model), index)

    def side_block(side):
        def index(i, at):
            row = grid - 1 - i
            j, sub = row // each, row % each
            ours = (j ^ at[1]) % 2 == side
            first = j == head_devices - 1
            j = jnp.where(ours, j, jnp.where(first, j - 1, j + 1))
            sub = jnp.where(ours, sub, jnp.where(first, each - 1, 0))
            return slot_of(j, at) % (head_devices // 2), sub, 0

        return pl.BlockSpec((1, tb, model), index)

    (
        normed,
        normh,
        gate_in,
        acted,
        slope,
        uv,
        uvh,
        pack,
        rowa,
        rowp,
        seg_row,
        halo_cols,
        tot,
        sf,
        rb,
        gates,
        gpre,
        gsuf,
        gtot,
        *ahead,
    ) = call(
        partial(front_kernel, nh, hops, head_devices, own),
        "front",
        grid,
        [piece_block(k) for k in range(head_devices)]
        + [
            whole((8, model)),
            whole((1, model)),
            whole((model, width)),
            whole((model, LANES)),
            whole((model, width)),
            whole((model, LANES)),
            whole((16, model)),
            whole((2, LANES)),
            whole((16, 2)),
            whole((4, wide)),
            whole(offsets.shape),
            lane_block(1, tb),
            whole(ex.shape),
            whole(tril.shape),
            whole(triu_tall.shape),
        ],
        [
            (rows(model), sds((length, model), BF16)),
            (whole((8, model)), sds((8, model), BF16)),
            (rows(width), sds((length, width), BF16)),
            (rows(wide), sds((length, wide), BF16)),
            (rows(wide), sds((length, wide), BF16)),
            (rows(wide), sds((length, wide), BF16)),
            (whole((8, wide)), sds((8, wide), F32)),
            (rows(LANES), sds((length, LANES), F32)),
            (lane_block(16, tb), sds((16, length), F32)),
            (lane_block(16, tb), sds((16, length), F32)),
            (lane_block(8, tb), sds((8, length), F32)),
            (whole((8, LANES)), sds((8, LANES), F32)),
            (tot_block, sds((nc * 8, LANES), F32)),
            (state_block, states),
            (whole(states.shape), states),
            (whole(gates_of.shape), gates_of),
            (whole(gates_of.shape), gates_of),
            (whole(gates_of.shape), gates_of),
            (whole((8, 2 * width)), sds((8, 2 * width), F32)),
        ]
        + messages,
        [
            pltpu.VMEM((tb + 8, wide), F32),
            pltpu.VMEM((HDIM, width), F32),
            pltpu.VMEM((nc, HDIM, width), F32),
            pltpu.VMEM((tb, LANES), F32),
            pltpu.VMEM((per * 8, LANES), F32),
            pltpu.VMEM((SPAN + 16, LANES), F32),
            pltpu.VMEM((tb + 16 * per, 2 * LANES), BF16),
            pltpu.VMEM((tb + 16 * per, 2 * LANES), F32),
            pltpu.VMEM((per * HDIM, LANES), BF16),
        ],
        25e9,
        token_pieces
        + [
            halo,
            gain,
            proj_gate,
            proj_state,
            proj_value,
            wst,
            wstr,
            pcol,
            prow,
            taps,
            offsets,
            live_row,
            ex,
            tril,
            triu_tall,
        ],
        scalars,
    )

    ahead = exchange_sides(ahead, hops)

    big_grid, big_rows, big_lanes, big_chunks, big_tot = sized(512)
    yin, dout = call(
        partial(inner_kernel, nh),
        "inner",
        big_grid,
        [
            big_rows(wide),
            big_rows(LANES),
            big_lanes(8),
            big_lanes(16),
            whole((1, width)),
            big_rows(model),
            whole((width, model)),
        ],
        [
            (big_rows(width), sds((length, width), F32)),
            (big_rows(width), sds((length, width), BF16)),
        ],
        [],
        6e9,
        [acted, pack, seg_row, rowp, skip, cot_all, proj_out],
    )

    y, stat, full = call(
        partial(merge_kernel, nh, hops),
        "merge",
        big_grid,
        [
            big_rows(LANES),
            big_rows(LANES),
            big_tot,
            big_chunks(HDIM, width),
            big_chunks(HDIM, width),
            big_chunks(8, 2 * width),
            big_chunks(8, 2 * width),
            big_rows(width),
            big_rows(width),
            big_rows(width),
            whole((1, width)),
            whole(ex.shape),
        ]
        + [whole(message.shape)] * (2 * hops),
        [
            (big_rows(width), sds((length, width), BF16)),
            (big_lanes(8), sds((8, length), F32)),
            (big_chunks(HDIM, 2 * width), sds((nc, HDIM, 2 * width), BF16)),
        ],
        [pltpu.VMEM((HDIM, width), F32)] * 2,
        6e9,
        [acted, pack, tot, sf, rb, gpre, gsuf, yin, gate_in, dout, mg, ex] + ahead,
        scalars,
    )

    shares = [stat]
    for k in range(1, head_devices):
        shares.append(lax.ppermute(stat, "head", [(i, i ^ k) for i in range(head_devices)]))

    aside, outin, dy, dgate, gmix, gskip, gout, ggate = call(
        partial(turn_kernel, inner, head_devices),
        "turn",
        grid,
        [
            rows(width),
            rows(width),
            rows(width),
            whole((1, width)),
            rows(wide),
            whole((16, LANES)),
            rows(model),
            rows(model),
            whole((width, model)),
        ]
        + [lane_block(8, tb)] * head_devices,
        [
            (row_block(ASIDE, model), sds((head_devices * ASIDE, model), BF16)),
            (rows(width), sds((length, width), BF16)),
            (rows(width), sds((length, width), BF16)),
            (rows(width), sds((length, width), BF16)),
            (whole((8, width)), sds((8, width), F32)),
            (whole((8, width)), sds((8, width), F32)),
            (whole((width, model)), sds((width, model), BF16)),
            (whole((model, width)), sds((model, width), BF16)),
        ],
        [pltpu.VMEM((width, model), F32), pltpu.VMEM((model, width), F32)],
        4e9,
        [y, gate_in, dout, mg, acted, eye, normed, cot_all, proj_out] + shares,
    )
    outs = call(
        partial(adjoint_kernel, nh, head_devices, hops, own),
        "adjoint",
        grid,
        [
            rows(LANES),
            rows(LANES),
            tot_block,
            whole(gates_of.shape),
            whole((8, 2 * width)),
            whole(ex.shape),
            rows(width),
            rows(width),
            whole((width, model)),
        ],
        [(whole((own - ASIDE, model)), sds((own - ASIDE, model), BF16))] * head_devices
        + [
            (whole(states.shape), states),
            (state_block, states),
        ]
        + messages,
        [
            pltpu.VMEM((HDIM, width), F32),
            pltpu.VMEM((nc, HDIM, width), F32),
            pltpu.VMEM((tb, 2 * LANES), BF16),
            pltpu.VMEM((tb, 2 * LANES), F32),
            pltpu.VMEM((per * HDIM, LANES), BF16),
        ],
        1e8,
        [acted, pack, tot, gates, gtot, ex, dy, outin, proj_out],
        scalars,
    )
    mixers = outs[:head_devices]
    dso, dro, *behind = outs[head_devices:]

    grad_proj_out, grad_proj_gate = lax.psum((gout, ggate), "seq")
    aside = lax.psum_scatter(aside, "head", scatter_dimension=0, tiled=True)
    behind = exchange_sides(behind, hops)
    mixer_shares = [mixers[0]] + [swap(mixers[k], "head", k) for k in range(1, head_devices)]

    mid_grid, mid_rows, mid_lanes, *_ = sized(256)
    dxin, dbc, pulls = call(
        partial(mid_kernel, nh),
        "mid",
        mid_grid,
        [
            mid_rows(wide),
            mid_rows(LANES),
            mid_lanes(8),
            mid_lanes(16),
            mid_rows(width),
            whole((16, LANES)),
        ],
        [
            (mid_rows(width), sds((length, width), BF16)),
            (mid_rows(LANES), sds((length, LANES), F32)),
            (mid_rows(LANES), sds((length, LANES), F32)),
        ],
        [pltpu.VMEM((16, SPAN), F32), pltpu.VMEM((nh, 4 * SPAN, LANES), BF16)],
        1e8,
        [acted, pack, seg_row, rowa, dy, eye16],
    )

    back = lambda i: grid - 1 - i

    def rev(spec):
        return pl.BlockSpec(spec.block_shape, lambda i, *_: spec.index_map(back(i)))

    mine, theirs, *chunks = call(
        partial(back_kernel, nh, peers, hops, own),
        "back",
        grid,
        [
            rev(rows(wide)),
            rev(rows(wide)),
            rev(rows(LANES)),
            rev(tot_block),
            rev(rows(width)),
            rev(chunk_block(per, HDIM, 2 * width)),
            rev(state_block),
            rev(state_block),
            rev(gate_block),
            rev(gate_block),
            rev(gate_block),
            rev(rows(width)),
            rev(rows(LANES)),
            rev(rows(LANES)),
            rev(rows(wide)),
            whole((8, wide)),
            whole((8, LANES)),
            whole((4, wide)),
            whole((1, width)),
            whole((2, LANES)),
            whole(ex.shape),
            whole(ext.shape),
            whole(tril.shape),
            whole(triu_wide.shape),
            rev(rows(model)),
            whole((8, model)),
            rev(rows(width)),
            whole((model, width)),
            whole((model, LANES + wide)),
            whole((8, width)),
            whole((8, width)),
        ]
        + [whole(message.shape)] * (2 * hops),
        [
            (side_block(0), sds((head_devices // 2, own, model), BF16)),
            (side_block(1), sds((head_devices // 2, own, model), BF16)),
        ]
        + [(whole((size, LANES + wide)), sds((size, LANES + wide), BF16))] * peers,
        [
            pltpu.VMEM((tb + 8, wide), F32),
            pltpu.VMEM((16, wide), F32),
            pltpu.VMEM((tb, LANES + wide), BF16),
            pltpu.VMEM((model, LANES + wide), F32),
            pltpu.VMEM((16, model), F32),
            pltpu.VMEM((HDIM, width), F32),
            pltpu.VMEM((HDIM, width), F32),
            pltpu.VMEM((tb, model), BF16),
            pltpu.VMEM((2 * tb, 2 * LANES), BF16),
            pltpu.VMEM((2 * tb, 2 * LANES), F32),
            pltpu.VMEM((2 * tb + 16 * per, 4 * LANES), BF16),
            pltpu.VMEM((2 * tb + 16 * per, LANES), F32),
        ],
        1e8,
        [
            acted,
            slope,
            pack,
            tot,
            dy,
            full,
            dso,
            dro,
            gsuf,
            gpre,
            gates,
            dxin,
            dbc,
            pulls,
            uv,
            uvh,
            halo_cols,
            taps,
            skip,
            pcol,
            ex,
            ext,
            tril,
            triu_wide,
            normed,
            normh,
            dgate,
            proj_gate,
            wcat,
            gmix,
            gskip,
        ]
        + behind,
        scalars,
    )

    chunks, theirs, mixer_shares = lax.optimization_barrier((chunks, theirs, mixer_shares))
    got = swap(theirs, "head", 1)
    summed = chunks[0].astype(F32)
    for k in range(1, peers):
        summed = summed + swap(chunks[k], "seq", k).astype(F32)
    shared = summed[:, : 2 * LANES]
    row_at = seq_index * size + jnp.arange(size)[:, None]
    lane_at = jnp.arange(2 * LANES)[None, :]
    common = (lane_at == 16) | (lane_at > 26)
    common = common | ((lane_at > 16) & (lane_at < 21) & (row_at < LANES))
    shared = jnp.where(common, sum_over(shared, "head"), shared)

    half = head_devices // 4
    own_in = mine[:half].astype(F32) + got[:half].astype(F32)
    going = (mine[half:].astype(F32) + got[half:].astype(F32)).astype(BF16)
    for b in range(1, bits):
        if b == 1:
            going, shared = lax.optimization_barrier((going, shared))
        got = swap(going, "head", 1 << b)
        if b < bits - 1:
            half = half // 2
            going = (own_in[half:] + got[half:].astype(F32)).astype(BF16)
            own_in = own_in[:half] + got[:half].astype(F32)

    reduced = jnp.concatenate([shared, summed[:, 2 * LANES :]], axis=1).astype(BF16)
    reduced, grad_proj_out, grad_proj_gate, mixer_shares = lax.optimization_barrier(
        (reduced, grad_proj_out, grad_proj_gate, mixer_shares)
    )
    spread_out = [reduced] + [swap(reduced, "seq", k) for k in range(1, peers)]
    grad_proj_out = grad_proj_out[:real_width].astype(F32)
    grad_proj_gate = grad_proj_gate[:, :real_width].astype(F32)
    mixer = sum(share.astype(F32) for share in mixer_shares)
    mixer = jnp.concatenate([aside.astype(F32), mixer], axis=0)
    layer_out = (tokens.astype(F32) + mixer).astype(BF16)
    spread_out, layer_out, grad_proj_out, grad_proj_gate = lax.optimization_barrier(
        (spread_out, layer_out, grad_proj_out, grad_proj_gate)
    )

    finals = [
        sds((model,), F32),
        sds((model, real_width), F32),
        sds((model, LANES), F32),
        sds((real_heads, 2, model), F32),
        sds((2, real_heads), F32),
        sds((1, real_heads), F32),
        sds((4, real_width), F32),
        sds((4, LANES), F32),
        sds((1, real_heads), F32),
        sds((real_width,), F32),
        sds((own, model), BF16),
    ]
    ggain, gvalue, gstate, gstep, gbias, gdecay, gconvv, gconvs, gskips, gmixer, grad_tokens = call(
        partial(finish_kernel, nh, peers, head_devices),
        "finish",
        1,
        [whole((size, LANES + wide))] * peers
        + [whole((32, LANES)), whole((1, model))]
        + [whole((own, model))] * 2
        + [whole((1, own, model))] * 2,
        [(whole(f.shape), f) for f in finals],
        [pltpu.VMEM((model, LANES), F32)],
        3e9,
        spread_out
        + [picked, input_gain[None, :]]
        + [tokens, cotangent, own_in, got],
        scalars,
    )
    return (
        layer_out,
        grad_tokens,
        ggain,
        grad_proj_gate,
        gvalue,
        gstate,
        jnp.transpose(gstep, (1, 2, 0)),
        gbias,
        gdecay[0],
        gconvv,
        gconvs,
        gskips[0],
        gmixer,
        grad_proj_out,
    )


def solution(mesh):
    return jax.shard_map(
        per_device,
        mesh=mesh,
        in_specs=(
            P(("seq", "head"), None),
            P(),
            P(None, "head"),
            P(None, "head"),
            P(),
            P(None, None, "head"),
            P(None, "head"),
            P("head"),
            P(None, "head"),
            P(),
            P("head"),
            P("head"),
            P("head", None),
            P(),
            P("seq"),
            P(("seq", "head"), None),
        ),
        out_specs=(
            P(("seq", "head"), None),
            P(("seq", "head"), None),
            P(),
            P(None, "head"),
            P(None, "head"),
            P(),
            P(None, None, "head"),
            P(None, "head"),
            P("head"),
            P(None, "head"),
            P(),
            P("head"),
            P("head"),
            P("head", None),
        ),
        check_vma=False,
    )
```

```python
from functools import partial

import jax
import jax.numpy as jnp
import numpy as np
from jax import lax
from jax.experimental import pallas as pl
from jax.experimental.pallas import tpu as pltpu
from jax.sharding import PartitionSpec as P

SPAN = 128
HDIM = 64
LANES = 128
LONGEST = 4096
EPSILON = 1e-05
TINY = 1e-30
F32 = jnp.float32
BF16 = jnp.bfloat16
BLOCK = 512
ASIDE = 256


def mm(a, b):
    return jnp.dot(a, b, preferred_element_type=F32)


def mm_nt(a, b):
    return lax.dot_general(a, b, (((1,), (1,)), ((), ())), preferred_element_type=F32)


def mm_tn(a, b):
    return lax.dot_general(a, b, (((0,), (0,)), ((), ())), preferred_element_type=F32)


def pieces(v):
    high = v.astype(BF16)
    rest = v - high.astype(F32)
    mid = rest.astype(BF16)
    return high, mid, (rest - mid.astype(F32)).astype(BF16)


def exact_tn(a, b):
    return lax.dot_general(
        a, b, (((0,), (0,)), ((), ())), precision=lax.Precision.HIGHEST, preferred_element_type=F32
    )


def split(v, axis):
    high = v.astype(BF16)
    return jnp.concatenate([high, (v - high.astype(F32)).astype(BF16)], axis=axis)


def sigmoid(v):
    return 1.0 / (1.0 + jnp.exp(-v))


def softplus(v):
    return jnp.maximum(v, 0.0) + jnp.log1p(jnp.exp(-jnp.abs(v)))


def iota(shape, dim):
    return lax.broadcasted_iota(jnp.int32, shape, dim)


def wide_tiles(width):
    return [slice(at, min(at + 2 * LANES, width)) for at in range(0, width, 2 * LANES)]


def groups(width):
    return [(n, n * LANES, (2 * n, 2 * n + 1)) for n in range(width // LANES)]


def sides(v, width):
    tiles = [v[:, at : at + LANES] for at in range(0, 2 * width, LANES)]
    return jnp.concatenate(tiles[::2], axis=1), jnp.concatenate(tiles[1::2], axis=1)


def stacked(v):
    first = iota(v.shape, 1) < HDIM
    zero = jnp.zeros_like(v)
    return jnp.concatenate([jnp.where(first, v, zero), jnp.where(first, zero, v)], axis=0)


def source_weights(pack, tot, dt, lane, nh):
    forward = lane < nh
    gap = jnp.where(forward, tot - pack, pack)
    kept = jnp.where(forward, pack[:, 38:39], pack[:, 40:41])
    return jnp.where(lane < 16, jnp.exp(jnp.where(lane < 16, gap, 0.0)) * kept * dt, 0.0)


def target_weights(pack, tot, lane, nh):
    forward = lane < nh
    gap = jnp.where(forward, pack, tot - pack)
    kept = jnp.where(forward, pack[:, 37:38], pack[:, 39:40])
    return jnp.where(lane < 16, jnp.exp(jnp.where(lane < 16, gap, 0.0)) * kept, 0.0)


def send_sides(at_ref, hops, up, down, refs):
    for d in range(1, hops + 1):
        low = (at_ref[0] // d) % 2 == 0
        refs[2 * d - 2][...] = jnp.where(low, up, down)
        refs[2 * d - 1][...] = jnp.where(low, down, up)


def land_sides(at_ref, hops, refs, from_earlier, from_later):
    for d in range(hops, 0, -1):
        low = (at_ref[0] // d) % 2 == 0
        first, second = refs[2 * d - 2][...], refs[2 * d - 1][...]
        for state, part in (
            (from_earlier, jnp.where(low, second, first)),
            (from_later, jnp.where(low, first, second)),
        ):
            if d == hops:
                state[...] = part[:HDIM]
            else:
                state[...] = part[:HDIM] + part[HDIM : HDIM + 1] * state[...]


def documents(off_ref, places):
    count = jnp.zeros(places.shape, F32)
    for at in range(0, off_ref.shape[1], LANES):
        begun = off_ref[0:1, at : at + LANES] <= places
        count = count + jnp.sum(jnp.where(begun, 1.0, 0.0), axis=1, keepdims=True)
    return count


def front_kernel(
    nh,
    hops,
    shares,
    own,
    at_ref,
    *refs,
):
    front_body(nh, hops, own, at_ref, refs[:shares], *refs[shares:])


def front_body(
    nh,
    hops,
    own,
    at_ref,
    x_refs,
    halo_ref,
    gain_ref,
    wg_ref,
    ws_ref,
    wv_ref,
    wst_ref,
    wstr_ref,
    pcol_ref,
    prow_ref,
    taps_ref,
    off_ref,
    live_ref,
    ex_ref,
    tril_ref,
    triu_ref,
    normed_ref,
    normh_ref,
    gate_ref,
    act_ref,
    slope_ref,
    uv_ref,
    uvh_ref,
    pack_ref,
    rowa_ref,
    rowp_ref,
    segrow_ref,
    halocols_ref,
    tot_ref,
    sf_ref,
    rb_ref,
    gates_ref,
    gpre_ref,
    gsuf_ref,
    gtot_ref,
    *rest,
):
    messages = rest[: 2 * hops]
    ubuf, state, incb, marks, ends, docs, wbuf, wides, bts = rest[2 * hops :]
    i = pl.program_id(0)
    tb = normed_ref.shape[0]
    per = tb // SPAN
    nc = rb_ref.shape[0]
    width = gate_ref.shape[1]
    piece = i * tb // own ^ at_ref[1]

    def norm(x):
        xf = x.astype(F32)
        s = lax.rsqrt(jnp.mean(xf * xf, axis=1, keepdims=True) + EPSILON)
        return (xf * s * gain_ref[0:1, :]).astype(BF16)

    @pl.when(i == 0)
    def _():
        edge = norm(halo_ref[...])
        normh_ref[...] = edge
        ubuf[0:8, :LANES] = mm(edge, ws_ref[...])
        ubuf[0:8, LANES:] = mm(edge, wv_ref[...])
        uvh_ref[...] = ubuf[0:8, :]
        state[...] = jnp.zeros_like(state)
        place = at_ref[2] - 8 + iota((8, 1), 0)
        here = documents(off_ref, place)
        lane8 = iota((8, LANES), 1)
        halo = jnp.zeros((8, LANES), F32)
        for k in (1, 2, 3):
            same = jnp.where(documents(off_ref, place + k) == here, 1.0, 0.0)
            halo = jnp.where(lane8 == k - 1, same, halo)
        halocols_ref[...] = halo

    @pl.when(i > 0)
    def _():
        ubuf[0:8, :] = ubuf[tb : tb + 8, :]

    for at in range(0, tb, 64):
        x = x_refs[0][at : at + 64, :]
        for k in range(1, len(x_refs)):
            x = jnp.where(piece == k, x_refs[k][at : at + 64, :], x)
        normed_ref[at : at + 64, :] = norm(x)
    nb = normed_ref[...]
    for tile in wide_tiles(width):
        gate_ref[:, tile] = mm(nb, wg_ref[:, tile]).astype(BF16)
    uv = mm(nb, ws_ref[...])
    ubuf[8 : 8 + tb, :LANES] = uv
    uv_ref[:, :LANES] = uv.astype(BF16)
    for tile in wide_tiles(width):
        uv = mm(nb, wv_ref[:, tile])
        at = slice(LANES + tile.start, LANES + tile.stop)
        ubuf[8 : 8 + tb, at] = uv
        uv_ref[:, at] = uv.astype(BF16)
    zr_all = mm_nt(wstr_ref[...], nb)
    lane = iota((SPAN, LANES), 1)
    forward = lane < nh
    forward_row = iota((16, SPAN), 0) < nh
    gate_lane = iota((8, LANES), 1) < nh
    for j in range(per):
        rows = slice(j * SPAN, (j + 1) * SPAN)
        base = at_ref[2] + (i * per + j) * SPAN
        around = documents(off_ref, base - 8 + iota((SPAN + 16, 1), 0))
        docs[...] = jnp.broadcast_to(around, docs.shape)
        seg = docs[8 : 8 + SPAN, :]
        prev_last, first = docs[7:8, :], docs[8:9, :]
        last, next_first = docs[7 + SPAN : 8 + SPAN, :], docs[8 + SPAN : 9 + SPAN, :]
        live = jnp.transpose(jnp.broadcast_to(live_ref[0:1, rows], (SPAN, SPAN)).astype(F32))
        mark = jnp.where(lane == 35, live, jnp.where(lane == 36, seg, 0.0))
        for k in (1, 2, 3):
            same = jnp.where(docs[8 - k : 8 - k + SPAN, :] == seg, 1.0, 0.0)
            mark = jnp.where(lane == 31 + k, same, mark)
            same = jnp.where(docs[8 + k : 8 + k + SPAN, :] == seg, 1.0, 0.0)
            mark = jnp.where(lane == 40 + k, same, mark)
        for k, bound in enumerate((prev_last, last, next_first, first)):
            mark = jnp.where(lane == 37 + k, jnp.where(seg == bound, 1.0, 0.0), mark)
        marks[rows, :] = mark
        opened = jnp.where(gate_lane, last - prev_last, next_first - first)
        ends[j * 8 : j * 8 + 8, :] = jnp.where(opened == 0.0, 1.0, 0.0)
        segrow_ref[:, rows] = jnp.transpose(seg)[:8]
    for at in range(0, LANES + width, LANES):
        tile = slice(at, at + LANES)
        for j in range(per):
            rows = slice(j * SPAN, (j + 1) * SPAN)
            keep = marks[rows, :]
            conv = taps_ref[0:1, tile] * ubuf[8 + j * SPAN : 8 + (j + 1) * SPAN, tile]
            for k in (1, 2, 3):
                moved = ubuf[8 - k + j * SPAN : 8 - k + (j + 1) * SPAN, tile]
                conv = conv + taps_ref[k : k + 1, tile] * moved * keep[:, 31 + k : 32 + k]
            sig = sigmoid(conv)
            live = keep[:, 35:36]
            act_ref[rows, tile] = (conv * sig * live).astype(BF16)
            slope_ref[rows, tile] = (live * sig * (1.0 + conv * (1.0 - sig))).astype(BF16)
    z_all = mm(nb, wst_ref[...])
    for j in range(per):
        rows = slice(j * SPAN, (j + 1) * SPAN)
        z = z_all[rows] + pcol_ref[0:1, :]
        dt = softplus(z)
        a = -dt * pcol_ref[1:2, :]
        total = mm(tril_ref[...], jnp.concatenate(pieces(a), axis=0))
        tot = total[SPAN - 1 : SPAN, :]
        cc = jnp.where(forward, total, total - a)
        pack = jnp.where(lane < 16, cc, jnp.where(lane < 32, z, marks[rows, :]))
        pack_ref[rows, :] = pack
        tot8 = jnp.broadcast_to(tot, (8, LANES))
        tot_ref[j * 8 : j * 8 + 8, :] = tot8
        dtr = softplus(zr_all[:, rows] + prow_ref[:, 0:1])
        ar = -dtr * prow_ref[:, 1:2]
        run = mm(jnp.concatenate(pieces(ar), axis=1), triu_ref[...])
        rowa = jnp.where(forward_row, run, run - ar)
        ldt = jnp.log(jnp.maximum(dtr, TINY))
        rowa_ref[:, rows] = rowa
        rowp_ref[:, rows] = jnp.where(forward_row, rowa - ldt, rowa + ldt)
        gate8 = jnp.exp(tot8) * ends[j * 8 : j * 8 + 8, :]
        bts[j * HDIM : (j + 1) * HDIM, :] = jnp.transpose(act_ref[rows, :LANES].astype(F32))[
            :HDIM
        ].astype(BF16)
        wbuf[rows, :] = split(source_weights(pack, tot, dt, lane, nh), 1)
        wbuf[tb + 16 * j : tb + 16 * j + 16, :] = split(jnp.concatenate([gate8, gate8], axis=0), 1)
    for n, at, _ in groups(width):
        tile = slice(at, at + LANES)
        both = slice(2 * at, 2 * at + 2 * LANES)
        wides[...] = mm(wbuf[...], ex_ref[:, both])
        for j in range(per):
            rows = slice(j * SPAN, (j + 1) * SPAN)
            c = i * per + j
            x = act_ref[rows, LANES + at : 2 * LANES + at].astype(F32)
            fed = jnp.concatenate(
                [
                    (x * wides[rows, :LANES]).astype(BF16),
                    (x * wides[rows, LANES:]).astype(BF16),
                ],
                axis=1,
            )
            bt = bts[j * HDIM : (j + 1) * HDIM, :]
            inc = mm(bt, fed)
            gate = wides[tb + 16 * j : tb + 16 * j + 8, :]
            gates_ref[c, :, both] = gate
            sf_ref[j, :, tile] = state[:, tile]
            state[:, tile] = state[:, tile] * gate[0:1, :LANES] + inc[:, :LANES]
            incb[c, :, tile] = inc[:, LANES:]
    @pl.when(i == pl.num_programs(0) - 1)
    def _():
        last_state = state[...]
        one = jnp.ones(gates_ref.shape[1:], F32)

        def up(c, p):
            gpre_ref[c] = p
            return p * gates_ref[c]

        p = lax.fori_loop(0, nc, up, one)
        tot_f, tot_b = sides(p, width)
        gtot_ref[:, :width] = tot_f
        gtot_ref[:, width:] = tot_b
        state[...] = jnp.zeros_like(state)

        def down(k, p):
            c = nc - 1 - k
            gsuf_ref[c] = p
            rb_ref[c] = state[...]
            gate = gates_ref[c]
            for n, at, _ in groups(width):
                tile = slice(at, at + LANES)
                second = slice(2 * at + LANES, 2 * at + 2 * LANES)
                state[:, tile] = state[:, tile] * gate[0:1, second] + incb[c, :, tile]
            return p * gate

        lax.fori_loop(0, nc, down, one)
        send_sides(
            at_ref,
            hops,
            jnp.concatenate([last_state, tot_f], axis=0),
            jnp.concatenate([state[...], tot_b], axis=0),
            messages,
        )


def inner_kernel(
    nh,
    act_ref,
    pack_ref,
    segrow_ref,
    rowp_ref,
    skip_ref,
    cot_ref,
    wo_ref,
    y_ref,
    dout_ref,
):
    tb, width = y_ref.shape
    for tile in wide_tiles(width):
        dout_ref[:, tile] = mm_nt(cot_ref[...], wo_ref[tile, :]).astype(BF16)
    t_at = iota((SPAN, SPAN), 0)
    s_at = iota((SPAN, SPAN), 1)
    lower = t_at > s_at
    for j in range(tb // SPAN):
        rows = slice(j * SPAN, (j + 1) * SPAN)
        bc = act_ref[rows, :LANES].astype(F32)
        b = bc[:, :HDIM].astype(BF16)
        c = pltpu.roll(bc, HDIM, 1)[:, :HDIM].astype(BF16)
        pack = pack_ref[rows, :]
        within = (pack[:, 36:37] == segrow_ref[0:1, rows]) & (t_at != s_at)
        score = jnp.where(within, mm_nt(c, b), 0.0)
        for n, at, heads in groups(width):
            tile = slice(at, at + LANES)
            mats = []
            for h in heads:
                gap = jnp.where(
                    lower,
                    pack[:, h : h + 1] - rowp_ref[h : h + 1, rows],
                    rowp_ref[nh + h : nh + h + 1, rows] - pack[:, nh + h : nh + h + 1],
                )
                mats.append((score * jnp.exp(gap)).astype(BF16))
            xp = act_ref[rows, LANES + at : 2 * LANES + at]
            y = mm(jnp.concatenate(mats, axis=1), stacked(xp))
            y_ref[rows, tile] = y + skip_ref[0:1, tile] * xp.astype(F32)


def merge_kernel(
    nh,
    hops,
    at_ref,
    bc_ref,
    pack_ref,
    tot_ref,
    sf_ref,
    rb_ref,
    gpre_ref,
    gsuf_ref,
    yin_ref,
    gate_ref,
    dout_ref,
    mg_ref,
    ex_ref,
    *rest,
):
    arrived = rest[: 2 * hops]
    y_ref, stat_ref, full_ref, sent_ref, rent_ref = rest[2 * hops :]
    tb, width = y_ref.shape

    @pl.when(pl.program_id(0) == 0)
    def _():
        land_sides(at_ref, hops, arrived, sent_ref, rent_ref)

    lane = iota((SPAN, LANES), 1)
    row8 = iota((8, SPAN), 0)
    for j in range(tb // SPAN):
        rows = slice(j * SPAN, (j + 1) * SPAN)
        pack = pack_ref[rows, :]
        bc = bc_ref[rows, :].astype(F32)
        c = pltpu.roll(bc, HDIM, 1)[:, :HDIM].astype(BF16)
        w = split(target_weights(pack, tot_ref[j * 8 : j * 8 + 1, :], lane, nh), 1)
        energy = jnp.zeros((SPAN, LANES), F32)
        cross = jnp.zeros((SPAN, LANES), F32)
        for n, at, _ in groups(width):
            tile = slice(at, at + LANES)
            both = slice(2 * at, 2 * at + 2 * LANES)
            second = slice(2 * at + LANES, 2 * at + 2 * LANES)
            first = slice(2 * at, 2 * at + LANES)
            sfull = sf_ref[j, :, tile] + gpre_ref[j, 0:1, first] * sent_ref[:, tile]
            rfull = rb_ref[j, :, tile] + gsuf_ref[j, 0:1, second] * rent_ref[:, tile]
            held = jnp.concatenate([sfull.astype(BF16), rfull.astype(BF16)], axis=1)
            full_ref[j, :, both] = held
            seen = mm(c, held) * mm(w, ex_ref[:, both])
            y = (yin_ref[rows, tile] + seen[:, :LANES] + seen[:, LANES:]).astype(BF16)
            y_ref[rows, tile] = y
            gate = gate_ref[rows, tile].astype(F32)
            g = y.astype(F32) * gate * sigmoid(gate)
            energy = energy + g * g
            cross = cross + dout_ref[rows, tile].astype(F32) * mg_ref[0:1, tile] * g
        energy = jnp.sum(jnp.transpose(energy), axis=0, keepdims=True)
        cross = jnp.sum(jnp.transpose(cross), axis=0, keepdims=True)
        stat_ref[:, rows] = jnp.where(row8 == 0, energy, jnp.where(row8 == 1, cross, 0.0))


def turn_kernel(
    inner,
    shares,
    y_ref,
    gate_ref,
    dout_ref,
    mg_ref,
    act_ref,
    eye_ref,
    normed_ref,
    cot_ref,
    wo_ref,
    *rest,
):
    stats_in = rest[:shares]
    (
        aside_ref,
        outin_ref,
        dy_ref,
        dgate_ref,
        gmix_ref,
        gskip_ref,
        gout_ref,
        ggate_ref,
        gout,
        ggate,
    ) = rest[shares:]
    i = pl.program_id(0)
    tb, width = y_ref.shape
    model = normed_ref.shape[1]

    @pl.when(i == 0)
    def _():
        gmix_ref[...] = jnp.zeros_like(gmix_ref)
        gskip_ref[...] = jnp.zeros_like(gskip_ref)
        gout[...] = jnp.zeros_like(gout)
        ggate[...] = jnp.zeros_like(ggate)

    for j in range(tb // SPAN):
        rows = slice(j * SPAN, (j + 1) * SPAN)
        stat = stats_in[0][:, rows]
        for more in stats_in[1:]:
            stat = stat + more[:, rows]
        stat = exact_tn(stat, eye_ref[0:8, :])
        q = lax.rsqrt(stat[:, 0:1] * (1.0 / inner) + EPSILON)
        k3 = q * q * q * stat[:, 1:2] * (1.0 / inner)
        for n, at, _ in groups(width):
            tile = slice(at, at + LANES)
            y = y_ref[rows, tile].astype(F32)
            gate = gate_ref[rows, tile].astype(F32)
            sig = sigmoid(gate)
            sg = gate * sig
            g = y * sg
            gq = g * q
            dout = dout_ref[rows, tile].astype(F32)
            mg = mg_ref[0:1, tile]
            outin_ref[rows, tile] = (gq * mg).astype(BF16)
            gmix_ref[0:1, tile] += jnp.sum(dout * gq, axis=0, keepdims=True)
            dg = dout * mg * q - g * k3
            dyb = (dg * sg).astype(BF16)
            dy_ref[rows, tile] = dyb
            dgate_ref[rows, tile] = (dg * y * (sig + sg * (1.0 - sig))).astype(BF16)
            x = act_ref[rows, LANES + at : 2 * LANES + at].astype(F32)
            gskip_ref[0:1, tile] += jnp.sum(dyb.astype(F32) * x, axis=0, keepdims=True)

    for tile in wide_tiles(model):
        aside_ref[:, tile] = mm(outin_ref[:ASIDE, :], wo_ref[:, tile]).astype(BF16)
    for at in range(0, width, LANES):
        tile = slice(at, at + LANES)
        gout[tile, :] += mm_tn(outin_ref[:, tile], cot_ref[...])
    for at in range(0, model, LANES):
        tile = slice(at, at + LANES)
        ggate[tile, :] += mm_tn(normed_ref[:, tile], dgate_ref[...])

    @pl.when(i == pl.num_programs(0) - 1)
    def _():
        gout_ref[...] = gout[...].astype(BF16)
        ggate_ref[...] = ggate[...].astype(BF16)


def adjoint_kernel(
    nh,
    shares,
    hops,
    own,
    at_ref,
    act_ref,
    pack_ref,
    tot_ref,
    gates_ref,
    gtot_ref,
    ex_ref,
    dy_ref,
    outin_ref,
    wo_ref,
    *rest,
):
    pieces_out = rest[:shares]
    dso_ref, dro_ref, *messages, state, incf, wbuf, wides, cts = rest[shares:]
    i = pl.program_id(0)
    tb, width = dy_ref.shape
    model = wo_ref.shape[1]
    per = tb // SPAN
    nc = dso_ref.shape[0]
    lane = iota((SPAN, LANES), 1)

    @pl.when(i == 0)
    def _():
        state[...] = jnp.zeros_like(state)

    for j in range(per):
        rows = slice(j * SPAN, (j + 1) * SPAN)
        pack = pack_ref[rows, :]
        tot = tot_ref[j * 8 : j * 8 + 1, :]
        wbuf[rows, :] = split(target_weights(pack, tot, lane, nh), 1)
        cts[j * HDIM : (j + 1) * HDIM, :] = jnp.transpose(act_ref[rows, :].astype(F32))[
            HDIM:
        ].astype(BF16)
    for n, at, _ in groups(width):
        tile = slice(at, at + LANES)
        both = slice(2 * at, 2 * at + 2 * LANES)
        second = slice(2 * at + LANES, 2 * at + 2 * LANES)
        wides[...] = mm(wbuf[...], ex_ref[:, both])
        for j in range(per):
            rows = slice(j * SPAN, (j + 1) * SPAN)
            c = i * per + j
            dy = dy_ref[rows, tile].astype(F32)
            fed = jnp.concatenate(
                [
                    (dy * wides[rows, :LANES]).astype(BF16),
                    (dy * wides[rows, LANES:]).astype(BF16),
                ],
                axis=1,
            )
            inc = mm(cts[j * HDIM : (j + 1) * HDIM, :], fed)
            incf[c, :, tile] = inc[:, :LANES]
            dro_ref[j, :, tile] = state[:, tile]
            state[:, tile] = state[:, tile] * gates_ref[c, 0:1, second] + inc[:, LANES:]

    for k in range(shares):

        @pl.when((i * tb // own ^ at_ref[1]) == k)
        def _():
            for tile in wide_tiles(model):
                pieces_out[k][:, tile] = mm(outin_ref[ASIDE:, :], wo_ref[:, tile]).astype(BF16)

    @pl.when(i == pl.num_programs(0) - 1)
    def _():
        last_state = state[...]
        state[...] = jnp.zeros_like(state)

        def down(k, _):
            c = nc - 1 - k
            dso_ref[c] = state[...]
            for n, at, _ in groups(width):
                tile = slice(at, at + LANES)
                first = slice(2 * at, 2 * at + LANES)
                state[:, tile] = state[:, tile] * gates_ref[c, 0:1, first] + incf[c, :, tile]
            return 0

        lax.fori_loop(0, nc, down, 0)
        send_sides(
            at_ref,
            hops,
            jnp.concatenate([last_state, gtot_ref[:, width:]], axis=0),
            jnp.concatenate([state[...], gtot_ref[:, :width]], axis=0),
            messages,
        )


def mid_kernel(
    nh,
    act_ref,
    pack_ref,
    segrow_ref,
    rowa_ref,
    dy_ref,
    eye_ref,
    dx_ref,
    dbc_ref,
    pulls_ref,
    qbuf,
    places,
):
    tb, width = dx_ref.shape

    @pl.when(pl.program_id(0) == 0)
    def _():
        qbuf[...] = jnp.zeros_like(qbuf)
        spot_row = iota((4 * SPAN, LANES), 0) < 2 * SPAN
        spot_lane = iota((4 * SPAN, LANES), 1)
        for h in range(nh):
            up = jnp.where(spot_lane == nh + h, jnp.where(spot_row, -1.0, 1.0), 0.0)
            places[h] = jnp.where(spot_row & (spot_lane == h), 1.0, up).astype(BF16)

    s_at = iota((SPAN, SPAN), 0)
    t_at = iota((SPAN, SPAN), 1)
    lower = t_at > s_at
    lane = iota((SPAN, LANES), 1)
    front_half = lane < HDIM
    for j in range(tb // SPAN):
        rows = slice(j * SPAN, (j + 1) * SPAN)
        pack = pack_ref[rows, :]
        bc = act_ref[rows, :LANES].astype(F32)
        cb = pltpu.roll(bc, HDIM, 1)
        within = (pack[:, 36:37] == segrow_ref[0:1, rows]) & (t_at != s_at)
        score = mm_nt(bc[:, :HDIM].astype(BF16), cb[:, :HDIM].astype(BF16))
        score = jnp.where(within, score, 0.0)
        ldt = jnp.log(jnp.maximum(softplus(pltpu.roll(pack, LANES - 16, 1)), TINY))
        pc = jnp.where(lane < nh, pack - ldt, pack + ldt)
        dscore = jnp.zeros((SPAN, SPAN), F32)
        kc = jnp.zeros((SPAN, LANES), F32)
        for n, at, heads in groups(width):
            tile = slice(at, at + LANES)
            dyp = dy_ref[rows, tile]
            dmats = mm_nt(stacked(act_ref[rows, LANES + at : 2 * LANES + at]), dyp)
            mats = []
            for m, h in enumerate(heads):
                decay = jnp.exp(
                    jnp.where(
                        lower,
                        rowa_ref[h : h + 1, rows] - pc[:, h : h + 1],
                        pc[:, nh + h : nh + h + 1] - rowa_ref[nh + h : nh + h + 1, rows],
                    )
                )
                spot = dmats[m * SPAN : (m + 1) * SPAN, :] * decay
                dscore = dscore + spot
                mats.append((score * decay).astype(BF16))
                pull = spot * score
                pull_low = jnp.where(lower, pull, 0.0)
                down = jnp.sum(pull_low, axis=0, keepdims=True)
                qbuf[h : h + 1, :] = down
                qbuf[nh + h : nh + h + 1, :] = jnp.sum(pull, axis=0, keepdims=True) - down
                both = jnp.concatenate([split(pull_low, 1), split(pull, 1)], axis=1)
                kc = kc + mm(both, places[h])
            dx_ref[rows, tile] = mm(jnp.concatenate(mats, axis=1), stacked(dyp)).astype(BF16)
        dscore = jnp.where(within, dscore, 0.0).astype(BF16)
        cpad = jnp.where(front_half, cb, 0.0).astype(BF16)
        bpad = jnp.where(front_half, 0.0, cb).astype(BF16)
        dbc_ref[rows, :] = mm(dscore, cpad) + mm_tn(dscore, bpad)
        pulls_ref[rows, :] = kc + exact_tn(qbuf[...], eye_ref[...])


def back_kernel(
    nh,
    peers,
    hops,
    own,
    at_ref,
    act_ref,
    slope_ref,
    pack_ref,
    tot_ref,
    dy_ref,
    full_ref,
    dso_ref,
    dro_ref,
    gsuf_ref,
    gpre_ref,
    gates_ref,
    dxin_ref,
    dbc_ref,
    pulls_ref,
    uv_ref,
    uvh_ref,
    halocols_ref,
    taps_ref,
    skip_ref,
    pcol_ref,
    ex_ref,
    ext_ref,
    tril_ref,
    triu_ref,
    normed_ref,
    normh_ref,
    dgate_ref,
    wg_ref,
    wcat_ref,
    gmix_ref,
    gskip_ref,
    *rest,
):
    arrived = rest[: 2 * hops]
    mine_ref, theirs_ref, *chunks = rest[2 * hops : 2 * hops + 2 + peers]
    scratch = rest[2 * hops + 2 + peers :]
    dbuf, hbuf, dcat, acc, lines, dsent_ref, drent_ref, parts, wbuf, wides, pbuf, sums = scratch
    i = pl.program_id(0)
    last = pl.num_programs(0) - 1
    tb = act_ref.shape[0]
    width = act_ref.shape[1] - LANES
    model = normed_ref.shape[1]

    @pl.when(i == 0)
    def _():
        dbuf[tb : tb + 8, :] = jnp.zeros((8, LANES + width), F32)
        acc[...] = jnp.zeros_like(acc)
        lines[...] = jnp.zeros_like(lines)
        land_sides(at_ref, hops, arrived, drent_ref, dsent_ref)

    lane = iota((SPAN, LANES), 1)
    forward = lane < nh
    head_lane = lane < 16
    none = jnp.zeros((HDIM, 2 * LANES), BF16)
    per = tb // SPAN
    pair = 2 * LANES

    def part_of(kind, j):
        return slice((kind * per + j) * SPAN, (kind * per + j + 1) * SPAN)

    for j in range(per):
        rows = slice(j * SPAN, (j + 1) * SPAN)
        pack = pack_ref[rows, :]
        tot = tot_ref[j * 8 : j * 8 + 1, :]
        dt = softplus(pltpu.roll(pack, LANES - 16, 1))
        wbuf[part_of(0, j), :] = split(source_weights(pack, tot, dt, lane, nh), 1)
        wbuf[part_of(1, j), :] = split(target_weights(pack, tot, lane, nh), 1)
        dbuf[rows, :LANES] = dbc_ref[rows, :]
    for n, at, _ in groups(width):
        tile = slice(at, at + LANES)
        wtile = slice(LANES + at, 2 * LANES + at)
        both = slice(2 * at, 2 * at + 2 * LANES)
        first = slice(2 * at, 2 * at + LANES)
        second = slice(2 * at + LANES, 2 * at + 2 * LANES)
        wides[...] = mm(wbuf[...], ex_ref[:, both])
        for j in range(per):
            rows = slice(j * SPAN, (j + 1) * SPAN)
            bc = act_ref[rows, :LANES].astype(F32)
            b = bc[:, :HDIM].astype(BF16)
            c = pltpu.roll(bc, HDIM, 1)[:, :HDIM].astype(BF16)
            x = act_ref[rows, wtile].astype(F32)
            dy = dy_ref[rows, tile].astype(F32)
            x2 = jnp.concatenate([x, x], axis=1)
            dy2 = jnp.concatenate([dy, dy], axis=1)
            held = full_ref[j, :, both]
            dheld = jnp.concatenate(
                [
                    dso_ref[j, :, tile] + gsuf_ref[j, 0:1, first] * dsent_ref[:, tile],
                    dro_ref[j, :, tile] + gpre_ref[j, 0:1, second] * drent_ref[:, tile],
                ],
                axis=1,
            )
            dheld_low = dheld.astype(BF16)
            to_wide = wides[part_of(0, j), :]
            fro_wide = wides[part_of(1, j), :]
            flow = mm(b, dheld_low) * to_wide
            seen = mm(c, held) * fro_wide
            dbc = mm_nt((x2 * to_wide).astype(BF16), jnp.concatenate([dheld_low, none], axis=0))
            dbc = dbc + mm_nt((dy2 * fro_wide).astype(BF16), jnp.concatenate([none, held], axis=0))
            dbuf[rows, :LANES] += dbc
            pbuf[part_of(0, j), :] = split(dy2 * seen, 1)
            pbuf[part_of(1, j), :] = split(x2 * flow, 1)
            product = jnp.sum(dheld * held.astype(F32), axis=0, keepdims=True) * gates_ref[j, :, both]
            pbuf[2 * tb + 16 * j : 2 * tb + 16 * j + 16, :] = split(
                jnp.concatenate([product, product], axis=0), 1
            )
            dx = dxin_ref[rows, tile].astype(F32) + flow[:, :LANES] + flow[:, LANES:]
            dx = dx + skip_ref[0:1, tile] * dy
            dbuf[rows, wtile] = dx * slope_ref[rows, wtile].astype(F32)
        ext = ext_ref[both, :]
        found = mm(pbuf[:, :pair], ext) + mm(pbuf[:, pair:], ext)
        if n == 0:
            sums[...] = found
        else:
            sums[...] += found
    for j in range(per):
        rows = slice(j * SPAN, (j + 1) * SPAN)
        pack = pack_ref[rows, :]
        z = pltpu.roll(pack, LANES - 16, 1)
        dt = softplus(z)
        carried = sums[part_of(0, j), :]
        leaving = sums[part_of(1, j), :]
        through = sums[2 * tb + 16 * j : 2 * tb + 16 * j + 8, :]
        dbuf[rows, :LANES] = dbuf[rows, :LANES] * slope_ref[rows, :LANES].astype(F32)
        pulls = pulls_ref[rows, :]
        kc = jnp.where(head_lane, pulls, 0.0)
        moved = jnp.where(head_lane, pltpu.roll(pulls, LANES - 16, 1), 0.0) + carried - kc
        before = mm(tril_ref[:, : 2 * SPAN], split(jnp.where(forward, leaving, moved), 0))
        after = mm(triu_ref[:, : 2 * SPAN], split(jnp.where(forward, moved, leaving), 0))
        dlog = before + after - leaving + through[0:1, :]
        sigz = sigmoid(z)
        rate = pcol_ref[1:2, :]
        dstep = (kc + leaving) * (sigz / jnp.maximum(dt, TINY)) - dlog * rate * sigz
        dstep = jnp.where(head_lane, dstep, 0.0)
        dcat[rows, :LANES] = dstep.astype(BF16)
        lines[7:8, :LANES] += jnp.sum(dstep, axis=0, keepdims=True)
        ends = jnp.where(head_lane, -dlog * dt * rate, 0.0)
        lines[8:9, :LANES] += jnp.sum(ends, axis=0, keepdims=True)
    for j in range(per):
        rows = slice(j * SPAN, (j + 1) * SPAN)
        pack = pack_ref[rows, :]
        for at in range(0, LANES + width, LANES):
            tile = slice(at, at + LANES)
            dconv = dbuf[rows, tile]
            uv = uv_ref[rows, tile].astype(F32)
            du = taps_ref[0:1, tile] * dconv
            lines[1:2, tile] += jnp.sum(uv * dconv, axis=0, keepdims=True)
            for k in (1, 2, 3):
                shifted = dbuf[j * SPAN + k : (j + 1) * SPAN + k, tile] * pack[:, 40 + k : 41 + k]
                du = du + taps_ref[k : k + 1, tile] * shifted
                lines[1 + k : 2 + k, tile] += jnp.sum(uv * shifted, axis=0, keepdims=True)
            dcat[rows, LANES + at : 2 * LANES + at] = du.astype(BF16)

    edge = dbuf[0:8, :]
    dbuf[tb : tb + 8, :] = edge
    for tile in wide_tiles(model):
        part = mm_nt(dgate_ref[...], wg_ref[tile, :])
        part = part + mm_nt(dcat[...], wcat_ref[tile, :])
        parts[:, tile] = part.astype(BF16)
        normed = normed_ref[:, tile]
        lines[0:1, tile] += jnp.sum(part * normed.astype(F32), axis=0, keepdims=True)
        acc[tile, :] += mm_tn(normed, dcat[...])
    side = ((last - i) * tb // own ^ at_ref[1]) % 2

    @pl.when(side == 0)
    def _():
        mine_ref[0] = parts[...]

    @pl.when(side == 1)
    def _():
        theirs_ref[0] = parts[...]

    @pl.when(i == last)
    def _():
        taps_at = slice(0, LANES + width)
        hbuf[0:8, :] = jnp.zeros_like(edge)
        hbuf[8:16, :] = edge
        duh = jnp.zeros_like(edge)
        for k in (1, 2, 3):
            shifted = hbuf[k : k + 8, :] * halocols_ref[:, k - 1 : k]
            duh = duh + taps_ref[k : k + 1, :] * shifted
            lines[1 + k : 2 + k, taps_at] += jnp.sum(uvh_ref[...] * shifted, axis=0, keepdims=True)
        duh = duh.astype(BF16)
        normh = normh_ref[...]
        parth = mm_nt(duh, wcat_ref[:, LANES:])
        lines[0:1, :] += jnp.sum(parth * normh.astype(F32), axis=0, keepdims=True)
        skips = jnp.zeros((8, LANES), F32)
        for n, at, _ in groups(width):
            ext = ext_ref[2 * at : 2 * at + LANES, :]
            high = gskip_ref[:, at : at + LANES].astype(BF16)
            low = (gskip_ref[:, at : at + LANES] - high.astype(F32)).astype(BF16)
            skips = skips + mm(high, ext) + mm(low, ext)
        lines[5:6, :LANES] = skips[0:1, :]
        lines[6:7, :width] = gmix_ref[0:1, :]
        acc[:, LANES:] += mm_tn(normh, duh)
        placed = jnp.where(iota((16, LANES), 1) == iota((16, LANES), 0) + 16, 1.0, 0.0)
        acc[:, :LANES] += exact_tn(lines[...], placed)
        row8 = iota((8, LANES), 0)
        taken = iota((8, LANES), 1) == 19 + 3 * at_ref[0] + row8
        taken = taken & (row8 > 4) & (at_ref[0] > 0)
        acc[:, :LANES] += exact_tn(parth, jnp.where(taken, 1.0, 0.0))
        size = model // peers
        for k in range(peers):
            start = pl.multiple_of((at_ref[0] ^ k) * size, 8)
            chunks[k][...] = acc[pl.ds(start, size), :].astype(BF16)


def finish_kernel(nh, peers, shares, at_ref, *refs):
    chunks = refs[:peers]
    eye_ref, ingain_ref, x_ref, cot_ref, kept_ref, got_ref = refs[peers : peers + 6]
    gain_ref, value_ref, state_ref, step_ref, bias_ref, decay_ref = refs[peers + 6 : peers + 12]
    convv_ref, convs_ref, skip_ref, mixer_ref, tokens_ref, extra = refs[peers + 12 :]
    size = chunks[0].shape[0]
    real_width = value_ref.shape[1]
    heads = step_ref.shape[0]
    for k in range(peers):
        rows = pl.ds(pl.multiple_of((at_ref[0] ^ k) * size, 8), size)
        extra[rows, :] = chunks[k][:, :LANES].astype(F32)
        state_ref[rows, :] = chunks[k][:, LANES : 2 * LANES].astype(F32)
        value_ref[rows, :] = chunks[k][:, 2 * LANES : 2 * LANES + real_width].astype(F32)
    found = extra[...].astype(BF16)
    lines = mm_nt(eye_ref[...], found)
    row16 = iota((16, LANES), 0)
    taken = iota((16, LANES), 1) == 27 + 3 * at_ref[0] + row16 - 13
    taken = taken & (row16 > 12) & (at_ref[1] == shares - 1)
    late = mm_nt(jnp.where(taken, 1.0, 0.0).astype(BF16), found)

    def token_rows(rows, more):
        x = x_ref[rows, :].astype(F32)
        s = lax.rsqrt(jnp.mean(x * x, axis=1, keepdims=True) + EPSILON)
        dn = kept_ref[0, rows, :] + got_ref[0, rows, :].astype(F32) + more
        scaled = dn * ingain_ref[...]
        inside = jnp.mean(scaled * x, axis=1, keepdims=True)
        cot = cot_ref[rows, :].astype(F32)
        tokens_ref[rows, :] = (cot + s * scaled - x * (s * s * s) * inside).astype(BF16)

    own = x_ref.shape[0]
    for at in range(0, own, 32):
        token_rows(slice(at, at + 32), 0.0)
    token_rows(slice(own - 16, own), late)
    for h in range(heads):
        step_ref[h, 0:1, :] = lines[h : h + 1, :]
        step_ref[h, 1:2, :] = lines[nh + h : nh + h + 1, :]
    gain_ref[...] = (lines[16:17, :] / ingain_ref[...])[0]
    convs_ref[...] = lines[17:21, :LANES]
    convv_ref[...] = lines[17:21, LANES : LANES + real_width]
    skip_ref[...] = lines[21:22, :heads]
    mixer_ref[...] = lines[22, :real_width]
    bias_ref[0:1, :] = lines[23:24, :heads]
    bias_ref[1:2, :] = lines[23:24, nh : nh + heads]
    decay_ref[...] = lines[24:25, :heads] + lines[24:25, nh : nh + heads]


def whole(shape):
    return pl.BlockSpec(shape, lambda i, *_: (0,) * len(shape))


def row_block(rows, width):
    return pl.BlockSpec((rows, width), lambda i, *_: (i, 0))


def lane_block(rows, width):
    return pl.BlockSpec((rows, width), lambda i, *_: (0, i))


def chunk_block(per, rows, width):
    return pl.BlockSpec((per, rows, width), lambda i, *_: (i, 0, 0))


def sds(shape, dtype):
    return jax.ShapeDtypeStruct(shape, dtype)


def call(kernel, name, grid, ins, outs, scratch, flops, operands, scalars=()):
    return pl.pallas_call(
        kernel,
        name=name,
        grid_spec=pltpu.PrefetchScalarGridSpec(
            num_scalar_prefetch=len(scalars),
            grid=(grid,),
            in_specs=ins,
            out_specs=[spec for spec, _ in outs],
            scratch_shapes=scratch,
        ),
        out_shape=[shape for _, shape in outs],
        compiler_params=pltpu.CompilerParams(
            dimension_semantics=("arbitrary",), vmem_limit_bytes=56 * 1024 * 1024
        ),
        cost_estimate=pl.CostEstimate(
            flops=int(flops), bytes_accessed=1, transcendentals=0
        ),
    )(*scalars, *operands)


def shifted_in(array, axis, by):
    length = lax.axis_size(axis)
    pairs = [(i, i + by) for i in range(length) if 0 <= i + by < length]
    return lax.ppermute(array, axis, pairs)


def exchange_sides(messages, hops):
    size = lax.axis_size("seq")
    arrived = []
    for d in range(1, hops + 1):
        for side in (0, 1):
            pairs = [(i, i + d) for i in range(size - d) if (i // d) % 2 == side]
            both = pairs + [(b, a) for a, b in pairs]
            arrived.append(lax.ppermute(messages[len(arrived)], "seq", both))
    return arrived


def swap(array, axis, k):
    n = lax.axis_size(axis)
    return lax.ppermute(array, axis, [(i, i ^ k) for i in range(n)])


def sum_over(array, axis):
    size = lax.axis_size(axis)
    result = array
    for k in range(1, size):
        result = result + lax.ppermute(array, axis, [(i, i ^ k) for i in range(size)])
    return result


def per_device(
    tokens,
    input_gain,
    proj_gate,
    proj_value,
    proj_state,
    proj_step,
    step_bias,
    decay_log,
    conv_value,
    conv_state,
    skip_gain,
    mixer_gain,
    proj_out,
    doc_lengths,
    pad_mask,
    cotangent,
):
    head_devices = lax.axis_size("head")
    length = pad_mask.shape[0]
    model = tokens.shape[1]
    real_width = proj_gate.shape[1]
    real_heads = proj_step.shape[2]
    inner = real_width * head_devices
    width = -(-real_width // LANES) * LANES
    nh = width // HDIM

    def padded(array, axis, size):
        if array.shape[axis] == size:
            return array
        widths = [(0, 0)] * array.ndim
        widths[axis] = (0, size - array.shape[axis])
        return jnp.pad(array, widths)

    proj_gate = padded(proj_gate, 1, width)
    proj_value = padded(proj_value, 1, width)
    proj_step = padded(proj_step, 2, nh)
    step_bias = padded(step_bias, 1, nh)
    conv_value = padded(conv_value, 1, width)
    skip_gain = padded(skip_gain, 0, nh)
    mixer_gain = padded(mixer_gain, 0, width)
    proj_out = padded(proj_out, 0, width)
    nc = length // SPAN
    tb = BLOCK
    per = tb // SPAN
    grid = length // tb
    wide = LANES + width
    hops = -(-(LONGEST - 1) // length)
    seq_index = lax.axis_index("seq")
    first_place = seq_index * length
    all_tokens = length * lax.axis_size("seq")

    edge_rows = shifted_in(tokens[tokens.shape[0] - 8 :], "seq", 1)
    here = lax.axis_index("head")
    halo = jnp.where(here == head_devices - 1, edge_rows, 0)
    for k in range(1, head_devices):
        halo = halo + jnp.where(here ^ k == head_devices - 1, swap(edge_rows, "head", k), 0)

    offsets = jnp.cumsum(doc_lengths) - doc_lengths
    room = -(-(offsets.shape[0] + 1) // LANES) * LANES - offsets.shape[0]
    fill = jnp.where(jnp.arange(room) == 0, all_tokens, 2 * all_tokens).astype(offsets.dtype)
    offsets = jnp.concatenate([offsets, fill])[None, :]
    live_row = pad_mask[None, :]
    lanes = np.arange(LANES)
    column = np.arange(2 * width)
    head_of = column // (2 * LANES) * 2 + column % LANES // HDIM
    head_of = head_of + np.where(column % (2 * LANES) >= LANES, nh, 0)
    ext = jnp.asarray(head_of[:, None] == lanes[None, :], BF16)
    ex = jnp.asarray(np.tile(head_of[None, :] == lanes[:, None], (2, 1)), BF16)
    at = np.arange(SPAN)
    tril = jnp.asarray(np.tile(at[:, None] >= at[None, :], (1, 3)), BF16)
    triu = at[:, None] <= at[None, :]
    triu_wide = jnp.asarray(np.tile(triu, (1, 2)), BF16)
    triu_tall = jnp.asarray(np.tile(triu, (3, 1)), BF16)
    eye = jnp.asarray(np.arange(16)[:, None] == lanes[None, :], F32)
    eye16 = jnp.asarray(np.arange(16)[:, None] + 16 == lanes[None, :], F32)
    picked = jnp.asarray(np.arange(32)[:, None] == lanes[None, :], BF16)
    peers = lax.axis_size("seq")
    own = length // head_devices
    bits = head_devices.bit_length() - 1
    scalars = [jnp.stack([seq_index, here, first_place]).astype(jnp.int32)]
    size = model // peers

    rate = padded(jnp.exp(decay_log), 0, nh)
    gap = 16 - 2 * nh
    bias16 = jnp.pad(step_bias.reshape(-1), (0, gap))
    rate16 = jnp.pad(jnp.concatenate([rate, rate]), (0, gap))
    prow = jnp.stack([bias16, rate16], axis=1)
    wide_bias = jnp.pad(jnp.concatenate([bias16, bias16]), (0, LANES - 32))
    pcol = jnp.stack([wide_bias, jnp.pad(rate16, (0, LANES - 16))], axis=0)
    steps = jnp.concatenate([proj_step[0], proj_step[1]], axis=1)
    steps = jnp.pad(steps, ((0, 0), (0, gap)))
    wst = jnp.pad(jnp.concatenate([steps, steps], axis=1), ((0, 0), (0, LANES - 32)))
    wstr = steps.T
    taps = jnp.concatenate([conv_state, conv_value], axis=1)
    gain = input_gain[None, :]
    mg = mixer_gain[None, :]
    skip = jnp.repeat(skip_gain, HDIM)[None, :]
    pieces_of = {0: tokens}
    for bit in [1 << b for b in range(bits - 1, 0, -1)]:
        pieces_of.update({k | bit: swap(v, "head", bit) for k, v in pieces_of.items()})
    wcat = jnp.concatenate([wst, proj_state, proj_value], axis=1)
    prelims = (halo, offsets, live_row, pcol, prow, wst, wstr, taps, wcat)
    pieces_of, late, prelims, scalars = lax.optimization_barrier(
        (pieces_of, cotangent, prelims, scalars)
    )
    halo, offsets, live_row, pcol, prow, wst, wstr, taps, wcat = prelims
    pieces_of.update({k | 1: swap(v, "head", 1) for k, v in pieces_of.items()})
    token_pieces = [pieces_of[k] for k in range(head_devices)]
    cot_all = lax.all_gather(late, "head", axis=0, tiled=True)

    rows = partial(row_block, tb)
    states = sds((nc, HDIM, width), F32)
    gates_of = sds((nc, 8, 2 * width), F32)
    message = sds((HDIM + 8, width), F32)
    state_block = chunk_block(per, HDIM, width)
    gate_block = chunk_block(per, 8, 2 * width)
    tot_block = row_block(per * 8, LANES)
    messages = [(whole(message.shape), message)] * (2 * hops)

    def sized(block):
        return (
            length // block,
            partial(row_block, block),
            partial(lane_block, width=block),
            partial(chunk_block, block // SPAN),
            row_block(block // SPAN * 8, LANES),
        )

    def slot_of(j, at):
        place = j ^ at[1]
        return sum(((place >> b) & 1) << (bits - 1 - b) for b in range(bits))

    each = own // tb

    def piece_block(k):
        def index(i, at):
            return jnp.clip(i - (at[1] ^ k) * each, 0, each - 1), 0

        return pl.BlockSpec((tb, model), index)

    def side_block(side):
        def index(i, at):
            row = grid - 1 - i
            j, sub = row // each, row % each
            ours = (j ^ at[1]) % 2 == side
            first = j == head_devices - 1
            j = jnp.where(ours, j, jnp.where(first, j - 1, j + 1))
            sub = jnp.where(ours, sub, jnp.where(first, each - 1, 0))
            return slot_of(j, at) % (head_devices // 2), sub, 0

        return pl.BlockSpec((1, tb, model), index)

    (
        normed,
        normh,
        gate_in,
        acted,
        slope,
        uv,
        uvh,
        pack,
        rowa,
        rowp,
        seg_row,
        halo_cols,
        tot,
        sf,
        rb,
        gates,
        gpre,
        gsuf,
        gtot,
        *ahead,
    ) = call(
        partial(front_kernel, nh, hops, head_devices, own),
        "front",
        grid,
        [piece_block(k) for k in range(head_devices)]
        + [
            whole((8, model)),
            whole((1, model)),
            whole((model, width)),
            whole((model, LANES)),
            whole((model, width)),
            whole((model, LANES)),
            whole((16, model)),
            whole((2, LANES)),
            whole((16, 2)),
            whole((4, wide)),
            whole(offsets.shape),
            lane_block(1, tb),
            whole(ex.shape),
            whole(tril.shape),
            whole(triu_tall.shape),
        ],
        [
            (rows(model), sds((length, model), BF16)),
            (whole((8, model)), sds((8, model), BF16)),
            (rows(width), sds((length, width), BF16)),
            (rows(wide), sds((length, wide), BF16)),
            (rows(wide), sds((length, wide), BF16)),
            (rows(wide), sds((length, wide), BF16)),
            (whole((8, wide)), sds((8, wide), F32)),
            (rows(LANES), sds((length, LANES), F32)),
            (lane_block(16, tb), sds((16, length), F32)),
            (lane_block(16, tb), sds((16, length), F32)),
            (lane_block(8, tb), sds((8, length), F32)),
            (whole((8, LANES)), sds((8, LANES), F32)),
            (tot_block, sds((nc * 8, LANES), F32)),
            (state_block, states),
            (whole(states.shape), states),
            (whole(gates_of.shape), gates_of),
            (whole(gates_of.shape), gates_of),
            (whole(gates_of.shape), gates_of),
            (whole((8, 2 * width)), sds((8, 2 * width), F32)),
        ]
        + messages,
        [
            pltpu.VMEM((tb + 8, wide), F32),
            pltpu.VMEM((HDIM, width), F32),
            pltpu.VMEM((nc, HDIM, width), F32),
            pltpu.VMEM((tb, LANES), F32),
            pltpu.VMEM((per * 8, LANES), F32),
            pltpu.VMEM((SPAN + 16, LANES), F32),
            pltpu.VMEM((tb + 16 * per, 2 * LANES), BF16),
            pltpu.VMEM((tb + 16 * per, 2 * LANES), F32),
            pltpu.VMEM((per * HDIM, LANES), BF16),
        ],
        25e9,
        token_pieces
        + [
            halo,
            gain,
            proj_gate,
            proj_state,
            proj_value,
            wst,
            wstr,
            pcol,
            prow,
            taps,
            offsets,
            live_row,
            ex,
            tril,
            triu_tall,
        ],
        scalars,
    )

    ahead = exchange_sides(ahead, hops)

    big_grid, big_rows, big_lanes, big_chunks, big_tot = sized(512)
    yin, dout = call(
        partial(inner_kernel, nh),
        "inner",
        big_grid,
        [
            big_rows(wide),
            big_rows(LANES),
            big_lanes(8),
            big_lanes(16),
            whole((1, width)),
            big_rows(model),
            whole((width, model)),
        ],
        [
            (big_rows(width), sds((length, width), F32)),
            (big_rows(width), sds((length, width), BF16)),
        ],
        [],
        6e9,
        [acted, pack, seg_row, rowp, skip, cot_all, proj_out],
    )

    y, stat, full = call(
        partial(merge_kernel, nh, hops),
        "merge",
        big_grid,
        [
            big_rows(LANES),
            big_rows(LANES),
            big_tot,
            big_chunks(HDIM, width),
            big_chunks(HDIM, width),
            big_chunks(8, 2 * width),
            big_chunks(8, 2 * width),
            big_rows(width),
            big_rows(width),
            big_rows(width),
            whole((1, width)),
            whole(ex.shape),
        ]
        + [whole(message.shape)] * (2 * hops),
        [
            (big_rows(width), sds((length, width), BF16)),
            (big_lanes(8), sds((8, length), F32)),
            (big_chunks(HDIM, 2 * width), sds((nc, HDIM, 2 * width), BF16)),
        ],
        [pltpu.VMEM((HDIM, width), F32)] * 2,
        6e9,
        [acted, pack, tot, sf, rb, gpre, gsuf, yin, gate_in, dout, mg, ex] + ahead,
        scalars,
    )

    shares = [stat]
    for k in range(1, head_devices):
        shares.append(lax.ppermute(stat, "head", [(i, i ^ k) for i in range(head_devices)]))

    aside, outin, dy, dgate, gmix, gskip, gout, ggate = call(
        partial(turn_kernel, inner, head_devices),
        "turn",
        grid,
        [
            rows(width),
            rows(width),
            rows(width),
            whole((1, width)),
            rows(wide),
            whole((16, LANES)),
            rows(model),
            rows(model),
            whole((width, model)),
        ]
        + [lane_block(8, tb)] * head_devices,
        [
            (row_block(ASIDE, model), sds((head_devices * ASIDE, model), BF16)),
            (rows(width), sds((length, width), BF16)),
            (rows(width), sds((length, width), BF16)),
            (rows(width), sds((length, width), BF16)),
            (whole((8, width)), sds((8, width), F32)),
            (whole((8, width)), sds((8, width), F32)),
            (whole((width, model)), sds((width, model), BF16)),
            (whole((model, width)), sds((model, width), BF16)),
        ],
        [pltpu.VMEM((width, model), F32), pltpu.VMEM((model, width), F32)],
        4e9,
        [y, gate_in, dout, mg, acted, eye, normed, cot_all, proj_out] + shares,
    )
    outs = call(
        partial(adjoint_kernel, nh, head_devices, hops, own),
        "adjoint",
        grid,
        [
            rows(LANES),
            rows(LANES),
            tot_block,
            whole(gates_of.shape),
            whole((8, 2 * width)),
            whole(ex.shape),
            rows(width),
            rows(width),
            whole((width, model)),
        ],
        [(whole((own - ASIDE, model)), sds((own - ASIDE, model), BF16))] * head_devices
        + [
            (whole(states.shape), states),
            (state_block, states),
        ]
        + messages,
        [
            pltpu.VMEM((HDIM, width), F32),
            pltpu.VMEM((nc, HDIM, width), F32),
            pltpu.VMEM((tb, 2 * LANES), BF16),
            pltpu.VMEM((tb, 2 * LANES), F32),
            pltpu.VMEM((per * HDIM, LANES), BF16),
        ],
        1e8,
        [acted, pack, tot, gates, gtot, ex, dy, outin, proj_out],
        scalars,
    )
    mixers = outs[:head_devices]
    dso, dro, *behind = outs[head_devices:]

    grad_proj_out, grad_proj_gate = lax.psum((gout, ggate), "seq")
    aside = lax.psum_scatter(aside, "head", scatter_dimension=0, tiled=True)
    behind = exchange_sides(behind, hops)
    mixer_shares = [mixers[0]] + [swap(mixers[k], "head", k) for k in range(1, head_devices)]

    mid_grid, mid_rows, mid_lanes, *_ = sized(256)
    dxin, dbc, pulls = call(
        partial(mid_kernel, nh),
        "mid",
        mid_grid,
        [
            mid_rows(wide),
            mid_rows(LANES),
            mid_lanes(8),
            mid_lanes(16),
            mid_rows(width),
            whole((16, LANES)),
        ],
        [
            (mid_rows(width), sds((length, width), BF16)),
            (mid_rows(LANES), sds((length, LANES), F32)),
            (mid_rows(LANES), sds((length, LANES), F32)),
        ],
        [pltpu.VMEM((16, SPAN), F32), pltpu.VMEM((nh, 4 * SPAN, LANES), BF16)],
        1e8,
        [acted, pack, seg_row, rowa, dy, eye16],
    )

    back = lambda i: grid - 1 - i

    def rev(spec):
        return pl.BlockSpec(spec.block_shape, lambda i, *_: spec.index_map(back(i)))

    mine, theirs, *chunks = call(
        partial(back_kernel, nh, peers, hops, own),
        "back",
        grid,
        [
            rev(rows(wide)),
            rev(rows(wide)),
            rev(rows(LANES)),
            rev(tot_block),
            rev(rows(width)),
            rev(chunk_block(per, HDIM, 2 * width)),
            rev(state_block),
            rev(state_block),
            rev(gate_block),
            rev(gate_block),
            rev(gate_block),
            rev(rows(width)),
            rev(rows(LANES)),
            rev(rows(LANES)),
            rev(rows(wide)),
            whole((8, wide)),
            whole((8, LANES)),
            whole((4, wide)),
            whole((1, width)),
            whole((2, LANES)),
            whole(ex.shape),
            whole(ext.shape),
            whole(tril.shape),
            whole(triu_wide.shape),
            rev(rows(model)),
            whole((8, model)),
            rev(rows(width)),
            whole((model, width)),
            whole((model, LANES + wide)),
            whole((8, width)),
            whole((8, width)),
        ]
        + [whole(message.shape)] * (2 * hops),
        [
            (side_block(0), sds((head_devices // 2, own, model), BF16)),
            (side_block(1), sds((head_devices // 2, own, model), BF16)),
        ]
        + [(whole((size, LANES + wide)), sds((size, LANES + wide), BF16))] * peers,
        [
            pltpu.VMEM((tb + 8, wide), F32),
            pltpu.VMEM((16, wide), F32),
            pltpu.VMEM((tb, LANES + wide), BF16),
            pltpu.VMEM((model, LANES + wide), F32),
            pltpu.VMEM((16, model), F32),
            pltpu.VMEM((HDIM, width), F32),
            pltpu.VMEM((HDIM, width), F32),
            pltpu.VMEM((tb, model), BF16),
            pltpu.VMEM((2 * tb, 2 * LANES), BF16),
            pltpu.VMEM((2 * tb, 2 * LANES), F32),
            pltpu.VMEM((2 * tb + 16 * per, 4 * LANES), BF16),
            pltpu.VMEM((2 * tb + 16 * per, LANES), F32),
        ],
        1e8,
        [
            acted,
            slope,
            pack,
            tot,
            dy,
            full,
            dso,
            dro,
            gsuf,
            gpre,
            gates,
            dxin,
            dbc,
            pulls,
            uv,
            uvh,
            halo_cols,
            taps,
            skip,
            pcol,
            ex,
            ext,
            tril,
            triu_wide,
            normed,
            normh,
            dgate,
            proj_gate,
            wcat,
            gmix,
            gskip,
        ]
        + behind,
        scalars,
    )

    chunks, theirs, mixer_shares = lax.optimization_barrier((chunks, theirs, mixer_shares))
    got = swap(theirs, "head", 1)
    summed = chunks[0].astype(F32)
    for k in range(1, peers):
        summed = summed + swap(chunks[k], "seq", k).astype(F32)
    shared = summed[:, : 2 * LANES]
    row_at = seq_index * size + jnp.arange(size)[:, None]
    lane_at = jnp.arange(2 * LANES)[None, :]
    common = (lane_at == 16) | (lane_at > 26)
    common = common | ((lane_at > 16) & (lane_at < 21) & (row_at < LANES))
    shared = jnp.where(common, sum_over(shared, "head"), shared)

    half = head_devices // 4
    own_in = mine[:half].astype(F32) + got[:half].astype(F32)
    going = (mine[half:].astype(F32) + got[half:].astype(F32)).astype(BF16)
    for b in range(1, bits):
        if b == 1:
            going, shared = lax.optimization_barrier((going, shared))
        got = swap(going, "head", 1 << b)
        if b < bits - 1:
            half = half // 2
            going = (own_in[half:] + got[half:].astype(F32)).astype(BF16)
            own_in = own_in[:half] + got[:half].astype(F32)

    reduced = jnp.concatenate([shared, summed[:, 2 * LANES :]], axis=1).astype(BF16)
    spread_out = [reduced] + [swap(reduced, "seq", k) for k in range(1, peers)]
    spread_out[2], grad_proj_out, grad_proj_gate, mixer_shares = lax.optimization_barrier(
        (spread_out[2], grad_proj_out, grad_proj_gate, mixer_shares)
    )
    grad_proj_out = grad_proj_out[:real_width].astype(F32)
    grad_proj_gate = grad_proj_gate[:, :real_width].astype(F32)
    mixer = sum(share.astype(F32) for share in mixer_shares)
    mixer = jnp.concatenate([aside.astype(F32), mixer], axis=0)
    layer_out = (tokens.astype(F32) + mixer).astype(BF16)
    spread_out, layer_out, grad_proj_out, grad_proj_gate = lax.optimization_barrier(
        (spread_out, layer_out, grad_proj_out, grad_proj_gate)
    )

    finals = [
        sds((model,), F32),
        sds((model, real_width), F32),
        sds((model, LANES), F32),
        sds((real_heads, 2, model), F32),
        sds((2, real_heads), F32),
        sds((1, real_heads), F32),
        sds((4, real_width), F32),
        sds((4, LANES), F32),
        sds((1, real_heads), F32),
        sds((real_width,), F32),
        sds((own, model), BF16),
    ]
    ggain, gvalue, gstate, gstep, gbias, gdecay, gconvv, gconvs, gskips, gmixer, grad_tokens = call(
        partial(finish_kernel, nh, peers, head_devices),
        "finish",
        1,
        [whole((size, LANES + wide))] * peers
        + [whole((32, LANES)), whole((1, model))]
        + [whole((own, model))] * 2
        + [whole((1, own, model))] * 2,
        [(whole(f.shape), f) for f in finals],
        [pltpu.VMEM((model, LANES), F32)],
        3e9,
        spread_out
        + [picked, input_gain[None, :]]
        + [tokens, cotangent, own_in, got],
        scalars,
    )
    return (
        layer_out,
        grad_tokens,
        ggain,
        grad_proj_gate,
        gvalue,
        gstate,
        jnp.transpose(gstep, (1, 2, 0)),
        gbias,
        gdecay[0],
        gconvv,
        gconvs,
        gskips[0],
        gmixer,
        grad_proj_out,
    )


def solution(mesh):
    return jax.shard_map(
        per_device,
        mesh=mesh,
        in_specs=(
            P(("seq", "head"), None),
            P(),
            P(None, "head"),
            P(None, "head"),
            P(),
            P(None, None, "head"),
            P(None, "head"),
            P("head"),
            P(None, "head"),
            P(),
            P("head"),
            P("head"),
            P("head", None),
            P(),
            P("seq"),
            P(("seq", "head"), None),
        ),
        out_specs=(
            P(("seq", "head"), None),
            P(("seq", "head"), None),
            P(),
            P(None, "head"),
            P(None, "head"),
            P(),
            P(None, None, "head"),
            P(None, "head"),
            P("head"),
            P(None, "head"),
            P(),
            P("head"),
            P("head"),
            P("head", None),
        ),
        check_vma=False,
    )
```

```python
from functools import partial

import jax
import jax.numpy as jnp
import numpy as np
from jax import lax
from jax.experimental import pallas as pl
from jax.experimental.pallas import tpu as pltpu
from jax.sharding import PartitionSpec as P

SPAN = 128
HDIM = 64
LANES = 128
LONGEST = 4096
EPSILON = 1e-05
TINY = 1e-30
F32 = jnp.float32
BF16 = jnp.bfloat16
BLOCK = 512
ASIDE = 256


def mm(a, b):
    return jnp.dot(a, b, preferred_element_type=F32)


def mm_nt(a, b):
    return lax.dot_general(a, b, (((1,), (1,)), ((), ())), preferred_element_type=F32)


def mm_tn(a, b):
    return lax.dot_general(a, b, (((0,), (0,)), ((), ())), preferred_element_type=F32)


def pieces(v):
    high = v.astype(BF16)
    rest = v - high.astype(F32)
    mid = rest.astype(BF16)
    return high, mid, (rest - mid.astype(F32)).astype(BF16)


def exact_tn(a, b):
    return lax.dot_general(
        a, b, (((0,), (0,)), ((), ())), precision=lax.Precision.HIGHEST, preferred_element_type=F32
    )


def split(v, axis):
    high = v.astype(BF16)
    return jnp.concatenate([high, (v - high.astype(F32)).astype(BF16)], axis=axis)


def sigmoid(v):
    return 1.0 / (1.0 + jnp.exp(-v))


def softplus(v):
    return jnp.maximum(v, 0.0) + jnp.log1p(jnp.exp(-jnp.abs(v)))


def iota(shape, dim):
    return lax.broadcasted_iota(jnp.int32, shape, dim)


def wide_tiles(width):
    return [slice(at, min(at + 2 * LANES, width)) for at in range(0, width, 2 * LANES)]


def groups(width):
    return [(n, n * LANES, (2 * n, 2 * n + 1)) for n in range(width // LANES)]


def sides(v, width):
    tiles = [v[:, at : at + LANES] for at in range(0, 2 * width, LANES)]
    return jnp.concatenate(tiles[::2], axis=1), jnp.concatenate(tiles[1::2], axis=1)


def stacked(v):
    first = iota(v.shape, 1) < HDIM
    zero = jnp.zeros_like(v)
    return jnp.concatenate([jnp.where(first, v, zero), jnp.where(first, zero, v)], axis=0)


def source_weights(pack, tot, dt, lane, nh):
    forward = lane < nh
    gap = jnp.where(forward, tot - pack, pack)
    kept = jnp.where(forward, pack[:, 38:39], pack[:, 40:41])
    return jnp.where(lane < 16, jnp.exp(jnp.where(lane < 16, gap, 0.0)) * kept * dt, 0.0)


def target_weights(pack, tot, lane, nh):
    forward = lane < nh
    gap = jnp.where(forward, pack, tot - pack)
    kept = jnp.where(forward, pack[:, 37:38], pack[:, 39:40])
    return jnp.where(lane < 16, jnp.exp(jnp.where(lane < 16, gap, 0.0)) * kept, 0.0)


def send_sides(at_ref, hops, up, down, refs):
    for d in range(1, hops + 1):
        low = (at_ref[0] // d) % 2 == 0
        refs[2 * d - 2][...] = jnp.where(low, up, down)
        refs[2 * d - 1][...] = jnp.where(low, down, up)


def land_sides(at_ref, hops, refs, from_earlier, from_later):
    for d in range(hops, 0, -1):
        low = (at_ref[0] // d) % 2 == 0
        first, second = refs[2 * d - 2][...], refs[2 * d - 1][...]
        for state, part in (
            (from_earlier, jnp.where(low, second, first)),
            (from_later, jnp.where(low, first, second)),
        ):
            if d == hops:
                state[...] = part[:HDIM]
            else:
                state[...] = part[:HDIM] + part[HDIM : HDIM + 1] * state[...]


def documents(off_ref, places):
    count = jnp.zeros(places.shape, F32)
    for at in range(0, off_ref.shape[1], LANES):
        begun = off_ref[0:1, at : at + LANES] <= places
        count = count + jnp.sum(jnp.where(begun, 1.0, 0.0), axis=1, keepdims=True)
    return count


def front_kernel(
    nh,
    hops,
    shares,
    own,
    at_ref,
    *refs,
):
    front_body(nh, hops, own, at_ref, refs[:shares], *refs[shares:])


def front_body(
    nh,
    hops,
    own,
    at_ref,
    x_refs,
    halo_ref,
    gain_ref,
    wg_ref,
    ws_ref,
    wv_ref,
    wst_ref,
    wstr_ref,
    pcol_ref,
    prow_ref,
    taps_ref,
    off_ref,
    live_ref,
    ex_ref,
    tril_ref,
    triu_ref,
    normed_ref,
    normh_ref,
    gate_ref,
    act_ref,
    slope_ref,
    uv_ref,
    uvh_ref,
    pack_ref,
    rowa_ref,
    rowp_ref,
    segrow_ref,
    halocols_ref,
    tot_ref,
    sf_ref,
    rb_ref,
    gates_ref,
    gpre_ref,
    gsuf_ref,
    gtot_ref,
    *rest,
):
    messages = rest[: 2 * hops]
    ubuf, state, incb, marks, ends, docs, wbuf, wides, bts = rest[2 * hops :]
    i = pl.program_id(0)
    tb = normed_ref.shape[0]
    per = tb // SPAN
    nc = rb_ref.shape[0]
    width = gate_ref.shape[1]
    piece = i * tb // own ^ at_ref[1]

    def norm(x):
        xf = x.astype(F32)
        s = lax.rsqrt(jnp.mean(xf * xf, axis=1, keepdims=True) + EPSILON)
        return (xf * s * gain_ref[0:1, :]).astype(BF16)

    @pl.when(i == 0)
    def _():
        edge = norm(halo_ref[...])
        normh_ref[...] = edge
        ubuf[0:8, :LANES] = mm(edge, ws_ref[...])
        ubuf[0:8, LANES:] = mm(edge, wv_ref[...])
        uvh_ref[...] = ubuf[0:8, :]
        state[...] = jnp.zeros_like(state)
        place = at_ref[2] - 8 + iota((8, 1), 0)
        here = documents(off_ref, place)
        lane8 = iota((8, LANES), 1)
        halo = jnp.zeros((8, LANES), F32)
        for k in (1, 2, 3):
            same = jnp.where(documents(off_ref, place + k) == here, 1.0, 0.0)
            halo = jnp.where(lane8 == k - 1, same, halo)
        halocols_ref[...] = halo

    @pl.when(i > 0)
    def _():
        ubuf[0:8, :] = ubuf[tb : tb + 8, :]

    for at in range(0, tb, 64):
        x = x_refs[0][at : at + 64, :]
        for k in range(1, len(x_refs)):
            x = jnp.where(piece == k, x_refs[k][at : at + 64, :], x)
        normed_ref[at : at + 64, :] = norm(x)
    nb = normed_ref[...]
    for tile in wide_tiles(width):
        gate_ref[:, tile] = mm(nb, wg_ref[:, tile]).astype(BF16)
    uv = mm(nb, ws_ref[...])
    ubuf[8 : 8 + tb, :LANES] = uv
    uv_ref[:, :LANES] = uv.astype(BF16)
    for tile in wide_tiles(width):
        uv = mm(nb, wv_ref[:, tile])
        at = slice(LANES + tile.start, LANES + tile.stop)
        ubuf[8 : 8 + tb, at] = uv
        uv_ref[:, at] = uv.astype(BF16)
    zr_all = mm_nt(wstr_ref[...], nb)
    lane = iota((SPAN, LANES), 1)
    forward = lane < nh
    forward_row = iota((16, SPAN), 0) < nh
    gate_lane = iota((8, LANES), 1) < nh
    for j in range(per):
        rows = slice(j * SPAN, (j + 1) * SPAN)
        base = at_ref[2] + (i * per + j) * SPAN
        around = documents(off_ref, base - 8 + iota((SPAN + 16, 1), 0))
        docs[...] = jnp.broadcast_to(around, docs.shape)
        seg = docs[8 : 8 + SPAN, :]
        prev_last, first = docs[7:8, :], docs[8:9, :]
        last, next_first = docs[7 + SPAN : 8 + SPAN, :], docs[8 + SPAN : 9 + SPAN, :]
        live = jnp.transpose(jnp.broadcast_to(live_ref[0:1, rows], (SPAN, SPAN)).astype(F32))
        mark = jnp.where(lane == 35, live, jnp.where(lane == 36, seg, 0.0))
        for k in (1, 2, 3):
            same = jnp.where(docs[8 - k : 8 - k + SPAN, :] == seg, 1.0, 0.0)
            mark = jnp.where(lane == 31 + k, same, mark)
            same = jnp.where(docs[8 + k : 8 + k + SPAN, :] == seg, 1.0, 0.0)
            mark = jnp.where(lane == 40 + k, same, mark)
        for k, bound in enumerate((prev_last, last, next_first, first)):
            mark = jnp.where(lane == 37 + k, jnp.where(seg == bound, 1.0, 0.0), mark)
        marks[rows, :] = mark
        opened = jnp.where(gate_lane, last - prev_last, next_first - first)
        ends[j * 8 : j * 8 + 8, :] = jnp.where(opened == 0.0, 1.0, 0.0)
        segrow_ref[:, rows] = jnp.transpose(seg)[:8]
    for at in range(0, LANES + width, LANES):
        tile = slice(at, at + LANES)
        for j in range(per):
            rows = slice(j * SPAN, (j + 1) * SPAN)
            keep = marks[rows, :]
            conv = taps_ref[0:1, tile] * ubuf[8 + j * SPAN : 8 + (j + 1) * SPAN, tile]
            for k in (1, 2, 3):
                moved = ubuf[8 - k + j * SPAN : 8 - k + (j + 1) * SPAN, tile]
                conv = conv + taps_ref[k : k + 1, tile] * moved * keep[:, 31 + k : 32 + k]
            sig = sigmoid(conv)
            live = keep[:, 35:36]
            act_ref[rows, tile] = (conv * sig * live).astype(BF16)
            slope_ref[rows, tile] = (live * sig * (1.0 + conv * (1.0 - sig))).astype(BF16)
    z_all = mm(nb, wst_ref[...])
    for j in range(per):
        rows = slice(j * SPAN, (j + 1) * SPAN)
        z = z_all[rows] + pcol_ref[0:1, :]
        dt = softplus(z)
        a = -dt * pcol_ref[1:2, :]
        total = mm(tril_ref[...], jnp.concatenate(pieces(a), axis=0))
        tot = total[SPAN - 1 : SPAN, :]
        cc = jnp.where(forward, total, total - a)
        pack = jnp.where(lane < 16, cc, jnp.where(lane < 32, z, marks[rows, :]))
        pack_ref[rows, :] = pack
        tot8 = jnp.broadcast_to(tot, (8, LANES))
        tot_ref[j * 8 : j * 8 + 8, :] = tot8
        dtr = softplus(zr_all[:, rows] + prow_ref[:, 0:1])
        ar = -dtr * prow_ref[:, 1:2]
        run = mm(jnp.concatenate(pieces(ar), axis=1), triu_ref[...])
        rowa = jnp.where(forward_row, run, run - ar)
        ldt = jnp.log(jnp.maximum(dtr, TINY))
        rowa_ref[:, rows] = rowa
        rowp_ref[:, rows] = jnp.where(forward_row, rowa - ldt, rowa + ldt)
        gate8 = jnp.exp(tot8) * ends[j * 8 : j * 8 + 8, :]
        bts[j * HDIM : (j + 1) * HDIM, :] = jnp.transpose(act_ref[rows, :LANES].astype(F32))[
            :HDIM
        ].astype(BF16)
        wbuf[rows, :] = split(source_weights(pack, tot, dt, lane, nh), 1)
        wbuf[tb + 16 * j : tb + 16 * j + 16, :] = split(jnp.concatenate([gate8, gate8], axis=0), 1)
    for n, at, _ in groups(width):
        tile = slice(at, at + LANES)
        both = slice(2 * at, 2 * at + 2 * LANES)
        wides[...] = mm(wbuf[...], ex_ref[:, both])
        for j in range(per):
            rows = slice(j * SPAN, (j + 1) * SPAN)
            c = i * per + j
            x = act_ref[rows, LANES + at : 2 * LANES + at].astype(F32)
            fed = jnp.concatenate(
                [
                    (x * wides[rows, :LANES]).astype(BF16),
                    (x * wides[rows, LANES:]).astype(BF16),
                ],
                axis=1,
            )
            bt = bts[j * HDIM : (j + 1) * HDIM, :]
            inc = mm(bt, fed)
            gate = wides[tb + 16 * j : tb + 16 * j + 8, :]
            gates_ref[c, :, both] = gate
            sf_ref[j, :, tile] = state[:, tile]
            state[:, tile] = state[:, tile] * gate[0:1, :LANES] + inc[:, :LANES]
            incb[c, :, tile] = inc[:, LANES:]
    @pl.when(i == pl.num_programs(0) - 1)
    def _():
        last_state = state[...]
        one = jnp.ones(gates_ref.shape[1:], F32)

        def up(c, p):
            gpre_ref[c] = p
            return p * gates_ref[c]

        p = lax.fori_loop(0, nc, up, one)
        tot_f, tot_b = sides(p, width)
        gtot_ref[:, :width] = tot_f
        gtot_ref[:, width:] = tot_b
        state[...] = jnp.zeros_like(state)

        def down(k, p):
            c = nc - 1 - k
            gsuf_ref[c] = p
            rb_ref[c] = state[...]
            gate = gates_ref[c]
            for n, at, _ in groups(width):
                tile = slice(at, at + LANES)
                second = slice(2 * at + LANES, 2 * at + 2 * LANES)
                state[:, tile] = state[:, tile] * gate[0:1, second] + incb[c, :, tile]
            return p * gate

        lax.fori_loop(0, nc, down, one)
        send_sides(
            at_ref,
            hops,
            jnp.concatenate([last_state, tot_f], axis=0),
            jnp.concatenate([state[...], tot_b], axis=0),
            messages,
        )


def inner_kernel(
    nh,
    act_ref,
    pack_ref,
    segrow_ref,
    rowp_ref,
    skip_ref,
    cot_ref,
    wo_ref,
    y_ref,
    dout_ref,
):
    tb, width = y_ref.shape
    for tile in wide_tiles(width):
        dout_ref[:, tile] = mm_nt(cot_ref[...], wo_ref[tile, :]).astype(BF16)
    t_at = iota((SPAN, SPAN), 0)
    s_at = iota((SPAN, SPAN), 1)
    lower = t_at > s_at
    for j in range(tb // SPAN):
        rows = slice(j * SPAN, (j + 1) * SPAN)
        bc = act_ref[rows, :LANES].astype(F32)
        b = bc[:, :HDIM].astype(BF16)
        c = pltpu.roll(bc, HDIM, 1)[:, :HDIM].astype(BF16)
        pack = pack_ref[rows, :]
        within = (pack[:, 36:37] == segrow_ref[0:1, rows]) & (t_at != s_at)
        score = jnp.where(within, mm_nt(c, b), 0.0)
        for n, at, heads in groups(width):
            tile = slice(at, at + LANES)
            mats = []
            for h in heads:
                gap = jnp.where(
                    lower,
                    pack[:, h : h + 1] - rowp_ref[h : h + 1, rows],
                    rowp_ref[nh + h : nh + h + 1, rows] - pack[:, nh + h : nh + h + 1],
                )
                mats.append((score * jnp.exp(gap)).astype(BF16))
            xp = act_ref[rows, LANES + at : 2 * LANES + at]
            y = mm(jnp.concatenate(mats, axis=1), stacked(xp))
            y_ref[rows, tile] = y + skip_ref[0:1, tile] * xp.astype(F32)


def merge_kernel(
    nh,
    hops,
    at_ref,
    bc_ref,
    pack_ref,
    tot_ref,
    sf_ref,
    rb_ref,
    gpre_ref,
    gsuf_ref,
    yin_ref,
    gate_ref,
    dout_ref,
    mg_ref,
    ex_ref,
    *rest,
):
    arrived = rest[: 2 * hops]
    y_ref, stat_ref, full_ref, sent_ref, rent_ref = rest[2 * hops :]
    tb, width = y_ref.shape

    @pl.when(pl.program_id(0) == 0)
    def _():
        land_sides(at_ref, hops, arrived, sent_ref, rent_ref)

    lane = iota((SPAN, LANES), 1)
    row8 = iota((8, SPAN), 0)
    for j in range(tb // SPAN):
        rows = slice(j * SPAN, (j + 1) * SPAN)
        pack = pack_ref[rows, :]
        bc = bc_ref[rows, :].astype(F32)
        c = pltpu.roll(bc, HDIM, 1)[:, :HDIM].astype(BF16)
        w = split(target_weights(pack, tot_ref[j * 8 : j * 8 + 1, :], lane, nh), 1)
        energy = jnp.zeros((SPAN, LANES), F32)
        cross = jnp.zeros((SPAN, LANES), F32)
        for n, at, _ in groups(width):
            tile = slice(at, at + LANES)
            both = slice(2 * at, 2 * at + 2 * LANES)
            second = slice(2 * at + LANES, 2 * at + 2 * LANES)
            first = slice(2 * at, 2 * at + LANES)
            sfull = sf_ref[j, :, tile] + gpre_ref[j, 0:1, first] * sent_ref[:, tile]
            rfull = rb_ref[j, :, tile] + gsuf_ref[j, 0:1, second] * rent_ref[:, tile]
            held = jnp.concatenate([sfull.astype(BF16), rfull.astype(BF16)], axis=1)
            full_ref[j, :, both] = held
            seen = mm(c, held) * mm(w, ex_ref[:, both])
            y = (yin_ref[rows, tile] + seen[:, :LANES] + seen[:, LANES:]).astype(BF16)
            y_ref[rows, tile] = y
            gate = gate_ref[rows, tile].astype(F32)
            g = y.astype(F32) * gate * sigmoid(gate)
            energy = energy + g * g
            cross = cross + dout_ref[rows, tile].astype(F32) * mg_ref[0:1, tile] * g
        energy = jnp.sum(jnp.transpose(energy), axis=0, keepdims=True)
        cross = jnp.sum(jnp.transpose(cross), axis=0, keepdims=True)
        stat_ref[:, rows] = jnp.where(row8 == 0, energy, jnp.where(row8 == 1, cross, 0.0))


def turn_kernel(
    inner,
    shares,
    y_ref,
    gate_ref,
    dout_ref,
    mg_ref,
    act_ref,
    eye_ref,
    normed_ref,
    cot_ref,
    wo_ref,
    *rest,
):
    stats_in = rest[:shares]
    (
        aside_ref,
        outin_ref,
        dy_ref,
        dgate_ref,
        gmix_ref,
        gskip_ref,
        gout_ref,
        ggate_ref,
        gout,
        ggate,
    ) = rest[shares:]
    i = pl.program_id(0)
    tb, width = y_ref.shape
    model = normed_ref.shape[1]

    @pl.when(i == 0)
    def _():
        gmix_ref[...] = jnp.zeros_like(gmix_ref)
        gskip_ref[...] = jnp.zeros_like(gskip_ref)
        gout[...] = jnp.zeros_like(gout)
        ggate[...] = jnp.zeros_like(ggate)

    for j in range(tb // SPAN):
        rows = slice(j * SPAN, (j + 1) * SPAN)
        stat = stats_in[0][:, rows]
        for more in stats_in[1:]:
            stat = stat + more[:, rows]
        stat = exact_tn(stat, eye_ref[0:8, :])
        q = lax.rsqrt(stat[:, 0:1] * (1.0 / inner) + EPSILON)
        k3 = q * q * q * stat[:, 1:2] * (1.0 / inner)
        for n, at, _ in groups(width):
            tile = slice(at, at + LANES)
            y = y_ref[rows, tile].astype(F32)
            gate = gate_ref[rows, tile].astype(F32)
            sig = sigmoid(gate)
            sg = gate * sig
            g = y * sg
            gq = g * q
            dout = dout_ref[rows, tile].astype(F32)
            mg = mg_ref[0:1, tile]
            outin_ref[rows, tile] = (gq * mg).astype(BF16)
            gmix_ref[0:1, tile] += jnp.sum(dout * gq, axis=0, keepdims=True)
            dg = dout * mg * q - g * k3
            dyb = (dg * sg).astype(BF16)
            dy_ref[rows, tile] = dyb
            dgate_ref[rows, tile] = (dg * y * (sig + sg * (1.0 - sig))).astype(BF16)
            x = act_ref[rows, LANES + at : 2 * LANES + at].astype(F32)
            gskip_ref[0:1, tile] += jnp.sum(dyb.astype(F32) * x, axis=0, keepdims=True)

    for tile in wide_tiles(model):
        aside_ref[:, tile] = mm(outin_ref[:ASIDE, :], wo_ref[:, tile]).astype(BF16)
    for at in range(0, width, LANES):
        tile = slice(at, at + LANES)
        gout[tile, :] += mm_tn(outin_ref[:, tile], cot_ref[...])
    for at in range(0, model, LANES):
        tile = slice(at, at + LANES)
        ggate[tile, :] += mm_tn(normed_ref[:, tile], dgate_ref[...])

    @pl.when(i == pl.num_programs(0) - 1)
    def _():
        gout_ref[...] = gout[...].astype(BF16)
        ggate_ref[...] = ggate[...].astype(BF16)


def adjoint_kernel(
    nh,
    shares,
    hops,
    own,
    at_ref,
    act_ref,
    pack_ref,
    tot_ref,
    gates_ref,
    gtot_ref,
    ex_ref,
    dy_ref,
    outin_ref,
    wo_ref,
    *rest,
):
    pieces_out = rest[:shares]
    dso_ref, dro_ref, *messages, state, incf, wbuf, wides, cts = rest[shares:]
    i = pl.program_id(0)
    tb, width = dy_ref.shape
    model = wo_ref.shape[1]
    per = tb // SPAN
    nc = dso_ref.shape[0]
    lane = iota((SPAN, LANES), 1)

    @pl.when(i == 0)
    def _():
        state[...] = jnp.zeros_like(state)

    for j in range(per):
        rows = slice(j * SPAN, (j + 1) * SPAN)
        pack = pack_ref[rows, :]
        tot = tot_ref[j * 8 : j * 8 + 1, :]
        wbuf[rows, :] = split(target_weights(pack, tot, lane, nh), 1)
        cts[j * HDIM : (j + 1) * HDIM, :] = jnp.transpose(act_ref[rows, :].astype(F32))[
            HDIM:
        ].astype(BF16)
    for n, at, _ in groups(width):
        tile = slice(at, at + LANES)
        both = slice(2 * at, 2 * at + 2 * LANES)
        second = slice(2 * at + LANES, 2 * at + 2 * LANES)
        wides[...] = mm(wbuf[...], ex_ref[:, both])
        for j in range(per):
            rows = slice(j * SPAN, (j + 1) * SPAN)
            c = i * per + j
            dy = dy_ref[rows, tile].astype(F32)
            fed = jnp.concatenate(
                [
                    (dy * wides[rows, :LANES]).astype(BF16),
                    (dy * wides[rows, LANES:]).astype(BF16),
                ],
                axis=1,
            )
            inc = mm(cts[j * HDIM : (j + 1) * HDIM, :], fed)
            incf[c, :, tile] = inc[:, :LANES]
            dro_ref[j, :, tile] = state[:, tile]
            state[:, tile] = state[:, tile] * gates_ref[c, 0:1, second] + inc[:, LANES:]

    for k in range(shares):

        @pl.when((i * tb // own ^ at_ref[1]) == k)
        def _():
            for tile in wide_tiles(model):
                pieces_out[k][:, tile] = mm(outin_ref[ASIDE:, :], wo_ref[:, tile]).astype(BF16)

    @pl.when(i == pl.num_programs(0) - 1)
    def _():
        last_state = state[...]
        state[...] = jnp.zeros_like(state)

        def down(k, _):
            c = nc - 1 - k
            dso_ref[c] = state[...]
            for n, at, _ in groups(width):
                tile = slice(at, at + LANES)
                first = slice(2 * at, 2 * at + LANES)
                state[:, tile] = state[:, tile] * gates_ref[c, 0:1, first] + incf[c, :, tile]
            return 0

        lax.fori_loop(0, nc, down, 0)
        send_sides(
            at_ref,
            hops,
            jnp.concatenate([last_state, gtot_ref[:, width:]], axis=0),
            jnp.concatenate([state[...], gtot_ref[:, :width]], axis=0),
            messages,
        )


def mid_kernel(
    nh,
    act_ref,
    pack_ref,
    segrow_ref,
    rowa_ref,
    dy_ref,
    eye_ref,
    dx_ref,
    dbc_ref,
    pulls_ref,
    qbuf,
    places,
):
    tb, width = dx_ref.shape

    @pl.when(pl.program_id(0) == 0)
    def _():
        qbuf[...] = jnp.zeros_like(qbuf)
        spot_row = iota((4 * SPAN, LANES), 0) < 2 * SPAN
        spot_lane = iota((4 * SPAN, LANES), 1)
        for h in range(nh):
            up = jnp.where(spot_lane == nh + h, jnp.where(spot_row, -1.0, 1.0), 0.0)
            places[h] = jnp.where(spot_row & (spot_lane == h), 1.0, up).astype(BF16)

    s_at = iota((SPAN, SPAN), 0)
    t_at = iota((SPAN, SPAN), 1)
    lower = t_at > s_at
    lane = iota((SPAN, LANES), 1)
    front_half = lane < HDIM
    for j in range(tb // SPAN):
        rows = slice(j * SPAN, (j + 1) * SPAN)
        pack = pack_ref[rows, :]
        bc = act_ref[rows, :LANES].astype(F32)
        cb = pltpu.roll(bc, HDIM, 1)
        within = (pack[:, 36:37] == segrow_ref[0:1, rows]) & (t_at != s_at)
        score = mm_nt(bc[:, :HDIM].astype(BF16), cb[:, :HDIM].astype(BF16))
        score = jnp.where(within, score, 0.0)
        ldt = jnp.log(jnp.maximum(softplus(pltpu.roll(pack, LANES - 16, 1)), TINY))
        pc = jnp.where(lane < nh, pack - ldt, pack + ldt)
        dscore = jnp.zeros((SPAN, SPAN), F32)
        kc = jnp.zeros((SPAN, LANES), F32)
        for n, at, heads in groups(width):
            tile = slice(at, at + LANES)
            dyp = dy_ref[rows, tile]
            dmats = mm_nt(stacked(act_ref[rows, LANES + at : 2 * LANES + at]), dyp)
            mats = []
            for m, h in enumerate(heads):
                decay = jnp.exp(
                    jnp.where(
                        lower,
                        rowa_ref[h : h + 1, rows] - pc[:, h : h + 1],
                        pc[:, nh + h : nh + h + 1] - rowa_ref[nh + h : nh + h + 1, rows],
                    )
                )
                spot = dmats[m * SPAN : (m + 1) * SPAN, :] * decay
                dscore = dscore + spot
                mats.append((score * decay).astype(BF16))
                pull = spot * score
                pull_low = jnp.where(lower, pull, 0.0)
                down = jnp.sum(pull_low, axis=0, keepdims=True)
                qbuf[h : h + 1, :] = down
                qbuf[nh + h : nh + h + 1, :] = jnp.sum(pull, axis=0, keepdims=True) - down
                both = jnp.concatenate([split(pull_low, 1), split(pull, 1)], axis=1)
                kc = kc + mm(both, places[h])
            dx_ref[rows, tile] = mm(jnp.concatenate(mats, axis=1), stacked(dyp)).astype(BF16)
        dscore = jnp.where(within, dscore, 0.0).astype(BF16)
        cpad = jnp.where(front_half, cb, 0.0).astype(BF16)
        bpad = jnp.where(front_half, 0.0, cb).astype(BF16)
        dbc_ref[rows, :] = mm(dscore, cpad) + mm_tn(dscore, bpad)
        pulls_ref[rows, :] = kc + exact_tn(qbuf[...], eye_ref[...])


def back_kernel(
    nh,
    peers,
    hops,
    own,
    at_ref,
    act_ref,
    slope_ref,
    pack_ref,
    tot_ref,
    dy_ref,
    full_ref,
    dso_ref,
    dro_ref,
    gsuf_ref,
    gpre_ref,
    gates_ref,
    dxin_ref,
    dbc_ref,
    pulls_ref,
    uv_ref,
    uvh_ref,
    halocols_ref,
    taps_ref,
    skip_ref,
    pcol_ref,
    ex_ref,
    ext_ref,
    tril_ref,
    triu_ref,
    normed_ref,
    normh_ref,
    dgate_ref,
    wg_ref,
    wcat_ref,
    gmix_ref,
    gskip_ref,
    *rest,
):
    arrived = rest[: 2 * hops]
    mine_ref, theirs_ref, *chunks = rest[2 * hops : 2 * hops + 2 + peers]
    scratch = rest[2 * hops + 2 + peers :]
    dbuf, hbuf, dcat, acc, lines, dsent_ref, drent_ref, parts, wbuf, wides, pbuf, sums = scratch
    i = pl.program_id(0)
    last = pl.num_programs(0) - 1
    tb = act_ref.shape[0]
    width = act_ref.shape[1] - LANES
    model = normed_ref.shape[1]

    @pl.when(i == 0)
    def _():
        dbuf[tb : tb + 8, :] = jnp.zeros((8, LANES + width), F32)
        acc[...] = jnp.zeros_like(acc)
        lines[...] = jnp.zeros_like(lines)
        land_sides(at_ref, hops, arrived, drent_ref, dsent_ref)

    lane = iota((SPAN, LANES), 1)
    forward = lane < nh
    head_lane = lane < 16
    none = jnp.zeros((HDIM, 2 * LANES), BF16)
    per = tb // SPAN
    pair = 2 * LANES

    def part_of(kind, j):
        return slice((kind * per + j) * SPAN, (kind * per + j + 1) * SPAN)

    for j in range(per):
        rows = slice(j * SPAN, (j + 1) * SPAN)
        pack = pack_ref[rows, :]
        tot = tot_ref[j * 8 : j * 8 + 1, :]
        dt = softplus(pltpu.roll(pack, LANES - 16, 1))
        wbuf[part_of(0, j), :] = split(source_weights(pack, tot, dt, lane, nh), 1)
        wbuf[part_of(1, j), :] = split(target_weights(pack, tot, lane, nh), 1)
        dbuf[rows, :LANES] = dbc_ref[rows, :]
    for n, at, _ in groups(width):
        tile = slice(at, at + LANES)
        wtile = slice(LANES + at, 2 * LANES + at)
        both = slice(2 * at, 2 * at + 2 * LANES)
        first = slice(2 * at, 2 * at + LANES)
        second = slice(2 * at + LANES, 2 * at + 2 * LANES)
        wides[...] = mm(wbuf[...], ex_ref[:, both])
        for j in range(per):
            rows = slice(j * SPAN, (j + 1) * SPAN)
            bc = act_ref[rows, :LANES].astype(F32)
            b = bc[:, :HDIM].astype(BF16)
            c = pltpu.roll(bc, HDIM, 1)[:, :HDIM].astype(BF16)
            x = act_ref[rows, wtile].astype(F32)
            dy = dy_ref[rows, tile].astype(F32)
            x2 = jnp.concatenate([x, x], axis=1)
            dy2 = jnp.concatenate([dy, dy], axis=1)
            held = full_ref[j, :, both]
            dheld = jnp.concatenate(
                [
                    dso_ref[j, :, tile] + gsuf_ref[j, 0:1, first] * dsent_ref[:, tile],
                    dro_ref[j, :, tile] + gpre_ref[j, 0:1, second] * drent_ref[:, tile],
                ],
                axis=1,
            )
            dheld_low = dheld.astype(BF16)
            to_wide = wides[part_of(0, j), :]
            fro_wide = wides[part_of(1, j), :]
            flow = mm(b, dheld_low) * to_wide
            seen = mm(c, held) * fro_wide
            dbc = mm_nt((x2 * to_wide).astype(BF16), jnp.concatenate([dheld_low, none], axis=0))
            dbc = dbc + mm_nt((dy2 * fro_wide).astype(BF16), jnp.concatenate([none, held], axis=0))
            dbuf[rows, :LANES] += dbc
            pbuf[part_of(0, j), :] = split(dy2 * seen, 1)
            pbuf[part_of(1, j), :] = split(x2 * flow, 1)
            product = jnp.sum(dheld * held.astype(F32), axis=0, keepdims=True) * gates_ref[j, :, both]
            pbuf[2 * tb + 16 * j : 2 * tb + 16 * j + 16, :] = split(
                jnp.concatenate([product, product], axis=0), 1
            )
            dx = dxin_ref[rows, tile].astype(F32) + flow[:, :LANES] + flow[:, LANES:]
            dx = dx + skip_ref[0:1, tile] * dy
            dbuf[rows, wtile] = dx * slope_ref[rows, wtile].astype(F32)
        ext = ext_ref[both, :]
        found = mm(pbuf[:, :pair], ext) + mm(pbuf[:, pair:], ext)
        if n == 0:
            sums[...] = found
        else:
            sums[...] += found
    for j in range(per):
        rows = slice(j * SPAN, (j + 1) * SPAN)
        pack = pack_ref[rows, :]
        z = pltpu.roll(pack, LANES - 16, 1)
        dt = softplus(z)
        carried = sums[part_of(0, j), :]
        leaving = sums[part_of(1, j), :]
        through = sums[2 * tb + 16 * j : 2 * tb + 16 * j + 8, :]
        dbuf[rows, :LANES] = dbuf[rows, :LANES] * slope_ref[rows, :LANES].astype(F32)
        pulls = pulls_ref[rows, :]
        kc = jnp.where(head_lane, pulls, 0.0)
        moved = jnp.where(head_lane, pltpu.roll(pulls, LANES - 16, 1), 0.0) + carried - kc
        before = mm(tril_ref[:, : 2 * SPAN], split(jnp.where(forward, leaving, moved), 0))
        after = mm(triu_ref[:, : 2 * SPAN], split(jnp.where(forward, moved, leaving), 0))
        dlog = before + after - leaving + through[0:1, :]
        sigz = sigmoid(z)
        rate = pcol_ref[1:2, :]
        dstep = (kc + leaving) * (sigz / jnp.maximum(dt, TINY)) - dlog * rate * sigz
        dstep = jnp.where(head_lane, dstep, 0.0)
        dcat[rows, :LANES] = dstep.astype(BF16)
        lines[7:8, :LANES] += jnp.sum(dstep, axis=0, keepdims=True)
        ends = jnp.where(head_lane, -dlog * dt * rate, 0.0)
        lines[8:9, :LANES] += jnp.sum(ends, axis=0, keepdims=True)
    for j in range(per):
        rows = slice(j * SPAN, (j + 1) * SPAN)
        pack = pack_ref[rows, :]
        for at in range(0, LANES + width, LANES):
            tile = slice(at, at + LANES)
            dconv = dbuf[rows, tile]
            uv = uv_ref[rows, tile].astype(F32)
            du = taps_ref[0:1, tile] * dconv
            lines[1:2, tile] += jnp.sum(uv * dconv, axis=0, keepdims=True)
            for k in (1, 2, 3):
                shifted = dbuf[j * SPAN + k : (j + 1) * SPAN + k, tile] * pack[:, 40 + k : 41 + k]
                du = du + taps_ref[k : k + 1, tile] * shifted
                lines[1 + k : 2 + k, tile] += jnp.sum(uv * shifted, axis=0, keepdims=True)
            dcat[rows, LANES + at : 2 * LANES + at] = du.astype(BF16)

    edge = dbuf[0:8, :]
    dbuf[tb : tb + 8, :] = edge
    for tile in wide_tiles(model):
        part = mm_nt(dgate_ref[...], wg_ref[tile, :])
        part = part + mm_nt(dcat[...], wcat_ref[tile, :])
        parts[:, tile] = part.astype(BF16)
        normed = normed_ref[:, tile]
        lines[0:1, tile] += jnp.sum(part * normed.astype(F32), axis=0, keepdims=True)
        acc[tile, :] += mm_tn(normed, dcat[...])
    side = ((last - i) * tb // own ^ at_ref[1]) % 2

    @pl.when(side == 0)
    def _():
        mine_ref[0] = parts[...]

    @pl.when(side == 1)
    def _():
        theirs_ref[0] = parts[...]

    @pl.when(i == last)
    def _():
        taps_at = slice(0, LANES + width)
        hbuf[0:8, :] = jnp.zeros_like(edge)
        hbuf[8:16, :] = edge
        duh = jnp.zeros_like(edge)
        for k in (1, 2, 3):
            shifted = hbuf[k : k + 8, :] * halocols_ref[:, k - 1 : k]
            duh = duh + taps_ref[k : k + 1, :] * shifted
            lines[1 + k : 2 + k, taps_at] += jnp.sum(uvh_ref[...] * shifted, axis=0, keepdims=True)
        duh = duh.astype(BF16)
        normh = normh_ref[...]
        parth = mm_nt(duh, wcat_ref[:, LANES:])
        lines[0:1, :] += jnp.sum(parth * normh.astype(F32), axis=0, keepdims=True)
        skips = jnp.zeros((8, LANES), F32)
        for n, at, _ in groups(width):
            ext = ext_ref[2 * at : 2 * at + LANES, :]
            high = gskip_ref[:, at : at + LANES].astype(BF16)
            low = (gskip_ref[:, at : at + LANES] - high.astype(F32)).astype(BF16)
            skips = skips + mm(high, ext) + mm(low, ext)
        lines[5:6, :LANES] = skips[0:1, :]
        lines[6:7, :width] = gmix_ref[0:1, :]
        acc[:, LANES:] += mm_tn(normh, duh)
        placed = jnp.where(iota((16, LANES), 1) == iota((16, LANES), 0) + 16, 1.0, 0.0)
        acc[:, :LANES] += exact_tn(lines[...], placed)
        row8 = iota((8, LANES), 0)
        taken = iota((8, LANES), 1) == 19 + 3 * at_ref[0] + row8
        taken = taken & (row8 > 4) & (at_ref[0] > 0)
        acc[:, :LANES] += exact_tn(parth, jnp.where(taken, 1.0, 0.0))
        size = model // peers
        for k in range(peers):
            start = pl.multiple_of((at_ref[0] ^ k) * size, 8)
            chunks[k][...] = acc[pl.ds(start, size), :].astype(BF16)


def finish_kernel(nh, peers, shares, at_ref, *refs):
    chunks = refs[:peers]
    eye_ref, ingain_ref, x_ref, cot_ref, kept_ref, got_ref = refs[peers : peers + 6]
    gain_ref, value_ref, state_ref, step_ref, bias_ref, decay_ref = refs[peers + 6 : peers + 12]
    convv_ref, convs_ref, skip_ref, mixer_ref, tokens_ref, extra = refs[peers + 12 :]
    size = chunks[0].shape[0]
    real_width = value_ref.shape[1]
    heads = step_ref.shape[0]
    for k in range(peers):
        rows = pl.ds(pl.multiple_of((at_ref[0] ^ k) * size, 8), size)
        extra[rows, :] = chunks[k][:, :LANES].astype(F32)
        state_ref[rows, :] = chunks[k][:, LANES : 2 * LANES].astype(F32)
        value_ref[rows, :] = chunks[k][:, 2 * LANES : 2 * LANES + real_width].astype(F32)
    found = extra[...].astype(BF16)
    lines = mm_nt(eye_ref[...], found)
    row16 = iota((16, LANES), 0)
    taken = iota((16, LANES), 1) == 27 + 3 * at_ref[0] + row16 - 13
    taken = taken & (row16 > 12) & (at_ref[1] == shares - 1)
    late = mm_nt(jnp.where(taken, 1.0, 0.0).astype(BF16), found)

    def token_rows(rows, more):
        x = x_ref[rows, :].astype(F32)
        s = lax.rsqrt(jnp.mean(x * x, axis=1, keepdims=True) + EPSILON)
        dn = kept_ref[0, rows, :] + got_ref[0, rows, :].astype(F32) + more
        scaled = dn * ingain_ref[...]
        inside = jnp.mean(scaled * x, axis=1, keepdims=True)
        cot = cot_ref[rows, :].astype(F32)
        tokens_ref[rows, :] = (cot + s * scaled - x * (s * s * s) * inside).astype(BF16)

    own = x_ref.shape[0]
    for at in range(0, own, 32):
        token_rows(slice(at, at + 32), 0.0)
    token_rows(slice(own - 16, own), late)
    for h in range(heads):
        step_ref[h, 0:1, :] = lines[h : h + 1, :]
        step_ref[h, 1:2, :] = lines[nh + h : nh + h + 1, :]
    gain_ref[...] = (lines[16:17, :] / ingain_ref[...])[0]
    convs_ref[...] = lines[17:21, :LANES]
    convv_ref[...] = lines[17:21, LANES : LANES + real_width]
    skip_ref[...] = lines[21:22, :heads]
    mixer_ref[...] = lines[22, :real_width]
    bias_ref[0:1, :] = lines[23:24, :heads]
    bias_ref[1:2, :] = lines[23:24, nh : nh + heads]
    decay_ref[...] = lines[24:25, :heads] + lines[24:25, nh : nh + heads]


def whole(shape):
    return pl.BlockSpec(shape, lambda i, *_: (0,) * len(shape))


def row_block(rows, width):
    return pl.BlockSpec((rows, width), lambda i, *_: (i, 0))


def lane_block(rows, width):
    return pl.BlockSpec((rows, width), lambda i, *_: (0, i))


def chunk_block(per, rows, width):
    return pl.BlockSpec((per, rows, width), lambda i, *_: (i, 0, 0))


def sds(shape, dtype):
    return jax.ShapeDtypeStruct(shape, dtype)


def call(kernel, name, grid, ins, outs, scratch, flops, operands, scalars=()):
    return pl.pallas_call(
        kernel,
        name=name,
        grid_spec=pltpu.PrefetchScalarGridSpec(
            num_scalar_prefetch=len(scalars),
            grid=(grid,),
            in_specs=ins,
            out_specs=[spec for spec, _ in outs],
            scratch_shapes=scratch,
        ),
        out_shape=[shape for _, shape in outs],
        compiler_params=pltpu.CompilerParams(
            dimension_semantics=("arbitrary",), vmem_limit_bytes=56 * 1024 * 1024
        ),
        cost_estimate=pl.CostEstimate(
            flops=int(flops), bytes_accessed=1, transcendentals=0
        ),
    )(*scalars, *operands)


def shifted_in(array, axis, by):
    length = lax.axis_size(axis)
    pairs = [(i, i + by) for i in range(length) if 0 <= i + by < length]
    return lax.ppermute(array, axis, pairs)


def exchange_sides(messages, hops):
    size = lax.axis_size("seq")
    arrived = []
    for d in range(1, hops + 1):
        for side in (0, 1):
            pairs = [(i, i + d) for i in range(size - d) if (i // d) % 2 == side]
            both = pairs + [(b, a) for a, b in pairs]
            arrived.append(lax.ppermute(messages[len(arrived)], "seq", both))
    return arrived


def swap(array, axis, k):
    n = lax.axis_size(axis)
    return lax.ppermute(array, axis, [(i, i ^ k) for i in range(n)])


def sum_over(array, axis):
    rounded = lax.reduce_precision(array, 8, 7)
    message = rounded.astype(BF16)
    terms = [rounded]
    for k in range(1, lax.axis_size(axis)):
        terms.append(swap(message, axis, k).astype(F32))
    while len(terms) > 1:
        terms = [a + b for a, b in zip(terms[::2], terms[1::2])]
    return terms[0]


def per_device(
    tokens,
    input_gain,
    proj_gate,
    proj_value,
    proj_state,
    proj_step,
    step_bias,
    decay_log,
    conv_value,
    conv_state,
    skip_gain,
    mixer_gain,
    proj_out,
    doc_lengths,
    pad_mask,
    cotangent,
):
    head_devices = lax.axis_size("head")
    length = pad_mask.shape[0]
    model = tokens.shape[1]
    real_width = proj_gate.shape[1]
    real_heads = proj_step.shape[2]
    inner = real_width * head_devices
    width = -(-real_width // LANES) * LANES
    nh = width // HDIM

    def padded(array, axis, size):
        if array.shape[axis] == size:
            return array
        widths = [(0, 0)] * array.ndim
        widths[axis] = (0, size - array.shape[axis])
        return jnp.pad(array, widths)

    proj_gate = padded(proj_gate, 1, width)
    proj_value = padded(proj_value, 1, width)
    proj_step = padded(proj_step, 2, nh)
    step_bias = padded(step_bias, 1, nh)
    conv_value = padded(conv_value, 1, width)
    skip_gain = padded(skip_gain, 0, nh)
    mixer_gain = padded(mixer_gain, 0, width)
    proj_out = padded(proj_out, 0, width)
    nc = length // SPAN
    tb = BLOCK
    per = tb // SPAN
    grid = length // tb
    wide = LANES + width
    hops = -(-(LONGEST - 1) // length)
    seq_index = lax.axis_index("seq")
    first_place = seq_index * length
    all_tokens = length * lax.axis_size("seq")

    edge_rows = shifted_in(tokens[tokens.shape[0] - 8 :], "seq", 1)
    here = lax.axis_index("head")
    halo = jnp.where(here == head_devices - 1, edge_rows, 0)
    for k in range(1, head_devices):
        halo = halo + jnp.where(here ^ k == head_devices - 1, swap(edge_rows, "head", k), 0)

    offsets = jnp.cumsum(doc_lengths) - doc_lengths
    room = -(-(offsets.shape[0] + 1) // LANES) * LANES - offsets.shape[0]
    fill = jnp.where(jnp.arange(room) == 0, all_tokens, 2 * all_tokens).astype(offsets.dtype)
    offsets = jnp.concatenate([offsets, fill])[None, :]
    live_row = pad_mask[None, :]
    lanes = np.arange(LANES)
    column = np.arange(2 * width)
    head_of = column // (2 * LANES) * 2 + column % LANES // HDIM
    head_of = head_of + np.where(column % (2 * LANES) >= LANES, nh, 0)
    ext = jnp.asarray(head_of[:, None] == lanes[None, :], BF16)
    ex = jnp.asarray(np.tile(head_of[None, :] == lanes[:, None], (2, 1)), BF16)
    at = np.arange(SPAN)
    tril = jnp.asarray(np.tile(at[:, None] >= at[None, :], (1, 3)), BF16)
    triu = at[:, None] <= at[None, :]
    triu_wide = jnp.asarray(np.tile(triu, (1, 2)), BF16)
    triu_tall = jnp.asarray(np.tile(triu, (3, 1)), BF16)
    eye = jnp.asarray(np.arange(16)[:, None] == lanes[None, :], F32)
    eye16 = jnp.asarray(np.arange(16)[:, None] + 16 == lanes[None, :], F32)
    picked = jnp.asarray(np.arange(32)[:, None] == lanes[None, :], BF16)
    peers = lax.axis_size("seq")
    own = length // head_devices
    bits = head_devices.bit_length() - 1
    scalars = [jnp.stack([seq_index, here, first_place]).astype(jnp.int32)]
    size = model // peers

    rate = padded(jnp.exp(decay_log), 0, nh)
    gap = 16 - 2 * nh
    bias16 = jnp.pad(step_bias.reshape(-1), (0, gap))
    rate16 = jnp.pad(jnp.concatenate([rate, rate]), (0, gap))
    prow = jnp.stack([bias16, rate16], axis=1)
    wide_bias = jnp.pad(jnp.concatenate([bias16, bias16]), (0, LANES - 32))
    pcol = jnp.stack([wide_bias, jnp.pad(rate16, (0, LANES - 16))], axis=0)
    steps = jnp.concatenate([proj_step[0], proj_step[1]], axis=1)
    steps = jnp.pad(steps, ((0, 0), (0, gap)))
    wst = jnp.pad(jnp.concatenate([steps, steps], axis=1), ((0, 0), (0, LANES - 32)))
    wstr = steps.T
    taps = jnp.concatenate([conv_state, conv_value], axis=1)
    gain = input_gain[None, :]
    mg = mixer_gain[None, :]
    skip = jnp.repeat(skip_gain, HDIM)[None, :]
    pieces_of = {0: tokens}
    for bit in [1 << b for b in range(bits - 1, 0, -1)]:
        pieces_of.update({k | bit: swap(v, "head", bit) for k, v in pieces_of.items()})
    wcat = jnp.concatenate([wst, proj_state, proj_value], axis=1)
    prelims = (halo, offsets, live_row, pcol, prow, wst, wstr, taps, wcat)
    pieces_of, late, prelims, scalars = lax.optimization_barrier(
        (pieces_of, cotangent, prelims, scalars)
    )
    halo, offsets, live_row, pcol, prow, wst, wstr, taps, wcat = prelims
    pieces_of.update({k | 1: swap(v, "head", 1) for k, v in pieces_of.items()})
    token_pieces = [pieces_of[k] for k in range(head_devices)]
    cot_all = lax.all_gather(late, "head", axis=0, tiled=True)

    rows = partial(row_block, tb)
    states = sds((nc, HDIM, width), F32)
    gates_of = sds((nc, 8, 2 * width), F32)
    message = sds((HDIM + 8, width), F32)
    state_block = chunk_block(per, HDIM, width)
    gate_block = chunk_block(per, 8, 2 * width)
    tot_block = row_block(per * 8, LANES)
    messages = [(whole(message.shape), message)] * (2 * hops)

    def sized(block):
        return (
            length // block,
            partial(row_block, block),
            partial(lane_block, width=block),
            partial(chunk_block, block // SPAN),
            row_block(block // SPAN * 8, LANES),
        )

    def slot_of(j, at):
        place = j ^ at[1]
        return sum(((place >> b) & 1) << (bits - 1 - b) for b in range(bits))

    each = own // tb

    def piece_block(k):
        def index(i, at):
            return jnp.clip(i - (at[1] ^ k) * each, 0, each - 1), 0

        return pl.BlockSpec((tb, model), index)

    def side_block(side):
        def index(i, at):
            row = grid - 1 - i
            j, sub = row // each, row % each
            ours = (j ^ at[1]) % 2 == side
            first = j == head_devices - 1
            j = jnp.where(ours, j, jnp.where(first, j - 1, j + 1))
            sub = jnp.where(ours, sub, jnp.where(first, each - 1, 0))
            return slot_of(j, at) % (head_devices // 2), sub, 0

        return pl.BlockSpec((1, tb, model), index)

    (
        normed,
        normh,
        gate_in,
        acted,
        slope,
        uv,
        uvh,
        pack,
        rowa,
        rowp,
        seg_row,
        halo_cols,
        tot,
        sf,
        rb,
        gates,
        gpre,
        gsuf,
        gtot,
        *ahead,
    ) = call(
        partial(front_kernel, nh, hops, head_devices, own),
        "front",
        grid,
        [piece_block(k) for k in range(head_devices)]
        + [
            whole((8, model)),
            whole((1, model)),
            whole((model, width)),
            whole((model, LANES)),
            whole((model, width)),
            whole((model, LANES)),
            whole((16, model)),
            whole((2, LANES)),
            whole((16, 2)),
            whole((4, wide)),
            whole(offsets.shape),
            lane_block(1, tb),
            whole(ex.shape),
            whole(tril.shape),
            whole(triu_tall.shape),
        ],
        [
            (rows(model), sds((length, model), BF16)),
            (whole((8, model)), sds((8, model), BF16)),
            (rows(width), sds((length, width), BF16)),
            (rows(wide), sds((length, wide), BF16)),
            (rows(wide), sds((length, wide), BF16)),
            (rows(wide), sds((length, wide), BF16)),
            (whole((8, wide)), sds((8, wide), F32)),
            (rows(LANES), sds((length, LANES), F32)),
            (lane_block(16, tb), sds((16, length), F32)),
            (lane_block(16, tb), sds((16, length), F32)),
            (lane_block(8, tb), sds((8, length), F32)),
            (whole((8, LANES)), sds((8, LANES), F32)),
            (tot_block, sds((nc * 8, LANES), F32)),
            (state_block, states),
            (whole(states.shape), states),
            (whole(gates_of.shape), gates_of),
            (whole(gates_of.shape), gates_of),
            (whole(gates_of.shape), gates_of),
            (whole((8, 2 * width)), sds((8, 2 * width), F32)),
        ]
        + messages,
        [
            pltpu.VMEM((tb + 8, wide), F32),
            pltpu.VMEM((HDIM, width), F32),
            pltpu.VMEM((nc, HDIM, width), F32),
            pltpu.VMEM((tb, LANES), F32),
            pltpu.VMEM((per * 8, LANES), F32),
            pltpu.VMEM((SPAN + 16, LANES), F32),
            pltpu.VMEM((tb + 16 * per, 2 * LANES), BF16),
            pltpu.VMEM((tb + 16 * per, 2 * LANES), F32),
            pltpu.VMEM((per * HDIM, LANES), BF16),
        ],
        25e9,
        token_pieces
        + [
            halo,
            gain,
            proj_gate,
            proj_state,
            proj_value,
            wst,
            wstr,
            pcol,
            prow,
            taps,
            offsets,
            live_row,
            ex,
            tril,
            triu_tall,
        ],
        scalars,
    )

    ahead = exchange_sides(ahead, hops)

    big_grid, big_rows, big_lanes, big_chunks, big_tot = sized(512)
    yin, dout = call(
        partial(inner_kernel, nh),
        "inner",
        big_grid,
        [
            big_rows(wide),
            big_rows(LANES),
            big_lanes(8),
            big_lanes(16),
            whole((1, width)),
            big_rows(model),
            whole((width, model)),
        ],
        [
            (big_rows(width), sds((length, width), F32)),
            (big_rows(width), sds((length, width), BF16)),
        ],
        [],
        6e9,
        [acted, pack, seg_row, rowp, skip, cot_all, proj_out],
    )

    y, stat, full = call(
        partial(merge_kernel, nh, hops),
        "merge",
        big_grid,
        [
            big_rows(LANES),
            big_rows(LANES),
            big_tot,
            big_chunks(HDIM, width),
            big_chunks(HDIM, width),
            big_chunks(8, 2 * width),
            big_chunks(8, 2 * width),
            big_rows(width),
            big_rows(width),
            big_rows(width),
            whole((1, width)),
            whole(ex.shape),
        ]
        + [whole(message.shape)] * (2 * hops),
        [
            (big_rows(width), sds((length, width), BF16)),
            (big_lanes(8), sds((8, length), F32)),
            (big_chunks(HDIM, 2 * width), sds((nc, HDIM, 2 * width), BF16)),
        ],
        [pltpu.VMEM((HDIM, width), F32)] * 2,
        6e9,
        [acted, pack, tot, sf, rb, gpre, gsuf, yin, gate_in, dout, mg, ex] + ahead,
        scalars,
    )

    shares = [stat]
    for k in range(1, head_devices):
        shares.append(lax.ppermute(stat, "head", [(i, i ^ k) for i in range(head_devices)]))

    aside, outin, dy, dgate, gmix, gskip, gout, ggate = call(
        partial(turn_kernel, inner, head_devices),
        "turn",
        grid,
        [
            rows(width),
            rows(width),
            rows(width),
            whole((1, width)),
            rows(wide),
            whole((16, LANES)),
            rows(model),
            rows(model),
            whole((width, model)),
        ]
        + [lane_block(8, tb)] * head_devices,
        [
            (row_block(ASIDE, model), sds((head_devices * ASIDE, model), BF16)),
            (rows(width), sds((length, width), BF16)),
            (rows(width), sds((length, width), BF16)),
            (rows(width), sds((length, width), BF16)),
            (whole((8, width)), sds((8, width), F32)),
            (whole((8, width)), sds((8, width), F32)),
            (whole((width, model)), sds((width, model), BF16)),
            (whole((model, width)), sds((model, width), BF16)),
        ],
        [pltpu.VMEM((width, model), F32), pltpu.VMEM((model, width), F32)],
        4e9,
        [y, gate_in, dout, mg, acted, eye, normed, cot_all, proj_out] + shares,
    )
    outs = call(
        partial(adjoint_kernel, nh, head_devices, hops, own),
        "adjoint",
        grid,
        [
            rows(LANES),
            rows(LANES),
            tot_block,
            whole(gates_of.shape),
            whole((8, 2 * width)),
            whole(ex.shape),
            rows(width),
            rows(width),
            whole((width, model)),
        ],
        [(whole((own - ASIDE, model)), sds((own - ASIDE, model), BF16))] * head_devices
        + [
            (whole(states.shape), states),
            (state_block, states),
        ]
        + messages,
        [
            pltpu.VMEM((HDIM, width), F32),
            pltpu.VMEM((nc, HDIM, width), F32),
            pltpu.VMEM((tb, 2 * LANES), BF16),
            pltpu.VMEM((tb, 2 * LANES), F32),
            pltpu.VMEM((per * HDIM, LANES), BF16),
        ],
        1e8,
        [acted, pack, tot, gates, gtot, ex, dy, outin, proj_out],
        scalars,
    )
    mixers = outs[:head_devices]
    dso, dro, *behind = outs[head_devices:]

    grad_proj_out, grad_proj_gate = lax.psum((gout, ggate), "seq")
    aside = lax.psum_scatter(aside, "head", scatter_dimension=0, tiled=True)
    behind = exchange_sides(behind, hops)
    mixer_shares = [mixers[0]] + [swap(mixers[k], "head", k) for k in range(1, head_devices)]

    mid_grid, mid_rows, mid_lanes, *_ = sized(256)
    dxin, dbc, pulls = call(
        partial(mid_kernel, nh),
        "mid",
        mid_grid,
        [
            mid_rows(wide),
            mid_rows(LANES),
            mid_lanes(8),
            mid_lanes(16),
            mid_rows(width),
            whole((16, LANES)),
        ],
        [
            (mid_rows(width), sds((length, width), BF16)),
            (mid_rows(LANES), sds((length, LANES), F32)),
            (mid_rows(LANES), sds((length, LANES), F32)),
        ],
        [pltpu.VMEM((16, SPAN), F32), pltpu.VMEM((nh, 4 * SPAN, LANES), BF16)],
        1e8,
        [acted, pack, seg_row, rowa, dy, eye16],
    )

    back = lambda i: grid - 1 - i

    def rev(spec):
        return pl.BlockSpec(spec.block_shape, lambda i, *_: spec.index_map(back(i)))

    mine, theirs, *chunks = call(
        partial(back_kernel, nh, peers, hops, own),
        "back",
        grid,
        [
            rev(rows(wide)),
            rev(rows(wide)),
            rev(rows(LANES)),
            rev(tot_block),
            rev(rows(width)),
            rev(chunk_block(per, HDIM, 2 * width)),
            rev(state_block),
            rev(state_block),
            rev(gate_block),
            rev(gate_block),
            rev(gate_block),
            rev(rows(width)),
            rev(rows(LANES)),
            rev(rows(LANES)),
            rev(rows(wide)),
            whole((8, wide)),
            whole((8, LANES)),
            whole((4, wide)),
            whole((1, width)),
            whole((2, LANES)),
            whole(ex.shape),
            whole(ext.shape),
            whole(tril.shape),
            whole(triu_wide.shape),
            rev(rows(model)),
            whole((8, model)),
            rev(rows(width)),
            whole((model, width)),
            whole((model, LANES + wide)),
            whole((8, width)),
            whole((8, width)),
        ]
        + [whole(message.shape)] * (2 * hops),
        [
            (side_block(0), sds((head_devices // 2, own, model), BF16)),
            (side_block(1), sds((head_devices // 2, own, model), BF16)),
        ]
        + [(whole((size, LANES + wide)), sds((size, LANES + wide), BF16))] * peers,
        [
            pltpu.VMEM((tb + 8, wide), F32),
            pltpu.VMEM((16, wide), F32),
            pltpu.VMEM((tb, LANES + wide), BF16),
            pltpu.VMEM((model, LANES + wide), F32),
            pltpu.VMEM((16, model), F32),
            pltpu.VMEM((HDIM, width), F32),
            pltpu.VMEM((HDIM, width), F32),
            pltpu.VMEM((tb, model), BF16),
            pltpu.VMEM((2 * tb, 2 * LANES), BF16),
            pltpu.VMEM((2 * tb, 2 * LANES), F32),
            pltpu.VMEM((2 * tb + 16 * per, 4 * LANES), BF16),
            pltpu.VMEM((2 * tb + 16 * per, LANES), F32),
        ],
        1e8,
        [
            acted,
            slope,
            pack,
            tot,
            dy,
            full,
            dso,
            dro,
            gsuf,
            gpre,
            gates,
            dxin,
            dbc,
            pulls,
            uv,
            uvh,
            halo_cols,
            taps,
            skip,
            pcol,
            ex,
            ext,
            tril,
            triu_wide,
            normed,
            normh,
            dgate,
            proj_gate,
            wcat,
            gmix,
            gskip,
        ]
        + behind,
        scalars,
    )

    chunks, theirs, mixer_shares = lax.optimization_barrier((chunks, theirs, mixer_shares))
    got = swap(theirs, "head", 1)
    summed = chunks[0].astype(F32)
    for k in range(1, peers):
        summed = summed + swap(chunks[k], "seq", k).astype(F32)
    shared = summed[:, : 2 * LANES]
    row_at = seq_index * size + jnp.arange(size)[:, None]
    lane_at = jnp.arange(2 * LANES)[None, :]
    common = (lane_at == 16) | (lane_at > 26)
    common = common | ((lane_at > 16) & (lane_at < 21) & (row_at < LANES))
    shared = jnp.where(common, sum_over(shared, "head"), shared)

    half = head_devices // 4
    own_in = mine[:half].astype(F32) + got[:half].astype(F32)
    going = (mine[half:].astype(F32) + got[half:].astype(F32)).astype(BF16)
    for b in range(1, bits):
        if b == 1:
            going, shared = lax.optimization_barrier((going, shared))
        got = swap(going, "head", 1 << b)
        if b < bits - 1:
            half = half // 2
            going = (own_in[half:] + got[half:].astype(F32)).astype(BF16)
            own_in = own_in[:half] + got[:half].astype(F32)

    reduced = jnp.concatenate([shared, summed[:, 2 * LANES :]], axis=1).astype(BF16)
    spread_out = [reduced] + [swap(reduced, "seq", k) for k in range(1, peers)]
    spread_out[2], grad_proj_out, grad_proj_gate, mixer_shares = lax.optimization_barrier(
        (spread_out[2], grad_proj_out, grad_proj_gate, mixer_shares)
    )
    grad_proj_out = grad_proj_out[:real_width].astype(F32)
    grad_proj_gate = grad_proj_gate[:, :real_width].astype(F32)
    mixer = sum(share.astype(F32) for share in mixer_shares)
    mixer = jnp.concatenate([aside.astype(F32), mixer], axis=0)
    layer_out = (tokens.astype(F32) + mixer).astype(BF16)
    spread_out, layer_out, grad_proj_out, grad_proj_gate = lax.optimization_barrier(
        (spread_out, layer_out, grad_proj_out, grad_proj_gate)
    )

    finals = [
        sds((model,), F32),
        sds((model, real_width), F32),
        sds((model, LANES), F32),
        sds((real_heads, 2, model), F32),
        sds((2, real_heads), F32),
        sds((1, real_heads), F32),
        sds((4, real_width), F32),
        sds((4, LANES), F32),
        sds((1, real_heads), F32),
        sds((real_width,), F32),
        sds((own, model), BF16),
    ]
    ggain, gvalue, gstate, gstep, gbias, gdecay, gconvv, gconvs, gskips, gmixer, grad_tokens = call(
        partial(finish_kernel, nh, peers, head_devices),
        "finish",
        1,
        [whole((size, LANES + wide))] * peers
        + [whole((32, LANES)), whole((1, model))]
        + [whole((own, model))] * 2
        + [whole((1, own, model))] * 2,
        [(whole(f.shape), f) for f in finals],
        [pltpu.VMEM((model, LANES), F32)],
        3e9,
        spread_out
        + [picked, input_gain[None, :]]
        + [tokens, cotangent, own_in, got],
        scalars,
    )
    return (
        layer_out,
        grad_tokens,
        ggain,
        grad_proj_gate,
        gvalue,
        gstate,
        jnp.transpose(gstep, (1, 2, 0)),
        gbias,
        gdecay[0],
        gconvv,
        gconvs,
        gskips[0],
        gmixer,
        grad_proj_out,
    )


def solution(mesh):
    return jax.shard_map(
        per_device,
        mesh=mesh,
        in_specs=(
            P(("seq", "head"), None),
            P(),
            P(None, "head"),
            P(None, "head"),
            P(),
            P(None, None, "head"),
            P(None, "head"),
            P("head"),
            P(None, "head"),
            P(),
            P("head"),
            P("head"),
            P("head", None),
            P(),
            P("seq"),
            P(("seq", "head"), None),
        ),
        out_specs=(
            P(("seq", "head"), None),
            P(("seq", "head"), None),
            P(),
            P(None, "head"),
            P(None, "head"),
            P(),
            P(None, None, "head"),
            P(None, "head"),
            P("head"),
            P(None, "head"),
            P(),
            P("head"),
            P("head"),
            P("head", None),
        ),
        check_vma=False,
    )
```
